32 devices in a mesh: dp: 8 (over y, x, core), tensor: 4 (over z).
Axes of the slice: x: 2, y: 2, z: 4, core: 2. Of those that a mesh axis runs over, the one named last changes fastest.
Arguments:
- tokens: bfloat16 [8192, 2048], P(('dp', 'tensor')), may hold values from -6 to 6
- gain_in: float32 [2048], replicated, may hold values from 0.1 to 1.9
- w_query: bfloat16 [2048, 2048], P(None, 'tensor'), may hold values from -0.125 to 0.125
- w_key: bfloat16 [2048, 2048], P(None, 'tensor'), may hold values from -0.125 to 0.125
- w_value: bfloat16 [2048, 2048], P(None, 'tensor'), may hold values from -0.125 to 0.125
- w_alpha: bfloat16 [2048, 16], P(None, 'tensor'), may hold values from -0.125 to 0.125
- w_beta: bfloat16 [2048, 16], P(None, 'tensor'), may hold values from -0.125 to 0.125
- w_gate_out: bfloat16 [2048, 2048], P(None, 'tensor'), may hold values from -0.125 to 0.125
- conv_query: float32 [4, 2048], P(None, 'tensor'), may hold values from -3 to 3
- conv_key: float32 [4, 2048], P(None, 'tensor'), may hold values from -3 to 3
- conv_value: float32 [4, 2048], P(None, 'tensor'), may hold values from -3 to 3
- decay_log: float32 [16], P('tensor'), may hold values from -7.5 to -1.5
- decay_bias: float32 [16], P('tensor'), may hold values from -1 to 1
- head_gain: float32 [2048], P('tensor'), may hold values from 0.1 to 1.9
- w_out: bfloat16 [2048, 2048], P('tensor'), may hold values from -0.1875 to 0.1875
- gain_mid: float32 [2048], replicated, may hold values from 0.1 to 1.9
- w_gate: bfloat16 [2048, 5632], P(None, 'tensor'), may hold values from -0.125 to 0.125
- w_up: bfloat16 [2048, 5632], P(None, 'tensor'), may hold values from -0.125 to 0.125
- w_down: bfloat16 [5632, 2048], P('tensor'), may hold values from -0.15625 to 0.15625
- out_grad: bfloat16 [8192, 2048], P('dp'), may hold values from -6 to 6
- doc_lengths: int32 [1, 4], replicated, may hold values from 1 to 4608, as said below
Outputs:
- output: bfloat16 [8192, 2048], P(('dp', 'tensor'))
- input_grad: float32 [8192, 2048], P(('dp', 'tensor'))
- gain_in_grad: float32 [2048], replicated
- w_query_grad: float32 [2048, 2048], P('dp', 'tensor')
- w_key_grad: float32 [2048, 2048], P('dp', 'tensor')
- w_value_grad: float32 [2048, 2048], P('dp', 'tensor')
- w_alpha_grad: float32 [2048, 16], P('dp', 'tensor')
- w_beta_grad: float32 [2048, 16], P('dp', 'tensor')
- w_gate_out_grad: float32 [2048, 2048], P('dp', 'tensor')
- conv_query_grad: float32 [4, 2048], replicated
- conv_key_grad: float32 [4, 2048], replicated
- conv_value_grad: float32 [4, 2048], replicated
- decay_log_grad: float32 [16], replicated
- decay_bias_grad: float32 [16], replicated
- head_gain_grad: float32 [2048], replicated
- w_out_grad: float32 [2048, 2048], P('tensor', 'dp')
- gain_mid_grad: float32 [2048], replicated
- w_gate_grad: float32 [2048, 5632], P('dp', 'tensor')
- w_up_grad: float32 [2048, 5632], P('dp', 'tensor')
- w_down_grad: float32 [5632, 2048], P('tensor', 'dp')
The draws below stay inside these ranges and needn't reach their ends.
Inputs may be any that keep to these rules, and one draw needn't show every extreme that they name: `doc_lengths`: each row holds the lengths of the 4 documents of one packed sequence in order; a row sums to 8192, and its longest document has exactly 4608 tokens.
All inputs are finite; a program needn't handle non-finite values.
Results may differ from the reference program's by a relative error of at most 0.013.
The reference program's roundings to bfloat16 on the way count: a program that leaves them out, or rounds other values in their place, can miss the bound.
Values may be sent and summed in bfloat16 or wider, within the bound.
A program may use at most 256 MiB of HBM per device.

```python
import math
from functools import partial
import jax
import jax.numpy as jnp
from jax import lax

D = 2048
HEADS = 16
FF = 5632
CONV = 4
BLOCK = 64
DOCS = 4
TOK_DEV = 1024
KEYS = 2048
SEQ = 8192
MOST = 4608
TOKENS = 8192


def draw_doc_lengths(key, part):
    pieces = SEQ // TOK_DEV
    half = pieces // 2
    pick_key = jax.random.fold_in(key, 11)
    offset_key = jax.random.fold_in(key, 23)
    candidates = jax.random.permutation(pick_key, pieces - half - 1) + half + 1
    chosen = jnp.sort(candidates[:DOCS - 2])
    offsets = jax.random.randint(offset_key, (DOCS - 2,), 1, TOK_DEV)
    bounds = jnp.concatenate([jnp.array([0, MOST], jnp.int32), (chosen * TOK_DEV + offsets).astype(jnp.int32), jnp.array([SEQ], jnp.int32)])
    lengths = bounds[1:] - bounds[:-1]
    return lengths.reshape(1, DOCS).astype(jnp.int32)


def spiked(values, key, source, target, blocks, factor):
    owner, partner = [(jnp.arange(values.shape[dim]) // (values.shape[dim] // blocks)).reshape([-1 if axis == dim else 1 for axis in range(values.ndim)]) for dim in (source, target)]
    chosen = jax.random.permutation(key, blocks)[partner]
    strong = (owner == chosen) | (owner == (partner + blocks // 2) % blocks)
    return jnp.where(strong, factor * values, values)


def shard_levels(rng, dims, cuts, low, largest):
    level, own = 1.0, jax.random.fold_in(rng, 6)
    for axis_at, blocks in cuts:
        steps = jnp.exp(jax.random.uniform(jax.random.fold_in(own, axis_at), (blocks,), jnp.float32, low / len(cuts), largest / len(cuts)))
        level = level * jnp.repeat(steps, dims[axis_at] // blocks).reshape([-1 if axis == axis_at else 1 for axis in range(len(dims))])
    return level


def bell_draw(rng, dims, width, reach, shards=(), held_as=jnp.bfloat16):
    entries = width * jax.random.normal(rng, dims, jnp.float32)
    if shards:
        entries = entries * shard_levels(rng, dims, shards, -0.22, 0.18)
    return jnp.clip(entries, -reach, reach).astype(held_as)


def noise_with(key, extent, scale, most, cuts, heavy, held_as=jnp.bfloat16):
    entries = scale * jax.random.normal(key, extent, jnp.float32)
    if cuts:
        entries = entries * shard_levels(key, extent, cuts, -0.22, 0.18)
    return jnp.clip(spiked(entries, jax.random.fold_in(key, 3), *heavy), -most, most).astype(held_as)


def setup_inputs(seed: int = 0) -> dict:
    streams_of = jax.random.split(jax.random.key(seed), 22)
    tokens = noise_with(streams_of[0], (TOKENS, D), 1.0, 6.0, ((0, 32),), (0, 1, 32, 2.75))
    gain_in = jnp.clip(1.0 + 0.18 * jax.random.normal(streams_of[1], (D,), jnp.float32), 0.1, 1.9)
    w_query = bell_draw(streams_of[2], (D, KEYS), D ** -0.5, 0.125, ((1, 4),))
    w_key = bell_draw(streams_of[3], (D, KEYS), D ** -0.5, 0.125, ((1, 4),))
    w_value = bell_draw(streams_of[4], (D, KEYS), D ** -0.5, 0.125, ((1, 4),))
    w_alpha = bell_draw(streams_of[5], (D, HEADS), D ** -0.5, 0.125, ((1, 4),))
    w_beta = bell_draw(streams_of[6], (D, HEADS), D ** -0.5, 0.125, ((1, 4),))
    w_gate_out = bell_draw(streams_of[7], (D, KEYS), D ** -0.5, 0.125, ((1, 4),))
    conv_query = bell_draw(streams_of[8], (CONV, KEYS), CONV ** -0.5, 3.0, ((1, 4),), jnp.float32)
    conv_key = bell_draw(streams_of[9], (CONV, KEYS), CONV ** -0.5, 3.0, ((1, 4),), jnp.float32)
    conv_value = bell_draw(streams_of[10], (CONV, KEYS), CONV ** -0.5, 3.0, ((1, 4),), jnp.float32)
    decay_log = jnp.clip(-7.5 + 6.0 * jax.random.uniform(streams_of[11], (HEADS,), jnp.float32) ** shard_levels(streams_of[11], (HEADS,), ((0, 4),), -0.2, 0.2), -7.5, -1.5)
    decay_bias = jnp.clip(jax.random.uniform(streams_of[12], (HEADS,), jnp.float32, -1.0, 1.0) * shard_levels(streams_of[12], (HEADS,), ((0, 4),), -0.4, 0.0), -1.0, 1.0)
    head_gain = jnp.clip(1.0 + 0.18 * jax.random.normal(streams_of[13], (KEYS,), jnp.float32), 0.1, 1.9)
    w_out = bell_draw(streams_of[14], (KEYS, D), (KEYS // 2) ** -0.5, 0.1875, ((0, 4),))
    gain_mid = jnp.clip(1.0 + 0.18 * jax.random.normal(streams_of[15], (D,), jnp.float32), 0.1, 1.9)
    w_gate = bell_draw(streams_of[16], (D, FF), D ** -0.5, 0.125, ((1, 4),))
    w_up = bell_draw(streams_of[17], (D, FF), D ** -0.5, 0.125, ((1, 4),))
    w_down = bell_draw(streams_of[18], (FF, D), (FF // 4) ** -0.5, 0.15625, ((0, 4),))
    out_grad = noise_with(streams_of[19], (TOKENS, D), 1.0, 6.0, ((0, 8),), (0, 1, 8, 2.0))
    doc_lengths = draw_doc_lengths(jax.random.fold_in(streams_of[21], 71), 0)
    return {"tokens": tokens, "gain_in": gain_in, "w_query": w_query, "w_key": w_key, "w_value": w_value, "w_alpha": w_alpha, "w_beta": w_beta, "w_gate_out": w_gate_out, "conv_query": conv_query, "conv_key": conv_key, "conv_value": conv_value, "decay_log": decay_log, "decay_bias": decay_bias, "head_gain": head_gain, "w_out": w_out, "gain_mid": gain_mid, "w_gate": w_gate, "w_up": w_up, "w_down": w_down, "out_grad": out_grad, "doc_lengths": doc_lengths}


HIGHEST_PRECISION = lax.Precision.HIGHEST
epsilon = 1e-06

@jax.custom_vjp
def low(v):
    return lax.optimization_barrier(v.astype(jnp.bfloat16)).astype(jnp.float32)

@jax.custom_vjp
def low_back(v):
    return v

def low_keep(v):
    return (low(v), None)

def low_pass(kept, grad):
    return (grad,)

def back_keep(v):
    return (v, None)

def back_low(kept, grad):
    return (low(grad),)
low.defvjp(low_keep, low_pass)
low_back.defvjp(back_keep, back_low)

def matmul(left, right):
    return jnp.dot(left, right, precision=HIGHEST_PRECISION, preferred_element_type=jnp.float32)

def batched(form, left, right):
    return jnp.einsum(form, left, right, precision=HIGHEST_PRECISION)

def row_norm(values, gain):
    return values * lax.rsqrt(lax.optimization_barrier(jnp.mean(values * values, axis=-1, keepdims=True)) + epsilon) * gain

def unit_rows(values):
    return values * lax.rsqrt(lax.optimization_barrier(jnp.sum(values * values, axis=-1, keepdims=True)) + epsilon)

def unit_inverse(lower_part):
    block_size = lower_part.shape[-1]
    identity = jnp.eye(block_size, dtype=lower_part.dtype)
    powers = -lower_part
    result = identity + powers
    for squaring in range(block_size.bit_length() - 2):
        powers = batched('hij,hjk->hik', powers, powers)
        result = batched('hij,hjk->hik', result, identity + powers)
    return result

def block_step(carry_state, block_inputs):
    query_block, key_block, value_block, beta_block, decay_block, doc_block, prior_doc = block_inputs
    block_size = query_block.shape[1]
    row_ids = lax.broadcasted_iota(jnp.int32, (block_size, block_size), 0)
    column_ids = lax.broadcasted_iota(jnp.int32, (block_size, block_size), 1)
    inside = (doc_block[:, None] == doc_block[None, :]) & (row_ids >= column_ids)
    strict = inside & (row_ids > column_ids)
    cumulative = jnp.cumsum(decay_block, axis=1)
    spread_log = cumulative[:, :, None] - cumulative[:, None, :]
    weights_in = jnp.where(inside, jnp.exp(jnp.where(inside, spread_log, 0.0)), 0.0)
    carried = jnp.where(doc_block == prior_doc, 1.0, 0.0)
    from_start = jnp.exp(cumulative) * carried
    key_gram = batched('hid,hjd->hij', key_block, key_block)
    lower_part = jnp.where(strict, beta_block[:, :, None] * key_gram * weights_in, 0.0)
    inverse = unit_inverse(lower_part)
    write_keys = batched('hij,hjd->hid', inverse, (beta_block * from_start)[:, :, None] * key_block)
    write_values = batched('hij,hjd->hid', inverse, beta_block[:, :, None] * value_block)
    fresh_values = write_values - batched('hid,hde->hie', write_keys, carry_state)
    scores = jnp.where(inside, batched('hid,hjd->hij', query_block, key_block) * weights_in, 0.0)
    outputs = batched('hid,hde->hie', query_block * from_start[:, :, None], carry_state) + batched('hij,hje->hie', scores, fresh_values)
    last_row = weights_in[:, block_size - 1, :]
    new_state = from_start[:, block_size - 1][:, None, None] * carry_state + batched('hcd,hce->hde', key_block * last_row[:, :, None], fresh_values)
    return (new_state, outputs)

def run_blocks(start_state, queries, keys_in, values_in, beta_rows, decays, doc_blocks, prior_docs):
    return lax.scan(jax.checkpoint(block_step), start_state, (queries, keys_in, values_in, beta_rows, decays, doc_blocks, prior_docs))

def features(extended, alpha_raw, beta_raw, conv_all, decay_log, decay_bias, doc_ext, block_size):
    conv_taps = conv_all.shape[1]
    row_total = alpha_raw.shape[0]
    head_count = alpha_raw.shape[1]
    doc_ids = doc_ext[conv_taps - 1:]
    summed = jnp.zeros((3, row_total, extended.shape[2]), jnp.float32)
    for offset in range(conv_taps):
        shifted = lax.slice_in_dim(extended, offset, offset + row_total, axis=1)
        same_doc = lax.slice_in_dim(doc_ext, offset, offset + row_total) == doc_ids
        summed = summed + jnp.where(same_doc[None, :, None], shifted, 0.0) * conv_all[:, offset][:, None, :]
    convolved = jax.nn.silu(summed).reshape(3, row_total, head_count, -1)
    head_size = convolved.shape[-1]
    queries = unit_rows(convolved[0]) / math.sqrt(head_size)
    keys_in = unit_rows(convolved[1])
    values_in = convolved[2]
    beta_rows = jax.nn.sigmoid(beta_raw)
    decays = -jnp.exp(decay_log) * jax.nn.softplus(alpha_raw + decay_bias)
    block_count = row_total // block_size

    def blocks_of(values):
        return jnp.swapaxes(values.reshape(block_count, block_size, head_count, -1), 1, 2)

    def flat_blocks(values):
        return jnp.swapaxes(values.reshape(block_count, block_size, head_count), 1, 2)
    return (blocks_of(queries), blocks_of(keys_in), blocks_of(values_in), flat_blocks(beta_rows), flat_blocks(decays))

def head_outputs(queries, keys_in, values_in, beta_rows, decays, gate_raw, gain_heads, start_state, doc_blocks, prior_docs):
    final_state, outputs = run_blocks(start_state, queries, keys_in, values_in, beta_rows, decays, doc_blocks, prior_docs)
    block_count, head_count, block_size, head_size = outputs.shape
    rows_out = jnp.swapaxes(outputs, 1, 2).reshape(block_count * block_size, head_count, head_size)
    normed = rows_out * lax.rsqrt(lax.optimization_barrier(jnp.mean(rows_out * rows_out, axis=-1, keepdims=True)) + epsilon)
    gated = normed * gain_heads.reshape(head_count, head_size) * jax.nn.silu(gate_raw).reshape(-1, head_count, head_size)
    return (gated.reshape(block_count * block_size, head_count * head_size), final_state)

def block_forward(doc_ids, tokens, gain_in, w_query, w_key, w_value, w_alpha, w_beta, w_gate_out, conv_query, conv_key, conv_value, decay_log, decay_bias, head_gain, w_out, gain_mid, w_gate, w_up, w_down):
    conv_taps = conv_query.shape[0]
    row_total = tokens.shape[0]
    normed_in = low(row_norm(tokens, gain_in))
    projected = low_back(jnp.stack([low(matmul(normed_in, w_query)), low(matmul(normed_in, w_key)), low(matmul(normed_in, w_value))]))
    alpha_raw = low_back(matmul(normed_in, w_alpha))
    beta_raw = low_back(matmul(normed_in, w_beta))
    gate_raw = low_back(matmul(normed_in, w_gate_out))
    extended = jnp.concatenate([jnp.zeros((3, conv_taps - 1, projected.shape[2]), jnp.float32), projected], axis=1)
    doc_ext = jnp.concatenate([jnp.full((conv_taps - 1,), -1, jnp.int32), doc_ids.astype(jnp.int32)])
    conv_all = jnp.stack([conv_query, conv_key, conv_value])
    queries, keys_in, values_in, beta_rows, decays = features(extended, alpha_raw, beta_raw, conv_all, decay_log, decay_bias, doc_ext, BLOCK)
    doc_blocks = doc_ids.reshape(row_total // BLOCK, BLOCK)
    prior_docs = doc_ext[conv_taps - 2:conv_taps - 2 + row_total:BLOCK]
    head_count = alpha_raw.shape[1]
    start_state = jnp.zeros((head_count, queries.shape[-1], values_in.shape[-1]), jnp.float32)
    mixed_out, final_state = head_outputs(queries, keys_in, values_in, beta_rows, decays, gate_raw, head_gain, start_state, doc_blocks, prior_docs)
    mixer_rows = low_back(matmul(low(mixed_out), w_out))
    residual = tokens + mixer_rows
    normed_mid = low(row_norm(residual, gain_mid))
    gate_pre = low_back(matmul(normed_mid, w_gate))
    up_pre = low_back(matmul(normed_mid, w_up))
    activated = low(jax.nn.silu(gate_pre) * up_pre)
    return residual + low_back(matmul(activated, w_down))

def reference(tokens, gain_in, w_query, w_key, w_value, w_alpha, w_beta, w_gate_out, conv_query, conv_key, conv_value, decay_log, decay_bias, head_gain, w_out, gain_mid, w_gate, w_up, w_down, out_grad, doc_lengths):
    params = (gain_in, w_query, w_key, w_value, w_alpha, w_beta, w_gate_out, conv_query, conv_key, conv_value, decay_log, decay_bias, head_gain, w_out, gain_mid, w_gate, w_up, w_down)
    weights = tuple((p.astype(jnp.float32) for p in params))
    seq_count = tokens.shape[0] // SEQ
    lengths_all = doc_lengths.astype(jnp.int32)
    starts = jnp.cumsum(lengths_all, axis=1) - lengths_all
    positions = jnp.arange(SEQ, dtype=jnp.int32)
    local_ids = lax.optimization_barrier(jnp.sum((positions[None, :, None] >= starts[:, None, :]).astype(jnp.int32), axis=2)) - 1
    doc_ids = local_ids + lengths_all.shape[1] * jnp.arange(seq_count, dtype=jnp.int32)[:, None]
    token_seqs = tokens.astype(jnp.float32).reshape(seq_count, SEQ, D)
    grad_seqs = out_grad.astype(jnp.float32).reshape(seq_count, SEQ, D)

    def scan_step(totals, sequence_items):
        token_rows, grad_rows, doc_rows = sequence_items
        result, backward = jax.vjp(partial(block_forward, doc_rows), token_rows, *weights)
        gradients = backward(grad_rows)
        totals = tuple((t + g for t, g in zip(totals, gradients[1:])))
        return (totals, (result.astype(jnp.bfloat16), gradients[0]))
    initial = tuple((jnp.zeros_like(w) for w in weights))
    totals, (outputs, input_grads) = lax.scan(scan_step, initial, (token_seqs, grad_seqs, doc_ids))
    return (outputs.reshape(-1, D), input_grads.reshape(-1, D), totals[0], totals[1], totals[2], totals[3], totals[4], totals[5], totals[6], totals[7], totals[8], totals[9], totals[10], totals[11], totals[12], totals[13], totals[14], totals[15], totals[16], totals[17])
```

```python
import functools
import math

import jax
import jax.numpy as jnp
from jax import lax
from jax.experimental import pallas as pl
from jax.experimental.pallas import tpu as pltpu
from jax.sharding import PartitionSpec as P

CHUNK = 128
HALO = 16
epsilon = 1e-06
F32 = jnp.float32
LOW = jnp.bfloat16
NN = (((1,), (0,)), ((), ()))
NT = (((1,), (1,)), ((), ()))
TN = (((0,), (0,)), ((), ()))


def mm(left, right, dims=NN):
    return lax.dot_general(
        left, right, dims, precision=lax.Precision.HIGH, preferred_element_type=F32
    )


def mm_full(left, right, dims=NN):
    return lax.dot_general(
        left, right, dims, precision=lax.Precision.HIGHEST, preferred_element_type=F32
    )


def iota(shape, dim):
    return lax.broadcasted_iota(jnp.int32, shape, dim)


def doc_of(positions, scalars, docs):
    total = jnp.zeros_like(positions) - 1
    for j in range(docs):
        total = total + jnp.where(positions >= scalars[1 + j], 1, 0)
    return total


def chunk_masks(position, scalars, docs):
    shape = (CHUNK, CHUNK)
    row, col = iota(shape, 0), iota(shape, 1)
    doc_row = doc_of(row + position, scalars, docs)
    doc_col = doc_of(col + position, scalars, docs)
    same = doc_row == doc_col
    prior = jnp.int32(-1)
    last = jnp.int32(-1)
    for j in range(docs):
        prior = prior + jnp.where(position - 1 >= scalars[1 + j], 1, 0)
        last = last + jnp.where(position + CHUNK - 1 >= scalars[1 + j], 1, 0)
    return {
        "row": row,
        "col": col,
        "inside": same & (row >= col),
        "strict": same & (row > col),
        "carried": (doc_row == prior)[:, :1],
        "in_last": (doc_row == last)[:, :1],
        "last_carried": last == prior,
        "back": [
            None if s == 0 else (doc_row == doc_of(row + (position - s), scalars, docs))[:, :1]
            for s in range(4)
        ],
    }


def shifted_rows(main, before, back):
    ext = jnp.concatenate([before[HALO - 8 :], main], axis=0)
    rows = [main]
    for s in range(1, 4):
        rows.append(jnp.where(back[s], pltpu.roll(ext, s, 0)[8:], 0.0))
    return rows


def conv_sum(rows, taps):
    total = rows[0] * taps[3:4, :]
    for s in range(1, 4):
        total = total + rows[s] * taps[3 - s : 4 - s, :]
    return total


def softplus(x):
    return jnp.maximum(x, 0.0) + jnp.log1p(jnp.exp(-jnp.abs(x)))


def gates(narrow, params, masks):
    shifted = narrow + params[0:1, :]
    rate = -jnp.exp(params[1:2, :])
    decays = rate * softplus(shifted)
    lower = jnp.where(masks["row"] >= masks["col"], 1.0, 0.0)
    total = mm_full(lower, decays)
    return shifted, rate, decays, jax.nn.sigmoid(narrow), total, total.T


def decay_terms(h, total, total_row, masks):
    col = total[:, h : h + 1]
    row = total_row[h : h + 1, :]
    spread = jnp.where(
        masks["inside"], jnp.exp(jnp.where(masks["inside"], col - row, 0.0)), 0.0
    )
    start = jnp.where(masks["carried"], jnp.exp(col), 0.0)
    end = total[CHUNK - 1 : CHUNK, h : h + 1]
    to_last = jnp.where(masks["in_last"], jnp.exp(jnp.where(masks["in_last"], end - col, 0.0)), 0.0)
    keep = jnp.where(masks["last_carried"], jnp.exp(end), 0.0)
    return spread, start, to_last, keep


def lanes(h):
    return slice(h * 128, h * 128 + 128)


def features(pieces, befores, taps, masks, heads):
    out = []
    for i in range(3):
        rows = shifted_rows(pieces[i], befores[i], masks["back"])
        pre = conv_sum(rows, taps[4 * i : 4 * i + 4, :])
        out.append((rows, pre, jax.nn.sigmoid(pre)))
    return out


def unit(values):
    return lax.rsqrt(jnp.sum(values * values, axis=-1, keepdims=True) + epsilon)


def load_pieces(step, mains, priors, rims):
    pieces = [m[...].astype(F32) for m in mains]
    befores = [
        jnp.where(step == 0, r[...].astype(F32), p[...].astype(F32)) for p, r in zip(priors, rims)
    ]
    return pieces, befores


def intra_kernel(docs, heads, scalars, *refs):
    mains, priors, rims = refs[0:3], refs[3:6], refs[6:9]
    narrow_ref, taps_ref, params_ref = refs[9:12]
    x_ref, p_ref, kg_ref, w_ref, u_ref, qt_ref, ou_ref, t_ref, o_ref, tot_ref = refs[12:22]
    run = refs[22]
    step = pl.program_id(0)
    position = scalars[0] + step * CHUNK
    masks = chunk_masks(position, scalars, docs)
    pieces, befores = load_pieces(step, mains, priors, rims)
    feats = features(pieces, befores, taps_ref[...], masks, heads)
    _, _, _, beta, total, total_row = gates(narrow_ref[...], params_ref[...], masks)
    eye = jnp.where(masks["row"] == masks["col"], 1.0, 0.0)
    conv = [pre * sg for _, pre, sg in feats]
    hs = range(heads)
    q, k, v, terms, b = [], [], [], [], []
    for h in hs:
        cq, ck = conv[0][:, lanes(h)], conv[1][:, lanes(h)]
        q.append(cq * (unit(cq) * (1.0 / math.sqrt(128.0))))
        k.append(ck * unit(ck))
        v.append(conv[2][:, lanes(h)])
        terms.append(decay_terms(h, total, total_row, masks))
        b.append(beta[:, heads + h : heads + h + 1])
    kg = [jnp.where(masks["strict"], mm(k[h], k[h], NT) * terms[h][0], 0.0) for h in hs]
    p = [mm(q[h], k[h], NT) * terms[h][0] for h in hs]
    a = [b[h] * kg[h] for h in hs]
    pair = (masks["row"] >> 1) == (masks["col"] >> 1)
    x = [eye - jnp.where(pair, a[h], 0.0) for h in hs]
    for level in range(1, 7):
        wide = (masks["row"] >> (level + 1)) == (masks["col"] >> (level + 1))
        off = wide & ((masks["row"] >> level) != (masks["col"] >> level))
        lx = [mm(jnp.where(off, a[h], 0.0), x[h]) for h in hs]
        x = [x[h] - mm(x[h], lx[h]) for h in hs]
    wu = [
        mm(x[h], jnp.concatenate([(b[h] * terms[h][1]) * k[h], b[h] * v[h]], axis=1)) for h in hs
    ]
    pwu = [mm(p[h], wu[h]) for h in hs]
    kwu = [mm(terms[h][2] * k[h], wu[h], TN) for h in hs]

    @pl.when(step == 0)
    def _():
        for h in hs:
            run[h] = jnp.concatenate([jnp.zeros((128, 128), F32), eye], axis=1)

    for h in hs:
        x_ref[0, h] = x[h]
        p_ref[0, h] = p[h]
        kg_ref[0, h] = kg[h]
        w_ref[:, lanes(h)] = wu[h][:, :128]
        u_ref[:, lanes(h)] = wu[h][:, 128:]
        qt_ref[:, lanes(h)] = terms[h][1] * q[h] - pwu[h][:, :128]
        ou_ref[:, lanes(h)] = pwu[h][:, 128:]
        transfer = terms[h][3] * eye - kwu[h][:, :128]
        offset = kwu[h][:, 128:]
        t_ref[0, h] = transfer
        o_ref[0, h] = offset
        new = mm(transfer, run[h])
        new = jnp.concatenate([new[:, :128] + offset, new[:, 128:]], axis=1)
        run[h] = new
        tot_ref[h] = new


def rows_spec(width, chunks, reverse=False):
    if reverse:
        return pl.BlockSpec((CHUNK, width), lambda c, *_: (chunks - 1 - c, 0))
    return pl.BlockSpec((CHUNK, width), lambda c, *_: (c, 0))


def halo_spec(width, chunks, reverse=False):
    per = CHUNK // HALO
    if reverse:
        return pl.BlockSpec(
            (HALO, width), lambda c, *_: (jnp.maximum((chunks - 1 - c) * per - 1, 0), 0)
        )
    return pl.BlockSpec((HALO, width), lambda c, *_: (jnp.maximum(c * per - 1, 0), 0))


def tile_spec(heads, chunks, reverse=False):
    if reverse:
        return pl.BlockSpec((1, heads, 128, 128), lambda c, *_: (chunks - 1 - c, 0, 0, 0))
    return pl.BlockSpec((1, heads, 128, 128), lambda c, *_: (c, 0, 0, 0))


def whole_spec(*shape):
    zeros = (0,) * len(shape)
    return pl.BlockSpec(shape, lambda c, *_: zeros)


def sds(*shape, dtype=F32):
    return jax.ShapeDtypeStruct(shape, dtype)


PARAMS = dict(vmem_limit_bytes=56 * 1024 * 1024, dimension_semantics=("arbitrary",))


def cost(flops, moved):
    return pl.CostEstimate(flops=int(flops), bytes_accessed=int(moved), transcendentals=0)


def intra(scalars, pieces, rims, narrow, taps, params, docs, heads):
    rows, width = pieces[0].shape
    chunks = rows // CHUNK
    tiles, flat = sds(chunks, heads, 128, 128), sds(rows, width)
    return pl.pallas_call(
        functools.partial(intra_kernel, docs, heads),
        out_shape=(tiles, tiles, tiles, flat, flat, flat, flat, tiles, tiles, sds(heads, 128, 256)),
        grid_spec=pltpu.PrefetchScalarGridSpec(
            num_scalar_prefetch=1,
            grid=(chunks,),
            in_specs=[rows_spec(width, chunks)] * 3
            + [halo_spec(width, chunks)] * 3
            + [whole_spec(HALO, width)] * 3
            + [rows_spec(128, chunks), whole_spec(16, width), whole_spec(8, 128)],
            out_specs=[tile_spec(heads, chunks)] * 3
            + [rows_spec(width, chunks)] * 4
            + [tile_spec(heads, chunks)] * 2
            + [whole_spec(heads, 128, 256)],
            scratch_shapes=[pltpu.VMEM((heads, 128, 256), F32)],
        ),
        compiler_params=pltpu.CompilerParams(**PARAMS),
        cost_estimate=cost(chunks * heads * 60 * 3 * 2 * 128**3, 30 * rows * width * 4),
        name="intra",
    )(scalars, *pieces, *pieces, *rims, narrow, taps, params)


def outward_kernel(heads, s_in, w_ref, u_ref, qt_ref, ou_ref, t_ref, o_ref, gate_ref, gain_ref,
                   out_ref, v2_ref, s_ref, mixed_ref, run):
    step = pl.program_id(0)

    @pl.when(step == 0)
    def _():
        run[...] = s_in[...]

    hs = range(heads)
    state = [run[h] for h in hs]
    full = [
        mm(
            jnp.concatenate([qt_ref[:, lanes(h)], w_ref[:, lanes(h)], t_ref[0, h]], axis=0),
            state[h],
        )
        for h in hs
    ]
    for h in hs:
        out = full[h][:128] + ou_ref[:, lanes(h)]
        v2_ref[:, lanes(h)] = u_ref[:, lanes(h)] - full[h][128:256]
        s_ref[0, h] = state[h]
        run[h] = full[h][256:] + o_ref[0, h]
        out_ref[:, lanes(h)] = out
        gate = gate_ref[:, lanes(h)]
        scale = lax.rsqrt(jnp.mean(out * out, axis=-1, keepdims=True) + epsilon)
        mixed_ref[:, lanes(h)] = (
            out * scale * gain_ref[0:1, lanes(h)] * (gate * jax.nn.sigmoid(gate))
        ).astype(LOW)


def outward(s_in, w, u, qt, ou, t, o, gate, gain, heads):
    rows, width = w.shape
    chunks = rows // CHUNK
    flat, tiles = rows_spec(width, chunks), tile_spec(heads, chunks)
    return pl.pallas_call(
        functools.partial(outward_kernel, heads),
        out_shape=(sds(rows, width), sds(rows, width), sds(chunks, heads, 128, 128), sds(rows, width, dtype=LOW)),
        grid=(chunks,),
        in_specs=[whole_spec(heads, 128, 128), flat, flat, flat, flat, tiles, tiles, flat, whole_spec(8, width)],
        out_specs=[flat, flat, tiles, flat],
        scratch_shapes=[pltpu.VMEM((heads, 128, 128), F32)],
        compiler_params=pltpu.CompilerParams(**PARAMS),
        cost_estimate=cost(chunks * heads * 9 * 2 * 128**3, 11 * rows * width * 4),
        name="outward",
    )(s_in, w, u, qt, ou, t, o, gate, gain)


def inward_kernel(heads, gm_ref, out_ref, gate_ref, gain_ref, qt_ref, t_ref,
                  do_ref, dgate_ref, dgain_ref, tot_ref, run):
    step = pl.program_id(0)

    @pl.when(step == 0)
    def _():
        run[...] = jnp.zeros_like(run)
        dgain_ref[...] = jnp.zeros_like(dgain_ref)

    hs = range(heads)
    grads = []
    for h in hs:
        out, gate, gm = out_ref[:, lanes(h)], gate_ref[:, lanes(h)], gm_ref[:, lanes(h)]
        gain = gain_ref[0:1, lanes(h)]
        scale = lax.rsqrt(jnp.mean(out * out, axis=-1, keepdims=True) + epsilon)
        normed = out * scale
        sg = jax.nn.sigmoid(gate)
        act = gate * sg
        gn = gm * normed
        dgate_ref[:, lanes(h)] = (gn * gain * (sg * (1.0 + gate * (1.0 - sg)))).astype(LOW)
        dgain_ref[:, lanes(h)] += jnp.sum((gn * act).reshape(CHUNK // 8, 8, 128), axis=0)
        dn = gm * gain * act
        do = scale * (dn - normed * jnp.mean(dn * normed, axis=-1, keepdims=True))
        do_ref[:, lanes(h)] = do
        grads.append(do)
    for h in hs:
        left = jnp.concatenate([qt_ref[:, lanes(h)], t_ref[0, h]], axis=0)
        new = mm(left, jnp.concatenate([grads[h], run[h]], axis=0), TN)
        run[h] = new
        tot_ref[h] = new


def inward(gm, out, gate, gain, qt, t, heads):
    rows, width = gm.shape
    chunks = rows // CHUNK
    flat, tiles = rows_spec(width, chunks, True), tile_spec(heads, chunks, True)
    return pl.pallas_call(
        functools.partial(inward_kernel, heads),
        out_shape=(sds(rows, width), sds(rows, width, dtype=LOW), sds(8, width), sds(heads, 128, 128)),
        grid=(chunks,),
        in_specs=[flat, flat, flat, whole_spec(8, width), flat, tiles],
        out_specs=[flat, flat, whole_spec(8, width), whole_spec(heads, 128, 128)],
        scratch_shapes=[pltpu.VMEM((heads, 128, 128), F32)],
        compiler_params=pltpu.CompilerParams(**PARAMS),
        cost_estimate=cost(chunks * heads * 6 * 2 * 128**3, 7 * rows * width * 4),
        name="inward",
    )(gm, out, gate, gain, qt, t)


def back_kernel(docs, heads, chunks, scalars, *refs):
    mains, priors, rims = refs[0:3], refs[3:6], refs[6:9]
    narrow_ref, taps_ref, params_ref, ds_in = refs[9:13]
    (do_ref, v2_ref, s_ref, x_ref, p_ref, kg_ref, w_ref, u_ref, qt_ref, t_ref) = refs[13:23]
    gq_ref, gk_ref, gv_ref, tail_ref, rim_ref, gnarrow_ref, gtaps_ref, gparams_ref = refs[23:31]
    run, after = refs[31:33]
    rev = pl.program_id(0)
    step = chunks - 1 - rev
    position = scalars[0] + step * CHUNK

    @pl.when(rev == 0)
    def _():
        run[...] = ds_in[...]
        after[...] = jnp.zeros_like(after)
        gtaps_ref[...] = jnp.zeros_like(gtaps_ref)
        gparams_ref[...] = jnp.zeros_like(gparams_ref)

    masks = chunk_masks(position, scalars, docs)
    pieces, befores = load_pieces(step, mains, priors, rims)
    taps = taps_ref[...]
    feats = features(pieces, befores, taps, masks, heads)
    shifted, rate, decays, beta, total, total_row = gates(narrow_ref[...], params_ref[...], masks)
    conv = [pre * sg for _, pre, sg in feats]
    lane = masks["col"]
    hs = range(heads)
    q, k, v, uq, uk, terms, b = [], [], [], [], [], [], []
    root = 1.0 / math.sqrt(128.0)
    for h in hs:
        cq, ck = conv[0][:, lanes(h)], conv[1][:, lanes(h)]
        uq.append(unit(cq))
        uk.append(unit(ck))
        q.append(cq * (uq[h] * root))
        k.append(ck * uk[h])
        v.append(conv[2][:, lanes(h)])
        terms.append(decay_terms(h, total, total_row, masks))
        b.append(beta[:, heads + h : heads + h + 1])
    do = [do_ref[:, lanes(h)] for h in hs]
    v2 = [v2_ref[:, lanes(h)] for h in hs]
    dsn = [run[h] for h in hs]
    kt = [terms[h][2] * k[h] for h in hs]
    dv2 = [mm(p_ref[0, h], do[h], TN) + mm(kt[h], dsn[h]) for h in hs]
    for h in hs:
        left = jnp.concatenate([qt_ref[:, lanes(h)], t_ref[0, h]], axis=0)
        run[h] = mm(left, jnp.concatenate([do[h], dsn[h]], axis=0), TN)
    states = [s_ref[0, h] for h in hs]
    both = [mm(jnp.concatenate([do[h], dv2[h]], axis=0), states[h], NT) for h in hs]
    dp = [jnp.where(masks["inside"], mm(do[h], v2[h], NT), 0.0) for h in hs]
    dkt = [mm(v2[h], dsn[h], NT) for h in hs]
    dx = [mm(x_ref[0, h], jnp.concatenate([-both[h][128:], dv2[h]], axis=1), TN) for h in hs]
    da = [
        jnp.where(
            masks["strict"],
            -mm(dx[h], jnp.concatenate([w_ref[:, lanes(h)], u_ref[:, lanes(h)]], axis=1), NT),
            0.0,
        )
        for h in hs
    ]
    gdecay = jnp.zeros((CHUNK, CHUNK), F32)
    gbeta = jnp.zeros((CHUNK, CHUNK), F32)
    minus = jnp.zeros((CHUNK, CHUNK), F32)
    dq, dk, dv = [], [], []
    for h in hs:
        spread, start, to_last, keep = terms[h]
        doq = both[h][:128]
        dqk = dp[h] * spread
        kgh = kg_ref[0, h]
        z = da[h] * kgh
        dkk = b[h] * da[h] * spread
        dxk, dxv = dx[h][:, :128], dx[h][:, 128:]
        stacked = jnp.concatenate([dqk, dkk], axis=0)
        forward = mm(stacked, k[h])
        backward = mm(stacked, jnp.concatenate([q[h], k[h]], axis=0), TN)
        kx = jnp.sum(k[h] * dxk, axis=-1, keepdims=True)
        dq.append(start * doq + forward[:128])
        dk.append(
            backward + forward[128:] + to_last * dkt[h] + (b[h] * start) * dxk
        )
        dv.append(b[h] * dxv)
        gb = (
            jnp.sum(z, axis=-1, keepdims=True)
            + jnp.sum(v[h] * dxv, axis=-1, keepdims=True)
            + start * kx
        )
        gamgrad = b[h] * z + dp[h] * p_ref[0, h]
        dstart = jnp.sum(q[h] * doq, axis=-1, keepdims=True) + b[h] * kx
        dlast = jnp.sum(k[h] * dkt[h], axis=-1, keepdims=True) * to_last
        dkeep = jnp.sum(states[h] * dsn[h], keepdims=True) * keep
        gcol = jnp.sum(gamgrad, axis=-1, keepdims=True) + dstart * start - dlast
        end = jnp.sum(dlast, keepdims=True) + dkeep
        gcol = gcol + jnp.where(masks["row"][:, :1] == CHUNK - 1, end, 0.0)
        grow = jnp.sum(gamgrad, axis=0, keepdims=True)
        gdecay = jnp.where(lane == h, gcol, gdecay)
        gbeta = jnp.where(lane == heads + h, gb, gbeta)
        minus = jnp.where(masks["row"] == h, grow, minus)
    gdecay = gdecay - minus.T
    upper = jnp.where(masks["row"] <= masks["col"], 1.0, 0.0)
    dg = mm_full(upper, gdecay)
    galpha = dg * rate * jax.nn.sigmoid(shifted)
    gnarrow_ref[...] = jnp.where(lane < heads, galpha, gbeta * beta * (1.0 - beta)).astype(LOW)
    gparams_ref[0:8, :] += jnp.sum((galpha).reshape(CHUNK // 8, 8, 128), axis=0)
    gparams_ref[8:16, :] += jnp.sum((dg * decays).reshape(CHUNK // 8, 8, 128), axis=0)

    outs = (gq_ref, gk_ref, gv_ref)
    for i in range(3):
        rows, pre, sg = feats[i]
        pieces_d = []
        for h in hs:
            if i == 2:
                pieces_d.append(dv[h])
            else:
                inv = uq[h] if i == 0 else uk[h]
                grad = dq[h] * root if i == 0 else dk[h]
                normal = conv[i][:, lanes(h)] * inv
                pieces_d.append(
                    inv * (grad - normal * jnp.sum(grad * normal, axis=-1, keepdims=True))
                )
        dc = jnp.concatenate(pieces_d, axis=1)
        ds = dc * (sg * (1.0 + pre * (1.0 - sg)))
        grad = ds * taps[4 * i + 3 : 4 * i + 4, :]
        rim = jnp.zeros((8, ds.shape[1]), F32)
        gtaps_ref[4 * i + 3] += jnp.sum((ds * rows[0]).reshape(CHUNK // 8, 8, -1), axis=0)
        for s in range(1, 4):
            tap = taps[4 * i + 3 - s : 4 * i + 4 - s, :]
            masked = jnp.where(masks["back"][s], ds, 0.0)
            gtaps_ref[4 * i + 3 - s] += jnp.sum((ds * rows[s]).reshape(CHUNK // 8, 8, -1), axis=0)
            ext = jnp.concatenate([masked, after[3 * i + s - 1]], axis=0)
            grad = grad + pltpu.roll(ext, CHUNK + 8 - s, 0)[:CHUNK] * tap
            after[3 * i + s - 1] = masked[:8]
            front = jnp.concatenate([jnp.zeros_like(masked[:8]), masked[:8]], axis=0)
            rim = rim + pltpu.roll(front, 16 - s, 0)[:8] * tap
        outs[i][...] = grad.astype(LOW)
        rim_ref[i] = rim

        @pl.when(rev == 0)
        def _():
            tail_ref[i] = grad[CHUNK - HALO :]


def back(scalars, pieces, rims, narrow, taps, params, ds_in, do, v2, s, x, p, kg, w, u, qt, t, docs, heads):
    rows, width = pieces[0].shape
    chunks = rows // CHUNK
    flat, tiles = rows_spec(width, chunks, True), tile_spec(heads, chunks, True)
    low = sds(rows, width, dtype=LOW)
    return pl.pallas_call(
        functools.partial(back_kernel, docs, heads, chunks),
        out_shape=(
            low, low, low, sds(3, HALO, width), sds(3, 8, width), sds(rows, 128, dtype=LOW),
            sds(12, 8, width), sds(16, 128),
        ),
        grid_spec=pltpu.PrefetchScalarGridSpec(
            num_scalar_prefetch=1,
            grid=(chunks,),
            in_specs=[flat] * 3
            + [halo_spec(width, chunks, True)] * 3
            + [whole_spec(HALO, width)] * 3
            + [rows_spec(128, chunks, True), whole_spec(16, width), whole_spec(8, 128)]
            + [whole_spec(heads, 128, 128), flat, flat, tiles, tiles, tiles, tiles, flat, flat, flat, tiles],
            out_specs=[flat] * 3
            + [whole_spec(3, HALO, width), whole_spec(3, 8, width), rows_spec(128, chunks, True)]
            + [whole_spec(12, 8, width), whole_spec(16, 128)],
            scratch_shapes=[pltpu.VMEM((heads, 128, 128), F32), pltpu.VMEM((9, 8, width), F32)],
        ),
        compiler_params=pltpu.CompilerParams(**PARAMS),
        cost_estimate=cost(chunks * heads * 60 * 2 * 128**3, 16 * rows * width * 4),
        name="back",
    )(scalars, *pieces, *pieces, *rims, narrow, taps, params, ds_in, do, v2, s, x, p, kg, w, u, qt, t)


def chain_kernel(heads, backward, scalars, *refs):
    mine, count = scalars[0], pl.num_programs(0)
    step = pl.program_id(0)
    out_ref = refs[-1]

    @pl.when(step == 0)
    def _():
        out_ref[...] = jnp.zeros_like(out_ref)

    if backward:
        maps_ref, sums_ref = refs[0], refs[1]

        @pl.when(count - 1 - step > mine)
        def _():
            for h in range(heads):
                out_ref[h] = mm(maps_ref[0, h][:, 128:], out_ref[h], TN) + sums_ref[0, h]
    else:
        maps_ref = refs[0]

        @pl.when(step < mine)
        def _():
            for h in range(heads):
                piece = maps_ref[0, h]
                out_ref[h] = mm(piece[:, 128:], out_ref[h]) + piece[:, :128]


def chain(mine, maps, sums, heads):
    count = maps.shape[0]
    backward = sums is not None
    at = (lambda c, *_: (count - 1 - c, 0, 0, 0)) if backward else (lambda c, *_: (c, 0, 0, 0))
    specs = [pl.BlockSpec((1, heads, 128, 256), at)]
    args = [maps]
    if backward:
        specs.append(pl.BlockSpec((1, heads, 128, 128), at))
        args.append(sums)
    return pl.pallas_call(
        functools.partial(chain_kernel, heads, backward),
        out_shape=sds(heads, 128, 128),
        grid_spec=pltpu.PrefetchScalarGridSpec(
            num_scalar_prefetch=1,
            grid=(count,),
            in_specs=specs,
            out_specs=whole_spec(heads, 128, 128),
        ),
        compiler_params=pltpu.CompilerParams(**PARAMS),
        cost_estimate=cost(count * heads * 3 * 2 * 128**3, count * heads * 3 * 128 * 128 * 4),
        name="chain",
    )(mine, *args)


def contract_rows(left, right):
    return lax.dot_general(left, right, TN, preferred_element_type=F32)


def contract_cols(left, right):
    return lax.dot_general(left, right, NT, preferred_element_type=F32)


def dot(left, right):
    return jnp.dot(left, right, preferred_element_type=F32)


def row_norm(values, gain):
    return values * lax.rsqrt(jnp.mean(values * values, axis=-1, keepdims=True) + epsilon) * gain


def norm_back(values, gain, grad):
    inv = lax.rsqrt(jnp.mean(values * values, axis=-1, keepdims=True) + epsilon)
    scaled = grad * gain
    inner = jnp.mean(scaled * values, axis=-1, keepdims=True)
    return inv * scaled - values * (inner * inv * inv * inv), jnp.sum(grad * values * inv, axis=0)


def after(values, *first):
    out = lax.optimization_barrier((values,) + first)
    return out[0]


def local(
    tokens,
    gain_in,
    w_query,
    w_key,
    w_value,
    w_alpha,
    w_beta,
    w_gate_out,
    conv_query,
    conv_key,
    conv_value,
    decay_log,
    decay_bias,
    head_gain,
    w_out,
    gain_mid,
    w_gate,
    w_up,
    w_down,
    out_grad,
    doc_lengths,
):
    rows_own, model = tokens.shape
    tensor_parts, dp_parts = lax.axis_size("tensor"), lax.axis_size("dp")
    tensor_index, dp_index = lax.axis_index("tensor"), lax.axis_index("dp")
    group_rows = rows_own * tensor_parts
    seq_total = group_rows * dp_parts
    heads = w_alpha.shape[1]
    width = w_query.shape[1]
    docs = doc_lengths.shape[0] * doc_lengths.shape[1]
    starts = (
        jnp.cumsum(doc_lengths, axis=1)
        - doc_lengths
        + seq_total * lax.broadcasted_iota(jnp.int32, doc_lengths.shape, 0)
    ).reshape(-1)
    scalars = jnp.concatenate([(dp_index * group_rows).reshape(1), starts]).astype(jnp.int32)
    mine = dp_index.reshape(1).astype(jnp.int32)
    taps = jnp.concatenate([conv_query, conv_key, conv_value, jnp.zeros((4, width), F32)])
    params = jnp.zeros((8, 128), F32).at[0, :heads].set(decay_bias).at[1, :heads].set(decay_log)
    gain_heads = jnp.broadcast_to(head_gain[None], (8, width))
    w_narrow = jnp.pad(jnp.concatenate([w_alpha, w_beta], axis=1), ((0, 0), (0, 128 - 2 * heads)))

    own_rows = tokens.astype(F32)
    normed_in = row_norm(own_rows, gain_in).astype(LOW)
    normed_all = lax.all_gather(normed_in, "tensor", axis=0, tiled=True)
    grad_act = contract_cols(out_grad, w_down)
    half = width // 2
    core = lax.rem(dp_index, 2)
    out_half = lax.dynamic_slice_in_dim(w_out, core * half, half, 0)
    out_mine = lax.all_gather(out_half, "tensor", axis=0)
    out_other = lax.ppermute(out_mine, "dp", [(i, i ^ 1) for i in range(dp_parts)])
    w_out_full = jnp.stack(
        [jnp.where(core == 0, out_mine, out_other), jnp.where(core == 0, out_other, out_mine)],
        axis=1,
    ).reshape(width * tensor_parts, model)

    pieces = [dot(normed_all, w).astype(LOW) for w in (w_query, w_key, w_value)]
    narrow = dot(normed_all, w_narrow)
    forth = [(i, i + 1) for i in range(dp_parts - 1)]
    rims = lax.ppermute(
        jnp.stack([piece[group_rows - HALO :] for piece in pieces]), "dp", forth
    )
    rims = [rims[i] for i in range(3)]
    x, p, kg, w, u, qt, ou, t, o, totals = intra(
        scalars, pieces, rims, narrow, taps, params, docs, heads
    )
    gate_raw = dot(normed_all, w_gate_out)
    maps = lax.all_gather(totals, "dp", axis=0)
    state_in = chain(mine, maps, None, heads)
    rows_out, v2, s, mixed = outward(state_in, w, u, qt, ou, t, o, gate_raw, gain_heads, heads)

    mixed_own = lax.all_to_all(mixed, "tensor", split_axis=0, concat_axis=1, tiled=True)
    residual = own_rows + dot(mixed_own, w_out_full)
    normed_mid = row_norm(residual, gain_mid).astype(LOW)
    mid_all = lax.all_gather(normed_mid, "tensor", axis=0, tiled=True)
    gate_pre = dot(mid_all, w_gate)
    up_pre = dot(mid_all, w_up)
    sigmoid_gate = jax.nn.sigmoid(gate_pre)
    act = gate_pre * sigmoid_gate
    activated = (act * up_pre).astype(LOW)
    grad_gate = (grad_act * up_pre * sigmoid_gate * (1.0 + gate_pre * (1.0 - sigmoid_gate))).astype(LOW)
    grad_up = (grad_act * act).astype(LOW)
    grad_mid_part = (contract_cols(grad_gate, w_gate) + contract_cols(grad_up, w_up)).astype(LOW)
    grad_mid = lax.psum_scatter(grad_mid_part, "tensor", scatter_dimension=0, tiled=True).astype(F32)

    gate_grad = contract_rows(mid_all, grad_gate).astype(LOW)
    up_grad = contract_rows(mid_all, grad_up).astype(LOW)
    down_grad = contract_rows(out_grad, activated).astype(LOW)
    mlp_part = dot(activated, w_down).astype(LOW)
    ffn_grads = [
        lax.psum_scatter(part, "dp", scatter_dimension=0, tiled=True)
        for part in (gate_grad, up_grad, down_grad)
    ]

    grad_res_norm, gain_mid_grad = norm_back(residual, gain_mid, grad_mid)
    grad_own = lax.dynamic_slice_in_dim(out_grad, tensor_index * rows_own, rows_own, 0)
    grad_residual = grad_own.astype(F32) + grad_res_norm
    grad_mixer = grad_residual.astype(LOW)
    grad_mixed_own = contract_cols(grad_mixer, w_out_full).astype(LOW)
    grad_mixed = lax.all_to_all(
        grad_mixed_own, "tensor", split_axis=1, concat_axis=0, tiled=True
    ).astype(F32)
    mlp_rows = lax.psum_scatter(after(mlp_part, grad_mid), "tensor", scatter_dimension=0, tiled=True)
    output = (residual + mlp_rows.astype(F32)).astype(LOW)
    grad_mixer_all = lax.all_gather(after(grad_mixer, grad_mixed), "tensor", axis=0, tiled=True)

    do, gate_low, head_gain_part, ds_total = inward(
        grad_mixed, rows_out, gate_raw, gain_heads, qt, t, heads
    )
    sums = lax.all_gather(ds_total, "dp", axis=0)
    gate_out_grad = lax.psum_scatter(
        contract_rows(normed_all, gate_low).astype(LOW), "dp", scatter_dimension=0, tiled=True
    )
    grad_end = chain(mine, maps, sums, heads)
    gq, gk, gv, tails, rim_grad, narrow_low, taps_grad, params_grad = back(
        scalars, pieces, rims, narrow, taps, params, grad_end, do, v2, s, x, p, kg, w, u, qt, t,
        docs, heads,
    )
    out_w_grad = lax.psum_scatter(
        contract_rows(grad_mixer_all, mixed).astype(LOW), "dp", scatter_dimension=0, tiled=True
    )
    rim_back = lax.ppermute(rim_grad, "dp", [(i + 1, i) for i in range(dp_parts - 1)])
    tails = tails.at[:, HALO - 8 :].add(rim_back).astype(LOW)
    grads = [
        lax.dynamic_update_slice_in_dim(g, tails[i], group_rows - HALO, 0)
        for i, g in enumerate((gq, gk, gv))
    ]
    summed = contract_cols(gate_low, w_gate_out) + contract_cols(narrow_low, w_narrow)
    for g, weight in zip(grads, (w_query, w_key, w_value)):
        summed = summed + contract_cols(g, weight)
    grad_normed = lax.psum_scatter(
        summed.astype(LOW), "tensor", scatter_dimension=0, tiled=True
    ).astype(F32)
    narrow_grad = contract_rows(normed_all, narrow_low)[:, : 2 * heads].astype(LOW)
    qkv_grads = [
        lax.psum_scatter(
            contract_rows(normed_all, g).astype(LOW), "dp", scatter_dimension=0, tiled=True
        )
        for g in grads
    ]
    narrow_grad = lax.psum_scatter(narrow_grad, "dp", scatter_dimension=0, tiled=True).astype(F32)
    grad_tokens, gain_in_grad = norm_back(own_rows, gain_in, grad_normed)
    input_grad = grad_residual + grad_tokens

    params_grad = params_grad.reshape(2, 8, 128).sum(1)[:, :heads]
    flat = jnp.concatenate(
        [taps_grad.sum(1), head_gain_part.sum(0)[None]], axis=0
    )
    wide = lax.dynamic_update_slice_in_dim(
        jnp.zeros((13, width * tensor_parts), F32), flat, tensor_index * width, 1
    )
    thin = lax.dynamic_update_slice_in_dim(
        jnp.zeros((2, heads * tensor_parts), F32), params_grad, tensor_index * heads, 1
    )
    packed = jnp.concatenate([wide.reshape(-1), thin.reshape(-1), gain_in_grad, gain_mid_grad])
    packed = lax.psum(packed, ("dp", "tensor"))
    channels = width * tensor_parts
    wide = packed[: 13 * channels].reshape(13, channels)
    rest = packed[13 * channels :]
    all_heads = heads * tensor_parts
    return (
        output,
        input_grad,
        rest[2 * all_heads : 2 * all_heads + model],
        qkv_grads[0].astype(F32),
        qkv_grads[1].astype(F32),
        qkv_grads[2].astype(F32),
        narrow_grad[:, :heads],
        narrow_grad[:, heads:],
        gate_out_grad.astype(F32),
        wide[0:4],
        wide[4:8],
        wide[8:12],
        rest[all_heads : 2 * all_heads],
        rest[:all_heads],
        wide[12],
        out_w_grad.T.astype(F32),
        rest[2 * all_heads + model :],
        ffn_grads[0].astype(F32),
        ffn_grads[1].astype(F32),
        ffn_grads[2].T.astype(F32),
    )


def solution(mesh):
    placed = (
        P(("dp", "tensor"), None),
        P(),
        P(None, "tensor"),
        P(None, "tensor"),
        P(None, "tensor"),
        P(None, "tensor"),
        P(None, "tensor"),
        P(None, "tensor"),
        P(None, "tensor"),
        P(None, "tensor"),
        P(None, "tensor"),
        P("tensor"),
        P("tensor"),
        P("tensor"),
        P("tensor", None),
        P(),
        P(None, "tensor"),
        P(None, "tensor"),
        P("tensor", None),
        P("dp", None),
        P(),
    )
    return jax.shard_map(
        local,
        mesh=mesh,
        in_specs=placed,
        out_specs=(
            P(("dp", "tensor"), None),
            P(("dp", "tensor"), None),
            P(),
            P("dp", "tensor"),
            P("dp", "tensor"),
            P("dp", "tensor"),
            P("dp", "tensor"),
            P("dp", "tensor"),
            P("dp", "tensor"),
            P(),
            P(),
            P(),
            P(),
            P(),
            P(),
            P("tensor", "dp"),
            P(),
            P("dp", "tensor"),
            P("dp", "tensor"),
            P("tensor", "dp"),
        ),
        check_vma=False,
    )
```

```python
import functools
import math

import jax
import jax.numpy as jnp
from jax import lax
from jax.experimental import pallas as pl
from jax.experimental.pallas import tpu as pltpu
from jax.sharding import PartitionSpec as P

CHUNK = 128
HALO = 16
epsilon = 1e-06
F32 = jnp.float32
LOW = jnp.bfloat16
NN = (((1,), (0,)), ((), ()))
NT = (((1,), (1,)), ((), ()))
TN = (((0,), (0,)), ((), ()))


def mm(left, right, dims=NN):
    return lax.dot_general(
        left, right, dims, precision=lax.Precision.HIGH, preferred_element_type=F32
    )


def mm_full(left, right, dims=NN):
    return lax.dot_general(
        left, right, dims, precision=lax.Precision.HIGHEST, preferred_element_type=F32
    )


def iota(shape, dim):
    return lax.broadcasted_iota(jnp.int32, shape, dim)


def doc_of(positions, scalars, docs):
    total = jnp.zeros_like(positions) - 1
    for j in range(docs):
        total = total + jnp.where(positions >= scalars[1 + j], 1, 0)
    return total


def chunk_masks(position, scalars, docs):
    shape = (CHUNK, CHUNK)
    row, col = iota(shape, 0), iota(shape, 1)
    doc_row = doc_of(row + position, scalars, docs)
    doc_col = doc_of(col + position, scalars, docs)
    same = doc_row == doc_col
    prior = jnp.int32(-1)
    last = jnp.int32(-1)
    for j in range(docs):
        prior = prior + jnp.where(position - 1 >= scalars[1 + j], 1, 0)
        last = last + jnp.where(position + CHUNK - 1 >= scalars[1 + j], 1, 0)
    return {
        "row": row,
        "col": col,
        "inside": same & (row >= col),
        "strict": same & (row > col),
        "carried": (doc_row == prior)[:, :1],
        "in_last": (doc_row == last)[:, :1],
        "last_carried": last == prior,
        "back": [
            None if s == 0 else (doc_row == doc_of(row + (position - s), scalars, docs))[:, :1]
            for s in range(4)
        ],
    }


def shifted_rows(main, before, back):
    ext = jnp.concatenate([before[HALO - 8 :], main], axis=0)
    rows = [main]
    for s in range(1, 4):
        rows.append(jnp.where(back[s], pltpu.roll(ext, s, 0)[8:], 0.0))
    return rows


def conv_sum(rows, taps):
    total = rows[0] * taps[3:4, :]
    for s in range(1, 4):
        total = total + rows[s] * taps[3 - s : 4 - s, :]
    return total


def softplus(x):
    return jnp.maximum(x, 0.0) + jnp.log1p(jnp.exp(-jnp.abs(x)))


def gates(narrow, params, masks):
    shifted = narrow + params[0:1, :]
    rate = -jnp.exp(params[1:2, :])
    decays = rate * softplus(shifted)
    lower = jnp.where(masks["row"] >= masks["col"], 1.0, 0.0)
    total = mm_full(lower, decays)
    return shifted, rate, decays, jax.nn.sigmoid(narrow), total, total.T


def decay_terms(h, total, total_row, masks):
    col = total[:, h : h + 1]
    row = total_row[h : h + 1, :]
    spread = jnp.where(
        masks["inside"], jnp.exp(jnp.where(masks["inside"], col - row, 0.0)), 0.0
    )
    start = jnp.where(masks["carried"], jnp.exp(col), 0.0)
    end = total[CHUNK - 1 : CHUNK, h : h + 1]
    to_last = jnp.where(masks["in_last"], jnp.exp(jnp.where(masks["in_last"], end - col, 0.0)), 0.0)
    keep = jnp.where(masks["last_carried"], jnp.exp(end), 0.0)
    return spread, start, to_last, keep


def lanes(h):
    return slice(h * 128, h * 128 + 128)


def features(pieces, befores, taps, masks, heads):
    out = []
    for i in range(3):
        rows = shifted_rows(pieces[i], befores[i], masks["back"])
        pre = conv_sum(rows, taps[4 * i : 4 * i + 4, :])
        out.append((rows, pre, jax.nn.sigmoid(pre)))
    return out


def unit(values):
    return lax.rsqrt(jnp.sum(values * values, axis=-1, keepdims=True) + epsilon)


def load_pieces(step, mains, priors, rims):
    pieces = [m[...].astype(F32) for m in mains]
    befores = [
        jnp.where(step == 0, r[...].astype(F32), p[...].astype(F32)) for p, r in zip(priors, rims)
    ]
    return pieces, befores


def intra_kernel(docs, heads, scalars, *refs):
    mains, priors, rims = refs[0:3], refs[3:6], refs[6:9]
    narrow_ref, taps_ref, params_ref = refs[9:12]
    x_ref, p_ref, kg_ref, w_ref, u_ref, qt_ref, ou_ref, t_ref, o_ref, tot_ref = refs[12:22]
    run = refs[22]
    step = pl.program_id(0)
    position = scalars[0] + step * CHUNK
    masks = chunk_masks(position, scalars, docs)
    pieces, befores = load_pieces(step, mains, priors, rims)
    feats = features(pieces, befores, taps_ref[...], masks, heads)
    _, _, _, beta, total, total_row = gates(narrow_ref[...], params_ref[...], masks)
    eye = jnp.where(masks["row"] == masks["col"], 1.0, 0.0)
    conv = [pre * sg for _, pre, sg in feats]
    hs = range(heads)
    q, k, v, terms, b = [], [], [], [], []
    for h in hs:
        cq, ck = conv[0][:, lanes(h)], conv[1][:, lanes(h)]
        q.append(cq * (unit(cq) * (1.0 / math.sqrt(128.0))))
        k.append(ck * unit(ck))
        v.append(conv[2][:, lanes(h)])
        terms.append(decay_terms(h, total, total_row, masks))
        b.append(beta[:, heads + h : heads + h + 1])
    kg = [jnp.where(masks["strict"], mm(k[h], k[h], NT) * terms[h][0], 0.0) for h in hs]
    p = [mm(q[h], k[h], NT) * terms[h][0] for h in hs]
    a = [b[h] * kg[h] for h in hs]
    pair = (masks["row"] >> 1) == (masks["col"] >> 1)
    x = [eye - jnp.where(pair, a[h], 0.0) for h in hs]
    for level in range(1, 7):
        wide = (masks["row"] >> (level + 1)) == (masks["col"] >> (level + 1))
        off = wide & ((masks["row"] >> level) != (masks["col"] >> level))
        lx = [mm(jnp.where(off, a[h], 0.0), x[h]) for h in hs]
        x = [x[h] - mm(x[h], lx[h]) for h in hs]
    wu = [
        mm(x[h], jnp.concatenate([(b[h] * terms[h][1]) * k[h], b[h] * v[h]], axis=1)) for h in hs
    ]
    pwu = [mm(p[h], wu[h]) for h in hs]
    kwu = [mm(terms[h][2] * k[h], wu[h], TN) for h in hs]

    @pl.when(step == 0)
    def _():
        for h in hs:
            run[h] = jnp.concatenate([jnp.zeros((128, 128), F32), eye], axis=1)

    for h in hs:
        x_ref[0, h] = x[h]
        p_ref[0, h] = p[h]
        kg_ref[0, h] = kg[h]
        w_ref[:, lanes(h)] = wu[h][:, :128]
        u_ref[:, lanes(h)] = wu[h][:, 128:]
        qt_ref[:, lanes(h)] = terms[h][1] * q[h] - pwu[h][:, :128]
        ou_ref[:, lanes(h)] = pwu[h][:, 128:]
        transfer = terms[h][3] * eye - kwu[h][:, :128]
        offset = kwu[h][:, 128:]
        t_ref[0, h] = transfer
        o_ref[0, h] = offset
        new = mm(transfer, run[h])
        new = jnp.concatenate([new[:, :128] + offset, new[:, 128:]], axis=1)
        run[h] = new
        tot_ref[h] = new


def rows_spec(width, chunks, reverse=False):
    if reverse:
        return pl.BlockSpec((CHUNK, width), lambda c, *_: (chunks - 1 - c, 0))
    return pl.BlockSpec((CHUNK, width), lambda c, *_: (c, 0))


def halo_spec(width, chunks, reverse=False):
    per = CHUNK // HALO
    if reverse:
        return pl.BlockSpec(
            (HALO, width), lambda c, *_: (jnp.maximum((chunks - 1 - c) * per - 1, 0), 0)
        )
    return pl.BlockSpec((HALO, width), lambda c, *_: (jnp.maximum(c * per - 1, 0), 0))


def tile_spec(heads, chunks, reverse=False):
    if reverse:
        return pl.BlockSpec((1, heads, 128, 128), lambda c, *_: (chunks - 1 - c, 0, 0, 0))
    return pl.BlockSpec((1, heads, 128, 128), lambda c, *_: (c, 0, 0, 0))


def whole_spec(*shape):
    zeros = (0,) * len(shape)
    return pl.BlockSpec(shape, lambda c, *_: zeros)


def sds(*shape, dtype=F32):
    return jax.ShapeDtypeStruct(shape, dtype)


PARAMS = dict(vmem_limit_bytes=56 * 1024 * 1024, dimension_semantics=("arbitrary",))


def cost(flops, moved):
    return pl.CostEstimate(flops=int(flops), bytes_accessed=int(moved), transcendentals=0)


def intra(scalars, pieces, rims, narrow, taps, params, docs, heads):
    rows, width = pieces[0].shape
    chunks = rows // CHUNK
    tiles, flat = sds(chunks, heads, 128, 128), sds(rows, width)
    return pl.pallas_call(
        functools.partial(intra_kernel, docs, heads),
        out_shape=(tiles, tiles, tiles, flat, flat, flat, flat, tiles, tiles, sds(heads, 128, 256)),
        grid_spec=pltpu.PrefetchScalarGridSpec(
            num_scalar_prefetch=1,
            grid=(chunks,),
            in_specs=[rows_spec(width, chunks)] * 3
            + [halo_spec(width, chunks)] * 3
            + [whole_spec(HALO, width)] * 3
            + [rows_spec(128, chunks), whole_spec(16, width), whole_spec(8, 128)],
            out_specs=[tile_spec(heads, chunks)] * 3
            + [rows_spec(width, chunks)] * 4
            + [tile_spec(heads, chunks)] * 2
            + [whole_spec(heads, 128, 256)],
            scratch_shapes=[pltpu.VMEM((heads, 128, 256), F32)],
        ),
        compiler_params=pltpu.CompilerParams(**PARAMS),
        cost_estimate=cost(chunks * heads * 60 * 3 * 2 * 128**3, 30 * rows * width * 4),
        name="intra",
    )(scalars, *pieces, *pieces, *rims, narrow, taps, params)


def outward_kernel(heads, s_in, w_ref, u_ref, qt_ref, ou_ref, t_ref, o_ref, gate_ref, gain_ref,
                   out_ref, v2_ref, s_ref, mixed_ref, run):
    step = pl.program_id(0)

    @pl.when(step == 0)
    def _():
        run[...] = s_in[...]

    hs = range(heads)
    state = [run[h] for h in hs]
    full = [
        mm(
            jnp.concatenate([qt_ref[:, lanes(h)], w_ref[:, lanes(h)], t_ref[0, h]], axis=0),
            state[h],
        )
        for h in hs
    ]
    for h in hs:
        out = full[h][:128] + ou_ref[:, lanes(h)]
        v2_ref[:, lanes(h)] = u_ref[:, lanes(h)] - full[h][128:256]
        s_ref[0, h] = state[h]
        run[h] = full[h][256:] + o_ref[0, h]
        out_ref[:, lanes(h)] = out
        gate = gate_ref[:, lanes(h)]
        scale = lax.rsqrt(jnp.mean(out * out, axis=-1, keepdims=True) + epsilon)
        mixed_ref[:, lanes(h)] = (
            out * scale * gain_ref[0:1, lanes(h)] * (gate * jax.nn.sigmoid(gate))
        ).astype(LOW)


def outward(s_in, w, u, qt, ou, t, o, gate, gain, heads):
    rows, width = w.shape
    chunks = rows // CHUNK
    flat, tiles = rows_spec(width, chunks), tile_spec(heads, chunks)
    return pl.pallas_call(
        functools.partial(outward_kernel, heads),
        out_shape=(sds(rows, width), sds(rows, width), sds(chunks, heads, 128, 128), sds(rows, width, dtype=LOW)),
        grid=(chunks,),
        in_specs=[whole_spec(heads, 128, 128), flat, flat, flat, flat, tiles, tiles, flat, whole_spec(8, width)],
        out_specs=[flat, flat, tiles, flat],
        scratch_shapes=[pltpu.VMEM((heads, 128, 128), F32)],
        compiler_params=pltpu.CompilerParams(**PARAMS),
        cost_estimate=cost(chunks * heads * 9 * 2 * 128**3, 11 * rows * width * 4),
        name="outward",
    )(s_in, w, u, qt, ou, t, o, gate, gain)


def inward_kernel(heads, gm_ref, out_ref, gate_ref, gain_ref, qt_ref, t_ref, maps_ref,
                  do_ref, dgate_ref, dgain_ref, tot_ref, run):
    step = pl.program_id(0)

    @pl.when(step == 0)
    def _():
        run[...] = jnp.zeros_like(run)
        dgain_ref[...] = jnp.zeros_like(dgain_ref)

    hs = range(heads)
    grads = []
    for h in hs:
        out, gate = out_ref[:, lanes(h)], gate_ref[:, lanes(h)]
        gm = gm_ref[:, lanes(h)].astype(F32)
        gain = gain_ref[0:1, lanes(h)]
        scale = lax.rsqrt(jnp.mean(out * out, axis=-1, keepdims=True) + epsilon)
        normed = out * scale
        sg = jax.nn.sigmoid(gate)
        act = gate * sg
        gn = gm * normed
        dgate_ref[:, lanes(h)] = (gn * gain * (sg * (1.0 + gate * (1.0 - sg)))).astype(LOW)
        dgain_ref[:, lanes(h)] += jnp.sum((gn * act).reshape(CHUNK // 8, 8, 128), axis=0)
        dn = gm * gain * act
        do = scale * (dn - normed * jnp.mean(dn * normed, axis=-1, keepdims=True))
        do_ref[:, lanes(h)] = do
        grads.append(do)
    for h in hs:
        left = jnp.concatenate([qt_ref[:, lanes(h)], t_ref[0, h]], axis=0)
        new = mm(left, jnp.concatenate([grads[h], run[h]], axis=0), TN)
        run[h] = new
        tot_ref[h] = jnp.concatenate([new, maps_ref[h, :, 128:]], axis=1)


def inward(gm, out, gate, gain, qt, t, maps, heads):
    rows, width = gm.shape
    chunks = rows // CHUNK
    flat, tiles = rows_spec(width, chunks, True), tile_spec(heads, chunks, True)
    return pl.pallas_call(
        functools.partial(inward_kernel, heads),
        out_shape=(sds(rows, width), sds(rows, width, dtype=LOW), sds(8, width), sds(heads, 128, 256)),
        grid=(chunks,),
        in_specs=[flat, flat, flat, whole_spec(8, width), flat, tiles, whole_spec(heads, 128, 256)],
        out_specs=[flat, flat, whole_spec(8, width), whole_spec(heads, 128, 256)],
        scratch_shapes=[pltpu.VMEM((heads, 128, 128), F32)],
        compiler_params=pltpu.CompilerParams(**PARAMS),
        cost_estimate=cost(chunks * heads * 6 * 2 * 128**3, 7 * rows * width * 4),
        name="inward",
    )(gm, out, gate, gain, qt, t, maps)


def back_kernel(docs, heads, chunks, scalars, *refs):
    mains, priors, rims = refs[0:3], refs[3:6], refs[6:9]
    narrow_ref, taps_ref, params_ref, ds_in = refs[9:13]
    (do_ref, v2_ref, s_ref, x_ref, p_ref, kg_ref, w_ref, u_ref, qt_ref, t_ref) = refs[13:23]
    grads_ref, tail_ref, rim_ref, gtaps_ref, gparams_ref = refs[23:28]
    run, after = refs[28:30]
    rev = pl.program_id(0)
    step = chunks - 1 - rev
    position = scalars[0] + step * CHUNK

    @pl.when(rev == 0)
    def _():
        run[...] = ds_in[...]
        after[...] = jnp.zeros_like(after)
        gtaps_ref[...] = jnp.zeros_like(gtaps_ref)
        gparams_ref[...] = jnp.zeros_like(gparams_ref)

    masks = chunk_masks(position, scalars, docs)
    pieces, befores = load_pieces(step, mains, priors, rims)
    taps = taps_ref[...]
    feats = features(pieces, befores, taps, masks, heads)
    shifted, rate, decays, beta, total, total_row = gates(narrow_ref[...], params_ref[...], masks)
    conv = [pre * sg for _, pre, sg in feats]
    lane = masks["col"]
    hs = range(heads)
    q, k, v, uq, uk, terms, b = [], [], [], [], [], [], []
    root = 1.0 / math.sqrt(128.0)
    for h in hs:
        cq, ck = conv[0][:, lanes(h)], conv[1][:, lanes(h)]
        uq.append(unit(cq))
        uk.append(unit(ck))
        q.append(cq * (uq[h] * root))
        k.append(ck * uk[h])
        v.append(conv[2][:, lanes(h)])
        terms.append(decay_terms(h, total, total_row, masks))
        b.append(beta[:, heads + h : heads + h + 1])
    do = [do_ref[:, lanes(h)] for h in hs]
    v2 = [v2_ref[:, lanes(h)] for h in hs]
    dsn = [run[h] for h in hs]
    kt = [terms[h][2] * k[h] for h in hs]
    dv2 = [mm(p_ref[0, h], do[h], TN) + mm(kt[h], dsn[h]) for h in hs]
    for h in hs:
        left = jnp.concatenate([qt_ref[:, lanes(h)], t_ref[0, h]], axis=0)
        run[h] = mm(left, jnp.concatenate([do[h], dsn[h]], axis=0), TN)
    states = [s_ref[0, h] for h in hs]
    both = [mm(jnp.concatenate([do[h], dv2[h]], axis=0), states[h], NT) for h in hs]
    dp = [jnp.where(masks["inside"], mm(do[h], v2[h], NT), 0.0) for h in hs]
    dkt = [mm(v2[h], dsn[h], NT) for h in hs]
    dx = [mm(x_ref[0, h], jnp.concatenate([-both[h][128:], dv2[h]], axis=1), TN) for h in hs]
    da = [
        jnp.where(
            masks["strict"],
            -mm(dx[h], jnp.concatenate([w_ref[:, lanes(h)], u_ref[:, lanes(h)]], axis=1), NT),
            0.0,
        )
        for h in hs
    ]
    gdecay = jnp.zeros((CHUNK, CHUNK), F32)
    gbeta = jnp.zeros((CHUNK, CHUNK), F32)
    minus = jnp.zeros((CHUNK, CHUNK), F32)
    dq, dk, dv = [], [], []
    for h in hs:
        spread, start, to_last, keep = terms[h]
        doq = both[h][:128]
        dqk = dp[h] * spread
        kgh = kg_ref[0, h]
        z = da[h] * kgh
        dkk = b[h] * da[h] * spread
        dxk, dxv = dx[h][:, :128], dx[h][:, 128:]
        stacked = jnp.concatenate([dqk, dkk], axis=0)
        forward = mm(stacked, k[h])
        backward = mm(stacked, jnp.concatenate([q[h], k[h]], axis=0), TN)
        kx = jnp.sum(k[h] * dxk, axis=-1, keepdims=True)
        dq.append(start * doq + forward[:128])
        dk.append(
            backward + forward[128:] + to_last * dkt[h] + (b[h] * start) * dxk
        )
        dv.append(b[h] * dxv)
        gb = (
            jnp.sum(z, axis=-1, keepdims=True)
            + jnp.sum(v[h] * dxv, axis=-1, keepdims=True)
            + start * kx
        )
        gamgrad = b[h] * z + dp[h] * p_ref[0, h]
        dstart = jnp.sum(q[h] * doq, axis=-1, keepdims=True) + b[h] * kx
        dlast = jnp.sum(k[h] * dkt[h], axis=-1, keepdims=True) * to_last
        dkeep = jnp.sum(states[h] * dsn[h], keepdims=True) * keep
        gcol = jnp.sum(gamgrad, axis=-1, keepdims=True) + dstart * start - dlast
        end = jnp.sum(dlast, keepdims=True) + dkeep
        gcol = gcol + jnp.where(masks["row"][:, :1] == CHUNK - 1, end, 0.0)
        grow = jnp.sum(gamgrad, axis=0, keepdims=True)
        gdecay = jnp.where(lane == h, gcol, gdecay)
        gbeta = jnp.where(lane == heads + h, gb, gbeta)
        minus = jnp.where(masks["row"] == h, grow, minus)
    gdecay = gdecay - minus.T
    upper = jnp.where(masks["row"] <= masks["col"], 1.0, 0.0)
    dg = mm_full(upper, gdecay)
    galpha = dg * rate * jax.nn.sigmoid(shifted)
    width = pieces[0].shape[1]
    grads_ref[:, 3 * width :] = jnp.where(
        lane < heads, galpha, gbeta * beta * (1.0 - beta)
    ).astype(LOW)
    gparams_ref[0:8, :] += jnp.sum((galpha).reshape(CHUNK // 8, 8, 128), axis=0)
    gparams_ref[8:16, :] += jnp.sum((dg * decays).reshape(CHUNK // 8, 8, 128), axis=0)

    for i in range(3):
        rows, pre, sg = feats[i]
        pieces_d = []
        for h in hs:
            if i == 2:
                pieces_d.append(dv[h])
            else:
                inv = uq[h] if i == 0 else uk[h]
                grad = dq[h] * root if i == 0 else dk[h]
                normal = conv[i][:, lanes(h)] * inv
                pieces_d.append(
                    inv * (grad - normal * jnp.sum(grad * normal, axis=-1, keepdims=True))
                )
        dc = jnp.concatenate(pieces_d, axis=1)
        ds = dc * (sg * (1.0 + pre * (1.0 - sg)))
        grad = ds * taps[4 * i + 3 : 4 * i + 4, :]
        rim = jnp.zeros((8, ds.shape[1]), F32)
        gtaps_ref[4 * i + 3] += jnp.sum((ds * rows[0]).reshape(CHUNK // 8, 8, -1), axis=0)
        for s in range(1, 4):
            tap = taps[4 * i + 3 - s : 4 * i + 4 - s, :]
            masked = jnp.where(masks["back"][s], ds, 0.0)
            gtaps_ref[4 * i + 3 - s] += jnp.sum((ds * rows[s]).reshape(CHUNK // 8, 8, -1), axis=0)
            ext = jnp.concatenate([masked, after[3 * i + s - 1]], axis=0)
            grad = grad + pltpu.roll(ext, CHUNK + 8 - s, 0)[:CHUNK] * tap
            after[3 * i + s - 1] = masked[:8]
            front = jnp.concatenate([jnp.zeros_like(masked[:8]), masked[:8]], axis=0)
            rim = rim + pltpu.roll(front, 16 - s, 0)[:8] * tap
        grads_ref[:, i * width : (i + 1) * width] = grad.astype(LOW)
        rim_ref[:, i * width : (i + 1) * width] = rim

        @pl.when(rev == 0)
        def _():
            tail_ref[:, i * width : (i + 1) * width] = grad[CHUNK - HALO :]


def back(scalars, pieces, rims, narrow, taps, params, ds_in, do, v2, s, x, p, kg, w, u, qt, t, docs, heads):
    rows, width = pieces[0].shape
    chunks = rows // CHUNK
    flat, tiles = rows_spec(width, chunks, True), tile_spec(heads, chunks, True)
    return pl.pallas_call(
        functools.partial(back_kernel, docs, heads, chunks),
        out_shape=(
            sds(rows, 3 * width + 128, dtype=LOW), sds(HALO, 3 * width), sds(8, 3 * width),
            sds(12, 8, width), sds(16, 128),
        ),
        grid_spec=pltpu.PrefetchScalarGridSpec(
            num_scalar_prefetch=1,
            grid=(chunks,),
            in_specs=[flat] * 3
            + [halo_spec(width, chunks, True)] * 3
            + [whole_spec(HALO, width)] * 3
            + [rows_spec(128, chunks, True), whole_spec(16, width), whole_spec(8, 128)]
            + [whole_spec(heads, 128, 128), flat, flat, tiles, tiles, tiles, tiles, flat, flat, flat, tiles],
            out_specs=[rows_spec(3 * width + 128, chunks, True)]
            + [whole_spec(HALO, 3 * width), whole_spec(8, 3 * width)]
            + [whole_spec(12, 8, width), whole_spec(16, 128)],
            scratch_shapes=[pltpu.VMEM((heads, 128, 128), F32), pltpu.VMEM((9, 8, width), F32)],
        ),
        compiler_params=pltpu.CompilerParams(**PARAMS),
        cost_estimate=cost(chunks * heads * 60 * 2 * 128**3, 16 * rows * width * 4),
        name="back",
    )(scalars, *pieces, *pieces, *rims, narrow, taps, params, ds_in, do, v2, s, x, p, kg, w, u, qt, t)


def contract_rows(left, right):
    return lax.dot_general(left, right, TN, preferred_element_type=F32)


def contract_cols(left, right):
    return lax.dot_general(left, right, NT, preferred_element_type=F32)


def dot(left, right):
    return jnp.dot(left, right, preferred_element_type=F32)


def row_norm(values, gain):
    return values * lax.rsqrt(jnp.mean(values * values, axis=-1, keepdims=True) + epsilon) * gain


def norm_back(values, gain, grad):
    inv = lax.rsqrt(jnp.mean(values * values, axis=-1, keepdims=True) + epsilon)
    scaled = grad * gain
    inner = jnp.mean(scaled * values, axis=-1, keepdims=True)
    return inv * scaled - values * (inner * inv * inv * inv), jnp.sum(grad * values * inv, axis=0)


MESH = pl.DeviceIdType.MESH


def greet(axis, parts):
    me = lax.axis_index(axis)
    barrier = pltpu.get_barrier_semaphore()

    @pl.when(me > 0)
    def _():
        pl.semaphore_signal(barrier, inc=1, device_id={axis: me - 1}, device_id_type=MESH)

    @pl.when(me < parts - 1)
    def _():
        pl.semaphore_signal(barrier, inc=1, device_id={axis: me + 1}, device_id_type=MESH)

    inner = (me > 0) & (me < parts - 1)

    @pl.when(inner)
    def _():
        pl.semaphore_wait(barrier, 2)

    @pl.when(jnp.logical_not(inner))
    def _():
        pl.semaphore_wait(barrier, 1)


def line_gather(parts, buf, sems, first, use):
    me = lax.axis_index("tensor")
    send_right, send_left, from_left, from_right = sems

    def rightward(piece, step):
        return pltpu.make_async_remote_copy(
            src_ref=buf.at[piece],
            dst_ref=buf.at[piece],
            send_sem=send_right.at[step],
            recv_sem=from_left.at[step],
            device_id={"tensor": me + 1},
            device_id_type=MESH,
        )

    def leftward(piece, step):
        return pltpu.make_async_remote_copy(
            src_ref=buf.at[piece],
            dst_ref=buf.at[piece],
            send_sem=send_left.at[step],
            recv_sem=from_right.at[step],
            device_id={"tensor": me - 1},
            device_id_type=MESH,
        )

    def body(step, _):
        low, high = me - step, me + step

        @pl.when((step > 0) & (low >= 0))
        def _():
            rightward(low, step - 1).wait_recv()

        @pl.when((low >= 0) & (me < parts - 1))
        def _():
            rightward(low, step).start()

        @pl.when((step > 0) & (high < parts))
        def _():
            leftward(high, step - 1).wait_recv()

        @pl.when((high < parts) & (me > 0))
        def _():
            leftward(high, step).start()

        @pl.when(step == 0)
        def _():
            first()

        @pl.when(low >= 0)
        def _():
            use(low)

        @pl.when((step > 0) & (high < parts))
        def _():
            use(high)

        return 0

    lax.fori_loop(0, parts, body, 0)

    def finish(step, _):
        low, high = me - step, me + step

        @pl.when((low >= 0) & (me < parts - 1))
        def _():
            rightward(low, step).wait_send()

        @pl.when((high < parts) & (me > 0))
        def _():
            leftward(high, step).wait_send()

        return 0

    lax.fori_loop(0, parts, finish, 0)


def norm_into(buf, me, source, gain):
    rows = source.shape[0]

    def body(i, _):
        at = pl.ds(pl.multiple_of(i * 64, 64), 64)
        values = source[at, :].astype(F32)
        scale = lax.rsqrt(jnp.mean(values * values, axis=-1, keepdims=True) + epsilon)
        buf[me, at, :] = (values * scale * gain[0:1, :]).astype(LOW)
        return 0

    lax.fori_loop(0, rows // 64, body, 0)


def project_kernel(parts, tok_ref, gain_ref, narrow_w, *refs):
    weights_in, all_ref = refs[0:4], refs[4]
    q_ref, k_ref, v_ref, gate_ref, narrow_ref = refs[5:10]
    buf, weights = refs[10], refs[11:15]
    sems, load_sem, store_sem = refs[15:19], refs[19], refs[20]
    me = lax.axis_index("tensor")
    rows = tok_ref.shape[0]
    loads = [
        pltpu.make_async_copy(weights_in[i], weights[i], load_sem.at[i]) for i in range(4)
    ]
    for load in loads:
        load.start()
    norm_into(buf, me, tok_ref, gain_ref)
    greet("tensor", parts)

    def first():
        for load in loads:
            load.wait()

    def stored(piece):
        at = pl.ds(pl.multiple_of(piece * rows, rows), rows)
        return pltpu.make_async_copy(buf.at[piece], all_ref.at[at, :], store_sem.at[piece])

    def use(piece):
        at = pl.ds(pl.multiple_of(piece * rows, rows), rows)
        stored(piece).start()
        values = buf[piece]
        for w, out in zip(weights, (q_ref, k_ref, v_ref, gate_ref)):
            out[at, :] = dot(values, w[...]).astype(out.dtype)
        narrow_ref[at, :] = dot(values, narrow_w[...])

    line_gather(parts, buf, sems, first, use)
    for piece in range(parts):
        stored(piece).wait()


def vmem():
    return pl.BlockSpec(memory_space=pltpu.VMEM)


def hbm():
    return pl.BlockSpec(memory_space=pl.ANY)


def line_sems(parts):
    return [pltpu.SemaphoreType.DMA((parts,))] * 4


def comm_params(number):
    return pltpu.CompilerParams(
        collective_id=number, has_side_effects=True, vmem_limit_bytes=60 * 1024 * 1024
    )


def project(parts, tokens, gain, narrow_w, weights):
    rows, model = tokens.shape
    width = weights[0].shape[1]
    total = rows * parts
    low = sds(total, width, dtype=LOW)
    return pl.pallas_call(
        functools.partial(project_kernel, parts),
        out_shape=(sds(total, model, dtype=LOW), low, low, low, sds(total, width), sds(total, 128)),
        in_specs=[vmem()] * 3 + [hbm()] * 4,
        out_specs=[hbm()] + [vmem()] * 5,
        scratch_shapes=[pltpu.VMEM((parts, rows, model), LOW)]
        + [pltpu.VMEM((model, width), LOW)] * 4
        + line_sems(parts)
        + [pltpu.SemaphoreType.DMA((4,)), pltpu.SemaphoreType.DMA((parts,))],
        compiler_params=comm_params(1),
        cost_estimate=cost(2 * total * model * (4 * width + 128), 60 * 2**20),
        name="project",
    )(tokens, gain, narrow_w, *weights)


def feed_kernel(parts, res_ref, gain_ref, *refs):
    weights_in, og_in = refs[0:3], refs[3]
    all_ref, act_ref, gu_ref = refs[4:7]
    buf, weights, og = refs[7], refs[8:11], refs[11]
    sems, load_sem, store_sem = refs[12:16], refs[16], refs[17]
    me = lax.axis_index("tensor")
    rows = res_ref.shape[0]
    units = weights_in[0].shape[1]
    loads = [
        pltpu.make_async_copy(src, dst, load_sem.at[i])
        for i, (src, dst) in enumerate(zip(weights_in + (og_in,), weights + (og,)))
    ]
    for load in loads:
        load.start()
    norm_into(buf, me, res_ref, gain_ref)
    greet("tensor", parts)
    wg, wu, wd = weights

    def first():
        for load in loads:
            load.wait()

    def stored(piece):
        at = pl.ds(pl.multiple_of(piece * rows, rows), rows)
        return pltpu.make_async_copy(buf.at[piece], all_ref.at[at, :], store_sem.at[piece])

    def tile(at, piece, column, size):
        cols = pl.ds(pl.multiple_of(column, 128), size)
        values = buf[piece]
        gate = dot(values, wg[:, cols])
        up = dot(values, wu[:, cols])
        grad = contract_cols(og[at, :], wd[cols, :])
        sg = jax.nn.sigmoid(gate)
        act = gate * sg
        act_ref[at, cols] = (act * up).astype(LOW)
        gu_ref[at, cols] = (grad * up * sg * (1.0 + gate * (1.0 - sg))).astype(LOW)
        gu_ref[at, pl.ds(pl.multiple_of(units + column, 128), size)] = (grad * act).astype(LOW)

    def use(piece):
        at = pl.ds(pl.multiple_of(piece * rows, rows), rows)
        stored(piece).start()

        def body(i, _):
            tile(at, piece, i * 256, 256)
            return 0

        lax.fori_loop(0, units // 256, body, 0)
        if units % 256:
            tile(at, piece, units - units % 256, units % 256)

    line_gather(parts, buf, sems, first, use)
    for piece in range(parts):
        stored(piece).wait()


def feed(parts, residual, gain, weights, out_grad):
    rows, model = residual.shape
    units = weights[0].shape[1]
    total = rows * parts
    return pl.pallas_call(
        functools.partial(feed_kernel, parts),
        out_shape=(
            sds(total, model, dtype=LOW), sds(total, units, dtype=LOW), sds(total, 2 * units, dtype=LOW),
        ),
        in_specs=[vmem()] * 2 + [hbm()] * 4,
        out_specs=[hbm()] + [vmem()] * 2,
        scratch_shapes=[pltpu.VMEM((parts, rows, model), LOW)]
        + [pltpu.VMEM(w.shape, LOW) for w in weights]
        + [pltpu.VMEM((total, model), LOW)]
        + line_sems(parts)
        + [pltpu.SemaphoreType.DMA((4,)), pltpu.SemaphoreType.DMA((parts,))],
        compiler_params=comm_params(2),
        cost_estimate=cost(6 * total * model * units, 120 * 2**20),
        name="feed",
    )(residual, gain, *weights, out_grad)


SUBS = 2


def scatter_kernel(parts, given, count, splits, *refs):
    lefts, rights_in, out_ref = refs[0:given], refs[given : given + count], refs[given + count]
    refs = refs[given + count + 1 :]
    rights, (part, send_r, send_l, got_l, got_r) = refs[0:count], refs[count : count + 5]
    sem_sr, sem_sl, sem_gl, sem_gr, load_sem = refs[count + 5 : count + 10]
    me = lax.axis_index("tensor")
    rows, model = out_ref.shape
    size = rows // SUBS
    loads = [
        pltpu.make_async_copy(rights_in[i], rights[i], load_sem.at[i]) for i in range(count)
    ]
    for load in loads:
        load.start()
    greet("tensor", parts)
    for load in loads:
        load.wait()

    def rightward(slot):
        return pltpu.make_async_remote_copy(
            src_ref=send_r.at[slot],
            dst_ref=got_l.at[slot],
            send_sem=sem_sr.at[slot],
            recv_sem=sem_gl.at[slot],
            device_id={"tensor": me + 1},
            device_id_type=MESH,
        )

    def leftward(slot):
        return pltpu.make_async_remote_copy(
            src_ref=send_l.at[slot],
            dst_ref=got_r.at[slot],
            send_sem=sem_sl.at[slot],
            recv_sem=sem_gr.at[slot],
            device_id={"tensor": me - 1},
            device_id_type=MESH,
        )

    def product(start, many, target):
        at = pl.ds(pl.multiple_of(start, 128), many)

        def body(j, _):
            cols = pl.ds(pl.multiple_of(j * 256, 256), 256)
            total = None
            for i, (index, first, wide) in enumerate(splits):
                term = contract_cols(lefts[index][at, first : first + wide], rights[i][cols, :])
                total = term if total is None else total + term
            target[:, cols] = total
            return 0

        lax.fori_loop(0, model // 256, body, 0)

    half = part.at[pl.ds(0, size), :]

    def go_right(piece, sub):
        slot = piece * SUBS + sub

        @pl.when(piece > me)
        def _():
            product(piece * rows + sub * size, size, half)

            @pl.when(me > 0)
            def _():
                rightward(slot).wait_recv()
                send_r[slot] = (half[...] + got_l[slot].astype(F32)).astype(LOW)

            @pl.when(me == 0)
            def _():
                send_r[slot] = half[...].astype(LOW)

            rightward(slot).start()

    def go_left(piece, sub):
        slot = piece * SUBS + sub

        @pl.when(piece < me)
        def _():
            product(piece * rows + sub * size, size, half)

            @pl.when(me < parts - 1)
            def _():
                leftward(slot).wait_recv()
                send_l[slot] = (half[...] + got_r[slot].astype(F32)).astype(LOW)

            @pl.when(me == parts - 1)
            def _():
                send_l[slot] = half[...].astype(LOW)

            leftward(slot).start()

    right_first = 2 * me < parts

    def body(item, _):
        step, sub = item // SUBS, item % SUBS
        right, left = parts - 1 - step, step

        @pl.when(right_first)
        def _():
            go_right(right, sub)

        go_left(left, sub)

        @pl.when(jnp.logical_not(right_first))
        def _():
            go_right(right, sub)

        return 0

    lax.fori_loop(0, (parts - 1) * SUBS, body, 0)
    product(me * rows, rows, part)
    for sub in range(SUBS):
        at = slice(sub * size, sub * size + size)
        slot = me * SUBS + sub
        out_ref[at, :] = part[at, :]

        @pl.when(me > 0)
        def _():
            rightward(slot).wait_recv()
            out_ref[at, :] = out_ref[at, :] + got_l[slot].astype(F32)

        @pl.when(me < parts - 1)
        def _():
            leftward(slot).wait_recv()
            out_ref[at, :] = out_ref[at, :] + got_r[slot].astype(F32)

    def finish(slot, _):
        piece = slot // SUBS

        @pl.when(piece > me)
        def _():
            rightward(slot).wait_send()

        @pl.when(piece < me)
        def _():
            leftward(slot).wait_send()

        return 0

    lax.fori_loop(0, parts * SUBS, finish, 0)


def scatter(parts, lefts, rights, splits, number):
    total = lefts[0].shape[0]
    model = rights[0].shape[0]
    rows = total // parts
    count = len(rights)
    slots = pltpu.VMEM((parts * SUBS, rows // SUBS, model), LOW)
    kernel = functools.partial(scatter_kernel, parts, len(lefts), count, splits)
    return pl.pallas_call(
        kernel,
        out_shape=sds(rows, model),
        in_specs=[vmem()] * len(lefts) + [hbm()] * count,
        out_specs=vmem(),
        scratch_shapes=[pltpu.VMEM(w.shape, LOW) for w in rights]
        + [pltpu.VMEM((rows, model), F32)]
        + [slots] * 4
        + line_sems(parts * SUBS)
        + [pltpu.SemaphoreType.DMA((count,))],
        compiler_params=comm_params(number),
        cost_estimate=cost(2 * total * model * sum(w.shape[1] for w in rights), 60 * 2**20),
        name="scatter%d" % number,
    )(*lefts, *rights)


def state_kernel(count, heads, backward, own_ref, out_ref, buf, send_sem, pass_sem, got_sem, own_sem):
    me = lax.axis_index("dp")
    core = lax.rem(me, 2)
    sibling = me + 1 - 2 * core
    half = count // 2
    barrier = pltpu.get_barrier_semaphore()

    def peer(k):
        return lax.rem(me + 2 * k, count)

    def hello(k, _):
        pl.semaphore_signal(barrier, inc=1, device_id={"dp": peer(k)}, device_id_type=MESH)
        return 0

    lax.fori_loop(1, half, hello, 0)
    pl.semaphore_signal(barrier, inc=1, device_id={"dp": sibling}, device_id_type=MESH)
    local = pltpu.make_async_copy(own_ref, buf.at[me], own_sem)
    local.start()
    local.wait()
    pl.semaphore_wait(barrier, half)

    def needed(source, target):
        return source > target if backward else source < target

    def copy(piece, target, sem):
        return pltpu.make_async_remote_copy(
            src_ref=buf.at[piece],
            dst_ref=buf.at[piece],
            send_sem=sem,
            recv_sem=got_sem.at[piece],
            device_id={"dp": target},
            device_id_type=MESH,
        )

    def send(k, _):
        target = peer(k)

        @pl.when(needed(me, target))
        def _():
            copy(me, target, send_sem.at[target]).start()

        return 0

    @pl.when(needed(me, sibling))
    def _():
        copy(me, sibling, pass_sem.at[me]).start()

    lax.fori_loop(1, half, send, 0)

    def relay(k, _):
        source = lax.rem(me + count - 2 * k, count)

        @pl.when(needed(source, me))
        def _():
            copy(source, me, send_sem.at[source]).wait_recv()

        @pl.when(needed(source, me) & needed(source, sibling))
        def _():
            copy(source, sibling, pass_sem.at[source]).start()

        return 0

    lax.fori_loop(1, half, relay, 0)
    for h in range(heads):
        out_ref[h] = jnp.zeros_like(out_ref[h])

    def chain(step, _):
        piece = count - 1 - step if backward else step

        @pl.when(needed(piece, me) & (lax.rem(piece, 2) != core))
        def _():
            copy(piece, me, pass_sem.at[piece]).wait_recv()

        @pl.when(needed(piece, me))
        def _():
            for h in range(heads):
                both = buf[piece, h]
                if backward:
                    out_ref[h] = mm(both[:, 128:], out_ref[h], TN) + both[:, :128]
                else:
                    out_ref[h] = mm(both[:, 128:], out_ref[h]) + both[:, :128]

        return 0

    lax.fori_loop(0, count, chain, 0)

    def finish(k, _):
        target = peer(k)
        source = lax.rem(me + count - 2 * k, count)

        @pl.when(needed(me, target))
        def _():
            copy(me, target, send_sem.at[target]).wait_send()

        @pl.when(needed(source, me) & needed(source, sibling))
        def _():
            copy(source, sibling, pass_sem.at[source]).wait_send()

        return 0

    lax.fori_loop(1, half, finish, 0)

    @pl.when(needed(me, sibling))
    def _():
        copy(me, sibling, pass_sem.at[me]).wait_send()


def exchange(count, own, heads, backward, number):
    return pl.pallas_call(
        functools.partial(state_kernel, count, heads, backward),
        out_shape=sds(heads, 128, 128),
        in_specs=[vmem()],
        out_specs=vmem(),
        scratch_shapes=[pltpu.VMEM((count, heads, 128, 256), F32)]
        + [pltpu.SemaphoreType.DMA((count,))] * 3
        + [pltpu.SemaphoreType.DMA],
        compiler_params=comm_params(number),
        cost_estimate=cost(count * heads * 6 * 128**3, count * heads * 256 * 128 * 4),
        name="exchange%d" % number,
    )(own)


def totals_kernel(count, parts, kept, own_ref, wide_ref, flat_ref, buf, mid, send1, got1, send2, got2):
    dp, z = lax.axis_index("dp"), lax.axis_index("tensor")
    barrier = pltpu.get_barrier_semaphore()

    def hello_dp(k, _):
        pl.semaphore_signal(
            barrier, inc=1, device_id={"dp": lax.rem(dp + k, count)}, device_id_type=MESH
        )
        return 0

    def hello_z(k, _):
        pl.semaphore_signal(
            barrier, inc=1, device_id={"tensor": lax.rem(z + k, parts)}, device_id_type=MESH
        )
        return 0

    lax.fori_loop(1, count, hello_dp, 0)
    lax.fori_loop(1, parts, hello_z, 0)
    buf[dp] = own_ref[...]
    pl.semaphore_wait(barrier, count + parts - 2)

    def over_dp(source, target):
        return pltpu.make_async_remote_copy(
            src_ref=buf.at[source],
            dst_ref=buf.at[source],
            send_sem=send1.at[target],
            recv_sem=got1.at[source],
            device_id={"dp": target},
            device_id_type=MESH,
        )

    def over_z(source, target):
        return pltpu.make_async_remote_copy(
            src_ref=mid.at[source],
            dst_ref=mid.at[source],
            send_sem=send2.at[target],
            recv_sem=got2.at[source],
            device_id={"tensor": target},
            device_id_type=MESH,
        )

    def each(total, me, action):
        def body(k, _):
            action(lax.rem(me + k, total))
            return 0

        lax.fori_loop(1, total, body, 0)

    each(count, dp, lambda other: over_dp(dp, other).start())
    each(count, dp, lambda other: over_dp(other, dp).wait_recv())
    total = buf[0]
    for i in range(1, count):
        total = total + buf[i]
    mid[z] = total
    each(parts, z, lambda other: over_z(z, other).start())
    each(parts, z, lambda other: over_z(other, z).wait_recv())
    width = own_ref.shape[1]
    flat = mid[0, kept:, :]
    for i in range(parts):
        wide_ref[:, i * width : (i + 1) * width] = mid[i, :kept, :]
        if i:
            flat = flat + mid[i, kept:, :]
    flat_ref[...] = flat
    each(count, dp, lambda other: over_dp(dp, other).wait_send())
    each(parts, z, lambda other: over_z(z, other).wait_send())


def totals_of(count, parts, own, kept, number):
    rows, width = own.shape
    return pl.pallas_call(
        functools.partial(totals_kernel, count, parts, kept),
        out_shape=(sds(kept, width * parts), sds(rows - kept, width)),
        in_specs=[vmem()],
        out_specs=[vmem(), vmem()],
        scratch_shapes=[pltpu.VMEM((count, rows, width), F32), pltpu.VMEM((parts, rows, width), F32)]
        + [pltpu.SemaphoreType.DMA((count,))] * 2
        + [pltpu.SemaphoreType.DMA((parts,))] * 2,
        compiler_params=comm_params(number),
        cost_estimate=cost(count * rows * width, count * rows * width * 4),
        name="totals",
    )(own)


def after(values, *first):
    out = lax.optimization_barrier((values,) + first)
    return out[0]


def local(
    tokens,
    gain_in,
    w_query,
    w_key,
    w_value,
    w_alpha,
    w_beta,
    w_gate_out,
    conv_query,
    conv_key,
    conv_value,
    decay_log,
    decay_bias,
    head_gain,
    w_out,
    gain_mid,
    w_gate,
    w_up,
    w_down,
    out_grad,
    doc_lengths,
):
    rows_own, model = tokens.shape
    tensor_parts, dp_parts = lax.axis_size("tensor"), lax.axis_size("dp")
    tensor_index, dp_index = lax.axis_index("tensor"), lax.axis_index("dp")
    group_rows = rows_own * tensor_parts
    seq_total = group_rows * dp_parts
    heads = w_alpha.shape[1]
    width = w_query.shape[1]
    docs = doc_lengths.shape[0] * doc_lengths.shape[1]
    starts = (
        jnp.cumsum(doc_lengths, axis=1)
        - doc_lengths
        + seq_total * lax.broadcasted_iota(jnp.int32, doc_lengths.shape, 0)
    ).reshape(-1)
    scalars = jnp.concatenate([(dp_index * group_rows).reshape(1), starts]).astype(jnp.int32)
    taps = jnp.concatenate([conv_query, conv_key, conv_value, jnp.zeros((4, width), F32)])
    params = jnp.zeros((8, 128), F32).at[0, :heads].set(decay_bias).at[1, :heads].set(decay_log)
    gain_heads = jnp.broadcast_to(head_gain[None], (8, width))
    w_narrow = jnp.pad(jnp.concatenate([w_alpha, w_beta], axis=1), ((0, 0), (0, 128 - 2 * heads)))

    own_rows = tokens.astype(F32)
    gain_in_rows = jnp.broadcast_to(gain_in[None], (8, model))
    gain_mid_rows = jnp.broadcast_to(gain_mid[None], (8, model))
    normed_all, *pieces, gate_raw, narrow = project(
        tensor_parts, tokens, gain_in_rows, w_narrow, (w_query, w_key, w_value, w_gate_out)
    )
    half = width // 2
    core = lax.rem(dp_index, 2)
    out_half = lax.dynamic_slice_in_dim(after(w_out, narrow), core * half, half, 0)
    out_mine = lax.all_gather(out_half, "tensor", axis=0)
    forth = [(i, i + 1) for i in range(dp_parts - 1)]
    rims = lax.ppermute(
        jnp.stack([piece[group_rows - HALO :] for piece in pieces]), "dp", forth
    )
    rims = [rims[i] for i in range(3)]
    x, p, kg, w, u, qt, ou, t, o, totals = intra(
        scalars, pieces, rims, narrow, taps, params, docs, heads
    )
    state_in = exchange(dp_parts, totals, heads, False, 3)
    out_other = lax.ppermute(after(out_mine, state_in), "dp", [(i, i ^ 1) for i in range(dp_parts)])
    w_out_full = jnp.stack(
        [jnp.where(core == 0, out_mine, out_other), jnp.where(core == 0, out_other, out_mine)],
        axis=1,
    ).reshape(width * tensor_parts, model)
    rows_out, v2, s, mixed = outward(state_in, w, u, qt, ou, t, o, gate_raw, gain_heads, heads)

    mixed_own = lax.all_to_all(mixed, "tensor", split_axis=0, concat_axis=1, tiled=True)
    residual = own_rows + dot(mixed_own, w_out_full)
    mid_all, activated, grad_units = feed(
        tensor_parts, residual, gain_mid_rows, (w_gate, w_up, w_down), out_grad
    )
    units = w_gate.shape[1]
    ring = [(i, (i + 1) % tensor_parts) for i in range(tensor_parts)]

    def piece_of(values, back_by):
        index = lax.rem(tensor_index - back_by + tensor_parts, tensor_parts)
        return lax.dynamic_slice_in_dim(values, index * rows_own, rows_own, 0)

    def added(values, back_by, got):
        return (piece_of(values, back_by).astype(F32) + got.astype(F32)).astype(LOW)

    mlp_part = dot(activated, w_down).astype(LOW)
    mlp_run = lax.ppermute(piece_of(mlp_part, 1), "tensor", ring)
    out_grad_2, activated_2, mlp_part = lax.optimization_barrier((out_grad, activated, mlp_part))
    down_grad = contract_rows(out_grad_2, activated_2).astype(LOW)
    units_grad = contract_rows(mid_all, after(grad_units, down_grad)).astype(LOW)
    down_grad_sum = lax.psum_scatter(down_grad, "dp", scatter_dimension=0, tiled=True)
    units_grad_sum = lax.psum_scatter(units_grad, "dp", scatter_dimension=0, tiled=True)

    grad_mid = scatter(
        tensor_parts, [after(grad_units, units_grad, mlp_run)], [w_gate, w_up],
        ((0, 0, units), (0, units, units)), 4,
    )
    grad_res_norm, gain_mid_grad = norm_back(residual, gain_mid, grad_mid)
    grad_own = lax.dynamic_slice_in_dim(out_grad, tensor_index * rows_own, rows_own, 0)
    grad_residual = grad_own.astype(F32) + grad_res_norm
    grad_mixer = grad_residual.astype(LOW)
    grad_mixed_own = contract_cols(grad_mixer, w_out_full).astype(LOW)
    grad_mixed = lax.all_to_all(
        grad_mixed_own, "tensor", split_axis=1, concat_axis=0, tiled=True
    )
    mixer_pieces = [grad_mixer]
    grad_mixer_1, mlp_run = lax.optimization_barrier((grad_mixer, mlp_run, grad_mixed))[:2]
    mixer_pieces.append(lax.ppermute(grad_mixer_1, "tensor", ring))
    for back_by in range(2, tensor_parts - 1):
        mlp_run = lax.ppermute(added(mlp_part, back_by, mlp_run), "tensor", ring)

    do, gate_low, head_gain_part, ds_total = inward(
        grad_mixed, rows_out, gate_raw, gain_heads, qt, t, totals, heads
    )
    grad_end = exchange(dp_parts, ds_total, heads, True, 5)
    grad_end, piece_1, mlp_run, _, _ = lax.optimization_barrier(
        (grad_end, mixer_pieces[1], mlp_run, units_grad_sum, down_grad_sum)
    )
    mixer_pieces[1] = piece_1
    mixer_pieces.append(lax.ppermute(piece_1, "tensor", ring))
    mlp_run = lax.ppermute(added(mlp_part, tensor_parts - 1, mlp_run), "tensor", ring)
    output = (residual + (piece_of(mlp_part, 0).astype(F32) + mlp_run.astype(F32))).astype(LOW)
    grads, tails, rim_grad, taps_grad, params_grad = back(
        scalars, pieces, rims, narrow, taps, params, grad_end, do, v2, s, x, p, kg, w, u, qt, t,
        docs, heads,
    )
    rim_back = lax.ppermute(rim_grad, "dp", [(i + 1, i) for i in range(dp_parts - 1)])
    tails = tails.at[HALO - 8 :].add(rim_back).astype(LOW)
    grads = lax.dynamic_update_slice(grads, tails, (group_rows - HALO, 0))
    grads, piece_last, _ = lax.optimization_barrier((grads, mixer_pieces[-1], mlp_run))
    for _ in range(3, tensor_parts):
        piece_last = lax.ppermute(piece_last, "tensor", ring)
        mixer_pieces.append(piece_last)
    grads_w = contract_rows(normed_all, grads).astype(LOW)
    gate_w = contract_rows(normed_all, gate_low).astype(LOW)
    grad_mixer_all = jnp.zeros((group_rows, model), LOW)
    for back_by, piece in enumerate(mixer_pieces):
        index = lax.rem(tensor_index - back_by + tensor_parts, tensor_parts)
        grad_mixer_all = lax.dynamic_update_slice_in_dim(
            grad_mixer_all, piece, index * rows_own, 0
        )
    out_w = contract_rows(after(grad_mixer_all, grads_w, gate_w), mixed).astype(LOW)
    mixer_grad = jnp.concatenate([grads_w, gate_w, out_w], axis=1)
    mixer_sum = lax.psum_scatter(mixer_grad, "dp", scatter_dimension=0, tiled=True).astype(F32)
    grad_normed = scatter(
        tensor_parts, [after(grads, mixer_grad), gate_low],
        [w_query, w_key, w_value, w_narrow, w_gate_out],
        ((0, 0, width), (0, width, width), (0, 2 * width, width), (0, 3 * width, 128), (1, 0, width)),
        6,
    )
    grad_tokens, gain_in_grad = norm_back(own_rows, gain_in, grad_normed)
    input_grad = grad_residual + grad_tokens

    params_grad = params_grad.reshape(2, 8, 128).sum(1)
    flat = jnp.concatenate(
        [
            taps_grad.sum(1),
            head_gain_part.sum(0)[None],
            jnp.pad(params_grad, ((0, 1), (0, width - 128))),
            gain_in_grad.reshape(-1, width),
            gain_mid_grad.reshape(-1, width),
        ],
        axis=0,
    )
    wide, gains = totals_of(dp_parts, tensor_parts, flat, 16, 7)
    by_head = wide[13:15].reshape(2, tensor_parts, width)[:, :, :heads].reshape(2, -1)
    gains = gains.reshape(2, model)
    start = 3 * width
    return (
        output,
        input_grad,
        gains[0],
        mixer_sum[:, :width],
        mixer_sum[:, width : 2 * width],
        mixer_sum[:, 2 * width : start],
        mixer_sum[:, start : start + heads],
        mixer_sum[:, start + heads : start + 2 * heads],
        mixer_sum[:, start + 128 : start + 128 + width],
        wide[0:4],
        wide[4:8],
        wide[8:12],
        by_head[1],
        by_head[0],
        wide[12],
        mixer_sum[:, start + 128 + width :].T,
        gains[1],
        units_grad_sum[:, :units].astype(F32),
        units_grad_sum[:, units:].astype(F32),
        down_grad_sum.T.astype(F32),
    )


def solution(mesh):
    placed = (
        P(("dp", "tensor"), None),
        P(),
        P(None, "tensor"),
        P(None, "tensor"),
        P(None, "tensor"),
        P(None, "tensor"),
        P(None, "tensor"),
        P(None, "tensor"),
        P(None, "tensor"),
        P(None, "tensor"),
        P(None, "tensor"),
        P("tensor"),
        P("tensor"),
        P("tensor"),
        P("tensor", None),
        P(),
        P(None, "tensor"),
        P(None, "tensor"),
        P("tensor", None),
        P("dp", None),
        P(),
    )
    return jax.shard_map(
        local,
        mesh=mesh,
        in_specs=placed,
        out_specs=(
            P(("dp", "tensor"), None),
            P(("dp", "tensor"), None),
            P(),
            P("dp", "tensor"),
            P("dp", "tensor"),
            P("dp", "tensor"),
            P("dp", "tensor"),
            P("dp", "tensor"),
            P("dp", "tensor"),
            P(),
            P(),
            P(),
            P(),
            P(),
            P(),
            P("tensor", "dp"),
            P(),
            P("dp", "tensor"),
            P("dp", "tensor"),
            P("tensor", "dp"),
        ),
        check_vma=False,
    )
```

```python
import functools
import math

import jax
import jax.numpy as jnp
from jax import lax
from jax.experimental import pallas as pl
from jax.experimental.pallas import tpu as pltpu
from jax.sharding import PartitionSpec as P

CHUNK = 128
HALO = 16
epsilon = 1e-06
F32 = jnp.float32
LOW = jnp.bfloat16
NN = (((1,), (0,)), ((), ()))
NT = (((1,), (1,)), ((), ()))
TN = (((0,), (0,)), ((), ()))


def mm(left, right, dims=NN):
    return lax.dot_general(
        left, right, dims, precision=lax.Precision.HIGH, preferred_element_type=F32
    )


def mm_full(left, right, dims=NN):
    return lax.dot_general(
        left, right, dims, precision=lax.Precision.HIGHEST, preferred_element_type=F32
    )


def iota(shape, dim):
    return lax.broadcasted_iota(jnp.int32, shape, dim)


def doc_of(positions, scalars, docs):
    total = jnp.zeros_like(positions) - 1
    for j in range(docs):
        total = total + jnp.where(positions >= scalars[1 + j], 1, 0)
    return total


def chunk_masks(position, scalars, docs):
    shape = (CHUNK, CHUNK)
    row, col = iota(shape, 0), iota(shape, 1)
    doc_row = doc_of(row + position, scalars, docs)
    doc_col = doc_of(col + position, scalars, docs)
    same = doc_row == doc_col
    prior = jnp.int32(-1)
    last = jnp.int32(-1)
    for j in range(docs):
        prior = prior + jnp.where(position - 1 >= scalars[1 + j], 1, 0)
        last = last + jnp.where(position + CHUNK - 1 >= scalars[1 + j], 1, 0)
    return {
        "row": row,
        "col": col,
        "inside": same & (row >= col),
        "strict": same & (row > col),
        "carried": (doc_row == prior)[:, :1],
        "in_last": (doc_row == last)[:, :1],
        "last_carried": last == prior,
        "back": [
            None if s == 0 else (doc_row == doc_of(row + (position - s), scalars, docs))[:, :1]
            for s in range(4)
        ],
    }


def shifted_rows(main, before, back):
    ext = jnp.concatenate([before[HALO - 8 :], main], axis=0)
    rows = [main]
    for s in range(1, 4):
        rows.append(jnp.where(back[s], pltpu.roll(ext, s, 0)[8:], 0.0))
    return rows


def conv_sum(rows, taps):
    total = rows[0] * taps[3:4, :]
    for s in range(1, 4):
        total = total + rows[s] * taps[3 - s : 4 - s, :]
    return total


def softplus(x):
    return jnp.maximum(x, 0.0) + jnp.log1p(jnp.exp(-jnp.abs(x)))


def gates(narrow, params, masks):
    shifted = narrow + params[0:1, :]
    rate = -jnp.exp(params[1:2, :])
    decays = rate * softplus(shifted)
    lower = jnp.where(masks["row"] >= masks["col"], 1.0, 0.0)
    total = mm_full(lower, decays)
    return shifted, rate, decays, jax.nn.sigmoid(narrow), total, total.T


def decay_terms(h, total, total_row, masks):
    col = total[:, h : h + 1]
    row = total_row[h : h + 1, :]
    spread = jnp.where(
        masks["inside"], jnp.exp(jnp.where(masks["inside"], col - row, 0.0)), 0.0
    )
    start = jnp.where(masks["carried"], jnp.exp(col), 0.0)
    end = total[CHUNK - 1 : CHUNK, h : h + 1]
    to_last = jnp.where(masks["in_last"], jnp.exp(jnp.where(masks["in_last"], end - col, 0.0)), 0.0)
    keep = jnp.where(masks["last_carried"], jnp.exp(end), 0.0)
    return spread, start, to_last, keep


def lanes(h):
    return slice(h * 128, h * 128 + 128)


def features(pieces, befores, taps, masks, heads):
    out = []
    for i in range(3):
        rows = shifted_rows(pieces[i], befores[i], masks["back"])
        pre = conv_sum(rows, taps[4 * i : 4 * i + 4, :])
        out.append((rows, pre, jax.nn.sigmoid(pre)))
    return out


def unit(values):
    return lax.rsqrt(jnp.sum(values * values, axis=-1, keepdims=True) + epsilon)


def load_pieces(step, mains, priors, rims):
    pieces = [m[...].astype(F32) for m in mains]
    befores = [
        jnp.where(step == 0, r[...].astype(F32), p[...].astype(F32)) for p, r in zip(priors, rims)
    ]
    return pieces, befores


def intra_kernel(docs, heads, scalars, *refs):
    mains, priors, rims = refs[0:3], refs[3:6], refs[6:9]
    narrow_ref, taps_ref, params_ref = refs[9:12]
    x_ref, p_ref, kg_ref, w_ref, u_ref, qt_ref, ou_ref, t_ref, o_ref, tot_ref = refs[12:22]
    run = refs[22]
    step = pl.program_id(0)
    position = scalars[0] + step * CHUNK
    masks = chunk_masks(position, scalars, docs)
    pieces, befores = load_pieces(step, mains, priors, rims)
    feats = features(pieces, befores, taps_ref[...], masks, heads)
    _, _, _, beta, total, total_row = gates(narrow_ref[...], params_ref[...], masks)
    eye = jnp.where(masks["row"] == masks["col"], 1.0, 0.0)
    conv = [pre * sg for _, pre, sg in feats]
    hs = range(heads)
    q, k, v, terms, b = [], [], [], [], []
    for h in hs:
        cq, ck = conv[0][:, lanes(h)], conv[1][:, lanes(h)]
        q.append(cq * (unit(cq) * (1.0 / math.sqrt(128.0))))
        k.append(ck * unit(ck))
        v.append(conv[2][:, lanes(h)])
        terms.append(decay_terms(h, total, total_row, masks))
        b.append(beta[:, heads + h : heads + h + 1])
    kg = [jnp.where(masks["strict"], mm(k[h], k[h], NT) * terms[h][0], 0.0) for h in hs]
    p = [mm(q[h], k[h], NT) * terms[h][0] for h in hs]
    a = [b[h] * kg[h] for h in hs]
    pair = (masks["row"] >> 1) == (masks["col"] >> 1)
    x = [eye - jnp.where(pair, a[h], 0.0) for h in hs]
    for level in range(1, 7):
        wide = (masks["row"] >> (level + 1)) == (masks["col"] >> (level + 1))
        off = wide & ((masks["row"] >> level) != (masks["col"] >> level))
        lx = [mm(jnp.where(off, a[h], 0.0), x[h]) for h in hs]
        x = [x[h] - mm(x[h], lx[h]) for h in hs]
    wu = [
        mm(x[h], jnp.concatenate([(b[h] * terms[h][1]) * k[h], b[h] * v[h]], axis=1)) for h in hs
    ]
    pwu = [mm(p[h], wu[h]) for h in hs]
    kwu = [mm(terms[h][2] * k[h], wu[h], TN) for h in hs]

    @pl.when(step == 0)
    def _():
        for h in hs:
            run[h] = jnp.concatenate([jnp.zeros((128, 128), F32), eye], axis=1)

    for h in hs:
        x_ref[0, h] = x[h]
        p_ref[0, h] = p[h]
        kg_ref[0, h] = kg[h]
        w_ref[:, lanes(h)] = wu[h][:, :128]
        u_ref[:, lanes(h)] = wu[h][:, 128:]
        qt_ref[:, lanes(h)] = terms[h][1] * q[h] - pwu[h][:, :128]
        ou_ref[:, lanes(h)] = pwu[h][:, 128:]
        transfer = terms[h][3] * eye - kwu[h][:, :128]
        offset = kwu[h][:, 128:]
        t_ref[0, h] = transfer
        o_ref[0, h] = offset
        new = mm(transfer, run[h])
        new = jnp.concatenate([new[:, :128] + offset, new[:, 128:]], axis=1)
        run[h] = new
        tot_ref[h] = new


def rows_spec(width, chunks, reverse=False):
    if reverse:
        return pl.BlockSpec((CHUNK, width), lambda c, *_: (chunks - 1 - c, 0))
    return pl.BlockSpec((CHUNK, width), lambda c, *_: (c, 0))


def halo_spec(width, chunks, reverse=False):
    per = CHUNK // HALO
    if reverse:
        return pl.BlockSpec(
            (HALO, width), lambda c, *_: (jnp.maximum((chunks - 1 - c) * per - 1, 0), 0)
        )
    return pl.BlockSpec((HALO, width), lambda c, *_: (jnp.maximum(c * per - 1, 0), 0))


def tile_spec(heads, chunks, reverse=False):
    if reverse:
        return pl.BlockSpec((1, heads, 128, 128), lambda c, *_: (chunks - 1 - c, 0, 0, 0))
    return pl.BlockSpec((1, heads, 128, 128), lambda c, *_: (c, 0, 0, 0))


def whole_spec(*shape):
    zeros = (0,) * len(shape)
    return pl.BlockSpec(shape, lambda c, *_: zeros)


def sds(*shape, dtype=F32):
    return jax.ShapeDtypeStruct(shape, dtype)


PARAMS = dict(vmem_limit_bytes=56 * 1024 * 1024, dimension_semantics=("arbitrary",))


def cost(flops, moved):
    return pl.CostEstimate(flops=int(flops), bytes_accessed=int(moved), transcendentals=0)


def intra(scalars, pieces, rims, narrow, taps, params, docs, heads):
    rows, width = pieces[0].shape
    chunks = rows // CHUNK
    tiles, flat = sds(chunks, heads, 128, 128), sds(rows, width)
    return pl.pallas_call(
        functools.partial(intra_kernel, docs, heads),
        out_shape=(tiles, tiles, tiles, flat, flat, flat, flat, tiles, tiles, sds(heads, 128, 256)),
        grid_spec=pltpu.PrefetchScalarGridSpec(
            num_scalar_prefetch=1,
            grid=(chunks,),
            in_specs=[rows_spec(width, chunks)] * 3
            + [halo_spec(width, chunks)] * 3
            + [whole_spec(HALO, width)] * 3
            + [rows_spec(128, chunks), whole_spec(16, width), whole_spec(8, 128)],
            out_specs=[tile_spec(heads, chunks)] * 3
            + [rows_spec(width, chunks)] * 4
            + [tile_spec(heads, chunks)] * 2
            + [whole_spec(heads, 128, 256)],
            scratch_shapes=[pltpu.VMEM((heads, 128, 256), F32)],
        ),
        compiler_params=pltpu.CompilerParams(**PARAMS),
        cost_estimate=cost(chunks * heads * 60 * 3 * 2 * 128**3, 30 * rows * width * 4),
        name="intra",
    )(scalars, *pieces, *pieces, *rims, narrow, taps, params)


def outward_kernel(heads, s_in, w_ref, u_ref, qt_ref, ou_ref, t_ref, o_ref, gate_ref, gain_ref,
                   out_ref, v2_ref, s_ref, mixed_ref, run):
    step = pl.program_id(0)

    @pl.when(step == 0)
    def _():
        run[...] = s_in[...]

    hs = range(heads)
    state = [run[h] for h in hs]
    full = [
        mm(
            jnp.concatenate([qt_ref[:, lanes(h)], w_ref[:, lanes(h)], t_ref[0, h]], axis=0),
            state[h],
        )
        for h in hs
    ]
    for h in hs:
        out = full[h][:128] + ou_ref[:, lanes(h)]
        v2_ref[:, lanes(h)] = u_ref[:, lanes(h)] - full[h][128:256]
        s_ref[0, h] = state[h]
        run[h] = full[h][256:] + o_ref[0, h]
        out_ref[:, lanes(h)] = out
        gate = gate_ref[:, lanes(h)]
        scale = lax.rsqrt(jnp.mean(out * out, axis=-1, keepdims=True) + epsilon)
        mixed_ref[:, lanes(h)] = (
            out * scale * gain_ref[0:1, lanes(h)] * (gate * jax.nn.sigmoid(gate))
        ).astype(LOW)


def outward(s_in, w, u, qt, ou, t, o, gate, gain, heads):
    rows, width = w.shape
    chunks = rows // CHUNK
    flat, tiles = rows_spec(width, chunks), tile_spec(heads, chunks)
    return pl.pallas_call(
        functools.partial(outward_kernel, heads),
        out_shape=(sds(rows, width), sds(rows, width), sds(chunks, heads, 128, 128), sds(rows, width, dtype=LOW)),
        grid=(chunks,),
        in_specs=[whole_spec(heads, 128, 128), flat, flat, flat, flat, tiles, tiles, flat, whole_spec(8, width)],
        out_specs=[flat, flat, tiles, flat],
        scratch_shapes=[pltpu.VMEM((heads, 128, 128), F32)],
        compiler_params=pltpu.CompilerParams(**PARAMS),
        cost_estimate=cost(chunks * heads * 9 * 2 * 128**3, 11 * rows * width * 4),
        name="outward",
    )(s_in, w, u, qt, ou, t, o, gate, gain)


def inward_kernel(heads, gm_ref, out_ref, gate_ref, gain_ref, qt_ref, t_ref, maps_ref,
                  do_ref, dgate_ref, dgain_ref, tot_ref, run):
    step = pl.program_id(0)

    @pl.when(step == 0)
    def _():
        run[...] = jnp.zeros_like(run)
        dgain_ref[...] = jnp.zeros_like(dgain_ref)

    hs = range(heads)
    grads = []
    for h in hs:
        out, gate = out_ref[:, lanes(h)], gate_ref[:, lanes(h)]
        gm = gm_ref[:, lanes(h)].astype(F32)
        gain = gain_ref[0:1, lanes(h)]
        scale = lax.rsqrt(jnp.mean(out * out, axis=-1, keepdims=True) + epsilon)
        normed = out * scale
        sg = jax.nn.sigmoid(gate)
        act = gate * sg
        gn = gm * normed
        dgate_ref[:, lanes(h)] = (gn * gain * (sg * (1.0 + gate * (1.0 - sg)))).astype(LOW)
        dgain_ref[:, lanes(h)] += jnp.sum((gn * act).reshape(CHUNK // 8, 8, 128), axis=0)
        dn = gm * gain * act
        do = scale * (dn - normed * jnp.mean(dn * normed, axis=-1, keepdims=True))
        do_ref[:, lanes(h)] = do
        grads.append(do)
    for h in hs:
        left = jnp.concatenate([qt_ref[:, lanes(h)], t_ref[0, h]], axis=0)
        new = mm(left, jnp.concatenate([grads[h], run[h]], axis=0), TN)
        run[h] = new
        tot_ref[h] = jnp.concatenate([new, maps_ref[h, :, 128:]], axis=1)


def inward(gm, out, gate, gain, qt, t, maps, heads):
    rows, width = gm.shape
    chunks = rows // CHUNK
    flat, tiles = rows_spec(width, chunks, True), tile_spec(heads, chunks, True)
    return pl.pallas_call(
        functools.partial(inward_kernel, heads),
        out_shape=(sds(rows, width), sds(rows, width, dtype=LOW), sds(8, width), sds(heads, 128, 256)),
        grid=(chunks,),
        in_specs=[flat, flat, flat, whole_spec(8, width), flat, tiles, whole_spec(heads, 128, 256)],
        out_specs=[flat, flat, whole_spec(8, width), whole_spec(heads, 128, 256)],
        scratch_shapes=[pltpu.VMEM((heads, 128, 128), F32)],
        compiler_params=pltpu.CompilerParams(**PARAMS),
        cost_estimate=cost(chunks * heads * 6 * 2 * 128**3, 7 * rows * width * 4),
        name="inward",
    )(gm, out, gate, gain, qt, t, maps)


def back_kernel(docs, heads, chunks, scalars, *refs):
    mains, priors, rims = refs[0:3], refs[3:6], refs[6:9]
    narrow_ref, taps_ref, params_ref, ds_in = refs[9:13]
    (do_ref, v2_ref, s_ref, x_ref, p_ref, kg_ref, w_ref, u_ref, qt_ref, t_ref) = refs[13:23]
    dgate_ref, grads_ref, tail_ref, rim_ref, gtaps_ref, gparams_ref = refs[23:29]
    run, after = refs[29:31]
    rev = pl.program_id(0)
    step = chunks - 1 - rev
    position = scalars[0] + step * CHUNK

    @pl.when(rev == 0)
    def _():
        run[...] = ds_in[...]
        after[...] = jnp.zeros_like(after)
        gtaps_ref[...] = jnp.zeros_like(gtaps_ref)
        gparams_ref[...] = jnp.zeros_like(gparams_ref)

    masks = chunk_masks(position, scalars, docs)
    pieces, befores = load_pieces(step, mains, priors, rims)
    taps = taps_ref[...]
    feats = features(pieces, befores, taps, masks, heads)
    shifted, rate, decays, beta, total, total_row = gates(narrow_ref[...], params_ref[...], masks)
    conv = [pre * sg for _, pre, sg in feats]
    lane = masks["col"]
    hs = range(heads)
    q, k, v, uq, uk, terms, b = [], [], [], [], [], [], []
    root = 1.0 / math.sqrt(128.0)
    for h in hs:
        cq, ck = conv[0][:, lanes(h)], conv[1][:, lanes(h)]
        uq.append(unit(cq))
        uk.append(unit(ck))
        q.append(cq * (uq[h] * root))
        k.append(ck * uk[h])
        v.append(conv[2][:, lanes(h)])
        terms.append(decay_terms(h, total, total_row, masks))
        b.append(beta[:, heads + h : heads + h + 1])
    do = [do_ref[:, lanes(h)] for h in hs]
    v2 = [v2_ref[:, lanes(h)] for h in hs]
    dsn = [run[h] for h in hs]
    kt = [terms[h][2] * k[h] for h in hs]
    dv2 = [mm(p_ref[0, h], do[h], TN) + mm(kt[h], dsn[h]) for h in hs]
    for h in hs:
        left = jnp.concatenate([qt_ref[:, lanes(h)], t_ref[0, h]], axis=0)
        run[h] = mm(left, jnp.concatenate([do[h], dsn[h]], axis=0), TN)
    states = [s_ref[0, h] for h in hs]
    both = [mm(jnp.concatenate([do[h], dv2[h]], axis=0), states[h], NT) for h in hs]
    dp = [jnp.where(masks["inside"], mm(do[h], v2[h], NT), 0.0) for h in hs]
    dkt = [mm(v2[h], dsn[h], NT) for h in hs]
    dx = [mm(x_ref[0, h], jnp.concatenate([-both[h][128:], dv2[h]], axis=1), TN) for h in hs]
    da = [
        jnp.where(
            masks["strict"],
            -mm(dx[h], jnp.concatenate([w_ref[:, lanes(h)], u_ref[:, lanes(h)]], axis=1), NT),
            0.0,
        )
        for h in hs
    ]
    gdecay = jnp.zeros((CHUNK, CHUNK), F32)
    gbeta = jnp.zeros((CHUNK, CHUNK), F32)
    minus = jnp.zeros((CHUNK, CHUNK), F32)
    dq, dk, dv = [], [], []
    for h in hs:
        spread, start, to_last, keep = terms[h]
        doq = both[h][:128]
        dqk = dp[h] * spread
        kgh = kg_ref[0, h]
        z = da[h] * kgh
        dkk = b[h] * da[h] * spread
        dxk, dxv = dx[h][:, :128], dx[h][:, 128:]
        stacked = jnp.concatenate([dqk, dkk], axis=0)
        forward = mm(stacked, k[h])
        backward = mm(stacked, jnp.concatenate([q[h], k[h]], axis=0), TN)
        kx = jnp.sum(k[h] * dxk, axis=-1, keepdims=True)
        dq.append(start * doq + forward[:128])
        dk.append(
            backward + forward[128:] + to_last * dkt[h] + (b[h] * start) * dxk
        )
        dv.append(b[h] * dxv)
        gb = (
            jnp.sum(z, axis=-1, keepdims=True)
            + jnp.sum(v[h] * dxv, axis=-1, keepdims=True)
            + start * kx
        )
        gamgrad = b[h] * z + dp[h] * p_ref[0, h]
        dstart = jnp.sum(q[h] * doq, axis=-1, keepdims=True) + b[h] * kx
        dlast = jnp.sum(k[h] * dkt[h], axis=-1, keepdims=True) * to_last
        dkeep = jnp.sum(states[h] * dsn[h], keepdims=True) * keep
        gcol = jnp.sum(gamgrad, axis=-1, keepdims=True) + dstart * start - dlast
        end = jnp.sum(dlast, keepdims=True) + dkeep
        gcol = gcol + jnp.where(masks["row"][:, :1] == CHUNK - 1, end, 0.0)
        grow = jnp.sum(gamgrad, axis=0, keepdims=True)
        gdecay = jnp.where(lane == h, gcol, gdecay)
        gbeta = jnp.where(lane == heads + h, gb, gbeta)
        minus = jnp.where(masks["row"] == h, grow, minus)
    gdecay = gdecay - minus.T
    upper = jnp.where(masks["row"] <= masks["col"], 1.0, 0.0)
    dg = mm_full(upper, gdecay)
    galpha = dg * rate * jax.nn.sigmoid(shifted)
    width = pieces[0].shape[1]
    grads_ref[:, 3 * width + 128 :] = dgate_ref[...]
    grads_ref[:, 3 * width : 3 * width + 128] = jnp.where(
        lane < heads, galpha, gbeta * beta * (1.0 - beta)
    ).astype(LOW)
    gparams_ref[0:8, :] += jnp.sum((galpha).reshape(CHUNK // 8, 8, 128), axis=0)
    gparams_ref[8:16, :] += jnp.sum((dg * decays).reshape(CHUNK // 8, 8, 128), axis=0)

    for i in range(3):
        rows, pre, sg = feats[i]
        pieces_d = []
        for h in hs:
            if i == 2:
                pieces_d.append(dv[h])
            else:
                inv = uq[h] if i == 0 else uk[h]
                grad = dq[h] * root if i == 0 else dk[h]
                normal = conv[i][:, lanes(h)] * inv
                pieces_d.append(
                    inv * (grad - normal * jnp.sum(grad * normal, axis=-1, keepdims=True))
                )
        dc = jnp.concatenate(pieces_d, axis=1)
        ds = dc * (sg * (1.0 + pre * (1.0 - sg)))
        grad = ds * taps[4 * i + 3 : 4 * i + 4, :]
        rim = jnp.zeros((8, ds.shape[1]), F32)
        gtaps_ref[4 * i + 3] += jnp.sum((ds * rows[0]).reshape(CHUNK // 8, 8, -1), axis=0)
        for s in range(1, 4):
            tap = taps[4 * i + 3 - s : 4 * i + 4 - s, :]
            masked = jnp.where(masks["back"][s], ds, 0.0)
            gtaps_ref[4 * i + 3 - s] += jnp.sum((ds * rows[s]).reshape(CHUNK // 8, 8, -1), axis=0)
            ext = jnp.concatenate([masked, after[3 * i + s - 1]], axis=0)
            grad = grad + pltpu.roll(ext, CHUNK + 8 - s, 0)[:CHUNK] * tap
            after[3 * i + s - 1] = masked[:8]
            front = jnp.concatenate([jnp.zeros_like(masked[:8]), masked[:8]], axis=0)
            rim = rim + pltpu.roll(front, 16 - s, 0)[:8] * tap
        grads_ref[:, i * width : (i + 1) * width] = grad.astype(LOW)
        rim_ref[:, i * width : (i + 1) * width] = rim

        @pl.when(rev == 0)
        def _():
            tail_ref[:, i * width : (i + 1) * width] = grad[CHUNK - HALO :]


def back(scalars, pieces, rims, narrow, taps, params, ds_in, do, v2, s, x, p, kg, w, u, qt, t, dgate, docs, heads):
    rows, width = pieces[0].shape
    chunks = rows // CHUNK
    flat, tiles = rows_spec(width, chunks, True), tile_spec(heads, chunks, True)
    return pl.pallas_call(
        functools.partial(back_kernel, docs, heads, chunks),
        out_shape=(
            sds(rows, 4 * width + 128, dtype=LOW), sds(HALO, 3 * width), sds(8, 3 * width),
            sds(12, 8, width), sds(16, 128),
        ),
        grid_spec=pltpu.PrefetchScalarGridSpec(
            num_scalar_prefetch=1,
            grid=(chunks,),
            in_specs=[flat] * 3
            + [halo_spec(width, chunks, True)] * 3
            + [whole_spec(HALO, width)] * 3
            + [rows_spec(128, chunks, True), whole_spec(16, width), whole_spec(8, 128)]
            + [whole_spec(heads, 128, 128), flat, flat, tiles, tiles, tiles, tiles, flat, flat, flat, tiles, flat],
            out_specs=[rows_spec(4 * width + 128, chunks, True)]
            + [whole_spec(HALO, 3 * width), whole_spec(8, 3 * width)]
            + [whole_spec(12, 8, width), whole_spec(16, 128)],
            scratch_shapes=[pltpu.VMEM((heads, 128, 128), F32), pltpu.VMEM((9, 8, width), F32)],
        ),
        compiler_params=pltpu.CompilerParams(**PARAMS),
        cost_estimate=cost(chunks * heads * 60 * 2 * 128**3, 16 * rows * width * 4),
        name="back",
    )(scalars, *pieces, *pieces, *rims, narrow, taps, params, ds_in, do, v2, s, x, p, kg, w, u, qt, t, dgate)


def contract_rows(left, right):
    return lax.dot_general(left, right, TN, preferred_element_type=F32)


def contract_cols(left, right):
    return lax.dot_general(left, right, NT, preferred_element_type=F32)


def dot(left, right):
    return jnp.dot(left, right, preferred_element_type=F32)


def row_norm(values, gain):
    return values * lax.rsqrt(jnp.mean(values * values, axis=-1, keepdims=True) + epsilon) * gain


def norm_back(values, gain, grad):
    inv = lax.rsqrt(jnp.mean(values * values, axis=-1, keepdims=True) + epsilon)
    scaled = grad * gain
    inner = jnp.mean(scaled * values, axis=-1, keepdims=True)
    return inv * scaled - values * (inner * inv * inv * inv), jnp.sum(grad * values * inv, axis=0)


MESH = pl.DeviceIdType.MESH


def greet(axis, parts):
    me = lax.axis_index(axis)
    barrier = pltpu.get_barrier_semaphore()

    @pl.when(me > 0)
    def _():
        pl.semaphore_signal(barrier, inc=1, device_id={axis: me - 1}, device_id_type=MESH)

    @pl.when(me < parts - 1)
    def _():
        pl.semaphore_signal(barrier, inc=1, device_id={axis: me + 1}, device_id_type=MESH)

    inner = (me > 0) & (me < parts - 1)

    @pl.when(inner)
    def _():
        pl.semaphore_wait(barrier, 2)

    @pl.when(jnp.logical_not(inner))
    def _():
        pl.semaphore_wait(barrier, 1)


def line_gather(parts, buf, sems, first, use):
    me = lax.axis_index("tensor")
    send_right, send_left, from_left, from_right = sems

    def rightward(piece, step):
        return pltpu.make_async_remote_copy(
            src_ref=buf.at[piece],
            dst_ref=buf.at[piece],
            send_sem=send_right.at[step],
            recv_sem=from_left.at[step],
            device_id={"tensor": me + 1},
            device_id_type=MESH,
        )

    def leftward(piece, step):
        return pltpu.make_async_remote_copy(
            src_ref=buf.at[piece],
            dst_ref=buf.at[piece],
            send_sem=send_left.at[step],
            recv_sem=from_right.at[step],
            device_id={"tensor": me - 1},
            device_id_type=MESH,
        )

    def body(step, _):
        low, high = me - step, me + step

        @pl.when((step > 0) & (low >= 0))
        def _():
            rightward(low, step - 1).wait_recv()

        @pl.when((low >= 0) & (me < parts - 1))
        def _():
            rightward(low, step).start()

        @pl.when((step > 0) & (high < parts))
        def _():
            leftward(high, step - 1).wait_recv()

        @pl.when((high < parts) & (me > 0))
        def _():
            leftward(high, step).start()

        @pl.when(step == 0)
        def _():
            first()

        @pl.when(low >= 0)
        def _():
            use(low)

        @pl.when((step > 0) & (high < parts))
        def _():
            use(high)

        return 0

    lax.fori_loop(0, parts, body, 0)

    def finish(step, _):
        low, high = me - step, me + step

        @pl.when((low >= 0) & (me < parts - 1))
        def _():
            rightward(low, step).wait_send()

        @pl.when((high < parts) & (me > 0))
        def _():
            leftward(high, step).wait_send()

        return 0

    lax.fori_loop(0, parts, finish, 0)


def norm_into(buf, me, source, gain):
    rows = source.shape[0]

    def body(i, _):
        at = pl.ds(pl.multiple_of(i * 64, 64), 64)
        values = source[at, :].astype(F32)
        scale = lax.rsqrt(jnp.mean(values * values, axis=-1, keepdims=True) + epsilon)
        buf[me, at, :] = (values * scale * gain[0:1, :]).astype(LOW)
        return 0

    lax.fori_loop(0, rows // 64, body, 0)


def project_kernel(parts, tok_ref, gain_ref, narrow_w, *refs):
    weights_in, all_ref = refs[0:4], refs[4]
    q_ref, k_ref, v_ref, gate_ref, narrow_ref = refs[5:10]
    buf, weights = refs[10], refs[11:15]
    sems, load_sem, store_sem = refs[15:19], refs[19], refs[20]
    me = lax.axis_index("tensor")
    rows = tok_ref.shape[0]
    loads = [
        pltpu.make_async_copy(weights_in[i], weights[i], load_sem.at[i]) for i in range(4)
    ]
    for load in loads:
        load.start()
    norm_into(buf, me, tok_ref, gain_ref)
    greet("tensor", parts)

    def first():
        for load in loads:
            load.wait()

    def stored(piece):
        at = pl.ds(pl.multiple_of(piece * rows, rows), rows)
        return pltpu.make_async_copy(buf.at[piece], all_ref.at[at, :], store_sem.at[piece])

    def use(piece):
        at = pl.ds(pl.multiple_of(piece * rows, rows), rows)
        stored(piece).start()
        values = buf[piece]
        for w, out in zip(weights, (q_ref, k_ref, v_ref, gate_ref)):
            out[at, :] = dot(values, w[...]).astype(out.dtype)
        narrow_ref[at, :] = dot(values, narrow_w[...])

    line_gather(parts, buf, sems, first, use)
    for piece in range(parts):
        stored(piece).wait()


def vmem():
    return pl.BlockSpec(memory_space=pltpu.VMEM)


def hbm():
    return pl.BlockSpec(memory_space=pl.ANY)


def line_sems(parts):
    return [pltpu.SemaphoreType.DMA((parts,))] * 4


def comm_params(number):
    return pltpu.CompilerParams(
        collective_id=number, has_side_effects=True, vmem_limit_bytes=60 * 1024 * 1024
    )


def project(parts, tokens, gain, narrow_w, weights):
    rows, model = tokens.shape
    width = weights[0].shape[1]
    total = rows * parts
    low = sds(total, width, dtype=LOW)
    return pl.pallas_call(
        functools.partial(project_kernel, parts),
        out_shape=(sds(total, model, dtype=LOW), low, low, low, sds(total, width), sds(total, 128)),
        in_specs=[vmem()] * 3 + [hbm()] * 4,
        out_specs=[hbm()] + [vmem()] * 5,
        scratch_shapes=[pltpu.VMEM((parts, rows, model), LOW)]
        + [pltpu.VMEM((model, width), LOW)] * 4
        + line_sems(parts)
        + [pltpu.SemaphoreType.DMA((4,)), pltpu.SemaphoreType.DMA((parts,))],
        compiler_params=comm_params(1),
        cost_estimate=cost(2 * total * model * (4 * width + 128), 60 * 2**20),
        name="project",
    )(tokens, gain, narrow_w, *weights)


def feed_kernel(parts, res_ref, gain_ref, *refs):
    weights_in, og_in = refs[0:3], refs[3]
    all_ref, act_ref, gu_ref, mlp_ref = refs[4:8]
    buf, weights, og = refs[8], refs[9:12], refs[12]
    sems, load_sem, store_sem = refs[13:17], refs[17], refs[18]
    me = lax.axis_index("tensor")
    rows = res_ref.shape[0]
    units = weights_in[0].shape[1]
    loads = [
        pltpu.make_async_copy(src, dst, load_sem.at[i])
        for i, (src, dst) in enumerate(zip(weights_in + (og_in,), weights + (og,)))
    ]
    for load in loads:
        load.start()
    norm_into(buf, me, res_ref, gain_ref)
    greet("tensor", parts)
    wg, wu, wd = weights

    def first():
        for load in loads:
            load.wait()

    def stored(piece):
        at = pl.ds(pl.multiple_of(piece * rows, rows), rows)
        return pltpu.make_async_copy(buf.at[piece], all_ref.at[at, :], store_sem.at[piece])

    def tile(at, piece, column, size):
        cols = pl.ds(pl.multiple_of(column, 128), size)
        values = buf[piece]
        gate = dot(values, wg[:, cols])
        up = dot(values, wu[:, cols])
        grad = contract_cols(og[at, :], wd[cols, :])
        sg = jax.nn.sigmoid(gate)
        act = gate * sg
        act_ref[at, cols] = (act * up).astype(LOW)
        gu_ref[at, cols] = (grad * up * sg * (1.0 + gate * (1.0 - sg))).astype(LOW)
        gu_ref[at, pl.ds(pl.multiple_of(units + column, 128), size)] = (grad * act).astype(LOW)

    def use(piece):
        at = pl.ds(pl.multiple_of(piece * rows, rows), rows)
        stored(piece).start()

        def body(i, _):
            tile(at, piece, i * 256, 256)
            return 0

        lax.fori_loop(0, units // 256, body, 0)
        if units % 256:
            tile(at, piece, units - units % 256, units % 256)

        def down(i, _):
            cols = pl.ds(pl.multiple_of(i * 256, 256), 256)
            mlp_ref[at, cols] = dot(act_ref[at, :], wd[:, cols]).astype(LOW)
            return 0

        lax.fori_loop(0, mlp_ref.shape[1] // 256, down, 0)

    line_gather(parts, buf, sems, first, use)
    for piece in range(parts):
        stored(piece).wait()


def feed(parts, residual, gain, weights, out_grad):
    rows, model = residual.shape
    units = weights[0].shape[1]
    total = rows * parts
    return pl.pallas_call(
        functools.partial(feed_kernel, parts),
        out_shape=(
            sds(total, model, dtype=LOW), sds(total, units, dtype=LOW), sds(total, 2 * units, dtype=LOW),
            sds(total, model, dtype=LOW),
        ),
        in_specs=[vmem()] * 2 + [hbm()] * 4,
        out_specs=[hbm()] + [vmem()] * 3,
        scratch_shapes=[pltpu.VMEM((parts, rows, model), LOW)]
        + [pltpu.VMEM(w.shape, LOW) for w in weights]
        + [pltpu.VMEM((total, model), LOW)]
        + line_sems(parts)
        + [pltpu.SemaphoreType.DMA((4,)), pltpu.SemaphoreType.DMA((parts,))],
        compiler_params=comm_params(2),
        cost_estimate=cost(8 * total * model * units, 120 * 2**20),
        name="feed",
    )(residual, gain, *weights, out_grad)


SUBS = 2


def scatter_kernel(parts, given, count, splits, *refs):
    lefts, rights_in, out_ref = refs[0:given], refs[given : given + count], refs[given + count]
    refs = refs[given + count + 1 :]
    rights, (part, send_r, send_l, got_l, got_r) = refs[0:count], refs[count : count + 5]
    sem_sr, sem_sl, sem_gl, sem_gr, load_sem = refs[count + 5 : count + 10]
    me = lax.axis_index("tensor")
    rows, model = out_ref.shape
    size = rows // SUBS
    loads = [
        pltpu.make_async_copy(rights_in[i], rights[i], load_sem.at[i]) for i in range(count)
    ]
    for load in loads:
        load.start()
    greet("tensor", parts)
    for load in loads:
        load.wait()

    def rightward(slot):
        return pltpu.make_async_remote_copy(
            src_ref=send_r.at[slot],
            dst_ref=got_l.at[slot],
            send_sem=sem_sr.at[slot],
            recv_sem=sem_gl.at[slot],
            device_id={"tensor": me + 1},
            device_id_type=MESH,
        )

    def leftward(slot):
        return pltpu.make_async_remote_copy(
            src_ref=send_l.at[slot],
            dst_ref=got_r.at[slot],
            send_sem=sem_sl.at[slot],
            recv_sem=sem_gr.at[slot],
            device_id={"tensor": me - 1},
            device_id_type=MESH,
        )

    def product(start, many, target):
        at = pl.ds(pl.multiple_of(start, 128), many)

        def body(j, _):
            cols = pl.ds(pl.multiple_of(j * 256, 256), 256)
            total = None
            for i, (index, first, wide) in enumerate(splits):
                term = contract_cols(lefts[index][at, first : first + wide], rights[i][cols, :])
                total = term if total is None else total + term
            target[:, cols] = total
            return 0

        lax.fori_loop(0, model // 256, body, 0)

    half = part.at[pl.ds(0, size), :]

    def go_right(piece, sub):
        slot = piece * SUBS + sub

        @pl.when(piece > me)
        def _():
            product(piece * rows + sub * size, size, half)

            @pl.when(me > 0)
            def _():
                rightward(slot).wait_recv()
                send_r[slot] = (half[...] + got_l[slot].astype(F32)).astype(LOW)

            @pl.when(me == 0)
            def _():
                send_r[slot] = half[...].astype(LOW)

            rightward(slot).start()

    def go_left(piece, sub):
        slot = piece * SUBS + sub

        @pl.when(piece < me)
        def _():
            product(piece * rows + sub * size, size, half)

            @pl.when(me < parts - 1)
            def _():
                leftward(slot).wait_recv()
                send_l[slot] = (half[...] + got_r[slot].astype(F32)).astype(LOW)

            @pl.when(me == parts - 1)
            def _():
                send_l[slot] = half[...].astype(LOW)

            leftward(slot).start()

    right_first = 2 * me < parts

    def body(item, _):
        step, sub = item // SUBS, item % SUBS
        right, left = parts - 1 - step, step

        @pl.when(right_first)
        def _():
            go_right(right, sub)

        go_left(left, sub)

        @pl.when(jnp.logical_not(right_first))
        def _():
            go_right(right, sub)

        return 0

    lax.fori_loop(0, (parts - 1) * SUBS, body, 0)
    product(me * rows, rows, part)
    for sub in range(SUBS):
        at = slice(sub * size, sub * size + size)
        slot = me * SUBS + sub
        out_ref[at, :] = part[at, :]

        @pl.when(me > 0)
        def _():
            rightward(slot).wait_recv()
            out_ref[at, :] = out_ref[at, :] + got_l[slot].astype(F32)

        @pl.when(me < parts - 1)
        def _():
            leftward(slot).wait_recv()
            out_ref[at, :] = out_ref[at, :] + got_r[slot].astype(F32)

    def finish(slot, _):
        piece = slot // SUBS

        @pl.when(piece > me)
        def _():
            rightward(slot).wait_send()

        @pl.when(piece < me)
        def _():
            leftward(slot).wait_send()

        return 0

    lax.fori_loop(0, parts * SUBS, finish, 0)


def scatter(parts, lefts, rights, splits, number):
    total = lefts[0].shape[0]
    model = rights[0].shape[0]
    rows = total // parts
    count = len(rights)
    slots = pltpu.VMEM((parts * SUBS, rows // SUBS, model), LOW)
    kernel = functools.partial(scatter_kernel, parts, len(lefts), count, splits)
    return pl.pallas_call(
        kernel,
        out_shape=sds(rows, model),
        in_specs=[vmem()] * len(lefts) + [hbm()] * count,
        out_specs=vmem(),
        scratch_shapes=[pltpu.VMEM(w.shape, LOW) for w in rights]
        + [pltpu.VMEM((rows, model), F32)]
        + [slots] * 4
        + line_sems(parts * SUBS)
        + [pltpu.SemaphoreType.DMA((count,))],
        compiler_params=comm_params(number),
        cost_estimate=cost(2 * total * model * sum(w.shape[1] for w in rights), 60 * 2**20),
        name="scatter%d" % number,
    )(*lefts, *rights)


def state_kernel(count, heads, backward, own_ref, out_ref, buf, send_sem, pass_sem, got_sem):
    me = lax.axis_index("dp")
    core = lax.rem(me, 2)
    sibling = me + 1 - 2 * core
    half = count // 2
    barrier = pltpu.get_barrier_semaphore()

    def peer(k):
        return lax.rem(me + 2 * k, count)

    def hello(k, _):
        pl.semaphore_signal(barrier, inc=1, device_id={"dp": peer(k)}, device_id_type=MESH)
        return 0

    lax.fori_loop(1, half, hello, 0)
    pl.semaphore_signal(barrier, inc=1, device_id={"dp": sibling}, device_id_type=MESH)
    buf[me] = own_ref[...].astype(LOW)
    pl.semaphore_wait(barrier, half)

    def needed(source, target):
        return source > target if backward else source < target

    def copy(piece, target, sem):
        return pltpu.make_async_remote_copy(
            src_ref=buf.at[piece],
            dst_ref=buf.at[piece],
            send_sem=sem,
            recv_sem=got_sem.at[piece],
            device_id={"dp": target},
            device_id_type=MESH,
        )

    def send(k, _):
        target = peer(k)

        @pl.when(needed(me, target))
        def _():
            copy(me, target, send_sem.at[target]).start()

        return 0

    @pl.when(needed(me, sibling))
    def _():
        copy(me, sibling, pass_sem.at[me]).start()

    lax.fori_loop(1, half, send, 0)

    def relay(k, _):
        source = lax.rem(me + count - 2 * k, count)

        @pl.when(needed(source, me))
        def _():
            copy(source, me, send_sem.at[source]).wait_recv()

        @pl.when(needed(source, me) & needed(source, sibling))
        def _():
            copy(source, sibling, pass_sem.at[source]).start()

        return 0

    lax.fori_loop(1, half, relay, 0)
    for h in range(heads):
        out_ref[h] = jnp.zeros_like(out_ref[h])

    def chain(step, _):
        piece = count - 1 - step if backward else step

        @pl.when(needed(piece, me) & (lax.rem(piece, 2) != core))
        def _():
            copy(piece, me, pass_sem.at[piece]).wait_recv()

        @pl.when(needed(piece, me))
        def _():
            for h in range(heads):
                both = buf[piece, h].astype(F32)
                if backward:
                    out_ref[h] = mm(both[:, 128:], out_ref[h], TN) + both[:, :128]
                else:
                    out_ref[h] = mm(both[:, 128:], out_ref[h]) + both[:, :128]

        return 0

    lax.fori_loop(0, count, chain, 0)

    def finish(k, _):
        target = peer(k)
        source = lax.rem(me + count - 2 * k, count)

        @pl.when(needed(me, target))
        def _():
            copy(me, target, send_sem.at[target]).wait_send()

        @pl.when(needed(source, me) & needed(source, sibling))
        def _():
            copy(source, sibling, pass_sem.at[source]).wait_send()

        return 0

    lax.fori_loop(1, half, finish, 0)

    @pl.when(needed(me, sibling))
    def _():
        copy(me, sibling, pass_sem.at[me]).wait_send()


def exchange(count, own, heads, backward, number):
    return pl.pallas_call(
        functools.partial(state_kernel, count, heads, backward),
        out_shape=sds(heads, 128, 128),
        in_specs=[vmem()],
        out_specs=vmem(),
        scratch_shapes=[pltpu.VMEM((count, heads, 128, 256), LOW)]
        + [pltpu.SemaphoreType.DMA((count,))] * 3,
        compiler_params=comm_params(number),
        cost_estimate=cost(count * heads * 6 * 128**3, count * heads * 256 * 128 * 4),
        name="exchange%d" % number,
    )(own)


def totals_kernel(count, parts, kept, own_ref, wide_ref, flat_ref, buf, mid, send1, got1, send2, got2):
    dp, z = lax.axis_index("dp"), lax.axis_index("tensor")
    barrier = pltpu.get_barrier_semaphore()

    def hello_dp(k, _):
        pl.semaphore_signal(
            barrier, inc=1, device_id={"dp": lax.rem(dp + k, count)}, device_id_type=MESH
        )
        return 0

    def hello_z(k, _):
        pl.semaphore_signal(
            barrier, inc=1, device_id={"tensor": lax.rem(z + k, parts)}, device_id_type=MESH
        )
        return 0

    lax.fori_loop(1, count, hello_dp, 0)
    lax.fori_loop(1, parts, hello_z, 0)
    buf[dp] = own_ref[...]
    pl.semaphore_wait(barrier, count + parts - 2)

    def over_dp(source, target):
        return pltpu.make_async_remote_copy(
            src_ref=buf.at[source],
            dst_ref=buf.at[source],
            send_sem=send1.at[target],
            recv_sem=got1.at[source],
            device_id={"dp": target},
            device_id_type=MESH,
        )

    def over_z(source, target):
        return pltpu.make_async_remote_copy(
            src_ref=mid.at[source],
            dst_ref=mid.at[source],
            send_sem=send2.at[target],
            recv_sem=got2.at[source],
            device_id={"tensor": target},
            device_id_type=MESH,
        )

    def each(total, me, action):
        def body(k, _):
            action(lax.rem(me + k, total))
            return 0

        lax.fori_loop(1, total, body, 0)

    each(count, dp, lambda other: over_dp(dp, other).start())
    each(count, dp, lambda other: over_dp(other, dp).wait_recv())
    total = buf[0]
    for i in range(1, count):
        total = total + buf[i]
    mid[z] = total
    each(parts, z, lambda other: over_z(z, other).start())
    each(parts, z, lambda other: over_z(other, z).wait_recv())
    width = own_ref.shape[1]
    flat = mid[0, kept:, :]
    for i in range(parts):
        wide_ref[:, i * width : (i + 1) * width] = mid[i, :kept, :]
        if i:
            flat = flat + mid[i, kept:, :]
    flat_ref[...] = flat
    each(count, dp, lambda other: over_dp(dp, other).wait_send())
    each(parts, z, lambda other: over_z(z, other).wait_send())


def totals_of(count, parts, own, kept, number):
    rows, width = own.shape
    return pl.pallas_call(
        functools.partial(totals_kernel, count, parts, kept),
        out_shape=(sds(kept, width * parts), sds(rows - kept, width)),
        in_specs=[vmem()],
        out_specs=[vmem(), vmem()],
        scratch_shapes=[pltpu.VMEM((count, rows, width), F32), pltpu.VMEM((parts, rows, width), F32)]
        + [pltpu.SemaphoreType.DMA((count,))] * 2
        + [pltpu.SemaphoreType.DMA((parts,))] * 2,
        compiler_params=comm_params(number),
        cost_estimate=cost(count * rows * width, count * rows * width * 4),
        name="totals",
    )(own)


def after(values, *first):
    out = lax.optimization_barrier((values,) + first)
    return out[0]


def local(
    tokens,
    gain_in,
    w_query,
    w_key,
    w_value,
    w_alpha,
    w_beta,
    w_gate_out,
    conv_query,
    conv_key,
    conv_value,
    decay_log,
    decay_bias,
    head_gain,
    w_out,
    gain_mid,
    w_gate,
    w_up,
    w_down,
    out_grad,
    doc_lengths,
):
    rows_own, model = tokens.shape
    tensor_parts, dp_parts = lax.axis_size("tensor"), lax.axis_size("dp")
    tensor_index, dp_index = lax.axis_index("tensor"), lax.axis_index("dp")
    group_rows = rows_own * tensor_parts
    seq_total = group_rows * dp_parts
    heads = w_alpha.shape[1]
    width = w_query.shape[1]
    docs = doc_lengths.shape[0] * doc_lengths.shape[1]
    starts = (
        jnp.cumsum(doc_lengths, axis=1)
        - doc_lengths
        + seq_total * lax.broadcasted_iota(jnp.int32, doc_lengths.shape, 0)
    ).reshape(-1)
    scalars = jnp.concatenate([(dp_index * group_rows).reshape(1), starts]).astype(jnp.int32)
    taps = jnp.concatenate([conv_query, conv_key, conv_value, jnp.zeros((4, width), F32)])
    params = jnp.zeros((8, 128), F32).at[0, :heads].set(decay_bias).at[1, :heads].set(decay_log)
    gain_heads = jnp.broadcast_to(head_gain[None], (8, width))
    w_narrow = jnp.pad(jnp.concatenate([w_alpha, w_beta], axis=1), ((0, 0), (0, 128 - 2 * heads)))

    own_rows = tokens.astype(F32)
    gain_in_rows = jnp.broadcast_to(gain_in[None], (8, model))
    gain_mid_rows = jnp.broadcast_to(gain_mid[None], (8, model))
    normed_all, *pieces, gate_raw, narrow = project(
        tensor_parts, tokens, gain_in_rows, w_narrow, (w_query, w_key, w_value, w_gate_out)
    )
    half = width // 2
    core = lax.rem(dp_index, 2)
    out_half = lax.dynamic_slice_in_dim(after(w_out, narrow), core * half, half, 0)
    out_mine = lax.all_gather(out_half, "tensor", axis=0)
    forth = [(i, i + 1) for i in range(dp_parts - 1)]
    rims = lax.ppermute(
        jnp.stack([piece[group_rows - HALO :] for piece in pieces]), "dp", forth
    )
    rims = [rims[i] for i in range(3)]
    x, p, kg, w, u, qt, ou, t, o, totals = intra(
        scalars, pieces, rims, narrow, taps, params, docs, heads
    )
    state_in = exchange(dp_parts, totals, heads, False, 3)
    out_other = lax.ppermute(after(out_mine, state_in), "dp", [(i, i ^ 1) for i in range(dp_parts)])
    w_out_full = jnp.stack(
        [jnp.where(core == 0, out_mine, out_other), jnp.where(core == 0, out_other, out_mine)],
        axis=1,
    ).reshape(width * tensor_parts, model)
    rows_out, v2, s, mixed = outward(state_in, w, u, qt, ou, t, o, gate_raw, gain_heads, heads)

    mixed_own = lax.all_to_all(mixed, "tensor", split_axis=0, concat_axis=1, tiled=True)
    residual = own_rows + dot(mixed_own, w_out_full)
    mid_all, activated, grad_units, mlp_part = feed(
        tensor_parts, residual, gain_mid_rows, (w_gate, w_up, w_down), out_grad
    )
    units = w_gate.shape[1]
    ring = [(i, (i + 1) % tensor_parts) for i in range(tensor_parts)]

    def piece_of(values, back_by):
        index = lax.rem(tensor_index - back_by + tensor_parts, tensor_parts)
        return lax.dynamic_slice_in_dim(values, index * rows_own, rows_own, 0)

    def added(values, back_by, got):
        return (piece_of(values, back_by).astype(F32) + got.astype(F32)).astype(LOW)

    mlp_run = lax.ppermute(piece_of(mlp_part, 1), "tensor", ring)
    down_grad = contract_rows(out_grad, activated).astype(LOW)
    units_grad = contract_rows(mid_all, after(grad_units, down_grad)).astype(LOW)
    units_grad, mlp_run = lax.optimization_barrier((units_grad, mlp_run))
    down_grad_sum = lax.psum_scatter(down_grad, "dp", scatter_dimension=0, tiled=True)
    units_grad_sum = lax.psum_scatter(units_grad, "dp", scatter_dimension=0, tiled=True)

    grad_mid = scatter(
        tensor_parts, [after(grad_units, units_grad)], [w_gate, w_up],
        ((0, 0, units), (0, units, units)), 4,
    )
    grad_res_norm, gain_mid_grad = norm_back(residual, gain_mid, grad_mid)
    grad_own = lax.dynamic_slice_in_dim(out_grad, tensor_index * rows_own, rows_own, 0)
    grad_residual = grad_own.astype(F32) + grad_res_norm
    grad_mixer = grad_residual.astype(LOW)
    grad_mixed_own = contract_cols(grad_mixer, w_out_full).astype(LOW)
    grad_mixed = lax.all_to_all(
        grad_mixed_own, "tensor", split_axis=1, concat_axis=0, tiled=True
    )
    grad_mixer_all, mlp_run = lax.optimization_barrier((grad_mixer, mlp_run, grad_mixed))[:2]
    grad_mixer_all = lax.all_gather(grad_mixer_all, "tensor", axis=0, tiled=True)
    for back_by in range(2, tensor_parts - 1):
        mlp_run = lax.ppermute(added(mlp_part, back_by, mlp_run), "tensor", ring)

    do, gate_low, head_gain_part, ds_total = inward(
        grad_mixed, rows_out, gate_raw, gain_heads, qt, t, totals, heads
    )
    grad_end = exchange(dp_parts, ds_total, heads, True, 5)
    grad_end, mlp_run, _, _ = lax.optimization_barrier(
        (grad_end, mlp_run, units_grad_sum, down_grad_sum)
    )
    grads, tails, rim_grad, taps_grad, params_grad = back(
        scalars, pieces, rims, narrow, taps, params, grad_end, do, v2, s, x, p, kg, w, u, qt, t,
        gate_low, docs, heads,
    )
    rim_back = lax.ppermute(rim_grad, "dp", [(i + 1, i) for i in range(dp_parts - 1)])
    tails = tails.at[HALO - 8 :].add(rim_back).astype(LOW)
    grads = lax.dynamic_update_slice(grads, tails, (group_rows - HALO, 0))
    mlp_run = lax.ppermute(
        added(mlp_part, tensor_parts - 1, after(mlp_run, rim_grad)), "tensor", ring
    )
    out_w = contract_rows(after(grad_mixer_all, rim_grad), mixed).astype(LOW)
    out_w_sum = lax.psum_scatter(out_w, "dp", scatter_dimension=0, tiled=True).astype(F32)
    mixer_grad = contract_rows(normed_all, after(grads, out_w)).astype(LOW)
    mixer_grad, mlp_run = lax.optimization_barrier((mixer_grad, mlp_run))
    mixer_sum = lax.psum_scatter(mixer_grad, "dp", scatter_dimension=0, tiled=True).astype(F32)
    output = (residual + (piece_of(mlp_part, 0).astype(F32) + mlp_run.astype(F32))).astype(LOW)
    grad_normed = scatter(
        tensor_parts, [after(grads, mixer_grad)],
        [w_query, w_key, w_value, w_narrow, w_gate_out],
        ((0, 0, width), (0, width, width), (0, 2 * width, width), (0, 3 * width, 128), (0, 3 * width + 128, width)),
        6,
    )
    grad_tokens, gain_in_grad = norm_back(own_rows, gain_in, grad_normed)
    input_grad = grad_residual + grad_tokens

    params_grad = params_grad.reshape(2, 8, 128).sum(1)
    flat = jnp.concatenate(
        [
            taps_grad.sum(1),
            head_gain_part.sum(0)[None],
            jnp.pad(params_grad, ((0, 1), (0, width - 128))),
            gain_in_grad.reshape(-1, width),
            gain_mid_grad.reshape(-1, width),
        ],
        axis=0,
    )
    wide, gains = totals_of(dp_parts, tensor_parts, flat, 16, 7)
    by_head = wide[13:15].reshape(2, tensor_parts, width)[:, :, :heads].reshape(2, -1)
    gains = gains.reshape(2, model)
    start = 3 * width
    return (
        output,
        input_grad,
        gains[0],
        mixer_sum[:, :width],
        mixer_sum[:, width : 2 * width],
        mixer_sum[:, 2 * width : start],
        mixer_sum[:, start : start + heads],
        mixer_sum[:, start + heads : start + 2 * heads],
        mixer_sum[:, start + 128 :],
        wide[0:4],
        wide[4:8],
        wide[8:12],
        by_head[1],
        by_head[0],
        wide[12],
        out_w_sum.T,
        gains[1],
        units_grad_sum[:, :units].astype(F32),
        units_grad_sum[:, units:].astype(F32),
        down_grad_sum.T.astype(F32),
    )


def solution(mesh):
    placed = (
        P(("dp", "tensor"), None),
        P(),
        P(None, "tensor"),
        P(None, "tensor"),
        P(None, "tensor"),
        P(None, "tensor"),
        P(None, "tensor"),
        P(None, "tensor"),
        P(None, "tensor"),
        P(None, "tensor"),
        P(None, "tensor"),
        P("tensor"),
        P("tensor"),
        P("tensor"),
        P("tensor", None),
        P(),
        P(None, "tensor"),
        P(None, "tensor"),
        P("tensor", None),
        P("dp", None),
        P(),
    )
    return jax.shard_map(
        local,
        mesh=mesh,
        in_specs=placed,
        out_specs=(
            P(("dp", "tensor"), None),
            P(("dp", "tensor"), None),
            P(),
            P("dp", "tensor"),
            P("dp", "tensor"),
            P("dp", "tensor"),
            P("dp", "tensor"),
            P("dp", "tensor"),
            P("dp", "tensor"),
            P(),
            P(),
            P(),
            P(),
            P(),
            P(),
            P("tensor", "dp"),
            P(),
            P("dp", "tensor"),
            P("dp", "tensor"),
            P("tensor", "dp"),
        ),
        check_vma=False,
    )
```

```python
import functools
import math

import jax
import jax.numpy as jnp
from jax import lax
from jax.experimental import pallas as pl
from jax.experimental.pallas import tpu as pltpu
from jax.sharding import PartitionSpec as P

CHUNK = 128
HALO = 16
epsilon = 1e-06
F32 = jnp.float32
LOW = jnp.bfloat16
NN = (((1,), (0,)), ((), ()))
NT = (((1,), (1,)), ((), ()))
TN = (((0,), (0,)), ((), ()))


def mm(left, right, dims=NN):
    return lax.dot_general(
        left, right, dims, precision=lax.Precision.HIGH, preferred_element_type=F32
    )


def halves(values):
    high = values.astype(LOW)
    return high, (values - high.astype(F32)).astype(LOW)


def mm_split(left, right):
    (lh, ll), (rh, rl) = left, right
    return lax.dot_general(
        jnp.concatenate([lh, ll, lh], axis=1),
        jnp.concatenate([rh, rh, rl], axis=0),
        NN,
        preferred_element_type=F32,
    )


def mm_sum(left, right):
    (lh, ll), (rh, rl) = left, right
    one = functools.partial(lax.dot_general, dimension_numbers=NN, preferred_element_type=F32)
    return one(lh, rh) + (one(ll, rh) + one(lh, rl))


def mm_full(left, right, dims=NN):
    return lax.dot_general(
        left, right, dims, precision=lax.Precision.HIGHEST, preferred_element_type=F32
    )


def iota(shape, dim):
    return lax.broadcasted_iota(jnp.int32, shape, dim)


def doc_of(positions, scalars, docs):
    total = jnp.zeros_like(positions) - 1
    for j in range(docs):
        total = total + jnp.where(positions >= scalars[1 + j], 1, 0)
    return total


def chunk_masks(position, scalars, docs):
    shape = (CHUNK, CHUNK)
    row, col = iota(shape, 0), iota(shape, 1)
    doc_row = doc_of(row + position, scalars, docs)
    doc_col = doc_of(col + position, scalars, docs)
    same = doc_row == doc_col
    prior = jnp.int32(-1)
    last = jnp.int32(-1)
    for j in range(docs):
        prior = prior + jnp.where(position - 1 >= scalars[1 + j], 1, 0)
        last = last + jnp.where(position + CHUNK - 1 >= scalars[1 + j], 1, 0)
    return {
        "row": row,
        "col": col,
        "inside": same & (row >= col),
        "strict": same & (row > col),
        "carried": (doc_row == prior)[:, :1],
        "in_last": (doc_row == last)[:, :1],
        "last_carried": last == prior,
        "back": [
            None if s == 0 else (doc_row == doc_of(row + (position - s), scalars, docs))[:, :1]
            for s in range(4)
        ],
    }


def shifted_rows(main, before, back):
    ext = jnp.concatenate([before[HALO - 8 :], main], axis=0)
    rows = [main]
    for s in range(1, 4):
        rows.append(jnp.where(back[s], pltpu.roll(ext, s, 0)[8:], 0.0))
    return rows


def conv_sum(rows, taps):
    total = rows[0] * taps[3:4, :]
    for s in range(1, 4):
        total = total + rows[s] * taps[3 - s : 4 - s, :]
    return total


def softplus(x):
    return jnp.maximum(x, 0.0) + jnp.log1p(jnp.exp(-jnp.abs(x)))


def gates(narrow, params, masks):
    shifted = narrow + params[0:1, :]
    rate = -jnp.exp(params[1:2, :])
    decays = rate * softplus(shifted)
    lower = jnp.where(masks["row"] >= masks["col"], 1.0, 0.0)
    total = mm_full(lower, decays)
    return shifted, rate, decays, jax.nn.sigmoid(narrow), total, total.T


def decay_terms(h, total, total_row, masks):
    col = total[:, h : h + 1]
    row = total_row[h : h + 1, :]
    spread = jnp.where(
        masks["inside"], jnp.exp(jnp.where(masks["inside"], col - row, 0.0)), 0.0
    )
    start = jnp.where(masks["carried"], jnp.exp(col), 0.0)
    end = total[CHUNK - 1 : CHUNK, h : h + 1]
    to_last = jnp.where(masks["in_last"], jnp.exp(jnp.where(masks["in_last"], end - col, 0.0)), 0.0)
    keep = jnp.where(masks["last_carried"], jnp.exp(end), 0.0)
    return spread, start, to_last, keep


def lanes(h):
    return slice(h * 128, h * 128 + 128)


def features(pieces, befores, taps, masks, heads):
    out = []
    for i in range(3):
        rows = shifted_rows(pieces[i], befores[i], masks["back"])
        pre = conv_sum(rows, taps[4 * i : 4 * i + 4, :])
        out.append((rows, pre, jax.nn.sigmoid(pre)))
    return out


def unit(values):
    return lax.rsqrt(jnp.sum(values * values, axis=-1, keepdims=True) + epsilon)


def load_pieces(step, mains, priors, rims):
    pieces = [m[...].astype(F32) for m in mains]
    befores = [
        jnp.where(step == 0, r[...].astype(F32), p[...].astype(F32)) for p, r in zip(priors, rims)
    ]
    return pieces, befores


def intra_kernel(docs, heads, scalars, *refs):
    mains, priors, rims = refs[0:3], refs[3:6], refs[6:9]
    narrow_ref, taps_ref, params_ref = refs[9:12]
    x_ref, p_ref, kg_ref, w_ref, u_ref, qt_ref, ou_ref, t_ref, o_ref, tot_ref = refs[12:22]
    run = refs[22]
    step = pl.program_id(0)
    position = scalars[0] + step * CHUNK
    masks = chunk_masks(position, scalars, docs)
    pieces, befores = load_pieces(step, mains, priors, rims)
    feats = features(pieces, befores, taps_ref[...], masks, heads)
    _, _, _, beta, total, total_row = gates(narrow_ref[...], params_ref[...], masks)
    eye = jnp.where(masks["row"] == masks["col"], 1.0, 0.0)
    conv = [pre * sg for _, pre, sg in feats]
    hs = range(heads)
    q, k, v, terms, b = [], [], [], [], []
    for h in hs:
        cq, ck = conv[0][:, lanes(h)], conv[1][:, lanes(h)]
        q.append(cq * (unit(cq) * (1.0 / math.sqrt(128.0))))
        k.append(ck * unit(ck))
        v.append(conv[2][:, lanes(h)])
        terms.append(decay_terms(h, total, total_row, masks))
        b.append(beta[:, heads + h : heads + h + 1])
    kg = [jnp.where(masks["strict"], mm(k[h], k[h], NT) * terms[h][0], 0.0) for h in hs]
    p = [mm(q[h], k[h], NT) * terms[h][0] for h in hs]
    a = [b[h] * kg[h] for h in hs]
    pair = (masks["row"] >> 1) == (masks["col"] >> 1)
    x = [eye - jnp.where(pair, a[h], 0.0) for h in hs]
    for level in range(1, 7):
        wide = (masks["row"] >> (level + 1)) == (masks["col"] >> (level + 1))
        off = wide & ((masks["row"] >> level) != (masks["col"] >> level))
        lx = [mm(jnp.where(off, a[h], 0.0), x[h]) for h in hs]
        x = [x[h] - mm(x[h], lx[h]) for h in hs]
    wu = [
        mm(x[h], jnp.concatenate([(b[h] * terms[h][1]) * k[h], b[h] * v[h]], axis=1)) for h in hs
    ]
    pwu = [mm(p[h], wu[h]) for h in hs]
    kwu = [mm(terms[h][2] * k[h], wu[h], TN) for h in hs]

    @pl.when(step == 0)
    def _():
        for h in hs:
            run[h] = jnp.concatenate([jnp.zeros((128, 128), F32), eye], axis=1)

    for h in hs:
        x_ref[0, h] = x[h]
        p_ref[0, h] = p[h]
        kg_ref[0, h] = kg[h]
        w_ref[:, lanes(h)] = wu[h][:, :128]
        u_ref[:, lanes(h)] = wu[h][:, 128:]
        qt_ref[:, lanes(h)] = terms[h][1] * q[h] - pwu[h][:, :128]
        ou_ref[:, lanes(h)] = pwu[h][:, 128:]
        transfer = terms[h][3] * eye - kwu[h][:, :128]
        offset = kwu[h][:, 128:]
        t_ref[0, h] = transfer
        o_ref[0, h] = offset
        new = mm(transfer, run[h])
        new = jnp.concatenate([new[:, :128] + offset, new[:, 128:]], axis=1)
        run[h] = new
        tot_ref[h] = new


def rows_spec(width, chunks, reverse=False):
    if reverse:
        return pl.BlockSpec((CHUNK, width), lambda c, *_: (chunks - 1 - c, 0))
    return pl.BlockSpec((CHUNK, width), lambda c, *_: (c, 0))


def halo_spec(width, chunks, reverse=False):
    per = CHUNK // HALO
    if reverse:
        return pl.BlockSpec(
            (HALO, width), lambda c, *_: (jnp.maximum((chunks - 1 - c) * per - 1, 0), 0)
        )
    return pl.BlockSpec((HALO, width), lambda c, *_: (jnp.maximum(c * per - 1, 0), 0))


def tile_spec(heads, chunks, reverse=False):
    if reverse:
        return pl.BlockSpec((1, heads, 128, 128), lambda c, *_: (chunks - 1 - c, 0, 0, 0))
    return pl.BlockSpec((1, heads, 128, 128), lambda c, *_: (c, 0, 0, 0))


def whole_spec(*shape):
    zeros = (0,) * len(shape)
    return pl.BlockSpec(shape, lambda c, *_: zeros)


def sds(*shape, dtype=F32):
    return jax.ShapeDtypeStruct(shape, dtype)


PARAMS = dict(vmem_limit_bytes=56 * 1024 * 1024, dimension_semantics=("arbitrary",))


def cost(flops, moved):
    return pl.CostEstimate(flops=int(flops), bytes_accessed=int(moved), transcendentals=0)


def intra(scalars, pieces, rims, narrow, taps, params, docs, heads):
    rows, width = pieces[0].shape
    chunks = rows // CHUNK
    tiles, flat = sds(chunks, heads, 128, 128), sds(rows, width)
    return pl.pallas_call(
        functools.partial(intra_kernel, docs, heads),
        out_shape=(tiles, tiles, tiles, flat, flat, flat, flat, tiles, tiles, sds(heads, 128, 256)),
        grid_spec=pltpu.PrefetchScalarGridSpec(
            num_scalar_prefetch=1,
            grid=(chunks,),
            in_specs=[rows_spec(width, chunks)] * 3
            + [halo_spec(width, chunks)] * 3
            + [whole_spec(HALO, width)] * 3
            + [rows_spec(128, chunks), whole_spec(16, width), whole_spec(8, 128)],
            out_specs=[tile_spec(heads, chunks)] * 3
            + [rows_spec(width, chunks)] * 4
            + [tile_spec(heads, chunks)] * 2
            + [whole_spec(heads, 128, 256)],
            scratch_shapes=[pltpu.VMEM((heads, 128, 256), F32)],
        ),
        compiler_params=pltpu.CompilerParams(**PARAMS),
        cost_estimate=cost(chunks * heads * 60 * 3 * 2 * 128**3, 30 * rows * width * 4),
        name="intra",
    )(scalars, *pieces, *pieces, *rims, narrow, taps, params)


def outward_kernel(heads, s_in, w_ref, u_ref, qt_ref, ou_ref, t_ref, o_ref, gate_ref, gain_ref,
                   out_ref, v2_ref, s_ref, mixed_ref, run):
    step = pl.program_id(0)

    @pl.when(step == 0)
    def _():
        run[...] = s_in[...]

    hs = range(heads)
    state = [run[h] for h in hs]
    full = [
        mm(
            jnp.concatenate([qt_ref[:, lanes(h)], w_ref[:, lanes(h)], t_ref[0, h]], axis=0),
            state[h],
        )
        for h in hs
    ]
    for h in hs:
        out = full[h][:128] + ou_ref[:, lanes(h)]
        v2_ref[:, lanes(h)] = u_ref[:, lanes(h)] - full[h][128:256]
        s_ref[0, h] = state[h]
        run[h] = full[h][256:] + o_ref[0, h]
        out_ref[:, lanes(h)] = out
        gate = gate_ref[:, lanes(h)]
        scale = lax.rsqrt(jnp.mean(out * out, axis=-1, keepdims=True) + epsilon)
        mixed_ref[:, lanes(h)] = (
            out * scale * gain_ref[0:1, lanes(h)] * (gate * jax.nn.sigmoid(gate))
        ).astype(LOW)


def outward(s_in, w, u, qt, ou, t, o, gate, gain, heads):
    rows, width = w.shape
    chunks = rows // CHUNK
    flat, tiles = rows_spec(width, chunks), tile_spec(heads, chunks)
    return pl.pallas_call(
        functools.partial(outward_kernel, heads),
        out_shape=(sds(rows, width), sds(rows, width), sds(chunks, heads, 128, 128), sds(rows, width, dtype=LOW)),
        grid=(chunks,),
        in_specs=[whole_spec(heads, 128, 128), flat, flat, flat, flat, tiles, tiles, flat, whole_spec(8, width)],
        out_specs=[flat, flat, tiles, flat],
        scratch_shapes=[pltpu.VMEM((heads, 128, 128), F32)],
        compiler_params=pltpu.CompilerParams(**PARAMS),
        cost_estimate=cost(chunks * heads * 9 * 2 * 128**3, 11 * rows * width * 4),
        name="outward",
    )(s_in, w, u, qt, ou, t, o, gate, gain)


def inward_kernel(heads, scalars, gm_ref, out_ref, gate_ref, gain_ref, qt_ref, t_ref, maps_ref,
                  do_ref, dgate_ref, dgain_ref, tot_ref, run):
    step = pl.program_id(0)

    @pl.when(step == 0)
    def _():
        run[...] = jnp.zeros_like(run)
        dgain_ref[...] = jnp.zeros_like(dgain_ref)

    hs = range(heads)
    grads = []
    core = scalars[scalars.shape[0] - 1]
    for h in hs:
        out, gate = out_ref[:, lanes(h)], gate_ref[:, lanes(h)]
        other = (h + heads // 2) % heads
        gm = jnp.where(
            core == 0, gm_ref[:, lanes(h)].astype(F32), gm_ref[:, lanes(other)].astype(F32)
        )
        gain = gain_ref[0:1, lanes(h)]
        scale = lax.rsqrt(jnp.mean(out * out, axis=-1, keepdims=True) + epsilon)
        normed = out * scale
        sg = jax.nn.sigmoid(gate)
        act = gate * sg
        gn = gm * normed
        dgate_ref[:, lanes(h)] = (gn * gain * (sg * (1.0 + gate * (1.0 - sg)))).astype(LOW)
        dgain_ref[:, lanes(h)] += jnp.sum((gn * act).reshape(CHUNK // 8, 8, 128), axis=0)
        dn = gm * gain * act
        do = scale * (dn - normed * jnp.mean(dn * normed, axis=-1, keepdims=True))
        do_ref[:, lanes(h)] = do
        grads.append(do)
    for h in hs:
        left = jnp.concatenate([qt_ref[:, lanes(h)], t_ref[0, h]], axis=0)
        new = mm(left, jnp.concatenate([grads[h], run[h]], axis=0), TN)
        run[h] = new
        tot_ref[h] = jnp.concatenate([new, maps_ref[h, :, 128:]], axis=1)


def inward(scalars, gm, out, gate, gain, qt, t, maps, heads):
    rows, width = gm.shape
    chunks = rows // CHUNK
    flat, tiles = rows_spec(width, chunks, True), tile_spec(heads, chunks, True)
    return pl.pallas_call(
        functools.partial(inward_kernel, heads),
        out_shape=(sds(rows, width), sds(rows, width, dtype=LOW), sds(8, width), sds(heads, 128, 256)),
        grid_spec=pltpu.PrefetchScalarGridSpec(
            num_scalar_prefetch=1,
            grid=(chunks,),
            in_specs=[flat, flat, flat, whole_spec(8, width), flat, tiles, whole_spec(heads, 128, 256)],
            out_specs=[flat, flat, whole_spec(8, width), whole_spec(heads, 128, 256)],
            scratch_shapes=[pltpu.VMEM((heads, 128, 128), F32)],
        ),
        compiler_params=pltpu.CompilerParams(**PARAMS),
        cost_estimate=cost(chunks * heads * 6 * 2 * 128**3, 7 * rows * width * 4),
        name="inward",
    )(scalars, gm, out, gate, gain, qt, t, maps)


def back_kernel(docs, heads, chunks, scalars, *refs):
    mains, priors, rims = refs[0:3], refs[3:6], refs[6:9]
    narrow_ref, taps_ref, params_ref, ds_in = refs[9:13]
    (do_ref, v2_ref, s_ref, x_ref, p_ref, kg_ref, w_ref, u_ref, qt_ref, t_ref) = refs[13:23]
    dgate_ref, grads_ref, tail_ref, rim_ref, gtaps_ref, gparams_ref = refs[23:29]
    run, after = refs[29:31]
    rev = pl.program_id(0)
    step = chunks - 1 - rev
    position = scalars[0] + step * CHUNK

    @pl.when(rev == 0)
    def _():
        run[...] = ds_in[...]
        after[...] = jnp.zeros_like(after)
        gtaps_ref[...] = jnp.zeros_like(gtaps_ref)
        gparams_ref[...] = jnp.zeros_like(gparams_ref)

    masks = chunk_masks(position, scalars, docs)
    pieces, befores = load_pieces(step, mains, priors, rims)
    taps = taps_ref[...]
    feats = features(pieces, befores, taps, masks, heads)
    shifted, rate, decays, beta, total, total_row = gates(narrow_ref[...], params_ref[...], masks)
    conv = [pre * sg for _, pre, sg in feats]
    lane = masks["col"]
    hs = range(heads)
    q, k, v, uq, uk, terms, b = [], [], [], [], [], [], []
    root = 1.0 / math.sqrt(128.0)
    for h in hs:
        cq, ck = conv[0][:, lanes(h)], conv[1][:, lanes(h)]
        uq.append(unit(cq))
        uk.append(unit(ck))
        q.append(cq * (uq[h] * root))
        k.append(ck * uk[h])
        v.append(conv[2][:, lanes(h)])
        terms.append(decay_terms(h, total, total_row, masks))
        b.append(beta[:, heads + h : heads + h + 1])
    do = [do_ref[:, lanes(h)] for h in hs]
    v2 = [v2_ref[:, lanes(h)] for h in hs]
    dsn = [run[h] for h in hs]
    kt = [terms[h][2] * k[h] for h in hs]
    dv2 = [mm(p_ref[0, h], do[h], TN) + mm(kt[h], dsn[h]) for h in hs]
    for h in hs:
        left = jnp.concatenate([qt_ref[:, lanes(h)], t_ref[0, h]], axis=0)
        run[h] = mm(left, jnp.concatenate([do[h], dsn[h]], axis=0), TN)
    states = [s_ref[0, h] for h in hs]
    both = [mm(jnp.concatenate([do[h], dv2[h]], axis=0), states[h], NT) for h in hs]
    dp = [jnp.where(masks["inside"], mm(do[h], v2[h], NT), 0.0) for h in hs]
    dkt = [mm(v2[h], dsn[h], NT) for h in hs]
    dx = [mm(x_ref[0, h], jnp.concatenate([-both[h][128:], dv2[h]], axis=1), TN) for h in hs]
    da = [
        jnp.where(
            masks["strict"],
            -mm(dx[h], jnp.concatenate([w_ref[:, lanes(h)], u_ref[:, lanes(h)]], axis=1), NT),
            0.0,
        )
        for h in hs
    ]
    gdecay = jnp.zeros((CHUNK, CHUNK), F32)
    gbeta = jnp.zeros((CHUNK, CHUNK), F32)
    minus = jnp.zeros((CHUNK, CHUNK), F32)
    dq, dk, dv = [], [], []
    for h in hs:
        spread, start, to_last, keep = terms[h]
        doq = both[h][:128]
        dqk = dp[h] * spread
        kgh = kg_ref[0, h]
        z = da[h] * kgh
        dkk = b[h] * da[h] * spread
        dxk, dxv = dx[h][:, :128], dx[h][:, 128:]
        stacked = jnp.concatenate([dqk, dkk], axis=0)
        forward = mm(stacked, k[h])
        backward = mm(stacked, jnp.concatenate([q[h], k[h]], axis=0), TN)
        kx = jnp.sum(k[h] * dxk, axis=-1, keepdims=True)
        dq.append(start * doq + forward[:128])
        dk.append(
            backward + forward[128:] + to_last * dkt[h] + (b[h] * start) * dxk
        )
        dv.append(b[h] * dxv)
        gb = (
            jnp.sum(z, axis=-1, keepdims=True)
            + jnp.sum(v[h] * dxv, axis=-1, keepdims=True)
            + start * kx
        )
        gamgrad = b[h] * z + dp[h] * p_ref[0, h]
        dstart = jnp.sum(q[h] * doq, axis=-1, keepdims=True) + b[h] * kx
        dlast = jnp.sum(k[h] * dkt[h], axis=-1, keepdims=True) * to_last
        dkeep = jnp.sum(states[h] * dsn[h], keepdims=True) * keep
        gcol = jnp.sum(gamgrad, axis=-1, keepdims=True) + dstart * start - dlast
        end = jnp.sum(dlast, keepdims=True) + dkeep
        gcol = gcol + jnp.where(masks["row"][:, :1] == CHUNK - 1, end, 0.0)
        grow = jnp.sum(gamgrad, axis=0, keepdims=True)
        gdecay = jnp.where(lane == h, gcol, gdecay)
        gbeta = jnp.where(lane == heads + h, gb, gbeta)
        minus = jnp.where(masks["row"] == h, grow, minus)
    gdecay = gdecay - minus.T
    upper = jnp.where(masks["row"] <= masks["col"], 1.0, 0.0)
    dg = mm_full(upper, gdecay)
    galpha = dg * rate * jax.nn.sigmoid(shifted)
    width = pieces[0].shape[1]
    grads_ref[:, 3 * width + 128 :] = dgate_ref[...]
    grads_ref[:, 3 * width : 3 * width + 128] = jnp.where(
        lane < heads, galpha, gbeta * beta * (1.0 - beta)
    ).astype(LOW)
    gparams_ref[0:8, :] += jnp.sum((galpha).reshape(CHUNK // 8, 8, 128), axis=0)
    gparams_ref[8:16, :] += jnp.sum((dg * decays).reshape(CHUNK // 8, 8, 128), axis=0)

    for i in range(3):
        rows, pre, sg = feats[i]
        pieces_d = []
        for h in hs:
            if i == 2:
                pieces_d.append(dv[h])
            else:
                inv = uq[h] if i == 0 else uk[h]
                grad = dq[h] * root if i == 0 else dk[h]
                normal = conv[i][:, lanes(h)] * inv
                pieces_d.append(
                    inv * (grad - normal * jnp.sum(grad * normal, axis=-1, keepdims=True))
                )
        dc = jnp.concatenate(pieces_d, axis=1)
        ds = dc * (sg * (1.0 + pre * (1.0 - sg)))
        grad = ds * taps[4 * i + 3 : 4 * i + 4, :]
        rim = jnp.zeros((8, ds.shape[1]), F32)
        gtaps_ref[4 * i + 3] += jnp.sum((ds * rows[0]).reshape(CHUNK // 8, 8, -1), axis=0)
        for s in range(1, 4):
            tap = taps[4 * i + 3 - s : 4 * i + 4 - s, :]
            masked = jnp.where(masks["back"][s], ds, 0.0)
            gtaps_ref[4 * i + 3 - s] += jnp.sum((ds * rows[s]).reshape(CHUNK // 8, 8, -1), axis=0)
            ext = jnp.concatenate([masked, after[3 * i + s - 1]], axis=0)
            grad = grad + pltpu.roll(ext, CHUNK + 8 - s, 0)[:CHUNK] * tap
            after[3 * i + s - 1] = masked[:8]
            front = jnp.concatenate([jnp.zeros_like(masked[:8]), masked[:8]], axis=0)
            rim = rim + pltpu.roll(front, 16 - s, 0)[:8] * tap
        grads_ref[:, i * width : (i + 1) * width] = grad.astype(LOW)
        rim_ref[:, i * width : (i + 1) * width] = rim

        @pl.when(rev == 0)
        def _():
            tail_ref[:, i * width : (i + 1) * width] = grad[CHUNK - HALO :]


def back(scalars, pieces, rims, narrow, taps, params, ds_in, do, v2, s, x, p, kg, w, u, qt, t, dgate, docs, heads):
    rows, width = pieces[0].shape
    chunks = rows // CHUNK
    flat, tiles = rows_spec(width, chunks, True), tile_spec(heads, chunks, True)
    return pl.pallas_call(
        functools.partial(back_kernel, docs, heads, chunks),
        out_shape=(
            sds(rows, 4 * width + 128, dtype=LOW), sds(HALO, 3 * width), sds(8, 3 * width),
            sds(12, 8, width), sds(16, 128),
        ),
        grid_spec=pltpu.PrefetchScalarGridSpec(
            num_scalar_prefetch=1,
            grid=(chunks,),
            in_specs=[flat] * 3
            + [halo_spec(width, chunks, True)] * 3
            + [whole_spec(HALO, width)] * 3
            + [rows_spec(128, chunks, True), whole_spec(16, width), whole_spec(8, 128)]
            + [whole_spec(heads, 128, 128), flat, flat, tiles, tiles, tiles, tiles, flat, flat, flat, tiles, flat],
            out_specs=[rows_spec(4 * width + 128, chunks, True)]
            + [whole_spec(HALO, 3 * width), whole_spec(8, 3 * width)]
            + [whole_spec(12, 8, width), whole_spec(16, 128)],
            scratch_shapes=[pltpu.VMEM((heads, 128, 128), F32), pltpu.VMEM((9, 8, width), F32)],
        ),
        compiler_params=pltpu.CompilerParams(**PARAMS),
        cost_estimate=cost(chunks * heads * 60 * 2 * 128**3, 16 * rows * width * 4),
        name="back",
    )(scalars, *pieces, *pieces, *rims, narrow, taps, params, ds_in, do, v2, s, x, p, kg, w, u, qt, t, dgate)


def contract_rows(left, right):
    return lax.dot_general(left, right, TN, preferred_element_type=F32)


def contract_cols(left, right):
    return lax.dot_general(left, right, NT, preferred_element_type=F32)


def dot(left, right):
    return jnp.dot(left, right, preferred_element_type=F32)


def row_norm(values, gain):
    return values * lax.rsqrt(jnp.mean(values * values, axis=-1, keepdims=True) + epsilon) * gain


def norm_back(values, gain, grad):
    inv = lax.rsqrt(jnp.mean(values * values, axis=-1, keepdims=True) + epsilon)
    scaled = grad * gain
    inner = jnp.mean(scaled * values, axis=-1, keepdims=True)
    return inv * scaled - values * (inner * inv * inv * inv), jnp.sum(grad * values * inv, axis=0)


MESH = pl.DeviceIdType.MESH


def greet(axis, parts):
    me = lax.axis_index(axis)
    barrier = pltpu.get_barrier_semaphore()

    @pl.when(me > 0)
    def _():
        pl.semaphore_signal(barrier, inc=1, device_id={axis: me - 1}, device_id_type=MESH)

    @pl.when(me < parts - 1)
    def _():
        pl.semaphore_signal(barrier, inc=1, device_id={axis: me + 1}, device_id_type=MESH)

    inner = (me > 0) & (me < parts - 1)

    @pl.when(inner)
    def _():
        pl.semaphore_wait(barrier, 2)

    @pl.when(jnp.logical_not(inner))
    def _():
        pl.semaphore_wait(barrier, 1)


def line_gather(parts, buf, sems, first, use):
    me = lax.axis_index("tensor")
    send_right, send_left, from_left, from_right = sems

    def rightward(piece, step):
        return pltpu.make_async_remote_copy(
            src_ref=buf.at[piece],
            dst_ref=buf.at[piece],
            send_sem=send_right.at[step],
            recv_sem=from_left.at[step],
            device_id={"tensor": me + 1},
            device_id_type=MESH,
        )

    def leftward(piece, step):
        return pltpu.make_async_remote_copy(
            src_ref=buf.at[piece],
            dst_ref=buf.at[piece],
            send_sem=send_left.at[step],
            recv_sem=from_right.at[step],
            device_id={"tensor": me - 1},
            device_id_type=MESH,
        )

    def body(step, _):
        low, high = me - step, me + step

        @pl.when((step > 0) & (low >= 0))
        def _():
            rightward(low, step - 1).wait_recv()

        @pl.when((low >= 0) & (me < parts - 1))
        def _():
            rightward(low, step).start()

        @pl.when((step > 0) & (high < parts))
        def _():
            leftward(high, step - 1).wait_recv()

        @pl.when((high < parts) & (me > 0))
        def _():
            leftward(high, step).start()

        @pl.when(step == 0)
        def _():
            first()

        @pl.when(low >= 0)
        def _():
            use(low)

        @pl.when((step > 0) & (high < parts))
        def _():
            use(high)

        return 0

    lax.fori_loop(0, parts, body, 0)

    def finish(step, _):
        low, high = me - step, me + step

        @pl.when((low >= 0) & (me < parts - 1))
        def _():
            rightward(low, step).wait_send()

        @pl.when((high < parts) & (me > 0))
        def _():
            leftward(high, step).wait_send()

        return 0

    lax.fori_loop(0, parts, finish, 0)


def norm_into(buf, me, source, gain):
    rows = source.shape[0]

    def body(i, _):
        at = pl.ds(pl.multiple_of(i * 64, 64), 64)
        values = source[at, :].astype(F32)
        scale = lax.rsqrt(jnp.mean(values * values, axis=-1, keepdims=True) + epsilon)
        buf[me, at, :] = (values * scale * gain[0:1, :]).astype(LOW)
        return 0

    lax.fori_loop(0, rows // 64, body, 0)


def project_kernel(parts, tok_ref, gain_ref, narrow_w, *refs):
    weights_in, all_ref = refs[0:4], refs[4]
    q_ref, k_ref, v_ref, gate_ref, narrow_ref = refs[5:10]
    buf, weights = refs[10], refs[11:15]
    sems, load_sem, store_sem = refs[15:19], refs[19], refs[20]
    me = lax.axis_index("tensor")
    rows = tok_ref.shape[0]
    loads = [
        pltpu.make_async_copy(weights_in[i], weights[i], load_sem.at[i]) for i in range(4)
    ]
    for load in loads:
        load.start()
    norm_into(buf, me, tok_ref, gain_ref)
    greet("tensor", parts)

    def first():
        for load in loads:
            load.wait()

    def stored(piece):
        at = pl.ds(pl.multiple_of(piece * rows, rows), rows)
        return pltpu.make_async_copy(buf.at[piece], all_ref.at[at, :], store_sem.at[piece])

    def use(piece):
        at = pl.ds(pl.multiple_of(piece * rows, rows), rows)
        stored(piece).start()
        values = buf[piece]
        for w, out in zip(weights, (q_ref, k_ref, v_ref, gate_ref)):
            out[at, :] = dot(values, w[...]).astype(out.dtype)
        narrow_ref[at, :] = dot(values, narrow_w[...])

    line_gather(parts, buf, sems, first, use)
    for piece in range(parts):
        stored(piece).wait()


def vmem():
    return pl.BlockSpec(memory_space=pltpu.VMEM)


def hbm():
    return pl.BlockSpec(memory_space=pl.ANY)


def line_sems(parts):
    return [pltpu.SemaphoreType.DMA((parts,))] * 4


def comm_params(number):
    return pltpu.CompilerParams(
        collective_id=number, has_side_effects=True, vmem_limit_bytes=60 * 1024 * 1024
    )


def project(parts, tokens, gain, narrow_w, weights):
    rows, model = tokens.shape
    width = weights[0].shape[1]
    total = rows * parts
    low = sds(total, width, dtype=LOW)
    return pl.pallas_call(
        functools.partial(project_kernel, parts),
        out_shape=(sds(total, model, dtype=LOW), low, low, low, sds(total, width), sds(total, 128)),
        in_specs=[vmem()] * 3 + [hbm()] * 4,
        out_specs=[hbm()] + [vmem()] * 5,
        scratch_shapes=[pltpu.VMEM((parts, rows, model), LOW)]
        + [pltpu.VMEM((model, width), LOW)] * 4
        + line_sems(parts)
        + [pltpu.SemaphoreType.DMA((4,)), pltpu.SemaphoreType.DMA((parts,))],
        compiler_params=comm_params(1),
        cost_estimate=cost(2 * total * model * (4 * width + 128), 60 * 2**20),
        name="project",
    )(tokens, gain, narrow_w, *weights)


def feed_kernel(parts, res_ref, gain_ref, *refs):
    weights_in, og_in = refs[0:3], refs[3]
    all_ref, act_ref, gu_ref, mlp_ref = refs[4:8]
    buf, weights, og = refs[8], refs[9:12], refs[12]
    sems, load_sem, store_sem = refs[13:17], refs[17], refs[18]
    me = lax.axis_index("tensor")
    rows = res_ref.shape[0]
    units = weights_in[0].shape[1]
    loads = [
        pltpu.make_async_copy(src, dst, load_sem.at[i])
        for i, (src, dst) in enumerate(zip(weights_in + (og_in,), weights + (og,)))
    ]
    for load in loads:
        load.start()
    norm_into(buf, me, res_ref, gain_ref)
    greet("tensor", parts)
    wg, wu, wd = weights

    def first():
        for load in loads:
            load.wait()

    def stored(piece):
        at = pl.ds(pl.multiple_of(piece * rows, rows), rows)
        return pltpu.make_async_copy(buf.at[piece], all_ref.at[at, :], store_sem.at[piece])

    def tile(at, piece, column, size):
        cols = pl.ds(pl.multiple_of(column, 128), size)
        values = buf[piece]
        gate = dot(values, wg[:, cols])
        up = dot(values, wu[:, cols])
        grad = contract_cols(og[at, :], wd[cols, :])
        sg = jax.nn.sigmoid(gate)
        act = gate * sg
        act_ref[at, cols] = (act * up).astype(LOW)
        gu_ref[at, cols] = (grad * up * sg * (1.0 + gate * (1.0 - sg))).astype(LOW)
        gu_ref[at, pl.ds(pl.multiple_of(units + column, 128), size)] = (grad * act).astype(LOW)

    def use(piece):
        at = pl.ds(pl.multiple_of(piece * rows, rows), rows)
        stored(piece).start()

        def body(i, _):
            tile(at, piece, i * 256, 256)
            return 0

        lax.fori_loop(0, units // 256, body, 0)
        if units % 256:
            tile(at, piece, units - units % 256, units % 256)

        def down(i, _):
            cols = pl.ds(pl.multiple_of(i * 256, 256), 256)
            mlp_ref[at, cols] = dot(act_ref[at, :], wd[:, cols]).astype(LOW)
            return 0

        lax.fori_loop(0, mlp_ref.shape[1] // 256, down, 0)

    line_gather(parts, buf, sems, first, use)
    for piece in range(parts):
        stored(piece).wait()


def feed(parts, residual, gain, weights, out_grad):
    rows, model = residual.shape
    units = weights[0].shape[1]
    total = rows * parts
    return pl.pallas_call(
        functools.partial(feed_kernel, parts),
        out_shape=(
            sds(total, model, dtype=LOW), sds(total, units, dtype=LOW), sds(total, 2 * units, dtype=LOW),
            sds(total, model, dtype=LOW),
        ),
        in_specs=[vmem()] * 2 + [hbm()] * 4,
        out_specs=[hbm()] + [vmem()] * 3,
        scratch_shapes=[pltpu.VMEM((parts, rows, model), LOW)]
        + [pltpu.VMEM(w.shape, LOW) for w in weights]
        + [pltpu.VMEM((total, model), LOW)]
        + line_sems(parts)
        + [pltpu.SemaphoreType.DMA((4,)), pltpu.SemaphoreType.DMA((parts,))],
        compiler_params=comm_params(2),
        cost_estimate=cost(8 * total * model * units, 120 * 2**20),
        name="feed",
    )(residual, gain, *weights, out_grad)


SUBS = 2


class Plain:
    inputs, outputs = 0, 1

    def __init__(self, parts):
        self.parts = parts

    def begin(self, given, scratch):
        greet("tensor", self.parts)

    def end(self, given, out, scratch):
        pass

    def shapes(self, rows, model):
        return (sds(rows, model),)

    def scratch(self, rows, model):
        return []


def each(total, me, action):
    def body(k, _):
        action(lax.rem(me + k, total))
        return 0

    lax.fori_loop(1, total, body, 0)


class Exchange:
    def __init__(self, axis, total, buf, send_sem, got_sem):
        self.axis, self.total = axis, total
        self.buf, self.send_sem, self.got_sem = buf, send_sem, got_sem

    def copy(self, source, target):
        return pltpu.make_async_remote_copy(
            src_ref=self.buf.at[source],
            dst_ref=self.buf.at[source],
            send_sem=self.send_sem.at[target],
            recv_sem=self.got_sem.at[source],
            device_id={self.axis: target},
            device_id_type=MESH,
        )

    def send(self):
        me = lax.axis_index(self.axis)
        each(self.total, me, lambda other: self.copy(me, other).start())

    def receive(self):
        me = lax.axis_index(self.axis)
        each(self.total, me, lambda other: self.copy(other, me).wait_recv())

    def drain(self):
        me = lax.axis_index(self.axis)
        each(self.total, me, lambda other: self.copy(me, other).wait_send())

    def sum(self, at=slice(None)):
        total = self.buf[0, at]
        for i in range(1, self.total):
            total = total + self.buf[i, at]
        return total


class Closing:
    inputs, outputs = 4, 4

    def __init__(self, count, parts, kept, flat):
        self.count, self.parts, self.kept, self.flat = count, parts, kept, flat

    def stages(self, scratch):
        return (
            Exchange("dp", self.count, *scratch[0:3]),
            Exchange("tensor", self.parts, *scratch[3:6]),
            Exchange("dp", self.count, *scratch[6:9]),
            Exchange("tensor", self.parts, *scratch[9:12]),
        )

    def begin(self, given, scratch):
        dp, z = lax.axis_index("dp"), lax.axis_index("tensor")
        barrier = pltpu.get_barrier_semaphore()

        def hello(axis):
            def one(other):
                pl.semaphore_signal(
                    barrier, inc=1, device_id={axis: other}, device_id_type=MESH
                )

            return one

        each(self.count, dp, hello("dp"))
        each(self.parts, z, hello("tensor"))
        first = self.stages(scratch)[0]
        first.buf[dp] = given[3][...]
        pl.semaphore_wait(barrier, self.count + self.parts - 2)
        first.send()

    def end(self, given, out, scratch):
        tok_ref, gain_ref, res_ref, flat_ref = given
        out_ref, wide_ref, rest_ref, gain_out = out
        dp, z = lax.axis_index("dp"), lax.axis_index("tensor")
        flat_dp, flat_z, gain_dp, gain_z = self.stages(scratch)
        sums = scratch[12]
        rows, model = out_ref.shape
        flat_dp.receive()
        flat_z.buf[z] = flat_dp.sum()
        flat_z.send()
        sums[...] = jnp.zeros_like(sums)

        def body(i, _):
            at = pl.ds(pl.multiple_of(i * 32, 32), 32)
            values, grad = tok_ref[at, :].astype(F32), out_ref[at, :]
            inv = lax.rsqrt(jnp.mean(values * values, axis=-1, keepdims=True) + epsilon)
            scaled = grad * gain_ref[0:1, :]
            inner = jnp.mean(scaled * values, axis=-1, keepdims=True)
            out_ref[at, :] = (
                res_ref[at, :] + inv * scaled - values * (inner * inv * inv * inv)
            )
            sums[...] += jnp.sum((grad * values * inv).reshape(4, 8, model), axis=0)
            return 0

        lax.fori_loop(0, rows // 32, body, 0)
        total = jnp.sum(sums[...], axis=0, keepdims=True)
        wide = model // 8
        gain_dp.buf[dp] = jnp.concatenate(
            [total[:, i * wide : (i + 1) * wide] for i in range(8)], axis=0
        )
        gain_dp.send()
        flat_z.receive()
        width = flat_ref.shape[1]
        for i in range(self.parts):
            wide_ref[:, i * width : (i + 1) * width] = flat_z.buf[i, : self.kept, :]
        rest_ref[...] = flat_z.sum(slice(self.kept, None))
        gain_dp.receive()
        gain_z.buf[z] = gain_dp.sum()
        gain_z.send()
        gain_z.receive()
        gain_out[...] = gain_z.sum()
        for stage in (flat_dp, flat_z, gain_dp, gain_z):
            stage.drain()

    def shapes(self, rows, model):
        height, width = self.flat
        return (
            sds(rows, model), sds(self.kept, width * self.parts), sds(height - self.kept, width),
            sds(8, model // 8),
        )

    def scratch(self, rows, model):
        out = []
        for shape in (self.flat, (8, model // 8)):
            for total in (self.count, self.parts):
                out.append(pltpu.VMEM((total,) + shape, F32))
                out.extend([pltpu.SemaphoreType.DMA((total,))] * 2)
        return out + [pltpu.VMEM((8, model), F32)]


def scatter_kernel(parts, given, count, splits, ending, *refs):
    lefts, rights_in = refs[0:given], refs[given : given + count]
    refs = refs[given + count :]
    extra_in, refs = refs[: ending.inputs], refs[ending.inputs :]
    extra_out, refs = refs[: ending.outputs], refs[ending.outputs :]
    rights, (part, send_r, send_l, got_l, got_r) = refs[0:count], refs[count : count + 5]
    sem_sr, sem_sl, sem_gl, sem_gr, load_sem = refs[count + 5 : count + 10]
    extra = refs[count + 10 :]
    out_ref = extra_out[0]
    me = lax.axis_index("tensor")
    rows, model = out_ref.shape
    size = rows // SUBS
    loads = [
        pltpu.make_async_copy(rights_in[i], rights[i], load_sem.at[i]) for i in range(count)
    ]
    for load in loads:
        load.start()
    ending.begin(extra_in, extra)
    for load in loads:
        load.wait()

    def rightward(slot):
        return pltpu.make_async_remote_copy(
            src_ref=send_r.at[slot],
            dst_ref=got_l.at[slot],
            send_sem=sem_sr.at[slot],
            recv_sem=sem_gl.at[slot],
            device_id={"tensor": me + 1},
            device_id_type=MESH,
        )

    def leftward(slot):
        return pltpu.make_async_remote_copy(
            src_ref=send_l.at[slot],
            dst_ref=got_r.at[slot],
            send_sem=sem_sl.at[slot],
            recv_sem=sem_gr.at[slot],
            device_id={"tensor": me - 1},
            device_id_type=MESH,
        )

    def product(start, many, target):
        at = pl.ds(pl.multiple_of(start, 128), many)

        def body(j, _):
            cols = pl.ds(pl.multiple_of(j * 256, 256), 256)
            total = None
            for i, (index, first, wide) in enumerate(splits):
                term = contract_cols(lefts[index][at, first : first + wide], rights[i][cols, :])
                total = term if total is None else total + term
            target[:, cols] = total
            return 0

        lax.fori_loop(0, model // 256, body, 0)

    half = part.at[pl.ds(0, size), :]

    def go_right(piece, sub):
        slot = piece * SUBS + sub

        @pl.when(piece > me)
        def _():
            product(piece * rows + sub * size, size, half)

            @pl.when(me > 0)
            def _():
                rightward(slot).wait_recv()
                send_r[slot] = (half[...] + got_l[slot].astype(F32)).astype(LOW)

            @pl.when(me == 0)
            def _():
                send_r[slot] = half[...].astype(LOW)

            rightward(slot).start()

    def go_left(piece, sub):
        slot = piece * SUBS + sub

        @pl.when(piece < me)
        def _():
            product(piece * rows + sub * size, size, half)

            @pl.when(me < parts - 1)
            def _():
                leftward(slot).wait_recv()
                send_l[slot] = (half[...] + got_r[slot].astype(F32)).astype(LOW)

            @pl.when(me == parts - 1)
            def _():
                send_l[slot] = half[...].astype(LOW)

            leftward(slot).start()

    right_first = 2 * me < parts

    def body(item, _):
        step, sub = item // SUBS, item % SUBS
        right, left = parts - 1 - step, step

        @pl.when(right_first)
        def _():
            go_right(right, sub)

        go_left(left, sub)

        @pl.when(jnp.logical_not(right_first))
        def _():
            go_right(right, sub)

        return 0

    lax.fori_loop(0, (parts - 1) * SUBS, body, 0)
    product(me * rows, rows, part)
    for sub in range(SUBS):
        at = slice(sub * size, sub * size + size)
        slot = me * SUBS + sub
        out_ref[at, :] = part[at, :]

        @pl.when(me > 0)
        def _():
            rightward(slot).wait_recv()
            out_ref[at, :] = out_ref[at, :] + got_l[slot].astype(F32)

        @pl.when(me < parts - 1)
        def _():
            leftward(slot).wait_recv()
            out_ref[at, :] = out_ref[at, :] + got_r[slot].astype(F32)

    ending.end(extra_in, extra_out, extra)

    def finish(slot, _):
        piece = slot // SUBS

        @pl.when(piece > me)
        def _():
            rightward(slot).wait_send()

        @pl.when(piece < me)
        def _():
            leftward(slot).wait_send()

        return 0

    lax.fori_loop(0, parts * SUBS, finish, 0)


def scatter(parts, lefts, rights, splits, number, ending=None, extra=()):
    total = lefts[0].shape[0]
    model = rights[0].shape[0]
    rows = total // parts
    count = len(rights)
    ending = ending or Plain(parts)
    slots = pltpu.VMEM((parts * SUBS, rows // SUBS, model), LOW)
    shapes = ending.shapes(rows, model)
    return pl.pallas_call(
        functools.partial(scatter_kernel, parts, len(lefts), count, splits, ending),
        out_shape=shapes,
        in_specs=[vmem()] * len(lefts) + [hbm()] * count + [vmem()] * len(extra),
        out_specs=[vmem()] * len(shapes),
        scratch_shapes=[pltpu.VMEM(w.shape, LOW) for w in rights]
        + [pltpu.VMEM((rows, model), F32)]
        + [slots] * 4
        + line_sems(parts * SUBS)
        + [pltpu.SemaphoreType.DMA((count,))]
        + ending.scratch(rows, model),
        compiler_params=comm_params(number),
        cost_estimate=cost(2 * total * model * sum(w.shape[1] for w in rights), 60 * 2**20),
        name="scatter%d" % number,
    )(*lefts, *rights, *extra)


def state_kernel(count, heads, backward, own_ref, out_ref, buf, send_sem, pass_sem, got_sem):
    me = lax.axis_index("dp")
    core = lax.rem(me, 2)
    sibling = me + 1 - 2 * core
    half = count // 2
    barrier = pltpu.get_barrier_semaphore()

    def peer(k):
        return lax.rem(me + 2 * k, count)

    def hello(k, _):
        pl.semaphore_signal(barrier, inc=1, device_id={"dp": peer(k)}, device_id_type=MESH)
        return 0

    lax.fori_loop(1, half, hello, 0)
    pl.semaphore_signal(barrier, inc=1, device_id={"dp": sibling}, device_id_type=MESH)
    buf[me] = own_ref[...].astype(LOW)
    pl.semaphore_wait(barrier, half)

    def needed(source, target):
        return source > target if backward else source < target

    def copy(piece, target, sem):
        return pltpu.make_async_remote_copy(
            src_ref=buf.at[piece],
            dst_ref=buf.at[piece],
            send_sem=sem,
            recv_sem=got_sem.at[piece],
            device_id={"dp": target},
            device_id_type=MESH,
        )

    def send(k, _):
        target = peer(k)

        @pl.when(needed(me, target))
        def _():
            copy(me, target, send_sem.at[target]).start()

        return 0

    @pl.when(needed(me, sibling))
    def _():
        copy(me, sibling, pass_sem.at[me]).start()

    lax.fori_loop(1, half, send, 0)

    def relay(k, _):
        source = lax.rem(me + count - 2 * k, count)

        @pl.when(needed(source, me))
        def _():
            copy(source, me, send_sem.at[source]).wait_recv()

        @pl.when(needed(source, me) & needed(source, sibling))
        def _():
            copy(source, sibling, pass_sem.at[source]).start()

        return 0

    lax.fori_loop(1, half, relay, 0)
    for h in range(heads):
        out_ref[h] = jnp.zeros_like(out_ref[h])

    def chain(step, _):
        piece = count - 1 - step if backward else step

        @pl.when(needed(piece, me) & (lax.rem(piece, 2) != core))
        def _():
            copy(piece, me, pass_sem.at[piece]).wait_recv()

        @pl.when(needed(piece, me))
        def _():
            for h in range(heads):
                both = buf[piece, h].astype(F32)
                if backward:
                    out_ref[h] = mm(both[:, 128:], out_ref[h], TN) + both[:, :128]
                else:
                    out_ref[h] = mm(both[:, 128:], out_ref[h]) + both[:, :128]

        return 0

    lax.fori_loop(0, count, chain, 0)

    def finish(k, _):
        target = peer(k)
        source = lax.rem(me + count - 2 * k, count)

        @pl.when(needed(me, target))
        def _():
            copy(me, target, send_sem.at[target]).wait_send()

        @pl.when(needed(source, me) & needed(source, sibling))
        def _():
            copy(source, sibling, pass_sem.at[source]).wait_send()

        return 0

    lax.fori_loop(1, half, finish, 0)

    @pl.when(needed(me, sibling))
    def _():
        copy(me, sibling, pass_sem.at[me]).wait_send()


def exchange(count, own, heads, backward, number):
    return pl.pallas_call(
        functools.partial(state_kernel, count, heads, backward),
        out_shape=sds(heads, 128, 128),
        in_specs=[vmem()],
        out_specs=vmem(),
        scratch_shapes=[pltpu.VMEM((count, heads, 128, 256), LOW)]
        + [pltpu.SemaphoreType.DMA((count,))] * 3,
        compiler_params=comm_params(number),
        cost_estimate=cost(count * heads * 6 * 128**3, count * heads * 256 * 128 * 4),
        name="exchange%d" % number,
    )(own)


def after(values, *first):
    out = lax.optimization_barrier((values,) + first)
    return out[0]


def local(
    tokens,
    gain_in,
    w_query,
    w_key,
    w_value,
    w_alpha,
    w_beta,
    w_gate_out,
    conv_query,
    conv_key,
    conv_value,
    decay_log,
    decay_bias,
    head_gain,
    w_out,
    gain_mid,
    w_gate,
    w_up,
    w_down,
    out_grad,
    doc_lengths,
):
    rows_own, model = tokens.shape
    tensor_parts, dp_parts = lax.axis_size("tensor"), lax.axis_size("dp")
    tensor_index, dp_index = lax.axis_index("tensor"), lax.axis_index("dp")
    group_rows = rows_own * tensor_parts
    seq_total = group_rows * dp_parts
    heads = w_alpha.shape[1]
    width = w_query.shape[1]
    core = lax.rem(dp_index, 2)
    docs = doc_lengths.shape[0] * doc_lengths.shape[1]
    starts = (
        jnp.cumsum(doc_lengths, axis=1)
        - doc_lengths
        + seq_total * lax.broadcasted_iota(jnp.int32, doc_lengths.shape, 0)
    ).reshape(-1)
    scalars = jnp.concatenate([(dp_index * group_rows).reshape(1), starts, core.reshape(1)]).astype(jnp.int32)
    taps = jnp.concatenate([conv_query, conv_key, conv_value, jnp.zeros((4, width), F32)])
    params = jnp.zeros((8, 128), F32).at[0, :heads].set(decay_bias).at[1, :heads].set(decay_log)
    gain_heads = jnp.broadcast_to(head_gain[None], (8, width))
    w_narrow = jnp.pad(jnp.concatenate([w_alpha, w_beta], axis=1), ((0, 0), (0, 128 - 2 * heads)))

    own_rows = tokens.astype(F32)
    gain_in_rows = jnp.broadcast_to(gain_in[None], (8, model))
    gain_mid_rows = jnp.broadcast_to(gain_mid[None], (8, model))
    normed_all, *pieces, gate_raw, narrow = project(
        tensor_parts, tokens, gain_in_rows, w_narrow, (w_query, w_key, w_value, w_gate_out)
    )
    half = width // 2
    out_half = lax.dynamic_slice_in_dim(after(w_out, narrow), core * half, half, 0)
    out_mine = lax.all_gather(out_half, "tensor", axis=0)
    forth = [(i, i + 1) for i in range(dp_parts - 1)]
    rims = lax.ppermute(
        jnp.stack([piece[group_rows - HALO :] for piece in pieces]), "dp", forth
    )
    rims = [rims[i] for i in range(3)]
    x, p, kg, w, u, qt, ou, t, o, totals = intra(
        scalars, pieces, rims, narrow, taps, params, docs, heads
    )
    state_in = exchange(dp_parts, totals, heads, False, 3)
    rows_out, v2, s, mixed = outward(state_in, w, u, qt, ou, t, o, gate_raw, gain_heads, heads)

    mixed_own = lax.all_to_all(mixed, "tensor", split_axis=0, concat_axis=1, tiled=True)
    out_mine, _ = lax.optimization_barrier((out_mine, mixed))
    out_other = lax.ppermute(out_mine, "dp", [(i, i ^ 1) for i in range(dp_parts)])
    out_mine = out_mine.reshape(tensor_parts * half, model)
    out_other = out_other.reshape(tensor_parts * half, model)
    split = mixed_own.reshape(rows_own, tensor_parts, 2, half)

    def of_core(index):
        return lax.dynamic_index_in_dim(split, index, 2, keepdims=False).reshape(rows_own, -1)

    residual = own_rows + (dot(of_core(core), out_mine) + dot(of_core(1 - core), out_other))
    mid_all, activated, grad_units, mlp_part = feed(
        tensor_parts, residual, gain_mid_rows, (w_gate, w_up, w_down), out_grad
    )
    units = w_gate.shape[1]
    ring = [(i, (i + 1) % tensor_parts) for i in range(tensor_parts)]

    def piece_of(values, back_by):
        index = lax.rem(tensor_index - back_by + tensor_parts, tensor_parts)
        return lax.dynamic_slice_in_dim(values, index * rows_own, rows_own, 0)

    def added(values, back_by, got):
        return (piece_of(values, back_by).astype(F32) + got.astype(F32)).astype(LOW)

    mlp_run = lax.ppermute(piece_of(mlp_part, 1), "tensor", ring)
    down_grad = contract_rows(out_grad, activated).astype(LOW)
    units_grad = contract_rows(mid_all, after(grad_units, down_grad)).astype(LOW)
    units_grad, mlp_run = lax.optimization_barrier((units_grad, mlp_run))
    down_grad_sum = lax.psum_scatter(down_grad, "dp", scatter_dimension=0, tiled=True)
    units_grad_sum = lax.psum_scatter(units_grad, "dp", scatter_dimension=0, tiled=True)

    (grad_mid,) = scatter(
        tensor_parts, [after(grad_units, units_grad)], [w_gate, w_up],
        ((0, 0, units), (0, units, units)), 4,
    )
    grad_res_norm, gain_mid_grad = norm_back(residual, gain_mid, grad_mid)
    grad_own = lax.dynamic_slice_in_dim(out_grad, tensor_index * rows_own, rows_own, 0)
    grad_residual = grad_own.astype(F32) + grad_res_norm
    grad_mixer = grad_residual.astype(LOW)
    grad_mixed = jnp.concatenate(
        [contract_cols(grad_mixer, weight).astype(LOW) for weight in (out_mine, out_other)], axis=1
    ).reshape(rows_own, 2, tensor_parts, half)
    grad_mixed = lax.all_to_all(
        grad_mixed, "tensor", split_axis=2, concat_axis=0, tiled=True
    ).reshape(group_rows, width)
    mlp_run = after(mlp_run, grad_mixed)
    out_w = contract_rows(after(grad_mixer, grad_mixed), mixed_own).astype(LOW)
    out_w_sum = lax.psum_scatter(out_w, "dp", scatter_dimension=0, tiled=True)
    for back_by in range(2, tensor_parts - 1):
        mlp_run = lax.ppermute(added(mlp_part, back_by, mlp_run), "tensor", ring)

    do, gate_low, head_gain_part, ds_total = inward(
        scalars, grad_mixed, rows_out, gate_raw, gain_heads, qt, t, totals, heads
    )
    grad_end = exchange(dp_parts, ds_total, heads, True, 5)
    grad_end, mlp_run, _, _ = lax.optimization_barrier(
        (grad_end, mlp_run, units_grad_sum, down_grad_sum)
    )
    mlp_run = lax.ppermute(added(mlp_part, tensor_parts - 1, mlp_run), "tensor", ring)
    grads, tails, rim_grad, taps_grad, params_grad = back(
        scalars, pieces, rims, narrow, taps, params, grad_end, do, v2, s, x, p, kg, w, u, qt, t,
        gate_low, docs, heads,
    )
    grads, tails, rim_grad, taps_grad, params_grad, mlp_run = lax.optimization_barrier(
        (grads, tails, rim_grad, taps_grad, params_grad, mlp_run)
    )
    rim_back = lax.ppermute(rim_grad, "dp", [(i + 1, i) for i in range(dp_parts - 1)])
    tails = tails.at[HALO - 8 :].add(rim_back).astype(LOW)
    grads = lax.dynamic_update_slice(grads, tails, (group_rows - HALO, 0))
    out_w_sum = lax.psum_scatter(
        out_w_sum, "tensor", scatter_dimension=1, tiled=True
    )
    mixer_grad = contract_rows(normed_all, grads).astype(LOW)
    mixer_sum = lax.psum_scatter(mixer_grad, "dp", scatter_dimension=0, tiled=True).astype(F32)
    output = (residual + (piece_of(mlp_part, 0).astype(F32) + mlp_run.astype(F32))).astype(LOW)
    params_grad = params_grad.reshape(2, 8, 128).sum(1)
    flat = jnp.concatenate(
        [
            taps_grad.sum(1),
            head_gain_part.sum(0)[None],
            jnp.pad(params_grad, ((0, 1), (0, width - 128))),
            jnp.pad(gain_mid_grad.reshape(-1, width), ((0, 4), (0, 0))),
        ],
        axis=0,
    )
    input_grad, wide, rest, gain_in_grad = scatter(
        tensor_parts, [after(grads, mixer_grad)],
        [w_query, w_key, w_value, w_narrow, w_gate_out],
        ((0, 0, width), (0, width, width), (0, 2 * width, width), (0, 3 * width, 128), (0, 3 * width + 128, width)),
        6, Closing(dp_parts, tensor_parts, 16, flat.shape),
        (tokens, gain_in_rows, grad_residual, flat),
    )
    out_w_sum = after(out_w_sum, gain_in_grad).astype(F32)
    by_head = wide[13:15].reshape(2, tensor_parts, width)[:, :, :heads].reshape(2, -1)
    start = 3 * width
    return (
        output,
        input_grad,
        gain_in_grad.reshape(model),
        mixer_sum[:, :width],
        mixer_sum[:, width : 2 * width],
        mixer_sum[:, 2 * width : start],
        mixer_sum[:, start : start + heads],
        mixer_sum[:, start + heads : start + 2 * heads],
        mixer_sum[:, start + 128 :],
        wide[0:4],
        wide[4:8],
        wide[8:12],
        by_head[1],
        by_head[0],
        wide[12],
        out_w_sum.T,
        rest[: model // width].reshape(model),
        units_grad_sum[:, :units].astype(F32),
        units_grad_sum[:, units:].astype(F32),
        down_grad_sum.T.astype(F32),
    )


def solution(mesh):
    placed = (
        P(("dp", "tensor"), None),
        P(),
        P(None, "tensor"),
        P(None, "tensor"),
        P(None, "tensor"),
        P(None, "tensor"),
        P(None, "tensor"),
        P(None, "tensor"),
        P(None, "tensor"),
        P(None, "tensor"),
        P(None, "tensor"),
        P("tensor"),
        P("tensor"),
        P("tensor"),
        P("tensor", None),
        P(),
        P(None, "tensor"),
        P(None, "tensor"),
        P("tensor", None),
        P("dp", None),
        P(),
    )
    return jax.shard_map(
        local,
        mesh=mesh,
        in_specs=placed,
        out_specs=(
            P(("dp", "tensor"), None),
            P(("dp", "tensor"), None),
            P(),
            P("dp", "tensor"),
            P("dp", "tensor"),
            P("dp", "tensor"),
            P("dp", "tensor"),
            P("dp", "tensor"),
            P("dp", "tensor"),
            P(),
            P(),
            P(),
            P(),
            P(),
            P(),
            P("tensor", "dp"),
            P(),
            P("dp", "tensor"),
            P("dp", "tensor"),
            P("tensor", "dp"),
        ),
        check_vma=False,
    )
```

```python
import functools
import math

import jax
import jax.numpy as jnp
from jax import lax
from jax.experimental import pallas as pl
from jax.experimental.pallas import tpu as pltpu
from jax.sharding import PartitionSpec as P

CHUNK = 128
HALO = 16
epsilon = 1e-06
F32 = jnp.float32
LOW = jnp.bfloat16
NN = (((1,), (0,)), ((), ()))
NT = (((1,), (1,)), ((), ()))
TN = (((0,), (0,)), ((), ()))


def mm(left, right, dims=NN):
    return lax.dot_general(
        left, right, dims, precision=lax.Precision.HIGH, preferred_element_type=F32
    )


def mm_full(left, right, dims=NN):
    return lax.dot_general(
        left, right, dims, precision=lax.Precision.HIGHEST, preferred_element_type=F32
    )


def iota(shape, dim):
    return lax.broadcasted_iota(jnp.int32, shape, dim)


def doc_of(positions, scalars, docs):
    total = jnp.zeros_like(positions) - 1
    for j in range(docs):
        total = total + jnp.where(positions >= scalars[1 + j], 1, 0)
    return total


def chunk_masks(position, scalars, docs):
    shape = (CHUNK, CHUNK)
    row, col = iota(shape, 0), iota(shape, 1)
    doc_row = doc_of(row + position, scalars, docs)
    doc_col = doc_of(col + position, scalars, docs)
    same = doc_row == doc_col
    prior = jnp.int32(-1)
    last = jnp.int32(-1)
    for j in range(docs):
        prior = prior + jnp.where(position - 1 >= scalars[1 + j], 1, 0)
        last = last + jnp.where(position + CHUNK - 1 >= scalars[1 + j], 1, 0)
    return {
        "row": row,
        "col": col,
        "inside": same & (row >= col),
        "strict": same & (row > col),
        "carried": (doc_row == prior)[:, :1],
        "in_last": (doc_row == last)[:, :1],
        "last_carried": last == prior,
        "back": [
            None if s == 0 else (doc_row == doc_of(row + (position - s), scalars, docs))[:, :1]
            for s in range(4)
        ],
    }


def shifted_rows(main, before, back):
    ext = jnp.concatenate([before[HALO - 8 :], main], axis=0)
    rows = [main]
    for s in range(1, 4):
        rows.append(jnp.where(back[s], pltpu.roll(ext, s, 0)[8:], 0.0))
    return rows


def conv_sum(rows, taps):
    total = rows[0] * taps[3:4, :]
    for s in range(1, 4):
        total = total + rows[s] * taps[3 - s : 4 - s, :]
    return total


def softplus(x):
    return jnp.maximum(x, 0.0) + jnp.log1p(jnp.exp(-jnp.abs(x)))


def gates(narrow, params, masks):
    shifted = narrow + params[0:1, :]
    rate = -jnp.exp(params[1:2, :])
    decays = rate * softplus(shifted)
    lower = jnp.where(masks["row"] >= masks["col"], 1.0, 0.0)
    total = mm_full(lower, decays)
    return shifted, rate, decays, jax.nn.sigmoid(narrow), total, total.T


def decay_terms(h, total, total_row, masks):
    col = total[:, h : h + 1]
    row = total_row[h : h + 1, :]
    spread = jnp.where(
        masks["inside"], jnp.exp(jnp.where(masks["inside"], col - row, 0.0)), 0.0
    )
    start = jnp.where(masks["carried"], jnp.exp(col), 0.0)
    end = total[CHUNK - 1 : CHUNK, h : h + 1]
    to_last = jnp.where(masks["in_last"], jnp.exp(jnp.where(masks["in_last"], end - col, 0.0)), 0.0)
    keep = jnp.where(masks["last_carried"], jnp.exp(end), 0.0)
    return spread, start, to_last, keep


def lanes(h):
    return slice(h * 128, h * 128 + 128)


def features(pieces, befores, taps, masks, heads):
    out = []
    for i in range(3):
        rows = shifted_rows(pieces[i], befores[i], masks["back"])
        pre = conv_sum(rows, taps[4 * i : 4 * i + 4, :])
        out.append((rows, pre, jax.nn.sigmoid(pre)))
    return out


def unit(values):
    return lax.rsqrt(jnp.sum(values * values, axis=-1, keepdims=True) + epsilon)


GROUP = 2


def chunk_inputs(step, position, mains, priors, rims, narrow_ref, taps, params, scalars, docs, heads):
    out = []
    whole = [m[...].astype(F32) for m in mains]
    befores = [
        jnp.where(step == 0, r[...].astype(F32), p[...].astype(F32)) for p, r in zip(priors, rims)
    ]
    for j in range(GROUP):
        rows = slice(j * CHUNK, j * CHUNK + CHUNK)
        masks = chunk_masks(position + j * CHUNK, scalars, docs)
        pieces = [w[rows] for w in whole]
        if j:
            befores = [w[j * CHUNK - HALO : j * CHUNK] for w in whole]
        feats = features(pieces, befores, taps, masks, heads)
        gate = gates(narrow_ref[rows, :], params, masks)
        out.append((rows, masks, feats, gate))
    return out


def intra_kernel(docs, heads, scalars, *refs):
    mains, priors, rims = refs[0:3], refs[3:6], refs[6:9]
    narrow_ref, taps_ref, params_ref = refs[9:12]
    x_ref, p_ref, kg_ref, w_ref, u_ref, qt_ref, ou_ref, t_ref, o_ref, tot_ref = refs[12:22]
    run = refs[22]
    step = pl.program_id(0)
    position = scalars[0] + step * (CHUNK * GROUP)
    inputs = chunk_inputs(
        step, position, mains, priors, rims, narrow_ref, taps_ref[...], params_ref[...], scalars,
        docs, heads,
    )
    masks = inputs[0][1]
    eye = jnp.where(masks["row"] == masks["col"], 1.0, 0.0)
    items = [(j, h) for j in range(GROUP) for h in range(heads)]
    every = range(len(items))
    q, k, v, terms, b, strict = [], [], [], [], [], []
    for j, h in items:
        _, masks, feats, (_, _, _, beta, total, total_row) = inputs[j]
        conv = [pre[:, lanes(h)] * sg[:, lanes(h)] for _, pre, sg in feats]
        q.append(conv[0] * (unit(conv[0]) * (1.0 / math.sqrt(128.0))))
        k.append(conv[1] * unit(conv[1]))
        v.append(conv[2])
        terms.append(decay_terms(h, total, total_row, masks))
        b.append(beta[:, heads + h : heads + h + 1])
        strict.append(masks["strict"])
    kg = [jnp.where(strict[i], mm(k[i], k[i], NT) * terms[i][0], 0.0) for i in every]
    p = [mm(q[i], k[i], NT) * terms[i][0] for i in every]
    a = [b[i] * kg[i] for i in every]
    pair = (masks["row"] >> 1) == (masks["col"] >> 1)
    x = [eye - jnp.where(pair, a[i], 0.0) for i in every]
    for level in range(1, 7):
        wide = (masks["row"] >> (level + 1)) == (masks["col"] >> (level + 1))
        off = wide & ((masks["row"] >> level) != (masks["col"] >> level))
        lx = [mm(jnp.where(off, a[i], 0.0), x[i]) for i in every]
        x = [x[i] - mm(x[i], lx[i]) for i in every]
    wu = [
        mm(x[i], jnp.concatenate([(b[i] * terms[i][1]) * k[i], b[i] * v[i]], axis=1)) for i in every
    ]
    pwu = [mm(p[i], wu[i]) for i in every]
    kwu = [mm(terms[i][2] * k[i], wu[i], TN) for i in every]

    @pl.when(step == 0)
    def _():
        for h in range(heads):
            run[h] = jnp.concatenate([jnp.zeros((128, 128), F32), eye], axis=1)

    for i, (j, h) in enumerate(items):
        rows = inputs[j][0]
        x_ref[j, h] = x[i]
        p_ref[j, h] = p[i]
        kg_ref[j, h] = kg[i]
        w_ref[rows, lanes(h)] = wu[i][:, :128]
        u_ref[rows, lanes(h)] = wu[i][:, 128:]
        qt_ref[rows, lanes(h)] = terms[i][1] * q[i] - pwu[i][:, :128]
        ou_ref[rows, lanes(h)] = pwu[i][:, 128:]
        transfer = terms[i][3] * eye - kwu[i][:, :128]
        offset = kwu[i][:, 128:]
        t_ref[j, h] = transfer
        o_ref[j, h] = offset
        new = mm(transfer, run[h])
        new = jnp.concatenate([new[:, :128] + offset, new[:, 128:]], axis=1)
        run[h] = new
        tot_ref[h] = new


def at_step(chunks, reverse, group):
    steps = chunks // group
    return (lambda c: steps - 1 - c) if reverse else (lambda c: c)


def rows_spec(width, chunks, reverse=False, group=1):
    at = at_step(chunks, reverse, group)
    return pl.BlockSpec((CHUNK * group, width), lambda c, *_: (at(c), 0))


def halo_spec(width, chunks, reverse=False, group=1):
    per = CHUNK * group // HALO
    at = at_step(chunks, reverse, group)
    return pl.BlockSpec((HALO, width), lambda c, *_: (jnp.maximum(at(c) * per - 1, 0), 0))


def tile_spec(heads, chunks, reverse=False, group=1):
    at = at_step(chunks, reverse, group)
    return pl.BlockSpec((group, heads, 128, 128), lambda c, *_: (at(c), 0, 0, 0))


def whole_spec(*shape):
    zeros = (0,) * len(shape)
    return pl.BlockSpec(shape, lambda c, *_: zeros)


def sds(*shape, dtype=F32):
    return jax.ShapeDtypeStruct(shape, dtype)


PARAMS = dict(vmem_limit_bytes=56 * 1024 * 1024, dimension_semantics=("arbitrary",))


def cost(flops, moved):
    return pl.CostEstimate(flops=int(flops), bytes_accessed=int(moved), transcendentals=0)


def intra(scalars, pieces, rims, narrow, taps, params, docs, heads):
    rows, width = pieces[0].shape
    chunks = rows // CHUNK
    tiles, flat = sds(chunks, heads, 128, 128), sds(rows, width)
    return pl.pallas_call(
        functools.partial(intra_kernel, docs, heads),
        out_shape=(tiles, tiles, tiles, flat, flat, flat, flat, tiles, tiles, sds(heads, 128, 256)),
        grid_spec=pltpu.PrefetchScalarGridSpec(
            num_scalar_prefetch=1,
            grid=(chunks // GROUP,),
            in_specs=[rows_spec(width, chunks, False, GROUP)] * 3
            + [halo_spec(width, chunks, False, GROUP)] * 3
            + [whole_spec(HALO, width)] * 3
            + [rows_spec(128, chunks, False, GROUP), whole_spec(16, width), whole_spec(8, 128)],
            out_specs=[tile_spec(heads, chunks, False, GROUP)] * 3
            + [rows_spec(width, chunks, False, GROUP)] * 4
            + [tile_spec(heads, chunks, False, GROUP)] * 2
            + [whole_spec(heads, 128, 256)],
            scratch_shapes=[pltpu.VMEM((heads, 128, 256), F32)],
        ),
        compiler_params=pltpu.CompilerParams(**PARAMS),
        cost_estimate=cost(chunks * heads * 60 * 3 * 2 * 128**3, 30 * rows * width * 4),
        name="intra",
    )(scalars, *pieces, *pieces, *rims, narrow, taps, params)


def outward_kernel(heads, s_in, w_ref, u_ref, qt_ref, ou_ref, t_ref, o_ref, gate_ref, gain_ref,
                   out_ref, v2_ref, s_ref, mixed_ref, run):
    step = pl.program_id(0)

    @pl.when(step == 0)
    def _():
        run[...] = s_in[...]

    hs = range(heads)
    state = [run[h] for h in hs]
    full = [
        mm(
            jnp.concatenate([qt_ref[:, lanes(h)], w_ref[:, lanes(h)], t_ref[0, h]], axis=0),
            state[h],
        )
        for h in hs
    ]
    for h in hs:
        out = full[h][:128] + ou_ref[:, lanes(h)]
        v2_ref[:, lanes(h)] = u_ref[:, lanes(h)] - full[h][128:256]
        s_ref[0, h] = state[h]
        run[h] = full[h][256:] + o_ref[0, h]
        out_ref[:, lanes(h)] = out
        gate = gate_ref[:, lanes(h)]
        scale = lax.rsqrt(jnp.mean(out * out, axis=-1, keepdims=True) + epsilon)
        mixed_ref[:, lanes(h)] = (
            out * scale * gain_ref[0:1, lanes(h)] * (gate * jax.nn.sigmoid(gate))
        ).astype(LOW)


def outward(s_in, w, u, qt, ou, t, o, gate, gain, heads):
    rows, width = w.shape
    chunks = rows // CHUNK
    flat, tiles = rows_spec(width, chunks), tile_spec(heads, chunks)
    return pl.pallas_call(
        functools.partial(outward_kernel, heads),
        out_shape=(sds(rows, width), sds(rows, width), sds(chunks, heads, 128, 128), sds(rows, width, dtype=LOW)),
        grid=(chunks,),
        in_specs=[whole_spec(heads, 128, 128), flat, flat, flat, flat, tiles, tiles, flat, whole_spec(8, width)],
        out_specs=[flat, flat, tiles, flat],
        scratch_shapes=[pltpu.VMEM((heads, 128, 128), F32)],
        compiler_params=pltpu.CompilerParams(**PARAMS),
        cost_estimate=cost(chunks * heads * 9 * 2 * 128**3, 11 * rows * width * 4),
        name="outward",
    )(s_in, w, u, qt, ou, t, o, gate, gain)


def inward_kernel(heads, scalars, gm_ref, out_ref, gate_ref, gain_ref, qt_ref, t_ref, maps_ref,
                  do_ref, dgate_ref, dgain_ref, tot_ref, run):
    step = pl.program_id(0)

    @pl.when(step == 0)
    def _():
        run[...] = jnp.zeros_like(run)
        dgain_ref[...] = jnp.zeros_like(dgain_ref)

    hs = range(heads)
    grads = []
    core = scalars[scalars.shape[0] - 1]
    for h in hs:
        out, gate = out_ref[:, lanes(h)], gate_ref[:, lanes(h)]
        other = (h + heads // 2) % heads
        gm = jnp.where(
            core == 0, gm_ref[:, lanes(h)].astype(F32), gm_ref[:, lanes(other)].astype(F32)
        )
        gain = gain_ref[0:1, lanes(h)]
        scale = lax.rsqrt(jnp.mean(out * out, axis=-1, keepdims=True) + epsilon)
        normed = out * scale
        sg = jax.nn.sigmoid(gate)
        act = gate * sg
        gn = gm * normed
        dgate_ref[:, lanes(h)] = (gn * gain * (sg * (1.0 + gate * (1.0 - sg)))).astype(LOW)
        dgain_ref[:, lanes(h)] += jnp.sum((gn * act).reshape(CHUNK // 8, 8, 128), axis=0)
        dn = gm * gain * act
        do = scale * (dn - normed * jnp.mean(dn * normed, axis=-1, keepdims=True))
        do_ref[:, lanes(h)] = do
        grads.append(do)
    for h in hs:
        left = jnp.concatenate([qt_ref[:, lanes(h)], t_ref[0, h]], axis=0)
        new = mm(left, jnp.concatenate([grads[h], run[h]], axis=0), TN)
        run[h] = new
        tot_ref[h] = jnp.concatenate([new, maps_ref[h, :, 128:]], axis=1)


def inward(scalars, gm, out, gate, gain, qt, t, maps, heads):
    rows, width = gm.shape
    chunks = rows // CHUNK
    flat, tiles = rows_spec(width, chunks, True), tile_spec(heads, chunks, True)
    return pl.pallas_call(
        functools.partial(inward_kernel, heads),
        out_shape=(sds(rows, width), sds(rows, width, dtype=LOW), sds(8, width), sds(heads, 128, 256)),
        grid_spec=pltpu.PrefetchScalarGridSpec(
            num_scalar_prefetch=1,
            grid=(chunks,),
            in_specs=[flat, flat, flat, whole_spec(8, width), flat, tiles, whole_spec(heads, 128, 256)],
            out_specs=[flat, flat, whole_spec(8, width), whole_spec(heads, 128, 256)],
            scratch_shapes=[pltpu.VMEM((heads, 128, 128), F32)],
        ),
        compiler_params=pltpu.CompilerParams(**PARAMS),
        cost_estimate=cost(chunks * heads * 6 * 2 * 128**3, 7 * rows * width * 4),
        name="inward",
    )(scalars, gm, out, gate, gain, qt, t, maps)


def back_kernel(docs, heads, steps, scalars, *refs):
    mains, priors, rims = refs[0:3], refs[3:6], refs[6:9]
    narrow_ref, taps_ref, params_ref, ds_in = refs[9:13]
    (do_ref, v2_ref, s_ref, x_ref, p_ref, kg_ref, w_ref, u_ref, qt_ref, t_ref) = refs[13:23]
    dgate_ref, grads_ref, tail_ref, rim_ref, gtaps_ref, gparams_ref = refs[23:29]
    run, after = refs[29:31]
    rev = pl.program_id(0)
    step = steps - 1 - rev
    position = scalars[0] + step * (CHUNK * GROUP)

    @pl.when(rev == 0)
    def _():
        run[...] = ds_in[...]
        after[...] = jnp.zeros_like(after)
        gtaps_ref[...] = jnp.zeros_like(gtaps_ref)
        gparams_ref[...] = jnp.zeros_like(gparams_ref)

    taps = taps_ref[...]
    inputs = chunk_inputs(
        step, position, mains, priors, rims, narrow_ref, taps, params_ref[...], scalars, docs, heads
    )
    lane, row = inputs[0][1]["col"], inputs[0][1]["row"]
    items = [(j, h) for j in reversed(range(GROUP)) for h in range(heads)]
    every = range(len(items))
    q, k, v, uq, uk, cq, ck, terms, b, rows, masks = [], [], [], [], [], [], [], [], [], [], []
    root = 1.0 / math.sqrt(128.0)
    for i, (j, h) in enumerate(items):
        rows_j, masks_j, feats, (_, _, _, beta, total, total_row) = inputs[j]
        conv = [pre[:, lanes(h)] * sg[:, lanes(h)] for _, pre, sg in feats]
        cq.append(conv[0])
        ck.append(conv[1])
        uq.append(unit(conv[0]))
        uk.append(unit(conv[1]))
        q.append(conv[0] * (uq[i] * root))
        k.append(conv[1] * uk[i])
        v.append(conv[2])
        terms.append(decay_terms(h, total, total_row, masks_j))
        b.append(beta[:, heads + h : heads + h + 1])
        rows.append(rows_j)
        masks.append(masks_j)
    do = [do_ref[rows[i], lanes(h)] for i, (j, h) in enumerate(items)]
    dsn = []
    for i, (j, h) in enumerate(items):
        dsn.append(run[h])
        left = jnp.concatenate([qt_ref[rows[i], lanes(h)], t_ref[j, h]], axis=0)
        run[h] = mm(left, jnp.concatenate([do[i], dsn[i]], axis=0), TN)
    v2 = [v2_ref[rows[i], lanes(h)] for i, (j, h) in enumerate(items)]
    kt = [terms[i][2] * k[i] for i in every]
    dv2 = [mm(p_ref[j, h], do[i], TN) + mm(kt[i], dsn[i]) for i, (j, h) in enumerate(items)]
    states = [s_ref[j, h] for j, h in items]
    both = [mm(jnp.concatenate([do[i], dv2[i]], axis=0), states[i], NT) for i in every]
    dp = [jnp.where(masks[i]["inside"], mm(do[i], v2[i], NT), 0.0) for i in every]
    dkt = [mm(v2[i], dsn[i], NT) for i in every]
    dx = [
        mm(x_ref[j, h], jnp.concatenate([-both[i][128:], dv2[i]], axis=1), TN)
        for i, (j, h) in enumerate(items)
    ]
    da = [
        jnp.where(
            masks[i]["strict"],
            -mm(
                dx[i],
                jnp.concatenate([w_ref[rows[i], lanes(h)], u_ref[rows[i], lanes(h)]], axis=1),
                NT,
            ),
            0.0,
        )
        for i, (j, h) in enumerate(items)
    ]
    zero = jnp.zeros((CHUNK, CHUNK), F32)
    gdecay, gbeta, minus = [zero] * GROUP, [zero] * GROUP, [zero] * GROUP
    dq, dk, dv = [], [], []
    for i, (j, h) in enumerate(items):
        spread, start, to_last, keep = terms[i]
        doq = both[i][:128]
        dqk = dp[i] * spread
        z = da[i] * kg_ref[j, h]
        dkk = b[i] * da[i] * spread
        dxk, dxv = dx[i][:, :128], dx[i][:, 128:]
        stacked = jnp.concatenate([dqk, dkk], axis=0)
        forward = mm(stacked, k[i])
        backward = mm(stacked, jnp.concatenate([q[i], k[i]], axis=0), TN)
        kx = jnp.sum(k[i] * dxk, axis=-1, keepdims=True)
        dq.append(start * doq + forward[:128])
        dk.append(backward + forward[128:] + to_last * dkt[i] + (b[i] * start) * dxk)
        dv.append(b[i] * dxv)
        gb = (
            jnp.sum(z, axis=-1, keepdims=True)
            + jnp.sum(v[i] * dxv, axis=-1, keepdims=True)
            + start * kx
        )
        gamgrad = b[i] * z + dp[i] * p_ref[j, h]
        dstart = jnp.sum(q[i] * doq, axis=-1, keepdims=True) + b[i] * kx
        dlast = jnp.sum(k[i] * dkt[i], axis=-1, keepdims=True) * to_last
        dkeep = jnp.sum(states[i] * dsn[i], keepdims=True) * keep
        gcol = jnp.sum(gamgrad, axis=-1, keepdims=True) + dstart * start - dlast
        end = jnp.sum(dlast, keepdims=True) + dkeep
        gcol = gcol + jnp.where(row[:, :1] == CHUNK - 1, end, 0.0)
        grow = jnp.sum(gamgrad, axis=0, keepdims=True)
        gdecay[j] = jnp.where(lane == h, gcol, gdecay[j])
        gbeta[j] = jnp.where(lane == heads + h, gb, gbeta[j])
        minus[j] = jnp.where(row == h, grow, minus[j])
    upper = jnp.where(row <= lane, 1.0, 0.0)
    width = mains[0].shape[1]
    grads_ref[:, 3 * width + 128 :] = dgate_ref[...]
    for j in reversed(range(GROUP)):
        rows_j, masks_j, feats, (shifted, rate, decays, beta, _, _) = inputs[j]
        dg = mm_full(upper, gdecay[j] - minus[j].T)
        galpha = dg * rate * jax.nn.sigmoid(shifted)
        grads_ref[rows_j, 3 * width : 3 * width + 128] = jnp.where(
            lane < heads, galpha, gbeta[j] * beta * (1.0 - beta)
        ).astype(LOW)
        gparams_ref[0:8, :] += jnp.sum((galpha).reshape(CHUNK // 8, 8, 128), axis=0)
        gparams_ref[8:16, :] += jnp.sum((dg * decays).reshape(CHUNK // 8, 8, 128), axis=0)
        for i in range(3):
            shift_rows, pre, sg = feats[i]
            pieces_d = []
            for h in range(heads):
                at = items.index((j, h))
                if i == 2:
                    pieces_d.append(dv[at])
                else:
                    inv = uq[at] if i == 0 else uk[at]
                    grad = dq[at] * root if i == 0 else dk[at]
                    normal = (cq[at] if i == 0 else ck[at]) * inv
                    pieces_d.append(
                        inv * (grad - normal * jnp.sum(grad * normal, axis=-1, keepdims=True))
                    )
            dc = jnp.concatenate(pieces_d, axis=1)
            ds = dc * (sg * (1.0 + pre * (1.0 - sg)))
            grad = ds * taps[4 * i + 3 : 4 * i + 4, :]
            rim = jnp.zeros((8, ds.shape[1]), F32)
            gtaps_ref[4 * i + 3] += jnp.sum((ds * shift_rows[0]).reshape(CHUNK // 8, 8, -1), axis=0)
            for s in range(1, 4):
                tap = taps[4 * i + 3 - s : 4 * i + 4 - s, :]
                masked = jnp.where(masks_j["back"][s], ds, 0.0)
                gtaps_ref[4 * i + 3 - s] += jnp.sum(
                    (ds * shift_rows[s]).reshape(CHUNK // 8, 8, -1), axis=0
                )
                ext = jnp.concatenate([masked, after[3 * i + s - 1]], axis=0)
                grad = grad + pltpu.roll(ext, CHUNK + 8 - s, 0)[:CHUNK] * tap
                after[3 * i + s - 1] = masked[:8]
                front = jnp.concatenate([jnp.zeros_like(masked[:8]), masked[:8]], axis=0)
                rim = rim + pltpu.roll(front, 16 - s, 0)[:8] * tap
            grads_ref[rows_j, i * width : (i + 1) * width] = grad.astype(LOW)
            if j == 0:
                rim_ref[:, i * width : (i + 1) * width] = rim
            if j == GROUP - 1:

                @pl.when(rev == 0)
                def _():
                    tail_ref[:, i * width : (i + 1) * width] = grad[CHUNK - HALO :]


def back(scalars, pieces, rims, narrow, taps, params, ds_in, do, v2, s, x, p, kg, w, u, qt, t, dgate, docs, heads):
    rows, width = pieces[0].shape
    chunks = rows // CHUNK
    flat, tiles = rows_spec(width, chunks, True, GROUP), tile_spec(heads, chunks, True, GROUP)
    return pl.pallas_call(
        functools.partial(back_kernel, docs, heads, chunks // GROUP),
        out_shape=(
            sds(rows, 4 * width + 128, dtype=LOW), sds(HALO, 3 * width), sds(8, 3 * width),
            sds(12, 8, width), sds(16, 128),
        ),
        grid_spec=pltpu.PrefetchScalarGridSpec(
            num_scalar_prefetch=1,
            grid=(chunks // GROUP,),
            in_specs=[flat] * 3
            + [halo_spec(width, chunks, True, GROUP)] * 3
            + [whole_spec(HALO, width)] * 3
            + [rows_spec(128, chunks, True, GROUP), whole_spec(16, width), whole_spec(8, 128)]
            + [whole_spec(heads, 128, 128), flat, flat, tiles, tiles, tiles, tiles, flat, flat, flat, tiles, flat],
            out_specs=[rows_spec(4 * width + 128, chunks, True, GROUP)]
            + [whole_spec(HALO, 3 * width), whole_spec(8, 3 * width)]
            + [whole_spec(12, 8, width), whole_spec(16, 128)],
            scratch_shapes=[pltpu.VMEM((heads, 128, 128), F32), pltpu.VMEM((9, 8, width), F32)],
        ),
        compiler_params=pltpu.CompilerParams(**PARAMS),
        cost_estimate=cost(chunks * heads * 60 * 2 * 128**3, 16 * rows * width * 4),
        name="back",
    )(scalars, *pieces, *pieces, *rims, narrow, taps, params, ds_in, do, v2, s, x, p, kg, w, u, qt, t, dgate)


def contract_rows(left, right):
    return lax.dot_general(left, right, TN, preferred_element_type=F32)


def contract_cols(left, right):
    return lax.dot_general(left, right, NT, preferred_element_type=F32)


def dot(left, right):
    return jnp.dot(left, right, preferred_element_type=F32)


def row_norm(values, gain):
    return values * lax.rsqrt(jnp.mean(values * values, axis=-1, keepdims=True) + epsilon) * gain


def norm_back(values, gain, grad):
    inv = lax.rsqrt(jnp.mean(values * values, axis=-1, keepdims=True) + epsilon)
    scaled = grad * gain
    inner = jnp.mean(scaled * values, axis=-1, keepdims=True)
    return inv * scaled - values * (inner * inv * inv * inv), jnp.sum(grad * values * inv, axis=0)


MESH = pl.DeviceIdType.MESH


def greet(axis, parts):
    me = lax.axis_index(axis)
    barrier = pltpu.get_barrier_semaphore()

    @pl.when(me > 0)
    def _():
        pl.semaphore_signal(barrier, inc=1, device_id={axis: me - 1}, device_id_type=MESH)

    @pl.when(me < parts - 1)
    def _():
        pl.semaphore_signal(barrier, inc=1, device_id={axis: me + 1}, device_id_type=MESH)

    inner = (me > 0) & (me < parts - 1)

    @pl.when(inner)
    def _():
        pl.semaphore_wait(barrier, 2)

    @pl.when(jnp.logical_not(inner))
    def _():
        pl.semaphore_wait(barrier, 1)


def line_gather(parts, buf, sems, first, use):
    me = lax.axis_index("tensor")
    send_right, send_left, from_left, from_right = sems

    def rightward(piece, step):
        return pltpu.make_async_remote_copy(
            src_ref=buf.at[piece],
            dst_ref=buf.at[piece],
            send_sem=send_right.at[step],
            recv_sem=from_left.at[step],
            device_id={"tensor": me + 1},
            device_id_type=MESH,
        )

    def leftward(piece, step):
        return pltpu.make_async_remote_copy(
            src_ref=buf.at[piece],
            dst_ref=buf.at[piece],
            send_sem=send_left.at[step],
            recv_sem=from_right.at[step],
            device_id={"tensor": me - 1},
            device_id_type=MESH,
        )

    def body(step, _):
        low, high = me - step, me + step

        @pl.when((step > 0) & (low >= 0))
        def _():
            rightward(low, step - 1).wait_recv()

        @pl.when((low >= 0) & (me < parts - 1))
        def _():
            rightward(low, step).start()

        @pl.when((step > 0) & (high < parts))
        def _():
            leftward(high, step - 1).wait_recv()

        @pl.when((high < parts) & (me > 0))
        def _():
            leftward(high, step).start()

        @pl.when(step == 0)
        def _():
            first()

        def visit(side, _):
            piece = me + step * (2 * side - 1)

            @pl.when((piece >= 0) & (piece < parts) & ((step > 0) | (side == 0)))
            def _():
                use(piece)

            return 0

        lax.fori_loop(0, 2, visit, 0)
        return 0

    lax.fori_loop(0, parts, body, 0)

    def finish(step, _):
        low, high = me - step, me + step

        @pl.when((low >= 0) & (me < parts - 1))
        def _():
            rightward(low, step).wait_send()

        @pl.when((high < parts) & (me > 0))
        def _():
            leftward(high, step).wait_send()

        return 0

    lax.fori_loop(0, parts, finish, 0)


def norm_into(buf, me, source, gain):
    rows = source.shape[0]

    def body(i, _):
        at = pl.ds(pl.multiple_of(i * 64, 64), 64)
        values = source[at, :].astype(F32)
        scale = lax.rsqrt(jnp.mean(values * values, axis=-1, keepdims=True) + epsilon)
        buf[me, at, :] = (values * scale * gain[0:1, :]).astype(LOW)
        return 0

    lax.fori_loop(0, rows // 64, body, 0)


def project_kernel(parts, tok_ref, gain_ref, narrow_w, *refs):
    weights_in, all_ref = refs[0:4], refs[4]
    q_ref, k_ref, v_ref, gate_ref, narrow_ref = refs[5:10]
    buf, weights = refs[10], refs[11:15]
    sems, load_sem, store_sem = refs[15:19], refs[19], refs[20]
    me = lax.axis_index("tensor")
    rows = tok_ref.shape[0]
    loads = [
        pltpu.make_async_copy(weights_in[i], weights[i], load_sem.at[i]) for i in range(4)
    ]
    for load in loads:
        load.start()
    norm_into(buf, me, tok_ref, gain_ref)
    greet("tensor", parts)

    def first():
        for load in loads:
            load.wait()

    def stored(piece):
        at = pl.ds(pl.multiple_of(piece * rows, rows), rows)
        return pltpu.make_async_copy(buf.at[piece], all_ref.at[at, :], store_sem.at[piece])

    def use(piece):
        at = pl.ds(pl.multiple_of(piece * rows, rows), rows)
        stored(piece).start()
        values = buf[piece]
        for w, out in zip(weights, (q_ref, k_ref, v_ref, gate_ref)):
            out[at, :] = dot(values, w[...]).astype(out.dtype)
        narrow_ref[at, :] = dot(values, narrow_w[...])

    line_gather(parts, buf, sems, first, use)
    for piece in range(parts):
        stored(piece).wait()


def vmem():
    return pl.BlockSpec(memory_space=pltpu.VMEM)


def hbm():
    return pl.BlockSpec(memory_space=pl.ANY)


def line_sems(parts):
    return [pltpu.SemaphoreType.DMA((parts,))] * 4


def comm_params(number):
    return pltpu.CompilerParams(
        collective_id=number, has_side_effects=True, vmem_limit_bytes=60 * 1024 * 1024
    )


def project(parts, tokens, gain, narrow_w, weights):
    rows, model = tokens.shape
    width = weights[0].shape[1]
    total = rows * parts
    low = sds(total, width, dtype=LOW)
    return pl.pallas_call(
        functools.partial(project_kernel, parts),
        out_shape=(sds(total, model, dtype=LOW), low, low, low, sds(total, width), sds(total, 128)),
        in_specs=[vmem()] * 3 + [hbm()] * 4,
        out_specs=[hbm()] + [vmem()] * 5,
        scratch_shapes=[pltpu.VMEM((parts, rows, model), LOW)]
        + [pltpu.VMEM((model, width), LOW)] * 4
        + line_sems(parts)
        + [pltpu.SemaphoreType.DMA((4,)), pltpu.SemaphoreType.DMA((parts,))],
        compiler_params=comm_params(1),
        cost_estimate=cost(2 * total * model * (4 * width + 128), 60 * 2**20),
        name="project",
    )(tokens, gain, narrow_w, *weights)


SUBS = 2
FEED_SUBS = 4


def feed_kernel(parts, res_ref, gain_ref, *refs):
    weights_in, og_in = refs[0:3], refs[3]
    mlp_ref, out_ref, grads_ref = refs[4:7]
    buf, weights, og, sent, got = refs[7], refs[8:11], refs[11], refs[12], refs[13]
    sems, load_sem = refs[14:18], refs[18]
    sem_sr, sem_sl, sem_gl, sem_gr = refs[19:23]
    act_ref, gu_ref, stage, stage_sem = refs[23:27]
    me = lax.axis_index("tensor")
    rows, model = res_ref.shape
    size = rows // FEED_SUBS
    units = weights_in[0].shape[1]
    loads = [
        pltpu.make_async_copy(src, dst, load_sem.at[i])
        for i, (src, dst) in enumerate(zip(weights_in + (og_in,), weights + (og,)))
    ]
    for load in loads:
        load.start()
    norm_into(buf, me, res_ref, gain_ref)
    greet("tensor", parts)
    wg, wu, wd = weights

    def first():
        for load in loads:
            load.wait()

    def rightward(piece, sub):
        slot = piece * FEED_SUBS + sub
        return pltpu.make_async_remote_copy(
            src_ref=sent.at[slot],
            dst_ref=got.at[slot],
            send_sem=sem_sr.at[slot],
            recv_sem=sem_gl.at[slot],
            device_id={"tensor": me + 1},
            device_id_type=MESH,
        )

    def leftward(piece, sub, to):
        slot = piece * FEED_SUBS + sub
        landing = jnp.where(piece == to, parts * FEED_SUBS + sub, slot)
        return pltpu.make_async_remote_copy(
            src_ref=sent.at[slot],
            dst_ref=got.at[landing],
            send_sem=sem_sl.at[slot],
            recv_sem=sem_gr.at[slot],
            device_id={"tensor": me - 1},
            device_id_type=MESH,
        )

    def tile(at, piece, column, wide):
        cols = pl.ds(pl.multiple_of(column, 128), wide)
        values = buf[piece]
        gate = dot(values, wg[:, cols])
        up = dot(values, wu[:, cols])
        grad = contract_cols(og[at, :], wd[cols, :])
        sg = jax.nn.sigmoid(gate)
        act = gate * sg
        act_ref[at, cols] = (act * up).astype(LOW)
        gu_ref[at, cols] = (grad * up * sg * (1.0 + gate * (1.0 - sg))).astype(LOW)
        gu_ref[at, pl.ds(pl.multiple_of(units + column, 128), wide)] = (grad * act).astype(LOW)

    def use(piece):
        at = pl.ds(pl.multiple_of(piece * rows, rows), rows)

        def body(i, _):
            tile(at, piece, i * 256, 256)
            return 0

        lax.fori_loop(0, units // 256, body, 0)
        if units % 256:
            tile(at, piece, units - units % 256, units % 256)

        def product(j, _):
            cols = pl.ds(pl.multiple_of(j * 256, 256), 256)
            total = contract_cols(gu_ref[at, :units], wg[cols, :])
            total = total + contract_cols(gu_ref[at, units:], wu[cols, :])

            @pl.when(piece == me)
            def _():
                out_ref[:, cols] = total

            @pl.when(piece != me)
            def _():
                for sub in range(FEED_SUBS):
                    sent[piece * FEED_SUBS + sub, :, cols] = total[sub * size : sub * size + size].astype(LOW)

            return 0

        lax.fori_loop(0, model // 256, product, 0)

        @pl.when((piece > me) & (me == 0))
        def _():
            for sub in range(FEED_SUBS):
                rightward(piece, sub).start()

        @pl.when((piece < me) & (me == parts - 1))
        def _():
            for sub in range(FEED_SUBS):
                leftward(piece, sub, me - 1).start()

    line_gather(parts, buf, sems, first, use)

    def down(item, _):
        piece, i = item // (model // 256), item % (model // 256)
        at = pl.ds(pl.multiple_of(piece * rows, rows), rows)
        cols = pl.ds(pl.multiple_of(i * 256, 256), 256)
        mlp_ref[at, cols] = dot(act_ref[at, :], wd[:, cols]).astype(LOW)
        return 0

    lax.fori_loop(0, parts * (model // 256), down, 0)
    talls = model // 256
    tiles = 3 * talls

    def staged(tile):
        at = pl.ds(pl.multiple_of((tile % talls) * 256, 256), 256)
        cols = pl.ds(pl.multiple_of((tile // talls) * units, 128), units)
        return pltpu.make_async_copy(
            stage.at[tile % 2], grads_ref.at[at, cols], stage_sem.at[tile % 2]
        )

    def grad_tile(tile):
        column = tile // talls
        over = pl.ds(pl.multiple_of((tile % talls) * 256, 256), 256)

        @pl.when(tile >= 2)
        def _():
            staged(tile - 2).wait()

        def summed(left, right):
            total = None
            for p in range(parts):
                term = contract_rows(left(p), right(slice(p * rows, p * rows + rows)))
                total = term if total is None else total + term
            stage[tile % 2] = total.astype(LOW)

        @pl.when(column < 2)
        def _():
            cols = pl.ds(pl.multiple_of(column * units, 128), units)
            summed(lambda p: buf[p, :, over], lambda at: gu_ref[at, cols])

        @pl.when(column == 2)
        def _():
            summed(lambda p: og[p * rows : p * rows + rows, over], lambda at: act_ref[at, :])

        staged(tile).start()

    turns = 2 * (parts - 1) * FEED_SUBS
    per_turn = -(-tiles // turns)
    right_first = 2 * me < parts

    def pass_on(item, _):
        turn = item // ((parts - 1) * FEED_SUBS)
        rest = item % ((parts - 1) * FEED_SUBS)
        step, sub = 1 + rest // FEED_SUBS, rest % FEED_SUBS
        right = (turn == 0) == right_first
        going_right = right & (me + step < parts) & (me > 0)
        going_left = jnp.logical_not(right) & (me - step >= 0) & (me < parts - 1)

        @pl.when(going_right)
        def _():
            piece = me + step
            slot = piece * FEED_SUBS + sub
            rightward(piece, sub).wait_recv()
            sent[slot] = (sent[slot].astype(F32) + got[slot].astype(F32)).astype(LOW)
            rightward(piece, sub).start()

        @pl.when(going_left)
        def _():
            piece = me - step
            slot = piece * FEED_SUBS + sub
            leftward(piece, sub, me).wait_recv()
            sent[slot] = (sent[slot].astype(F32) + got[slot].astype(F32)).astype(LOW)
            leftward(piece, sub, me - 1).start()

        for i in range(per_turn):
            tile = item * per_turn + i
            if per_turn * turns == tiles:
                grad_tile(tile)
            else:
                pl.when(tile < tiles)(functools.partial(grad_tile, tile))
        return 0

    lax.fori_loop(0, turns, pass_on, 0)
    for sub in range(FEED_SUBS):
        at = slice(sub * size, sub * size + size)

        @pl.when(me > 0)
        def _():
            rightward(me, sub).wait_recv()
            out_ref[at, :] = out_ref[at, :] + got[me * FEED_SUBS + sub].astype(F32)

        @pl.when(me < parts - 1)
        def _():
            leftward(me, sub, me).wait_recv()
            out_ref[at, :] = out_ref[at, :] + got[parts * FEED_SUBS + sub].astype(F32)

    def finish(slot, _):
        piece, sub = slot // FEED_SUBS, slot % FEED_SUBS

        @pl.when(piece > me)
        def _():
            rightward(piece, sub).wait_send()

        @pl.when(piece < me)
        def _():
            leftward(piece, sub, me - 1).wait_send()

        return 0

    lax.fori_loop(0, parts * FEED_SUBS, finish, 0)
    for slot in range(2):
        staged(tiles - 2 + slot).wait()


def feed(parts, residual, gain, weights, out_grad):
    rows, model = residual.shape
    units = weights[0].shape[1]
    total = rows * parts
    low = sds(total, model, dtype=LOW)
    return pl.pallas_call(
        functools.partial(feed_kernel, parts),
        out_shape=(low, sds(rows, model), sds(model, 3 * units, dtype=LOW)),
        in_specs=[vmem()] * 2 + [hbm()] * 4,
        out_specs=[vmem()] * 2 + [hbm()],
        scratch_shapes=[pltpu.VMEM((parts, rows, model), LOW)]
        + [pltpu.VMEM(w.shape, LOW) for w in weights]
        + [pltpu.VMEM((total, model), LOW)]
        + [pltpu.VMEM((parts * FEED_SUBS, rows // FEED_SUBS, model), LOW)]
        + [pltpu.VMEM((parts * FEED_SUBS + FEED_SUBS, rows // FEED_SUBS, model), LOW)]
        + line_sems(parts)
        + [pltpu.SemaphoreType.DMA((4,))]
        + line_sems(parts * FEED_SUBS)
        + [
            pltpu.VMEM((total, units), LOW),
            pltpu.VMEM((total, 2 * units), LOW),
            pltpu.VMEM((2, 256, units), LOW),
            pltpu.SemaphoreType.DMA((2,)),
        ],
        compiler_params=comm_params(2),
        cost_estimate=cost(18 * total * model * units, 120 * 2**20),
        name="feed",
    )(residual, gain, *weights, out_grad)


class Plain:
    inputs, outputs = 0, 1

    def __init__(self, parts):
        self.parts = parts

    def begin(self, given, scratch):
        greet("tensor", self.parts)

    def end(self, given, out, scratch):
        pass

    def shapes(self, rows, model):
        return (sds(rows, model),)

    def scratch(self, rows, model):
        return []


def each(total, me, action):
    def body(k, _):
        action(lax.rem(me + k, total))
        return 0

    lax.fori_loop(1, total, body, 0)


class Exchange:
    def __init__(self, axis, total, buf, send_sem, got_sem):
        self.axis, self.total = axis, total
        self.buf, self.send_sem, self.got_sem = buf, send_sem, got_sem

    def copy(self, source, target):
        return pltpu.make_async_remote_copy(
            src_ref=self.buf.at[source],
            dst_ref=self.buf.at[source],
            send_sem=self.send_sem.at[target],
            recv_sem=self.got_sem.at[source],
            device_id={self.axis: target},
            device_id_type=MESH,
        )

    def send(self):
        me = lax.axis_index(self.axis)
        each(self.total, me, lambda other: self.copy(me, other).start())

    def receive(self):
        me = lax.axis_index(self.axis)
        each(self.total, me, lambda other: self.copy(other, me).wait_recv())

    def drain(self):
        me = lax.axis_index(self.axis)
        each(self.total, me, lambda other: self.copy(me, other).wait_send())

    def sum(self, at=slice(None)):
        total = self.buf[0, at]
        for i in range(1, self.total):
            total = total + self.buf[i, at]
        return total


class Closing:
    inputs, outputs = 4, 4

    def __init__(self, count, parts, kept, flat):
        self.count, self.parts, self.kept, self.flat = count, parts, kept, flat

    def stages(self, scratch):
        return (
            Exchange("dp", self.count, *scratch[0:3]),
            Exchange("tensor", self.parts, *scratch[3:6]),
            Exchange("dp", self.count, *scratch[6:9]),
            Exchange("tensor", self.parts, *scratch[9:12]),
        )

    def begin(self, given, scratch):
        dp, z = lax.axis_index("dp"), lax.axis_index("tensor")
        barrier = pltpu.get_barrier_semaphore()

        def hello(axis):
            def one(other):
                pl.semaphore_signal(
                    barrier, inc=1, device_id={axis: other}, device_id_type=MESH
                )

            return one

        each(self.count, dp, hello("dp"))
        each(self.parts, z, hello("tensor"))
        first = self.stages(scratch)[0]
        first.buf[dp] = given[3][...]
        pl.semaphore_wait(barrier, self.count + self.parts - 2)
        first.send()

    def end(self, given, out, scratch):
        tok_ref, gain_ref, res_ref, flat_ref = given
        out_ref, wide_ref, rest_ref, gain_out = out
        dp, z = lax.axis_index("dp"), lax.axis_index("tensor")
        flat_dp, flat_z, gain_dp, gain_z = self.stages(scratch)
        sums = scratch[12]
        rows, model = out_ref.shape
        flat_dp.receive()
        flat_z.buf[z] = flat_dp.sum()
        flat_z.send()
        sums[...] = jnp.zeros_like(sums)

        def body(i, _):
            at = pl.ds(pl.multiple_of(i * 32, 32), 32)
            values, grad = tok_ref[at, :].astype(F32), out_ref[at, :]
            inv = lax.rsqrt(jnp.mean(values * values, axis=-1, keepdims=True) + epsilon)
            scaled = grad * gain_ref[0:1, :]
            inner = jnp.mean(scaled * values, axis=-1, keepdims=True)
            out_ref[at, :] = (
                res_ref[at, :] + inv * scaled - values * (inner * inv * inv * inv)
            )
            sums[...] += jnp.sum((grad * values * inv).reshape(4, 8, model), axis=0)
            return 0

        lax.fori_loop(0, rows // 32, body, 0)
        total = jnp.sum(sums[...], axis=0, keepdims=True)
        wide = model // 8
        gain_dp.buf[dp] = jnp.concatenate(
            [total[:, i * wide : (i + 1) * wide] for i in range(8)], axis=0
        )
        gain_dp.send()
        flat_z.receive()
        width = flat_ref.shape[1]
        for i in range(self.parts):
            wide_ref[:, i * width : (i + 1) * width] = flat_z.buf[i, : self.kept, :]
        rest_ref[...] = flat_z.sum(slice(self.kept, None))
        gain_dp.receive()
        gain_z.buf[z] = gain_dp.sum()
        gain_z.send()
        gain_z.receive()
        gain_out[...] = gain_z.sum()
        for stage in (flat_dp, flat_z, gain_dp, gain_z):
            stage.drain()

    def shapes(self, rows, model):
        height, width = self.flat
        return (
            sds(rows, model), sds(self.kept, width * self.parts), sds(height - self.kept, width),
            sds(8, model // 8),
        )

    def scratch(self, rows, model):
        out = []
        for shape in (self.flat, (8, model // 8)):
            for total in (self.count, self.parts):
                out.append(pltpu.VMEM((total,) + shape, F32))
                out.extend([pltpu.SemaphoreType.DMA((total,))] * 2)
        return out + [pltpu.VMEM((8, model), F32)]


def scatter_kernel(parts, given, count, splits, ending, *refs):
    lefts, rights_in = refs[0:given], refs[given : given + count]
    refs = refs[given + count :]
    extra_in, refs = refs[: ending.inputs], refs[ending.inputs :]
    extra_out, refs = refs[: ending.outputs], refs[ending.outputs :]
    rights, (part, send_r, send_l, got_l, got_r) = refs[0:count], refs[count : count + 5]
    sem_sr, sem_sl, sem_gl, sem_gr, load_sem = refs[count + 5 : count + 10]
    extra = refs[count + 10 :]
    out_ref = extra_out[0]
    me = lax.axis_index("tensor")
    rows, model = out_ref.shape
    size = rows // SUBS
    loads = [
        pltpu.make_async_copy(rights_in[i], rights[i], load_sem.at[i]) for i in range(count)
    ]
    for load in loads:
        load.start()
    ending.begin(extra_in, extra)
    for load in loads:
        load.wait()

    def rightward(slot):
        return pltpu.make_async_remote_copy(
            src_ref=send_r.at[slot],
            dst_ref=got_l.at[slot],
            send_sem=sem_sr.at[slot],
            recv_sem=sem_gl.at[slot],
            device_id={"tensor": me + 1},
            device_id_type=MESH,
        )

    def leftward(slot):
        return pltpu.make_async_remote_copy(
            src_ref=send_l.at[slot],
            dst_ref=got_r.at[slot],
            send_sem=sem_sl.at[slot],
            recv_sem=sem_gr.at[slot],
            device_id={"tensor": me - 1},
            device_id_type=MESH,
        )

    def product(start, many, target):
        at = pl.ds(pl.multiple_of(start, 128), many)

        def body(j, _):
            cols = pl.ds(pl.multiple_of(j * 256, 256), 256)
            total = None
            for i, (index, first, wide) in enumerate(splits):
                term = contract_cols(lefts[index][at, first : first + wide], rights[i][cols, :])
                total = term if total is None else total + term
            target[:, cols] = total
            return 0

        lax.fori_loop(0, model // 256, body, 0)

    half = part.at[pl.ds(0, size), :]

    right_first = 2 * me < parts

    def body(item, _):
        step, sub = item // (2 * SUBS), (item // 2) % SUBS
        right = (item % 2 == 0) == right_first
        piece = jnp.where(right, parts - 1 - step, step)
        slot = piece * SUBS + sub
        go_right = right & (piece > me)
        go_left = jnp.logical_not(right) & (piece < me)

        @pl.when(go_right | go_left)
        def _():
            product(piece * rows + sub * size, size, half)

        @pl.when(go_right)
        def _():
            @pl.when(me > 0)
            def _():
                rightward(slot).wait_recv()
                send_r[slot] = (half[...] + got_l[slot].astype(F32)).astype(LOW)

            @pl.when(me == 0)
            def _():
                send_r[slot] = half[...].astype(LOW)

            rightward(slot).start()

        @pl.when(go_left)
        def _():
            @pl.when(me < parts - 1)
            def _():
                leftward(slot).wait_recv()
                send_l[slot] = (half[...] + got_r[slot].astype(F32)).astype(LOW)

            @pl.when(me == parts - 1)
            def _():
                send_l[slot] = half[...].astype(LOW)

            leftward(slot).start()

        return 0

    lax.fori_loop(0, (parts - 1) * SUBS * 2, body, 0)
    product(me * rows, rows, part)
    for sub in range(SUBS):
        at = slice(sub * size, sub * size + size)
        slot = me * SUBS + sub
        out_ref[at, :] = part[at, :]

        @pl.when(me > 0)
        def _():
            rightward(slot).wait_recv()
            out_ref[at, :] = out_ref[at, :] + got_l[slot].astype(F32)

        @pl.when(me < parts - 1)
        def _():
            leftward(slot).wait_recv()
            out_ref[at, :] = out_ref[at, :] + got_r[slot].astype(F32)

    ending.end(extra_in, extra_out, extra)

    def finish(slot, _):
        piece = slot // SUBS

        @pl.when(piece > me)
        def _():
            rightward(slot).wait_send()

        @pl.when(piece < me)
        def _():
            leftward(slot).wait_send()

        return 0

    lax.fori_loop(0, parts * SUBS, finish, 0)


def scatter(parts, lefts, rights, splits, number, ending=None, extra=()):
    total = lefts[0].shape[0]
    model = rights[0].shape[0]
    rows = total // parts
    count = len(rights)
    ending = ending or Plain(parts)
    slots = pltpu.VMEM((parts * SUBS, rows // SUBS, model), LOW)
    shapes = ending.shapes(rows, model)
    return pl.pallas_call(
        functools.partial(scatter_kernel, parts, len(lefts), count, splits, ending),
        out_shape=shapes,
        in_specs=[vmem()] * len(lefts) + [hbm()] * count + [vmem()] * len(extra),
        out_specs=[vmem()] * len(shapes),
        scratch_shapes=[pltpu.VMEM(w.shape, LOW) for w in rights]
        + [pltpu.VMEM((rows, model), F32)]
        + [slots] * 4
        + line_sems(parts * SUBS)
        + [pltpu.SemaphoreType.DMA((count,))]
        + ending.scratch(rows, model),
        compiler_params=comm_params(number),
        cost_estimate=cost(2 * total * model * sum(w.shape[1] for w in rights), 60 * 2**20),
        name="scatter%d" % number,
    )(*lefts, *rights, *extra)


def state_kernel(count, heads, backward, own_ref, out_ref, buf, send_sem, pass_sem, got_sem):
    me = lax.axis_index("dp")
    core = lax.rem(me, 2)
    sibling = me + 1 - 2 * core
    half = count // 2
    barrier = pltpu.get_barrier_semaphore()

    def peer(k):
        return lax.rem(me + 2 * k, count)

    def hello(k, _):
        pl.semaphore_signal(barrier, inc=1, device_id={"dp": peer(k)}, device_id_type=MESH)
        return 0

    lax.fori_loop(1, half, hello, 0)
    pl.semaphore_signal(barrier, inc=1, device_id={"dp": sibling}, device_id_type=MESH)
    buf[me] = own_ref[...].astype(LOW)
    pl.semaphore_wait(barrier, half)

    def needed(source, target):
        return source > target if backward else source < target

    def copy(piece, target, sem):
        return pltpu.make_async_remote_copy(
            src_ref=buf.at[piece],
            dst_ref=buf.at[piece],
            send_sem=sem,
            recv_sem=got_sem.at[piece],
            device_id={"dp": target},
            device_id_type=MESH,
        )

    def send(k, _):
        target = peer(k)

        @pl.when(needed(me, target))
        def _():
            copy(me, target, send_sem.at[target]).start()

        return 0

    @pl.when(needed(me, sibling))
    def _():
        copy(me, sibling, pass_sem.at[me]).start()

    lax.fori_loop(1, half, send, 0)

    def relay(k, _):
        source = lax.rem(me + count - 2 * k, count)

        @pl.when(needed(source, me))
        def _():
            copy(source, me, send_sem.at[source]).wait_recv()

        @pl.when(needed(source, me) & needed(source, sibling))
        def _():
            copy(source, sibling, pass_sem.at[source]).start()

        return 0

    lax.fori_loop(1, half, relay, 0)
    for h in range(heads):
        out_ref[h] = jnp.zeros_like(out_ref[h])

    def chain(step, _):
        piece = count - 1 - step if backward else step

        @pl.when(needed(piece, me) & (lax.rem(piece, 2) != core))
        def _():
            copy(piece, me, pass_sem.at[piece]).wait_recv()

        @pl.when(needed(piece, me))
        def _():
            for h in range(heads):
                both = buf[piece, h].astype(F32)
                if backward:
                    out_ref[h] = mm(both[:, 128:], out_ref[h], TN) + both[:, :128]
                else:
                    out_ref[h] = mm(both[:, 128:], out_ref[h]) + both[:, :128]

        return 0

    lax.fori_loop(0, count, chain, 0)

    def finish(k, _):
        target = peer(k)
        source = lax.rem(me + count - 2 * k, count)

        @pl.when(needed(me, target))
        def _():
            copy(me, target, send_sem.at[target]).wait_send()

        @pl.when(needed(source, me) & needed(source, sibling))
        def _():
            copy(source, sibling, pass_sem.at[source]).wait_send()

        return 0

    lax.fori_loop(1, half, finish, 0)

    @pl.when(needed(me, sibling))
    def _():
        copy(me, sibling, pass_sem.at[me]).wait_send()


def exchange(count, own, heads, backward, number):
    return pl.pallas_call(
        functools.partial(state_kernel, count, heads, backward),
        out_shape=sds(heads, 128, 128),
        in_specs=[vmem()],
        out_specs=vmem(),
        scratch_shapes=[pltpu.VMEM((count, heads, 128, 256), LOW)]
        + [pltpu.SemaphoreType.DMA((count,))] * 3,
        compiler_params=comm_params(number),
        cost_estimate=cost(count * heads * 6 * 128**3, count * heads * 256 * 128 * 4),
        name="exchange%d" % number,
    )(own)


def after(values, *first):
    out = lax.optimization_barrier((values,) + first)
    return out[0]


def local(
    tokens,
    gain_in,
    w_query,
    w_key,
    w_value,
    w_alpha,
    w_beta,
    w_gate_out,
    conv_query,
    conv_key,
    conv_value,
    decay_log,
    decay_bias,
    head_gain,
    w_out,
    gain_mid,
    w_gate,
    w_up,
    w_down,
    out_grad,
    doc_lengths,
):
    rows_own, model = tokens.shape
    tensor_parts, dp_parts = lax.axis_size("tensor"), lax.axis_size("dp")
    tensor_index, dp_index = lax.axis_index("tensor"), lax.axis_index("dp")
    group_rows = rows_own * tensor_parts
    seq_total = group_rows * dp_parts
    heads = w_alpha.shape[1]
    width = w_query.shape[1]
    core = lax.rem(dp_index, 2)
    docs = doc_lengths.shape[0] * doc_lengths.shape[1]
    starts = (
        jnp.cumsum(doc_lengths, axis=1)
        - doc_lengths
        + seq_total * lax.broadcasted_iota(jnp.int32, doc_lengths.shape, 0)
    ).reshape(-1)
    scalars = jnp.concatenate([(dp_index * group_rows).reshape(1), starts, core.reshape(1)]).astype(jnp.int32)
    taps = jnp.concatenate([conv_query, conv_key, conv_value, jnp.zeros((4, width), F32)])
    params = jnp.zeros((8, 128), F32).at[0, :heads].set(decay_bias).at[1, :heads].set(decay_log)
    gain_heads = jnp.broadcast_to(head_gain[None], (8, width))
    w_narrow = jnp.pad(jnp.concatenate([w_alpha, w_beta], axis=1), ((0, 0), (0, 128 - 2 * heads)))

    own_rows = tokens.astype(F32)
    gain_in_rows = jnp.broadcast_to(gain_in[None], (8, model))
    gain_mid_rows = jnp.broadcast_to(gain_mid[None], (8, model))
    normed_all, *pieces, gate_raw, narrow = project(
        tensor_parts, tokens, gain_in_rows, w_narrow, (w_query, w_key, w_value, w_gate_out)
    )
    half = width // 2
    out_half = lax.dynamic_slice_in_dim(after(w_out, narrow), core * half, half, 0)
    out_mine = lax.all_gather(out_half, "tensor", axis=0)
    forth = [(i, i + 1) for i in range(dp_parts - 1)]
    rims = lax.ppermute(
        jnp.stack([piece[group_rows - HALO :] for piece in pieces]), "dp", forth
    )
    rims = [rims[i] for i in range(3)]
    x, p, kg, w, u, qt, ou, t, o, totals = intra(
        scalars, pieces, rims, narrow, taps, params, docs, heads
    )
    state_in = exchange(dp_parts, totals, heads, False, 3)
    rows_out, v2, s, mixed = outward(state_in, w, u, qt, ou, t, o, gate_raw, gain_heads, heads)

    mixed_own = lax.all_to_all(mixed, "tensor", split_axis=0, concat_axis=1, tiled=True)
    out_mine, _ = lax.optimization_barrier((out_mine, mixed))
    out_other = lax.ppermute(out_mine, "dp", [(i, i ^ 1) for i in range(dp_parts)])
    out_mine = out_mine.reshape(tensor_parts * half, model)
    out_other = out_other.reshape(tensor_parts * half, model)
    split = mixed_own.reshape(rows_own, tensor_parts, 2, half)

    def of_core(index):
        return lax.dynamic_index_in_dim(split, index, 2, keepdims=False).reshape(rows_own, -1)

    residual = own_rows + (dot(of_core(core), out_mine) + dot(of_core(1 - core), out_other))
    mlp_part, grad_mid, units_grad = feed(
        tensor_parts, residual, gain_mid_rows, (w_gate, w_up, w_down), out_grad
    )
    units = w_gate.shape[1]
    ring = [(i, (i + 1) % tensor_parts) for i in range(tensor_parts)]

    def piece_of(values, back_by):
        index = lax.rem(tensor_index - back_by + tensor_parts, tensor_parts)
        return lax.dynamic_slice_in_dim(values, index * rows_own, rows_own, 0)

    def added(values, back_by, got):
        return (piece_of(values, back_by).astype(F32) + got.astype(F32)).astype(LOW)

    units_grad_sum = lax.psum_scatter(units_grad, "dp", scatter_dimension=0, tiled=True)
    grad_res_norm, gain_mid_grad = norm_back(residual, gain_mid, grad_mid)
    grad_own = lax.dynamic_slice_in_dim(out_grad, tensor_index * rows_own, rows_own, 0)
    grad_residual = grad_own.astype(F32) + grad_res_norm
    grad_mixer = grad_residual.astype(LOW)
    grad_mixed = jnp.concatenate(
        [contract_cols(grad_mixer, weight).astype(LOW) for weight in (out_mine, out_other)], axis=1
    ).reshape(rows_own, 2, tensor_parts, half)
    grad_mixed = lax.all_to_all(
        grad_mixed, "tensor", split_axis=2, concat_axis=0, tiled=True
    ).reshape(group_rows, width)
    mlp_run = lax.ppermute(piece_of(after(mlp_part, grad_mixed), 1), "tensor", ring)
    out_w = contract_rows(after(grad_mixer, grad_mixed), mixed_own).astype(LOW)
    out_w_sum = lax.psum_scatter(out_w, "dp", scatter_dimension=0, tiled=True)
    do, gate_low, head_gain_part, ds_total = inward(
        scalars, grad_mixed, rows_out, gate_raw, gain_heads, qt, t, totals, heads
    )
    grad_end = exchange(dp_parts, ds_total, heads, True, 5)
    grad_end, mlp_run = lax.optimization_barrier((grad_end, mlp_run))
    for back_by in range(2, tensor_parts - 1):
        mlp_run = lax.ppermute(added(mlp_part, back_by, mlp_run), "tensor", ring)
    grads, tails, rim_grad, taps_grad, params_grad = back(
        scalars, pieces, rims, narrow, taps, params, grad_end, do, v2, s, x, p, kg, w, u, qt, t,
        gate_low, docs, heads,
    )
    grads, tails, rim_grad, taps_grad, params_grad, mlp_run, units_grad_sum = (
        lax.optimization_barrier(
            (grads, tails, rim_grad, taps_grad, params_grad, mlp_run, units_grad_sum)
        )
    )
    mlp_run = lax.ppermute(added(mlp_part, tensor_parts - 1, mlp_run), "tensor", ring)
    rim_back = lax.ppermute(rim_grad, "dp", [(i + 1, i) for i in range(dp_parts - 1)])
    tails = tails.at[HALO - 8 :].add(rim_back).astype(LOW)
    grads = lax.dynamic_update_slice(grads, tails, (group_rows - HALO, 0))
    mixer_grad = contract_rows(normed_all, grads).astype(LOW)
    mixer_grad, mlp_run = lax.optimization_barrier((mixer_grad, mlp_run))
    mixer_sum = lax.psum_scatter(mixer_grad, "dp", scatter_dimension=0, tiled=True).astype(F32)
    params_grad = params_grad.reshape(2, 8, 128).sum(1)
    flat = jnp.concatenate(
        [
            taps_grad.sum(1),
            head_gain_part.sum(0)[None],
            jnp.pad(params_grad, ((0, 1), (0, width - 128))),
            jnp.pad(gain_mid_grad.reshape(-1, width), ((0, 4), (0, 0))),
        ],
        axis=0,
    )
    input_grad, wide, rest, gain_in_grad = scatter(
        tensor_parts, [after(grads, mixer_grad)],
        [w_query, w_key, w_value, w_narrow, w_gate_out],
        ((0, 0, width), (0, width, width), (0, 2 * width, width), (0, 3 * width, 128), (0, 3 * width + 128, width)),
        6, Closing(dp_parts, tensor_parts, 16, flat.shape),
        (tokens, gain_in_rows, grad_residual, flat),
    )
    out_w_sum, mlp_run, _ = lax.optimization_barrier((out_w_sum, mlp_run, gain_in_grad))
    output = (residual + (piece_of(mlp_part, 0).astype(F32) + mlp_run.astype(F32))).astype(LOW)
    def out_piece(ahead):
        index = lax.rem(tensor_index + ahead, tensor_parts)
        return lax.dynamic_slice_in_dim(out_w_dp, index * width, width, 1)

    out_w_dp = out_w_sum
    out_w_sum = out_piece(0).astype(F32)
    for ahead in range(1, tensor_parts):
        shift = [(i, (i + ahead) % tensor_parts) for i in range(tensor_parts)]
        out_w_sum = out_w_sum + lax.ppermute(out_piece(ahead), "tensor", shift).astype(F32)
    by_head = wide[13:15].reshape(2, tensor_parts, width)[:, :, :heads].reshape(2, -1)
    start = 3 * width
    return (
        output,
        input_grad,
        gain_in_grad.reshape(model),
        mixer_sum[:, :width],
        mixer_sum[:, width : 2 * width],
        mixer_sum[:, 2 * width : start],
        mixer_sum[:, start : start + heads],
        mixer_sum[:, start + heads : start + 2 * heads],
        mixer_sum[:, start + 128 :],
        wide[0:4],
        wide[4:8],
        wide[8:12],
        by_head[1],
        by_head[0],
        wide[12],
        out_w_sum.T,
        rest[: model // width].reshape(model),
        units_grad_sum[:, :units].astype(F32),
        units_grad_sum[:, units : 2 * units].astype(F32),
        units_grad_sum[:, 2 * units :].T.astype(F32),
    )


def solution(mesh):
    placed = (
        P(("dp", "tensor"), None),
        P(),
        P(None, "tensor"),
        P(None, "tensor"),
        P(None, "tensor"),
        P(None, "tensor"),
        P(None, "tensor"),
        P(None, "tensor"),
        P(None, "tensor"),
        P(None, "tensor"),
        P(None, "tensor"),
        P("tensor"),
        P("tensor"),
        P("tensor"),
        P("tensor", None),
        P(),
        P(None, "tensor"),
        P(None, "tensor"),
        P("tensor", None),
        P("dp", None),
        P(),
    )
    return jax.shard_map(
        local,
        mesh=mesh,
        in_specs=placed,
        out_specs=(
            P(("dp", "tensor"), None),
            P(("dp", "tensor"), None),
            P(),
            P("dp", "tensor"),
            P("dp", "tensor"),
            P("dp", "tensor"),
            P("dp", "tensor"),
            P("dp", "tensor"),
            P("dp", "tensor"),
            P(),
            P(),
            P(),
            P(),
            P(),
            P(),
            P("tensor", "dp"),
            P(),
            P("dp", "tensor"),
            P("dp", "tensor"),
            P("tensor", "dp"),
        ),
        check_vma=False,
    )
```

```python
import functools
import math

import jax
import jax.numpy as jnp
from jax import lax
from jax.experimental import pallas as pl
from jax.experimental.pallas import tpu as pltpu
from jax.sharding import PartitionSpec as P

CHUNK = 128
HALO = 16
epsilon = 1e-06
F32 = jnp.float32
LOW = jnp.bfloat16
NN = (((1,), (0,)), ((), ()))
NT = (((1,), (1,)), ((), ()))
TN = (((0,), (0,)), ((), ()))


def mm(left, right, dims=NN):
    return lax.dot_general(
        left, right, dims, precision=lax.Precision.HIGH, preferred_element_type=F32
    )


def mm_full(left, right, dims=NN):
    return lax.dot_general(
        left, right, dims, precision=lax.Precision.HIGHEST, preferred_element_type=F32
    )


def iota(shape, dim):
    return lax.broadcasted_iota(jnp.int32, shape, dim)


def doc_of(positions, scalars, docs):
    total = jnp.zeros_like(positions) - 1
    for j in range(docs):
        total = total + jnp.where(positions >= scalars[1 + j], 1, 0)
    return total


def chunk_masks(position, scalars, docs):
    shape = (CHUNK, CHUNK)
    row, col = iota(shape, 0), iota(shape, 1)
    doc_row = doc_of(row + position, scalars, docs)
    doc_col = doc_of(col + position, scalars, docs)
    same = doc_row == doc_col
    prior = jnp.int32(-1)
    last = jnp.int32(-1)
    for j in range(docs):
        prior = prior + jnp.where(position - 1 >= scalars[1 + j], 1, 0)
        last = last + jnp.where(position + CHUNK - 1 >= scalars[1 + j], 1, 0)
    return {
        "row": row,
        "col": col,
        "inside": same & (row >= col),
        "strict": same & (row > col),
        "carried": (doc_row == prior)[:, :1],
        "in_last": (doc_row == last)[:, :1],
        "last_carried": last == prior,
        "back": [
            None if s == 0 else (doc_row == doc_of(row + (position - s), scalars, docs))[:, :1]
            for s in range(4)
        ],
    }


def shifted_rows(main, before, back):
    ext = jnp.concatenate([before[HALO - 8 :], main], axis=0)
    rows = [main]
    for s in range(1, 4):
        rows.append(jnp.where(back[s], pltpu.roll(ext, s, 0)[8:], 0.0))
    return rows


def conv_sum(rows, taps):
    total = rows[0] * taps[3:4, :]
    for s in range(1, 4):
        total = total + rows[s] * taps[3 - s : 4 - s, :]
    return total


def softplus(x):
    return jnp.maximum(x, 0.0) + jnp.log1p(jnp.exp(-jnp.abs(x)))


def gates(narrow, params, masks):
    shifted = narrow + params[0:1, :]
    rate = -jnp.exp(params[1:2, :])
    decays = rate * softplus(shifted)
    lower = jnp.where(masks["row"] >= masks["col"], 1.0, 0.0)
    total = mm_full(lower, decays)
    return shifted, rate, decays, jax.nn.sigmoid(narrow), total, total.T


def decay_terms(h, total, total_row, masks):
    col = total[:, h : h + 1]
    row = total_row[h : h + 1, :]
    spread = jnp.where(
        masks["inside"], jnp.exp(jnp.where(masks["inside"], col - row, 0.0)), 0.0
    )
    start = jnp.where(masks["carried"], jnp.exp(col), 0.0)
    end = total[CHUNK - 1 : CHUNK, h : h + 1]
    to_last = jnp.where(masks["in_last"], jnp.exp(jnp.where(masks["in_last"], end - col, 0.0)), 0.0)
    keep = jnp.where(masks["last_carried"], jnp.exp(end), 0.0)
    return spread, start, to_last, keep


def lanes(h):
    return slice(h * 128, h * 128 + 128)


def features(pieces, befores, taps, masks, heads):
    out = []
    for i in range(3):
        rows = shifted_rows(pieces[i], befores[i], masks["back"])
        pre = conv_sum(rows, taps[4 * i : 4 * i + 4, :])
        out.append((rows, pre, jax.nn.sigmoid(pre)))
    return out


def unit(values):
    return lax.rsqrt(jnp.sum(values * values, axis=-1, keepdims=True) + epsilon)


GROUP = 2


def chunk_inputs(step, position, mains, priors, rims, narrow_ref, taps, params, scalars, docs, heads):
    out = []
    whole = [m[...].astype(F32) for m in mains]
    befores = [
        jnp.where(step == 0, r[...].astype(F32), p[...].astype(F32)) for p, r in zip(priors, rims)
    ]
    for j in range(GROUP):
        rows = slice(j * CHUNK, j * CHUNK + CHUNK)
        masks = chunk_masks(position + j * CHUNK, scalars, docs)
        pieces = [w[rows] for w in whole]
        if j:
            befores = [w[j * CHUNK - HALO : j * CHUNK] for w in whole]
        feats = features(pieces, befores, taps, masks, heads)
        gate = gates(narrow_ref[rows, :], params, masks)
        out.append((rows, masks, feats, gate))
    return out


def intra_kernel(docs, heads, scalars, *refs):
    mains, priors, rims = refs[0:3], refs[3:6], refs[6:9]
    narrow_ref, taps_ref, params_ref = refs[9:12]
    x_ref, p_ref, kg_ref, w_ref, u_ref, qt_ref, ou_ref, t_ref, o_ref, tot_ref = refs[12:22]
    run = refs[22]
    step = pl.program_id(0)
    position = scalars[0] + step * (CHUNK * GROUP)
    inputs = chunk_inputs(
        step, position, mains, priors, rims, narrow_ref, taps_ref[...], params_ref[...], scalars,
        docs, heads,
    )
    masks = inputs[0][1]
    eye = jnp.where(masks["row"] == masks["col"], 1.0, 0.0)
    items = [(j, h) for j in range(GROUP) for h in range(heads)]
    every = range(len(items))
    q, k, v, terms, b, strict = [], [], [], [], [], []
    for j, h in items:
        _, masks, feats, (_, _, _, beta, total, total_row) = inputs[j]
        conv = [pre[:, lanes(h)] * sg[:, lanes(h)] for _, pre, sg in feats]
        q.append(conv[0] * (unit(conv[0]) * (1.0 / math.sqrt(128.0))))
        k.append(conv[1] * unit(conv[1]))
        v.append(conv[2])
        terms.append(decay_terms(h, total, total_row, masks))
        b.append(beta[:, heads + h : heads + h + 1])
        strict.append(masks["strict"])
    kg = [jnp.where(strict[i], mm(k[i], k[i], NT) * terms[i][0], 0.0) for i in every]
    p = [mm(q[i], k[i], NT) * terms[i][0] for i in every]
    a = [b[i] * kg[i] for i in every]
    pair = (masks["row"] >> 1) == (masks["col"] >> 1)
    x = [eye - jnp.where(pair, a[i], 0.0) for i in every]
    for level in range(1, 7):
        wide = (masks["row"] >> (level + 1)) == (masks["col"] >> (level + 1))
        off = wide & ((masks["row"] >> level) != (masks["col"] >> level))
        lx = [mm(jnp.where(off, a[i], 0.0), x[i]) for i in every]
        x = [x[i] - mm(x[i], lx[i]) for i in every]
    wu = [
        mm(x[i], jnp.concatenate([(b[i] * terms[i][1]) * k[i], b[i] * v[i]], axis=1)) for i in every
    ]
    pwu = [mm(p[i], wu[i]) for i in every]
    kwu = [mm(terms[i][2] * k[i], wu[i], TN) for i in every]

    @pl.when(step == 0)
    def _():
        for h in range(heads):
            run[h] = jnp.concatenate([jnp.zeros((128, 128), F32), eye], axis=1)

    for i, (j, h) in enumerate(items):
        rows = inputs[j][0]
        x_ref[j, h] = x[i]
        p_ref[j, h] = p[i]
        kg_ref[j, h] = kg[i]
        w_ref[rows, lanes(h)] = wu[i][:, :128]
        u_ref[rows, lanes(h)] = wu[i][:, 128:]
        qt_ref[rows, lanes(h)] = terms[i][1] * q[i] - pwu[i][:, :128]
        ou_ref[rows, lanes(h)] = pwu[i][:, 128:]
        transfer = terms[i][3] * eye - kwu[i][:, :128]
        offset = kwu[i][:, 128:]
        t_ref[j, h] = transfer
        o_ref[j, h] = offset
        new = mm(transfer, run[h])
        new = jnp.concatenate([new[:, :128] + offset, new[:, 128:]], axis=1)
        run[h] = new
        tot_ref[h] = new


def at_step(chunks, reverse, group):
    steps = chunks // group
    return (lambda c: steps - 1 - c) if reverse else (lambda c: c)


def rows_spec(width, chunks, reverse=False, group=1):
    at = at_step(chunks, reverse, group)
    return pl.BlockSpec((CHUNK * group, width), lambda c, *_: (at(c), 0))


def halo_spec(width, chunks, reverse=False, group=1):
    per = CHUNK * group // HALO
    at = at_step(chunks, reverse, group)
    return pl.BlockSpec((HALO, width), lambda c, *_: (jnp.maximum(at(c) * per - 1, 0), 0))


def tile_spec(heads, chunks, reverse=False, group=1):
    at = at_step(chunks, reverse, group)
    return pl.BlockSpec((group, heads, 128, 128), lambda c, *_: (at(c), 0, 0, 0))


def whole_spec(*shape):
    zeros = (0,) * len(shape)
    return pl.BlockSpec(shape, lambda c, *_: zeros)


def sds(*shape, dtype=F32):
    return jax.ShapeDtypeStruct(shape, dtype)


PARAMS = dict(vmem_limit_bytes=56 * 1024 * 1024, dimension_semantics=("arbitrary",))


def cost(flops, moved):
    return pl.CostEstimate(flops=int(flops), bytes_accessed=int(moved), transcendentals=0)


def intra(scalars, pieces, rims, narrow, taps, params, docs, heads):
    rows, width = pieces[0].shape
    chunks = rows // CHUNK
    tiles, flat = sds(chunks, heads, 128, 128), sds(rows, width)
    return pl.pallas_call(
        functools.partial(intra_kernel, docs, heads),
        out_shape=(tiles, tiles, tiles, flat, flat, flat, flat, tiles, tiles, sds(heads, 128, 256)),
        grid_spec=pltpu.PrefetchScalarGridSpec(
            num_scalar_prefetch=1,
            grid=(chunks // GROUP,),
            in_specs=[rows_spec(width, chunks, False, GROUP)] * 3
            + [halo_spec(width, chunks, False, GROUP)] * 3
            + [whole_spec(HALO, width)] * 3
            + [rows_spec(128, chunks, False, GROUP), whole_spec(16, width), whole_spec(8, 128)],
            out_specs=[tile_spec(heads, chunks, False, GROUP)] * 3
            + [rows_spec(width, chunks, False, GROUP)] * 4
            + [tile_spec(heads, chunks, False, GROUP)] * 2
            + [whole_spec(heads, 128, 256)],
            scratch_shapes=[pltpu.VMEM((heads, 128, 256), F32)],
        ),
        compiler_params=pltpu.CompilerParams(**PARAMS),
        cost_estimate=cost(chunks * heads * 60 * 3 * 2 * 128**3, 30 * rows * width * 4),
        name="intra",
    )(scalars, *pieces, *pieces, *rims, narrow, taps, params)


def outward_kernel(heads, s_in, w_ref, u_ref, qt_ref, ou_ref, t_ref, o_ref, gate_ref, gain_ref,
                   out_ref, v2_ref, s_ref, mixed_ref, run):
    step = pl.program_id(0)

    @pl.when(step == 0)
    def _():
        run[...] = s_in[...]

    hs = range(heads)
    state = [run[h] for h in hs]
    full = [
        mm(
            jnp.concatenate([qt_ref[:, lanes(h)], w_ref[:, lanes(h)], t_ref[0, h]], axis=0),
            state[h],
        )
        for h in hs
    ]
    for h in hs:
        out = full[h][:128] + ou_ref[:, lanes(h)]
        v2_ref[:, lanes(h)] = u_ref[:, lanes(h)] - full[h][128:256]
        s_ref[0, h] = state[h]
        run[h] = full[h][256:] + o_ref[0, h]
        out_ref[:, lanes(h)] = out
        gate = gate_ref[:, lanes(h)]
        scale = lax.rsqrt(jnp.mean(out * out, axis=-1, keepdims=True) + epsilon)
        mixed_ref[:, lanes(h)] = (
            out * scale * gain_ref[0:1, lanes(h)] * (gate * jax.nn.sigmoid(gate))
        ).astype(LOW)


def outward(s_in, w, u, qt, ou, t, o, gate, gain, heads):
    rows, width = w.shape
    chunks = rows // CHUNK
    flat, tiles = rows_spec(width, chunks), tile_spec(heads, chunks)
    return pl.pallas_call(
        functools.partial(outward_kernel, heads),
        out_shape=(sds(rows, width), sds(rows, width), sds(chunks, heads, 128, 128), sds(rows, width, dtype=LOW)),
        grid=(chunks,),
        in_specs=[whole_spec(heads, 128, 128), flat, flat, flat, flat, tiles, tiles, flat, whole_spec(8, width)],
        out_specs=[flat, flat, tiles, flat],
        scratch_shapes=[pltpu.VMEM((heads, 128, 128), F32)],
        compiler_params=pltpu.CompilerParams(**PARAMS),
        cost_estimate=cost(chunks * heads * 9 * 2 * 128**3, 11 * rows * width * 4),
        name="outward",
    )(s_in, w, u, qt, ou, t, o, gate, gain)


def inward_kernel(heads, scalars, gm_ref, out_ref, gate_ref, gain_ref, qt_ref, t_ref, maps_ref,
                  do_ref, dgate_ref, dgain_ref, tot_ref, run):
    step = pl.program_id(0)

    @pl.when(step == 0)
    def _():
        run[...] = jnp.zeros_like(run)
        dgain_ref[...] = jnp.zeros_like(dgain_ref)

    hs = range(heads)
    grads = []
    core = scalars[scalars.shape[0] - 1]
    for h in hs:
        out, gate = out_ref[:, lanes(h)], gate_ref[:, lanes(h)]
        other = (h + heads // 2) % heads
        gm = jnp.where(
            core == 0, gm_ref[:, lanes(h)].astype(F32), gm_ref[:, lanes(other)].astype(F32)
        )
        gain = gain_ref[0:1, lanes(h)]
        scale = lax.rsqrt(jnp.mean(out * out, axis=-1, keepdims=True) + epsilon)
        normed = out * scale
        sg = jax.nn.sigmoid(gate)
        act = gate * sg
        gn = gm * normed
        dgate_ref[:, lanes(h)] = (gn * gain * (sg * (1.0 + gate * (1.0 - sg)))).astype(LOW)
        dgain_ref[:, lanes(h)] += jnp.sum((gn * act).reshape(CHUNK // 8, 8, 128), axis=0)
        dn = gm * gain * act
        do = scale * (dn - normed * jnp.mean(dn * normed, axis=-1, keepdims=True))
        do_ref[:, lanes(h)] = do
        grads.append(do)
    for h in hs:
        left = jnp.concatenate([qt_ref[:, lanes(h)], t_ref[0, h]], axis=0)
        new = mm(left, jnp.concatenate([grads[h], run[h]], axis=0), TN)
        run[h] = new
        tot_ref[h] = jnp.concatenate([new, maps_ref[h, :, 128:]], axis=1)


def inward(scalars, gm, out, gate, gain, qt, t, maps, heads):
    rows, width = gm.shape
    chunks = rows // CHUNK
    flat, tiles = rows_spec(width, chunks, True), tile_spec(heads, chunks, True)
    return pl.pallas_call(
        functools.partial(inward_kernel, heads),
        out_shape=(sds(rows, width), sds(rows, width, dtype=LOW), sds(8, width), sds(heads, 128, 256)),
        grid_spec=pltpu.PrefetchScalarGridSpec(
            num_scalar_prefetch=1,
            grid=(chunks,),
            in_specs=[flat, flat, flat, whole_spec(8, width), flat, tiles, whole_spec(heads, 128, 256)],
            out_specs=[flat, flat, whole_spec(8, width), whole_spec(heads, 128, 256)],
            scratch_shapes=[pltpu.VMEM((heads, 128, 128), F32)],
        ),
        compiler_params=pltpu.CompilerParams(**PARAMS),
        cost_estimate=cost(chunks * heads * 6 * 2 * 128**3, 7 * rows * width * 4),
        name="inward",
    )(scalars, gm, out, gate, gain, qt, t, maps)


def back_kernel(docs, heads, steps, scalars, *refs):
    mains, priors, rims = refs[0:3], refs[3:6], refs[6:9]
    narrow_ref, taps_ref, params_ref, ds_in = refs[9:13]
    (do_ref, v2_ref, s_ref, x_ref, p_ref, kg_ref, w_ref, u_ref, qt_ref, t_ref) = refs[13:23]
    dgate_ref, grads_ref, tail_ref, rim_ref, gtaps_ref, gparams_ref = refs[23:29]
    run, after = refs[29:31]
    rev = pl.program_id(0)
    step = steps - 1 - rev
    position = scalars[0] + step * (CHUNK * GROUP)

    @pl.when(rev == 0)
    def _():
        run[...] = ds_in[...]
        after[...] = jnp.zeros_like(after)
        gtaps_ref[...] = jnp.zeros_like(gtaps_ref)
        gparams_ref[...] = jnp.zeros_like(gparams_ref)

    taps = taps_ref[...]
    inputs = chunk_inputs(
        step, position, mains, priors, rims, narrow_ref, taps, params_ref[...], scalars, docs, heads
    )
    lane, row = inputs[0][1]["col"], inputs[0][1]["row"]
    items = [(j, h) for j in reversed(range(GROUP)) for h in range(heads)]
    every = range(len(items))
    q, k, v, uq, uk, cq, ck, terms, b, rows, masks = [], [], [], [], [], [], [], [], [], [], []
    root = 1.0 / math.sqrt(128.0)
    for i, (j, h) in enumerate(items):
        rows_j, masks_j, feats, (_, _, _, beta, total, total_row) = inputs[j]
        conv = [pre[:, lanes(h)] * sg[:, lanes(h)] for _, pre, sg in feats]
        cq.append(conv[0])
        ck.append(conv[1])
        uq.append(unit(conv[0]))
        uk.append(unit(conv[1]))
        q.append(conv[0] * (uq[i] * root))
        k.append(conv[1] * uk[i])
        v.append(conv[2])
        terms.append(decay_terms(h, total, total_row, masks_j))
        b.append(beta[:, heads + h : heads + h + 1])
        rows.append(rows_j)
        masks.append(masks_j)
    do = [do_ref[rows[i], lanes(h)] for i, (j, h) in enumerate(items)]
    dsn = []
    for i, (j, h) in enumerate(items):
        dsn.append(run[h])
        left = jnp.concatenate([qt_ref[rows[i], lanes(h)], t_ref[j, h]], axis=0)
        run[h] = mm(left, jnp.concatenate([do[i], dsn[i]], axis=0), TN)
    v2 = [v2_ref[rows[i], lanes(h)] for i, (j, h) in enumerate(items)]
    kt = [terms[i][2] * k[i] for i in every]
    dv2 = [mm(p_ref[j, h], do[i], TN) + mm(kt[i], dsn[i]) for i, (j, h) in enumerate(items)]
    states = [s_ref[j, h] for j, h in items]
    both = [mm(jnp.concatenate([do[i], dv2[i]], axis=0), states[i], NT) for i in every]
    dp = [jnp.where(masks[i]["inside"], mm(do[i], v2[i], NT), 0.0) for i in every]
    dkt = [mm(v2[i], dsn[i], NT) for i in every]
    dx = [
        mm(x_ref[j, h], jnp.concatenate([-both[i][128:], dv2[i]], axis=1), TN)
        for i, (j, h) in enumerate(items)
    ]
    da = [
        jnp.where(
            masks[i]["strict"],
            -mm(
                dx[i],
                jnp.concatenate([w_ref[rows[i], lanes(h)], u_ref[rows[i], lanes(h)]], axis=1),
                NT,
            ),
            0.0,
        )
        for i, (j, h) in enumerate(items)
    ]
    zero = jnp.zeros((CHUNK, CHUNK), F32)
    gdecay, gbeta, minus = [zero] * GROUP, [zero] * GROUP, [zero] * GROUP
    dq, dk, dv = [], [], []
    for i, (j, h) in enumerate(items):
        spread, start, to_last, keep = terms[i]
        doq = both[i][:128]
        dqk = dp[i] * spread
        z = da[i] * kg_ref[j, h]
        dkk = b[i] * da[i] * spread
        dxk, dxv = dx[i][:, :128], dx[i][:, 128:]
        stacked = jnp.concatenate([dqk, dkk], axis=0)
        forward = mm(stacked, k[i])
        backward = mm(stacked, jnp.concatenate([q[i], k[i]], axis=0), TN)
        kx = jnp.sum(k[i] * dxk, axis=-1, keepdims=True)
        dq.append(start * doq + forward[:128])
        dk.append(backward + forward[128:] + to_last * dkt[i] + (b[i] * start) * dxk)
        dv.append(b[i] * dxv)
        gb = (
            jnp.sum(z, axis=-1, keepdims=True)
            + jnp.sum(v[i] * dxv, axis=-1, keepdims=True)
            + start * kx
        )
        gamgrad = b[i] * z + dp[i] * p_ref[j, h]
        dstart = jnp.sum(q[i] * doq, axis=-1, keepdims=True) + b[i] * kx
        dlast = jnp.sum(k[i] * dkt[i], axis=-1, keepdims=True) * to_last
        dkeep = jnp.sum(states[i] * dsn[i], keepdims=True) * keep
        gcol = jnp.sum(gamgrad, axis=-1, keepdims=True) + dstart * start - dlast
        end = jnp.sum(dlast, keepdims=True) + dkeep
        gcol = gcol + jnp.where(row[:, :1] == CHUNK - 1, end, 0.0)
        grow = jnp.sum(gamgrad, axis=0, keepdims=True)
        gdecay[j] = jnp.where(lane == h, gcol, gdecay[j])
        gbeta[j] = jnp.where(lane == heads + h, gb, gbeta[j])
        minus[j] = jnp.where(row == h, grow, minus[j])
    upper = jnp.where(row <= lane, 1.0, 0.0)
    width = mains[0].shape[1]
    grads_ref[:, 3 * width + 128 :] = dgate_ref[...]
    for j in reversed(range(GROUP)):
        rows_j, masks_j, feats, (shifted, rate, decays, beta, _, _) = inputs[j]
        dg = mm_full(upper, gdecay[j] - minus[j].T)
        galpha = dg * rate * jax.nn.sigmoid(shifted)
        grads_ref[rows_j, 3 * width : 3 * width + 128] = jnp.where(
            lane < heads, galpha, gbeta[j] * beta * (1.0 - beta)
        ).astype(LOW)
        gparams_ref[0:8, :] += jnp.sum((galpha).reshape(CHUNK // 8, 8, 128), axis=0)
        gparams_ref[8:16, :] += jnp.sum((dg * decays).reshape(CHUNK // 8, 8, 128), axis=0)
        for i in range(3):
            shift_rows, pre, sg = feats[i]
            pieces_d = []
            for h in range(heads):
                at = items.index((j, h))
                if i == 2:
                    pieces_d.append(dv[at])
                else:
                    inv = uq[at] if i == 0 else uk[at]
                    grad = dq[at] * root if i == 0 else dk[at]
                    normal = (cq[at] if i == 0 else ck[at]) * inv
                    pieces_d.append(
                        inv * (grad - normal * jnp.sum(grad * normal, axis=-1, keepdims=True))
                    )
            dc = jnp.concatenate(pieces_d, axis=1)
            ds = dc * (sg * (1.0 + pre * (1.0 - sg)))
            grad = ds * taps[4 * i + 3 : 4 * i + 4, :]
            rim = jnp.zeros((8, ds.shape[1]), F32)
            gtaps_ref[4 * i + 3] += jnp.sum((ds * shift_rows[0]).reshape(CHUNK // 8, 8, -1), axis=0)
            for s in range(1, 4):
                tap = taps[4 * i + 3 - s : 4 * i + 4 - s, :]
                masked = jnp.where(masks_j["back"][s], ds, 0.0)
                gtaps_ref[4 * i + 3 - s] += jnp.sum(
                    (ds * shift_rows[s]).reshape(CHUNK // 8, 8, -1), axis=0
                )
                ext = jnp.concatenate([masked, after[3 * i + s - 1]], axis=0)
                grad = grad + pltpu.roll(ext, CHUNK + 8 - s, 0)[:CHUNK] * tap
                after[3 * i + s - 1] = masked[:8]
                front = jnp.concatenate([jnp.zeros_like(masked[:8]), masked[:8]], axis=0)
                rim = rim + pltpu.roll(front, 16 - s, 0)[:8] * tap
            grads_ref[rows_j, i * width : (i + 1) * width] = grad.astype(LOW)
            if j == 0:
                rim_ref[:, i * width : (i + 1) * width] = rim
            if j == GROUP - 1:

                @pl.when(rev == 0)
                def _():
                    tail_ref[:, i * width : (i + 1) * width] = grad[CHUNK - HALO :]


def back(scalars, pieces, rims, narrow, taps, params, ds_in, do, v2, s, x, p, kg, w, u, qt, t, dgate, docs, heads):
    rows, width = pieces[0].shape
    chunks = rows // CHUNK
    flat, tiles = rows_spec(width, chunks, True, GROUP), tile_spec(heads, chunks, True, GROUP)
    return pl.pallas_call(
        functools.partial(back_kernel, docs, heads, chunks // GROUP),
        out_shape=(
            sds(rows, 4 * width + 128, dtype=LOW), sds(HALO, 3 * width), sds(8, 3 * width),
            sds(12, 8, width), sds(16, 128),
        ),
        grid_spec=pltpu.PrefetchScalarGridSpec(
            num_scalar_prefetch=1,
            grid=(chunks // GROUP,),
            in_specs=[flat] * 3
            + [halo_spec(width, chunks, True, GROUP)] * 3
            + [whole_spec(HALO, width)] * 3
            + [rows_spec(128, chunks, True, GROUP), whole_spec(16, width), whole_spec(8, 128)]
            + [whole_spec(heads, 128, 128), flat, flat, tiles, tiles, tiles, tiles, flat, flat, flat, tiles, flat],
            out_specs=[rows_spec(4 * width + 128, chunks, True, GROUP)]
            + [whole_spec(HALO, 3 * width), whole_spec(8, 3 * width)]
            + [whole_spec(12, 8, width), whole_spec(16, 128)],
            scratch_shapes=[pltpu.VMEM((heads, 128, 128), F32), pltpu.VMEM((9, 8, width), F32)],
        ),
        compiler_params=pltpu.CompilerParams(**PARAMS),
        cost_estimate=cost(chunks * heads * 60 * 2 * 128**3, 16 * rows * width * 4),
        name="back",
    )(scalars, *pieces, *pieces, *rims, narrow, taps, params, ds_in, do, v2, s, x, p, kg, w, u, qt, t, dgate)


def contract_rows(left, right):
    return lax.dot_general(left, right, TN, preferred_element_type=F32)


def contract_cols(left, right):
    return lax.dot_general(left, right, NT, preferred_element_type=F32)


def dot(left, right):
    return jnp.dot(left, right, preferred_element_type=F32)


def row_norm(values, gain):
    return values * lax.rsqrt(jnp.mean(values * values, axis=-1, keepdims=True) + epsilon) * gain


def norm_back(values, gain, grad):
    inv = lax.rsqrt(jnp.mean(values * values, axis=-1, keepdims=True) + epsilon)
    scaled = grad * gain
    inner = jnp.mean(scaled * values, axis=-1, keepdims=True)
    return inv * scaled - values * (inner * inv * inv * inv), jnp.sum(grad * values * inv, axis=0)


MESH = pl.DeviceIdType.MESH


def greet(axis, parts):
    me = lax.axis_index(axis)
    barrier = pltpu.get_barrier_semaphore()

    @pl.when(me > 0)
    def _():
        pl.semaphore_signal(barrier, inc=1, device_id={axis: me - 1}, device_id_type=MESH)

    @pl.when(me < parts - 1)
    def _():
        pl.semaphore_signal(barrier, inc=1, device_id={axis: me + 1}, device_id_type=MESH)

    inner = (me > 0) & (me < parts - 1)

    @pl.when(inner)
    def _():
        pl.semaphore_wait(barrier, 2)

    @pl.when(jnp.logical_not(inner))
    def _():
        pl.semaphore_wait(barrier, 1)


def line_gather(parts, buf, sems, first, use):
    me = lax.axis_index("tensor")
    send_right, send_left, from_left, from_right = sems

    def rightward(piece, step):
        return pltpu.make_async_remote_copy(
            src_ref=buf.at[piece],
            dst_ref=buf.at[piece],
            send_sem=send_right.at[step],
            recv_sem=from_left.at[step],
            device_id={"tensor": me + 1},
            device_id_type=MESH,
        )

    def leftward(piece, step):
        return pltpu.make_async_remote_copy(
            src_ref=buf.at[piece],
            dst_ref=buf.at[piece],
            send_sem=send_left.at[step],
            recv_sem=from_right.at[step],
            device_id={"tensor": me - 1},
            device_id_type=MESH,
        )

    def body(step, _):
        low, high = me - step, me + step

        @pl.when((step > 0) & (low >= 0))
        def _():
            rightward(low, step - 1).wait_recv()

        @pl.when((low >= 0) & (me < parts - 1))
        def _():
            rightward(low, step).start()

        @pl.when((step > 0) & (high < parts))
        def _():
            leftward(high, step - 1).wait_recv()

        @pl.when((high < parts) & (me > 0))
        def _():
            leftward(high, step).start()

        @pl.when(step == 0)
        def _():
            first()

        def visit(side, _):
            piece = me + step * (2 * side - 1)

            @pl.when((piece >= 0) & (piece < parts) & ((step > 0) | (side == 0)))
            def _():
                use(piece)

            return 0

        lax.fori_loop(0, 2, visit, 0)
        return 0

    lax.fori_loop(0, parts, body, 0)

    def finish(step, _):
        low, high = me - step, me + step

        @pl.when((low >= 0) & (me < parts - 1))
        def _():
            rightward(low, step).wait_send()

        @pl.when((high < parts) & (me > 0))
        def _():
            leftward(high, step).wait_send()

        return 0

    lax.fori_loop(0, parts, finish, 0)


def norm_into(buf, me, source, gain):
    rows = source.shape[0]

    def body(i, _):
        at = pl.ds(pl.multiple_of(i * 64, 64), 64)
        values = source[at, :].astype(F32)
        scale = lax.rsqrt(jnp.mean(values * values, axis=-1, keepdims=True) + epsilon)
        buf[me, at, :] = (values * scale * gain[0:1, :]).astype(LOW)
        return 0

    lax.fori_loop(0, rows // 64, body, 0)


def project_kernel(parts, tok_ref, gain_ref, narrow_w, *refs):
    weights_in, all_ref = refs[0:4], refs[4]
    q_ref, k_ref, v_ref, gate_ref, narrow_ref = refs[5:10]
    buf, weights = refs[10], refs[11:15]
    sems, load_sem, store_sem = refs[15:19], refs[19], refs[20]
    me = lax.axis_index("tensor")
    rows = tok_ref.shape[0]
    loads = [
        pltpu.make_async_copy(weights_in[i], weights[i], load_sem.at[i]) for i in range(4)
    ]
    for load in loads:
        load.start()
    norm_into(buf, me, tok_ref, gain_ref)
    greet("tensor", parts)

    def first():
        for load in loads:
            load.wait()

    def stored(piece):
        at = pl.ds(pl.multiple_of(piece * rows, rows), rows)
        return pltpu.make_async_copy(buf.at[piece], all_ref.at[at, :], store_sem.at[piece])

    def use(piece):
        at = pl.ds(pl.multiple_of(piece * rows, rows), rows)
        stored(piece).start()
        values = buf[piece]
        for w, out in zip(weights, (q_ref, k_ref, v_ref, gate_ref)):
            out[at, :] = dot(values, w[...]).astype(out.dtype)
        narrow_ref[at, :] = dot(values, narrow_w[...])

    line_gather(parts, buf, sems, first, use)
    for piece in range(parts):
        stored(piece).wait()


def vmem():
    return pl.BlockSpec(memory_space=pltpu.VMEM)


def hbm():
    return pl.BlockSpec(memory_space=pl.ANY)


def line_sems(parts):
    return [pltpu.SemaphoreType.DMA((parts,))] * 4


def comm_params(number):
    return pltpu.CompilerParams(
        collective_id=number, has_side_effects=True, vmem_limit_bytes=60 * 1024 * 1024
    )


def project(parts, tokens, gain, narrow_w, weights):
    rows, model = tokens.shape
    width = weights[0].shape[1]
    total = rows * parts
    low = sds(total, width, dtype=LOW)
    return pl.pallas_call(
        functools.partial(project_kernel, parts),
        out_shape=(sds(total, model, dtype=LOW), low, low, low, sds(total, width), sds(total, 128)),
        in_specs=[vmem()] * 3 + [hbm()] * 4,
        out_specs=[hbm()] + [vmem()] * 5,
        scratch_shapes=[pltpu.VMEM((parts, rows, model), LOW)]
        + [pltpu.VMEM((model, width), LOW)] * 4
        + line_sems(parts)
        + [pltpu.SemaphoreType.DMA((4,)), pltpu.SemaphoreType.DMA((parts,))],
        compiler_params=comm_params(1),
        cost_estimate=cost(2 * total * model * (4 * width + 128), 60 * 2**20),
        name="project",
    )(tokens, gain, narrow_w, *weights)


SUBS = 2
FEED_SUBS = 4


def feed_kernel(parts, res_ref, gain_ref, *refs):
    weights_in, og_in = refs[0:3], refs[3]
    mlp_ref, out_ref, grads_ref = refs[4:7]
    buf, weights, og, sent, got = refs[7], refs[8:11], refs[11], refs[12], refs[13]
    sems, load_sem = refs[14:18], refs[18]
    sem_sr, sem_sl, sem_gl, sem_gr = refs[19:23]
    act_ref, gu_ref, stage, stage_sem = refs[23:27]
    me = lax.axis_index("tensor")
    rows, model = res_ref.shape
    size = rows // FEED_SUBS
    units = weights_in[0].shape[1]
    loads = [
        pltpu.make_async_copy(src, dst, load_sem.at[i])
        for i, (src, dst) in enumerate(zip(weights_in + (og_in,), weights + (og,)))
    ]
    for load in loads:
        load.start()
    norm_into(buf, me, res_ref, gain_ref)
    greet("tensor", parts)
    wg, wu, wd = weights

    def first():
        for load in loads:
            load.wait()

    def rightward(piece, sub):
        slot = piece * FEED_SUBS + sub
        return pltpu.make_async_remote_copy(
            src_ref=sent.at[slot],
            dst_ref=got.at[slot],
            send_sem=sem_sr.at[slot],
            recv_sem=sem_gl.at[slot],
            device_id={"tensor": me + 1},
            device_id_type=MESH,
        )

    def leftward(piece, sub, to):
        slot = piece * FEED_SUBS + sub
        landing = jnp.where(piece == to, parts * FEED_SUBS + sub, slot)
        return pltpu.make_async_remote_copy(
            src_ref=sent.at[slot],
            dst_ref=got.at[landing],
            send_sem=sem_sl.at[slot],
            recv_sem=sem_gr.at[slot],
            device_id={"tensor": me - 1},
            device_id_type=MESH,
        )

    def tile(at, piece, column, wide):
        cols = pl.ds(pl.multiple_of(column, 128), wide)
        values = buf[piece]
        gate = dot(values, wg[:, cols])
        up = dot(values, wu[:, cols])
        grad = contract_cols(og[at, :], wd[cols, :])
        sg = jax.nn.sigmoid(gate)
        act = gate * sg
        act_ref[at, cols] = (act * up).astype(LOW)
        gu_ref[at, cols] = (grad * up * sg * (1.0 + gate * (1.0 - sg))).astype(LOW)
        gu_ref[at, pl.ds(pl.multiple_of(units + column, 128), wide)] = (grad * act).astype(LOW)

    def use(piece):
        at = pl.ds(pl.multiple_of(piece * rows, rows), rows)

        def body(i, _):
            tile(at, piece, i * 256, 256)
            return 0

        lax.fori_loop(0, units // 256, body, 0)
        if units % 256:
            tile(at, piece, units - units % 256, units % 256)

        def product(j, _):
            cols = pl.ds(pl.multiple_of(j * 256, 256), 256)
            total = contract_cols(gu_ref[at, :units], wg[cols, :])
            total = total + contract_cols(gu_ref[at, units:], wu[cols, :])

            @pl.when(piece == me)
            def _():
                out_ref[:, cols] = total

            @pl.when(piece != me)
            def _():
                for sub in range(FEED_SUBS):
                    sent[piece * FEED_SUBS + sub, :, cols] = total[sub * size : sub * size + size].astype(LOW)

            return 0

        lax.fori_loop(0, model // 256, product, 0)

        @pl.when((piece > me) & (me == 0))
        def _():
            for sub in range(FEED_SUBS):
                rightward(piece, sub).start()

        @pl.when((piece < me) & (me == parts - 1))
        def _():
            for sub in range(FEED_SUBS):
                leftward(piece, sub, me - 1).start()

    line_gather(parts, buf, sems, first, use)

    def down(item, _):
        piece, i = item // (model // 256), item % (model // 256)
        at = pl.ds(pl.multiple_of(piece * rows, rows), rows)
        cols = pl.ds(pl.multiple_of(i * 256, 256), 256)
        mlp_ref[at, cols] = dot(act_ref[at, :], wd[:, cols]).astype(LOW)
        return 0

    lax.fori_loop(0, parts * (model // 256), down, 0)
    talls = model // 256
    tiles = 3 * talls

    def staged(tile):
        at = pl.ds(pl.multiple_of((tile % talls) * 256, 256), 256)
        cols = pl.ds(pl.multiple_of((tile // talls) * units, 128), units)
        return pltpu.make_async_copy(
            stage.at[tile % 2], grads_ref.at[at, cols], stage_sem.at[tile % 2]
        )

    def grad_tile(tile):
        column = tile // talls
        over = pl.ds(pl.multiple_of((tile % talls) * 256, 256), 256)

        @pl.when(tile >= 2)
        def _():
            staged(tile - 2).wait()

        def summed(left, right):
            total = None
            for p in range(parts):
                term = contract_rows(left(p), right(slice(p * rows, p * rows + rows)))
                total = term if total is None else total + term
            stage[tile % 2] = total.astype(LOW)

        @pl.when(column < 2)
        def _():
            cols = pl.ds(pl.multiple_of(column * units, 128), units)
            summed(lambda p: buf[p, :, over], lambda at: gu_ref[at, cols])

        @pl.when(column == 2)
        def _():
            summed(lambda p: og[p * rows : p * rows + rows, over], lambda at: act_ref[at, :])

        staged(tile).start()

    turns = 2 * (parts - 1) * FEED_SUBS
    per_turn = -(-tiles // turns)
    right_first = 2 * me < parts

    def pass_on(item, _):
        turn = item // ((parts - 1) * FEED_SUBS)
        rest = item % ((parts - 1) * FEED_SUBS)
        step, sub = 1 + rest // FEED_SUBS, rest % FEED_SUBS
        right = (turn == 0) == right_first
        going_right = right & (me + step < parts) & (me > 0)
        going_left = jnp.logical_not(right) & (me - step >= 0) & (me < parts - 1)

        @pl.when(going_right)
        def _():
            piece = me + step
            slot = piece * FEED_SUBS + sub
            rightward(piece, sub).wait_recv()
            sent[slot] = (sent[slot].astype(F32) + got[slot].astype(F32)).astype(LOW)
            rightward(piece, sub).start()

        @pl.when(going_left)
        def _():
            piece = me - step
            slot = piece * FEED_SUBS + sub
            leftward(piece, sub, me).wait_recv()
            sent[slot] = (sent[slot].astype(F32) + got[slot].astype(F32)).astype(LOW)
            leftward(piece, sub, me - 1).start()

        for i in range(per_turn):
            tile = item * per_turn + i
            if per_turn * turns == tiles:
                grad_tile(tile)
            else:
                pl.when(tile < tiles)(functools.partial(grad_tile, tile))
        return 0

    lax.fori_loop(0, turns, pass_on, 0)
    for sub in range(FEED_SUBS):
        at = slice(sub * size, sub * size + size)

        @pl.when(me > 0)
        def _():
            rightward(me, sub).wait_recv()
            out_ref[at, :] = out_ref[at, :] + got[me * FEED_SUBS + sub].astype(F32)

        @pl.when(me < parts - 1)
        def _():
            leftward(me, sub, me).wait_recv()
            out_ref[at, :] = out_ref[at, :] + got[parts * FEED_SUBS + sub].astype(F32)

    def finish(slot, _):
        piece, sub = slot // FEED_SUBS, slot % FEED_SUBS

        @pl.when(piece > me)
        def _():
            rightward(piece, sub).wait_send()

        @pl.when(piece < me)
        def _():
            leftward(piece, sub, me - 1).wait_send()

        return 0

    lax.fori_loop(0, parts * FEED_SUBS, finish, 0)
    for slot in range(2):
        staged(tiles - 2 + slot).wait()


def feed(parts, residual, gain, weights, out_grad):
    rows, model = residual.shape
    units = weights[0].shape[1]
    total = rows * parts
    low = sds(total, model, dtype=LOW)
    return pl.pallas_call(
        functools.partial(feed_kernel, parts),
        out_shape=(low, sds(rows, model), sds(model, 3 * units, dtype=LOW)),
        in_specs=[vmem()] * 2 + [hbm()] * 4,
        out_specs=[vmem()] * 2 + [hbm()],
        scratch_shapes=[pltpu.VMEM((parts, rows, model), LOW)]
        + [pltpu.VMEM(w.shape, LOW) for w in weights]
        + [pltpu.VMEM((total, model), LOW)]
        + [pltpu.VMEM((parts * FEED_SUBS, rows // FEED_SUBS, model), LOW)]
        + [pltpu.VMEM((parts * FEED_SUBS + FEED_SUBS, rows // FEED_SUBS, model), LOW)]
        + line_sems(parts)
        + [pltpu.SemaphoreType.DMA((4,))]
        + line_sems(parts * FEED_SUBS)
        + [
            pltpu.VMEM((total, units), LOW),
            pltpu.VMEM((total, 2 * units), LOW),
            pltpu.VMEM((2, 256, units), LOW),
            pltpu.SemaphoreType.DMA((2,)),
        ],
        compiler_params=comm_params(2),
        cost_estimate=cost(18 * total * model * units, 120 * 2**20),
        name="feed",
    )(residual, gain, *weights, out_grad)


class Plain:
    inputs, outputs = 0, 1

    def __init__(self, parts):
        self.parts = parts

    def begin(self, given, scratch):
        greet("tensor", self.parts)

    def tile(self, at, cols, total, given, scratch):
        pass

    def middle(self, given, scratch):
        pass

    def end(self, given, out, scratch):
        pass

    def shapes(self, rows, model):
        return (sds(rows, model),)

    def scratch(self, rows, model):
        return []


def each(total, me, action):
    def body(k, _):
        action(lax.rem(me + k, total))
        return 0

    lax.fori_loop(1, total, body, 0)


class Exchange:
    def __init__(self, axis, total, buf, send_sem, got_sem):
        self.axis, self.total = axis, total
        self.buf, self.send_sem, self.got_sem = buf, send_sem, got_sem

    def copy(self, source, target):
        return pltpu.make_async_remote_copy(
            src_ref=self.buf.at[source],
            dst_ref=self.buf.at[source],
            send_sem=self.send_sem.at[target],
            recv_sem=self.got_sem.at[source],
            device_id={self.axis: target},
            device_id_type=MESH,
        )

    def send(self):
        me = lax.axis_index(self.axis)
        each(self.total, me, lambda other: self.copy(me, other).start())

    def receive(self):
        me = lax.axis_index(self.axis)
        each(self.total, me, lambda other: self.copy(other, me).wait_recv())

    def drain(self):
        me = lax.axis_index(self.axis)
        each(self.total, me, lambda other: self.copy(me, other).wait_send())

    def sum(self, at=slice(None)):
        total = self.buf[0, at]
        for i in range(1, self.total):
            total = total + self.buf[i, at]
        return total


class Closing:
    inputs, outputs = 4, 4

    def __init__(self, count, parts, kept, flat):
        self.count, self.parts, self.kept, self.flat = count, parts, kept, flat

    def stages(self, scratch):
        return (
            Exchange("dp", self.count, *scratch[0:3]),
            Exchange("tensor", self.parts, *scratch[3:6]),
            Exchange("dp", self.count, *scratch[6:9]),
            Exchange("tensor", self.parts, *scratch[9:12]),
        )

    def begin(self, given, scratch):
        dp, z = lax.axis_index("dp"), lax.axis_index("tensor")
        barrier = pltpu.get_barrier_semaphore()

        def hello(axis):
            def one(other):
                pl.semaphore_signal(
                    barrier, inc=1, device_id={axis: other}, device_id_type=MESH
                )

            return one

        each(self.count, dp, hello("dp"))
        each(self.parts, z, hello("tensor"))
        first = self.stages(scratch)[0]
        first.buf[dp] = given[2][...]
        scratch[12][...] = jnp.zeros_like(scratch[12])
        pl.semaphore_wait(barrier, self.count + self.parts - 2)
        first.send()

    def tile(self, at, cols, total, given, scratch):
        terms = total * given[3][at, cols].astype(F32)
        scratch[12][:, cols] += jnp.sum(terms.reshape(terms.shape[0] // 8, 8, -1), axis=0)

    def middle(self, given, scratch):
        dp, z = lax.axis_index("dp"), lax.axis_index("tensor")
        flat_dp, flat_z, gain_dp, gain_z = self.stages(scratch)
        total = jnp.sum(scratch[12][...], axis=0, keepdims=True) / given[1][0:1, :]
        wide = total.shape[1] // 8
        gain_dp.buf[dp] = jnp.concatenate(
            [total[:, i * wide : (i + 1) * wide] for i in range(8)], axis=0
        )
        gain_dp.send()
        flat_dp.receive()
        flat_z.buf[z] = flat_dp.sum()
        flat_z.send()
        gain_dp.receive()
        gain_z.buf[z] = gain_dp.sum()
        gain_z.send()

    def end(self, given, out, scratch):
        tok_ref, gain_ref, flat_ref, _ = given
        out_ref, wide_ref, rest_ref, gain_out = out
        flat_dp, flat_z, gain_dp, gain_z = self.stages(scratch)
        rows, model = out_ref.shape

        def body(i, _):
            at = pl.ds(pl.multiple_of(i * 32, 32), 32)
            values, grad = tok_ref[at, :].astype(F32), out_ref[at, :]
            inv = lax.rsqrt(jnp.mean(values * values, axis=-1, keepdims=True) + epsilon)
            scaled = grad * gain_ref[0:1, :]
            inner = jnp.mean(scaled * values, axis=-1, keepdims=True)
            out_ref[at, :] = inv * scaled - values * (inner * inv * inv * inv)
            return 0

        lax.fori_loop(0, rows // 32, body, 0)
        flat_z.receive()
        width = flat_ref.shape[1]
        for i in range(self.parts):
            wide_ref[:, i * width : (i + 1) * width] = flat_z.buf[i, : self.kept, :]
        rest_ref[...] = flat_z.sum(slice(self.kept, None))
        gain_z.receive()
        gain_out[...] = gain_z.sum()
        for stage in (flat_dp, flat_z, gain_dp, gain_z):
            stage.drain()

    def shapes(self, rows, model):
        height, width = self.flat
        return (
            sds(rows, model), sds(self.kept, width * self.parts), sds(height - self.kept, width),
            sds(8, model // 8),
        )

    def scratch(self, rows, model):
        out = []
        for shape in (self.flat, (8, model // 8)):
            for total in (self.count, self.parts):
                out.append(pltpu.VMEM((total,) + shape, F32))
                out.extend([pltpu.SemaphoreType.DMA((total,))] * 2)
        return out + [pltpu.VMEM((8, model), F32)]


def scatter_kernel(parts, given, count, splits, ending, *refs):
    lefts, rights_in = refs[0:given], refs[given : given + count]
    refs = refs[given + count :]
    extra_in, refs = refs[: ending.inputs], refs[ending.inputs :]
    extra_out, refs = refs[: ending.outputs], refs[ending.outputs :]
    rights, (part, send_r, send_l, got_l, got_r) = refs[0:count], refs[count : count + 5]
    sem_sr, sem_sl, sem_gl, sem_gr, load_sem = refs[count + 5 : count + 10]
    extra = refs[count + 10 :]
    out_ref = extra_out[0]
    me = lax.axis_index("tensor")
    rows, model = out_ref.shape
    size = rows // SUBS
    loads = [
        pltpu.make_async_copy(rights_in[i], rights[i], load_sem.at[i]) for i in range(count)
    ]
    for load in loads:
        load.start()
    ending.begin(extra_in, extra)
    for load in loads:
        load.wait()

    def rightward(slot):
        return pltpu.make_async_remote_copy(
            src_ref=send_r.at[slot],
            dst_ref=got_l.at[slot],
            send_sem=sem_sr.at[slot],
            recv_sem=sem_gl.at[slot],
            device_id={"tensor": me + 1},
            device_id_type=MESH,
        )

    def leftward(slot):
        return pltpu.make_async_remote_copy(
            src_ref=send_l.at[slot],
            dst_ref=got_r.at[slot],
            send_sem=sem_sl.at[slot],
            recv_sem=sem_gr.at[slot],
            device_id={"tensor": me - 1},
            device_id_type=MESH,
        )

    def product(start, many, target):
        at = pl.ds(pl.multiple_of(start, 128), many)

        def body(j, _):
            cols = pl.ds(pl.multiple_of(j * 256, 256), 256)
            total = None
            for i, (index, first, wide) in enumerate(splits):
                term = contract_cols(lefts[index][at, first : first + wide], rights[i][cols, :])
                total = term if total is None else total + term
            target[:, cols] = total
            ending.tile(at, cols, total, extra_in, extra)
            return 0

        lax.fori_loop(0, model // 256, body, 0)

    half = part.at[pl.ds(0, size), :]

    right_first = 2 * me < parts

    def body(item, _):
        step, sub = item // (2 * SUBS), (item // 2) % SUBS
        right = (item % 2 == 0) == right_first
        piece = jnp.where(right, parts - 1 - step, step)
        slot = piece * SUBS + sub
        go_right = right & (piece > me)
        go_left = jnp.logical_not(right) & (piece < me)

        @pl.when(go_right | go_left)
        def _():
            product(piece * rows + sub * size, size, half)

        @pl.when(go_right)
        def _():
            @pl.when(me > 0)
            def _():
                rightward(slot).wait_recv()
                send_r[slot] = (half[...] + got_l[slot].astype(F32)).astype(LOW)

            @pl.when(me == 0)
            def _():
                send_r[slot] = half[...].astype(LOW)

            rightward(slot).start()

        @pl.when(go_left)
        def _():
            @pl.when(me < parts - 1)
            def _():
                leftward(slot).wait_recv()
                send_l[slot] = (half[...] + got_r[slot].astype(F32)).astype(LOW)

            @pl.when(me == parts - 1)
            def _():
                send_l[slot] = half[...].astype(LOW)

            leftward(slot).start()

        return 0

    lax.fori_loop(0, (parts - 1) * SUBS * 2, body, 0)
    product(me * rows, rows, part)
    ending.middle(extra_in, extra)
    for sub in range(SUBS):
        at = slice(sub * size, sub * size + size)
        slot = me * SUBS + sub
        out_ref[at, :] = part[at, :]

        @pl.when(me > 0)
        def _():
            rightward(slot).wait_recv()
            out_ref[at, :] = out_ref[at, :] + got_l[slot].astype(F32)

        @pl.when(me < parts - 1)
        def _():
            leftward(slot).wait_recv()
            out_ref[at, :] = out_ref[at, :] + got_r[slot].astype(F32)

    ending.end(extra_in, extra_out, extra)

    def finish(slot, _):
        piece = slot // SUBS

        @pl.when(piece > me)
        def _():
            rightward(slot).wait_send()

        @pl.when(piece < me)
        def _():
            leftward(slot).wait_send()

        return 0

    lax.fori_loop(0, parts * SUBS, finish, 0)


def scatter(parts, lefts, rights, splits, number, ending=None, extra=()):
    total = lefts[0].shape[0]
    model = rights[0].shape[0]
    rows = total // parts
    count = len(rights)
    ending = ending or Plain(parts)
    slots = pltpu.VMEM((parts * SUBS, rows // SUBS, model), LOW)
    shapes = ending.shapes(rows, model)
    return pl.pallas_call(
        functools.partial(scatter_kernel, parts, len(lefts), count, splits, ending),
        out_shape=shapes,
        in_specs=[vmem()] * len(lefts) + [hbm()] * count + [vmem()] * len(extra),
        out_specs=[vmem()] * len(shapes),
        scratch_shapes=[pltpu.VMEM(w.shape, LOW) for w in rights]
        + [pltpu.VMEM((rows, model), F32)]
        + [slots] * 4
        + line_sems(parts * SUBS)
        + [pltpu.SemaphoreType.DMA((count,))]
        + ending.scratch(rows, model),
        compiler_params=comm_params(number),
        cost_estimate=cost(2 * total * model * sum(w.shape[1] for w in rights), 60 * 2**20),
        name="scatter%d" % number,
    )(*lefts, *rights, *extra)


def state_kernel(count, heads, backward, own_ref, out_ref, buf, send_sem, pass_sem, got_sem):
    me = lax.axis_index("dp")
    core = lax.rem(me, 2)
    sibling = me + 1 - 2 * core
    half = count // 2
    barrier = pltpu.get_barrier_semaphore()

    def peer(k):
        return lax.rem(me + 2 * k, count)

    def hello(k, _):
        pl.semaphore_signal(barrier, inc=1, device_id={"dp": peer(k)}, device_id_type=MESH)
        return 0

    lax.fori_loop(1, half, hello, 0)
    pl.semaphore_signal(barrier, inc=1, device_id={"dp": sibling}, device_id_type=MESH)
    buf[me] = own_ref[...].astype(LOW)
    pl.semaphore_wait(barrier, half)

    def needed(source, target):
        return source > target if backward else source < target

    def copy(piece, target, sem):
        return pltpu.make_async_remote_copy(
            src_ref=buf.at[piece],
            dst_ref=buf.at[piece],
            send_sem=sem,
            recv_sem=got_sem.at[piece],
            device_id={"dp": target},
            device_id_type=MESH,
        )

    def send(k, _):
        target = peer(k)

        @pl.when(needed(me, target))
        def _():
            copy(me, target, send_sem.at[target]).start()

        return 0

    @pl.when(needed(me, sibling))
    def _():
        copy(me, sibling, pass_sem.at[me]).start()

    lax.fori_loop(1, half, send, 0)

    def relay(k, _):
        source = lax.rem(me + count - 2 * k, count)

        @pl.when(needed(source, me))
        def _():
            copy(source, me, send_sem.at[source]).wait_recv()

        @pl.when(needed(source, me) & needed(source, sibling))
        def _():
            copy(source, sibling, pass_sem.at[source]).start()

        return 0

    lax.fori_loop(1, half, relay, 0)
    for h in range(heads):
        out_ref[h] = jnp.zeros_like(out_ref[h])

    def chain(step, _):
        piece = count - 1 - step if backward else step

        @pl.when(needed(piece, me) & (lax.rem(piece, 2) != core))
        def _():
            copy(piece, me, pass_sem.at[piece]).wait_recv()

        @pl.when(needed(piece, me))
        def _():
            for h in range(heads):
                both = buf[piece, h].astype(F32)
                if backward:
                    out_ref[h] = mm(both[:, 128:], out_ref[h], TN) + both[:, :128]
                else:
                    out_ref[h] = mm(both[:, 128:], out_ref[h]) + both[:, :128]

        return 0

    lax.fori_loop(0, count, chain, 0)

    def finish(k, _):
        target = peer(k)
        source = lax.rem(me + count - 2 * k, count)

        @pl.when(needed(me, target))
        def _():
            copy(me, target, send_sem.at[target]).wait_send()

        @pl.when(needed(source, me) & needed(source, sibling))
        def _():
            copy(source, sibling, pass_sem.at[source]).wait_send()

        return 0

    lax.fori_loop(1, half, finish, 0)

    @pl.when(needed(me, sibling))
    def _():
        copy(me, sibling, pass_sem.at[me]).wait_send()


def exchange(count, own, heads, backward, number):
    return pl.pallas_call(
        functools.partial(state_kernel, count, heads, backward),
        out_shape=sds(heads, 128, 128),
        in_specs=[vmem()],
        out_specs=vmem(),
        scratch_shapes=[pltpu.VMEM((count, heads, 128, 256), LOW)]
        + [pltpu.SemaphoreType.DMA((count,))] * 3,
        compiler_params=comm_params(number),
        cost_estimate=cost(count * heads * 6 * 128**3, count * heads * 256 * 128 * 4),
        name="exchange%d" % number,
    )(own)


def after(values, *first):
    out = lax.optimization_barrier((values,) + first)
    return out[0]


def local(
    tokens,
    gain_in,
    w_query,
    w_key,
    w_value,
    w_alpha,
    w_beta,
    w_gate_out,
    conv_query,
    conv_key,
    conv_value,
    decay_log,
    decay_bias,
    head_gain,
    w_out,
    gain_mid,
    w_gate,
    w_up,
    w_down,
    out_grad,
    doc_lengths,
):
    rows_own, model = tokens.shape
    tensor_parts, dp_parts = lax.axis_size("tensor"), lax.axis_size("dp")
    tensor_index, dp_index = lax.axis_index("tensor"), lax.axis_index("dp")
    group_rows = rows_own * tensor_parts
    seq_total = group_rows * dp_parts
    heads = w_alpha.shape[1]
    width = w_query.shape[1]
    core = lax.rem(dp_index, 2)
    docs = doc_lengths.shape[0] * doc_lengths.shape[1]
    starts = (
        jnp.cumsum(doc_lengths, axis=1)
        - doc_lengths
        + seq_total * lax.broadcasted_iota(jnp.int32, doc_lengths.shape, 0)
    ).reshape(-1)
    scalars = jnp.concatenate([(dp_index * group_rows).reshape(1), starts, core.reshape(1)]).astype(jnp.int32)
    taps = jnp.concatenate([conv_query, conv_key, conv_value, jnp.zeros((4, width), F32)])
    params = jnp.zeros((8, 128), F32).at[0, :heads].set(decay_bias).at[1, :heads].set(decay_log)
    gain_heads = jnp.broadcast_to(head_gain[None], (8, width))
    w_narrow = jnp.pad(jnp.concatenate([w_alpha, w_beta], axis=1), ((0, 0), (0, 128 - 2 * heads)))

    own_rows = tokens.astype(F32)
    gain_in_rows = gain_in[None]
    gain_mid_rows = gain_mid[None]
    normed_all, *pieces, gate_raw, narrow = project(
        tensor_parts, tokens, gain_in_rows, w_narrow, (w_query, w_key, w_value, w_gate_out)
    )
    half = width // 2
    out_half = lax.dynamic_slice_in_dim(after(w_out, narrow), core * half, half, 0)
    out_mine = lax.all_gather(out_half, "tensor", axis=0)
    forth = [(i, i + 1) for i in range(dp_parts - 1)]
    rims = lax.ppermute(
        jnp.stack([piece[group_rows - HALO :] for piece in pieces]), "dp", forth
    )
    rims = [rims[i] for i in range(3)]
    x, p, kg, w, u, qt, ou, t, o, totals = intra(
        scalars, pieces, rims, narrow, taps, params, docs, heads
    )
    state_in = exchange(dp_parts, totals, heads, False, 3)
    rows_out, v2, s, mixed = outward(state_in, w, u, qt, ou, t, o, gate_raw, gain_heads, heads)

    mixed_own = lax.all_to_all(mixed, "tensor", split_axis=0, concat_axis=1, tiled=True)
    out_mine, _ = lax.optimization_barrier((out_mine, mixed))
    out_other = lax.ppermute(out_mine, "dp", [(i, i ^ 1) for i in range(dp_parts)])
    out_mine = out_mine.reshape(tensor_parts * half, model)
    out_other = out_other.reshape(tensor_parts * half, model)
    split = mixed_own.reshape(rows_own, tensor_parts, 2, half)

    def of_core(index):
        return lax.dynamic_index_in_dim(split, index, 2, keepdims=False).reshape(rows_own, -1)

    residual = own_rows + (dot(of_core(core), out_mine) + dot(of_core(1 - core), out_other))
    mlp_part, grad_mid, units_grad = feed(
        tensor_parts, residual, gain_mid_rows, (w_gate, w_up, w_down), out_grad
    )
    units = w_gate.shape[1]
    right = [(i, (i + 1) % tensor_parts) for i in range(tensor_parts)]
    left = [(i, (i - 1) % tensor_parts) for i in range(tensor_parts)]

    def part_for(values, ahead):
        index = lax.rem(tensor_index + ahead + tensor_parts, tensor_parts)
        return lax.dynamic_slice_in_dim(values, index * rows_own, rows_own, 0)

    units_grad_sum = lax.psum_scatter(units_grad, "dp", scatter_dimension=0, tiled=True)
    grad_res_norm, gain_mid_grad = norm_back(residual, gain_mid, grad_mid)
    grad_own = lax.dynamic_slice_in_dim(out_grad, tensor_index * rows_own, rows_own, 0)
    grad_residual = grad_own.astype(F32) + grad_res_norm
    grad_mixer = grad_residual.astype(LOW)
    grad_mixed = jnp.concatenate(
        [
            lax.dot_general(
                grad_mixer, weight.reshape(tensor_parts, half, model), (((1,), (2,)), ((), ())),
                preferred_element_type=F32,
            ).astype(LOW).swapaxes(0, 1)
            for weight in (out_mine, out_other)
        ],
        axis=2,
    )
    grad_mixed = lax.all_to_all(
        grad_mixed, "tensor", split_axis=0, concat_axis=0, tiled=True
    ).reshape(group_rows, width)
    mlp_late = after(mlp_part, grad_mixed)
    mlp_run = part_for(mlp_late, tensor_parts - 2)
    for ahead in range(tensor_parts - 2, 1, -1):
        mlp_run = lax.ppermute(mlp_run, "tensor", right)
        if ahead > 2:
            mlp_run = (mlp_run.astype(F32) + part_for(mlp_part, ahead - 1).astype(F32)).astype(LOW)
    mlp_left = lax.ppermute(part_for(mlp_late, -1), "tensor", left)
    out_w = contract_rows(grad_mixer, mixed_own).astype(LOW)
    out_w_sum = lax.psum_scatter(out_w, "dp", scatter_dimension=0, tiled=True)
    do, gate_low, head_gain_part, ds_total = inward(
        scalars, grad_mixed, rows_out, gate_raw, gain_heads, qt, t, totals, heads
    )
    grad_end = exchange(dp_parts, ds_total, heads, True, 5)
    grad_end, mlp_run = lax.optimization_barrier((grad_end, mlp_run))
    mlp_right = lax.ppermute(
        (mlp_run.astype(F32) + part_for(mlp_part, 1).astype(F32)).astype(LOW), "tensor", right
    )
    grads, tails, rim_grad, taps_grad, params_grad = back(
        scalars, pieces, rims, narrow, taps, params, grad_end, do, v2, s, x, p, kg, w, u, qt, t,
        gate_low, docs, heads,
    )
    grads, tails, rim_grad, taps_grad, params_grad, mlp_right, mlp_left, units_grad_sum = (
        lax.optimization_barrier(
            (grads, tails, rim_grad, taps_grad, params_grad, mlp_right, mlp_left, units_grad_sum)
        )
    )
    rim_back = lax.ppermute(rim_grad, "dp", [(i + 1, i) for i in range(dp_parts - 1)])
    tails = tails.at[HALO - 8 :].add(rim_back).astype(LOW)
    grads = lax.dynamic_update_slice(grads, tails, (group_rows - HALO, 0))
    mixer_grad = contract_rows(normed_all, grads).astype(LOW)
    mixer_sum = lax.psum_scatter(mixer_grad, "dp", scatter_dimension=0, tiled=True).astype(F32)
    params_grad = params_grad.reshape(2, 8, 128).sum(1)
    flat = jnp.concatenate(
        [
            taps_grad.sum(1),
            head_gain_part.sum(0)[None],
            jnp.pad(params_grad, ((0, 1), (0, width - 128))),
            jnp.pad(gain_mid_grad.reshape(-1, width), ((0, 4), (0, 0))),
        ],
        axis=0,
    )
    grad_tokens, wide, rest, gain_in_grad = scatter(
        tensor_parts, [after(grads, mixer_grad)],
        [w_query, w_key, w_value, w_narrow, w_gate_out],
        ((0, 0, width), (0, width, width), (0, 2 * width, width), (0, 3 * width, 128), (0, 3 * width + 128, width)),
        6, Closing(dp_parts, tensor_parts, 16, flat.shape),
        (tokens, gain_in_rows, flat, normed_all),
    )
    out_w_dp, units_grad_sum, mlp_right, mlp_left, _ = lax.optimization_barrier(
        (out_w_sum, units_grad_sum, mlp_right, mlp_left, gain_in_grad)
    )
    out_pieces = [
        lax.dynamic_slice_in_dim(
            out_w_dp, lax.rem(tensor_index + ahead, tensor_parts) * width, width, 1
        )
        for ahead in range(tensor_parts)
    ]
    wide, rest, units_grad_sum, mlp_right, *out_pieces = lax.optimization_barrier(
        (wide, rest, units_grad_sum, mlp_right, *out_pieces)
    )
    for ahead in range(1, tensor_parts):
        shift = [(i, (i + ahead) % tensor_parts) for i in range(tensor_parts)]
        out_pieces[ahead] = lax.ppermute(out_pieces[ahead], "tensor", shift)
    output = residual + part_for(mlp_part, 0).astype(F32)
    output = (output + (mlp_right.astype(F32) + mlp_left.astype(F32))).astype(LOW)
    start = 3 * width
    ready = [
        output,
        grad_residual + grad_tokens,
        mixer_sum[:, :width],
        mixer_sum[:, width : 2 * width],
        mixer_sum[:, 2 * width : start],
        mixer_sum[:, start : start + heads],
        mixer_sum[:, start + heads : start + 2 * heads],
        mixer_sum[:, start + 128 :],
        units_grad_sum[:, :units].astype(F32),
        units_grad_sum[:, units : 2 * units].astype(F32),
        units_grad_sum[:, 2 * units :].T.astype(F32),
    ]
    ready, out_pieces = lax.optimization_barrier((ready, out_pieces))
    out_w_sum = sum(piece.astype(F32) for piece in out_pieces)
    by_head = wide[13:15].reshape(2, tensor_parts, width)[:, :, :heads].reshape(2, -1)
    return (
        ready[0],
        ready[1],
        gain_in_grad.reshape(model),
        *ready[2:8],
        wide[0:4],
        wide[4:8],
        wide[8:12],
        by_head[1],
        by_head[0],
        wide[12],
        out_w_sum.T,
        rest[: model // width].reshape(model),
        *ready[8:11],
    )


def solution(mesh):
    placed = (
        P(("dp", "tensor"), None),
        P(),
        P(None, "tensor"),
        P(None, "tensor"),
        P(None, "tensor"),
        P(None, "tensor"),
        P(None, "tensor"),
        P(None, "tensor"),
        P(None, "tensor"),
        P(None, "tensor"),
        P(None, "tensor"),
        P("tensor"),
        P("tensor"),
        P("tensor"),
        P("tensor", None),
        P(),
        P(None, "tensor"),
        P(None, "tensor"),
        P("tensor", None),
        P("dp", None),
        P(),
    )
    return jax.shard_map(
        local,
        mesh=mesh,
        in_specs=placed,
        out_specs=(
            P(("dp", "tensor"), None),
            P(("dp", "tensor"), None),
            P(),
            P("dp", "tensor"),
            P("dp", "tensor"),
            P("dp", "tensor"),
            P("dp", "tensor"),
            P("dp", "tensor"),
            P("dp", "tensor"),
            P(),
            P(),
            P(),
            P(),
            P(),
            P(),
            P("tensor", "dp"),
            P(),
            P("dp", "tensor"),
            P("dp", "tensor"),
            P("tensor", "dp"),
        ),
        check_vma=False,
    )
```

```python
import functools
import math

import jax
import jax.numpy as jnp
from jax import lax
from jax.experimental import pallas as pl
from jax.experimental.pallas import tpu as pltpu
from jax.sharding import PartitionSpec as P

CHUNK = 128
HALO = 16
epsilon = 1e-06
F32 = jnp.float32
LOW = jnp.bfloat16
NN = (((1,), (0,)), ((), ()))
NT = (((1,), (1,)), ((), ()))
TN = (((0,), (0,)), ((), ()))


def mm(left, right, dims=NN):
    return lax.dot_general(
        left, right, dims, precision=lax.Precision.HIGH, preferred_element_type=F32
    )


def mm_full(left, right, dims=NN):
    return lax.dot_general(
        left, right, dims, precision=lax.Precision.HIGHEST, preferred_element_type=F32
    )


def iota(shape, dim):
    return lax.broadcasted_iota(jnp.int32, shape, dim)


def doc_of(positions, scalars, docs):
    total = jnp.zeros_like(positions) - 1
    for j in range(docs):
        total = total + jnp.where(positions >= scalars[1 + j], 1, 0)
    return total


def chunk_masks(position, scalars, docs):
    shape = (CHUNK, CHUNK)
    row, col = iota(shape, 0), iota(shape, 1)
    doc_row = doc_of(row + position, scalars, docs)
    doc_col = doc_of(col + position, scalars, docs)
    same = doc_row == doc_col
    prior = jnp.int32(-1)
    last = jnp.int32(-1)
    for j in range(docs):
        prior = prior + jnp.where(position - 1 >= scalars[1 + j], 1, 0)
        last = last + jnp.where(position + CHUNK - 1 >= scalars[1 + j], 1, 0)
    return {
        "row": row,
        "col": col,
        "inside": same & (row >= col),
        "strict": same & (row > col),
        "carried": (doc_row == prior)[:, :1],
        "in_last": (doc_row == last)[:, :1],
        "last_carried": last == prior,
        "back": [
            None if s == 0 else (doc_row == doc_of(row + (position - s), scalars, docs))[:, :1]
            for s in range(4)
        ],
    }


def shifted_rows(main, before, back):
    ext = jnp.concatenate([before[HALO - 8 :], main], axis=0)
    rows = [main]
    for s in range(1, 4):
        rows.append(jnp.where(back[s], pltpu.roll(ext, s, 0)[8:], 0.0))
    return rows


def conv_sum(rows, taps):
    total = rows[0] * taps[3:4, :]
    for s in range(1, 4):
        total = total + rows[s] * taps[3 - s : 4 - s, :]
    return total


def softplus(x):
    return jnp.maximum(x, 0.0) + jnp.log1p(jnp.exp(-jnp.abs(x)))


def gates(narrow, params, masks):
    shifted = narrow + params[0:1, :]
    rate = -jnp.exp(params[1:2, :])
    decays = rate * softplus(shifted)
    lower = jnp.where(masks["row"] >= masks["col"], 1.0, 0.0)
    total = mm_full(lower, decays)
    return shifted, rate, decays, jax.nn.sigmoid(narrow), total, total.T


def decay_terms(h, total, total_row, masks):
    col = total[:, h : h + 1]
    row = total_row[h : h + 1, :]
    spread = jnp.where(
        masks["inside"], jnp.exp(jnp.where(masks["inside"], col - row, 0.0)), 0.0
    )
    start = jnp.where(masks["carried"], jnp.exp(col), 0.0)
    end = total[CHUNK - 1 : CHUNK, h : h + 1]
    to_last = jnp.where(masks["in_last"], jnp.exp(jnp.where(masks["in_last"], end - col, 0.0)), 0.0)
    keep = jnp.where(masks["last_carried"], jnp.exp(end), 0.0)
    return spread, start, to_last, keep


def lanes(h):
    return slice(h * 128, h * 128 + 128)


def features(pieces, befores, taps, masks, heads):
    out = []
    for i in range(3):
        rows = shifted_rows(pieces[i], befores[i], masks["back"])
        pre = conv_sum(rows, taps[4 * i : 4 * i + 4, :])
        out.append((rows, pre, jax.nn.sigmoid(pre)))
    return out


def unit(values):
    return lax.rsqrt(jnp.sum(values * values, axis=-1, keepdims=True) + epsilon)


GROUP = 2


def chunk_inputs(step, position, mains, priors, rims, narrow_ref, taps, params, scalars, docs, heads):
    out = []
    whole = [m[...].astype(F32) for m in mains]
    befores = [
        jnp.where(step == 0, r[...].astype(F32), p[...].astype(F32)) for p, r in zip(priors, rims)
    ]
    for j in range(GROUP):
        rows = slice(j * CHUNK, j * CHUNK + CHUNK)
        masks = chunk_masks(position + j * CHUNK, scalars, docs)
        pieces = [w[rows] for w in whole]
        if j:
            befores = [w[j * CHUNK - HALO : j * CHUNK] for w in whole]
        feats = features(pieces, befores, taps, masks, heads)
        gate = gates(narrow_ref[rows, :], params, masks)
        out.append((rows, masks, feats, gate))
    return out


def intra_kernel(docs, heads, scalars, *refs):
    mains, priors, rims = refs[0:3], refs[3:6], refs[6:9]
    narrow_ref, taps_ref, params_ref = refs[9:12]
    x_ref, p_ref, kg_ref, w_ref, u_ref, qt_ref, ou_ref, t_ref, o_ref, tot_ref = refs[12:22]
    run = refs[22]
    step = pl.program_id(0)
    position = scalars[0] + step * (CHUNK * GROUP)
    inputs = chunk_inputs(
        step, position, mains, priors, rims, narrow_ref, taps_ref[...], params_ref[...], scalars,
        docs, heads,
    )
    masks = inputs[0][1]
    eye = jnp.where(masks["row"] == masks["col"], 1.0, 0.0)
    items = [(j, h) for j in range(GROUP) for h in range(heads)]
    every = range(len(items))
    q, k, v, terms, b, strict = [], [], [], [], [], []
    for j, h in items:
        _, masks, feats, (_, _, _, beta, total, total_row) = inputs[j]
        conv = [pre[:, lanes(h)] * sg[:, lanes(h)] for _, pre, sg in feats]
        q.append(conv[0] * (unit(conv[0]) * (1.0 / math.sqrt(128.0))))
        k.append(conv[1] * unit(conv[1]))
        v.append(conv[2])
        terms.append(decay_terms(h, total, total_row, masks))
        b.append(beta[:, heads + h : heads + h + 1])
        strict.append(masks["strict"])
    kg = [jnp.where(strict[i], mm(k[i], k[i], NT) * terms[i][0], 0.0) for i in every]
    p = [mm(q[i], k[i], NT) * terms[i][0] for i in every]
    a = [b[i] * kg[i] for i in every]
    pair = (masks["row"] >> 1) == (masks["col"] >> 1)
    x = [eye - jnp.where(pair, a[i], 0.0) for i in every]
    for level in range(1, 7):
        wide = (masks["row"] >> (level + 1)) == (masks["col"] >> (level + 1))
        off = wide & ((masks["row"] >> level) != (masks["col"] >> level))
        lx = [mm(jnp.where(off, a[i], 0.0), x[i]) for i in every]
        x = [x[i] - mm(x[i], lx[i]) for i in every]
    wu = [
        mm(x[i], jnp.concatenate([(b[i] * terms[i][1]) * k[i], b[i] * v[i]], axis=1)) for i in every
    ]
    pwu = [mm(p[i], wu[i]) for i in every]
    kwu = [mm(terms[i][2] * k[i], wu[i], TN) for i in every]

    @pl.when(step == 0)
    def _():
        for h in range(heads):
            run[h] = jnp.concatenate([jnp.zeros((128, 128), F32), eye], axis=1)

    for i, (j, h) in enumerate(items):
        rows = inputs[j][0]
        x_ref[j, h] = x[i]
        p_ref[j, h] = p[i]
        kg_ref[j, h] = kg[i]
        w_ref[rows, lanes(h)] = wu[i][:, :128]
        u_ref[rows, lanes(h)] = wu[i][:, 128:]
        qt_ref[rows, lanes(h)] = terms[i][1] * q[i] - pwu[i][:, :128]
        ou_ref[rows, lanes(h)] = pwu[i][:, 128:]
        transfer = terms[i][3] * eye - kwu[i][:, :128]
        offset = kwu[i][:, 128:]
        t_ref[j, h] = transfer
        o_ref[j, h] = offset
        new = mm(transfer, run[h])
        new = jnp.concatenate([new[:, :128] + offset, new[:, 128:]], axis=1)
        run[h] = new
        tot_ref[h] = new


def at_step(chunks, reverse, group):
    steps = chunks // group
    return (lambda c: steps - 1 - c) if reverse else (lambda c: c)


def rows_spec(width, chunks, reverse=False, group=1):
    at = at_step(chunks, reverse, group)
    return pl.BlockSpec((CHUNK * group, width), lambda c, *_: (at(c), 0))


def halo_spec(width, chunks, reverse=False, group=1):
    per = CHUNK * group // HALO
    at = at_step(chunks, reverse, group)
    return pl.BlockSpec((HALO, width), lambda c, *_: (jnp.maximum(at(c) * per - 1, 0), 0))


def tile_spec(heads, chunks, reverse=False, group=1):
    at = at_step(chunks, reverse, group)
    return pl.BlockSpec((group, heads, 128, 128), lambda c, *_: (at(c), 0, 0, 0))


def whole_spec(*shape):
    zeros = (0,) * len(shape)
    return pl.BlockSpec(shape, lambda c, *_: zeros)


def sds(*shape, dtype=F32):
    return jax.ShapeDtypeStruct(shape, dtype)


PARAMS = dict(vmem_limit_bytes=56 * 1024 * 1024, dimension_semantics=("arbitrary",))


def cost(flops, moved):
    return pl.CostEstimate(flops=int(flops), bytes_accessed=int(moved), transcendentals=0)


def intra(scalars, pieces, rims, narrow, taps, params, docs, heads):
    rows, width = pieces[0].shape
    chunks = rows // CHUNK
    tiles, flat = sds(chunks, heads, 128, 128), sds(rows, width)
    return pl.pallas_call(
        functools.partial(intra_kernel, docs, heads),
        out_shape=(tiles, tiles, tiles, flat, flat, flat, flat, tiles, tiles, sds(heads, 128, 256)),
        grid_spec=pltpu.PrefetchScalarGridSpec(
            num_scalar_prefetch=1,
            grid=(chunks // GROUP,),
            in_specs=[rows_spec(width, chunks, False, GROUP)] * 3
            + [halo_spec(width, chunks, False, GROUP)] * 3
            + [whole_spec(HALO, width)] * 3
            + [rows_spec(128, chunks, False, GROUP), whole_spec(16, width), whole_spec(8, 128)],
            out_specs=[tile_spec(heads, chunks, False, GROUP)] * 3
            + [rows_spec(width, chunks, False, GROUP)] * 4
            + [tile_spec(heads, chunks, False, GROUP)] * 2
            + [whole_spec(heads, 128, 256)],
            scratch_shapes=[pltpu.VMEM((heads, 128, 256), F32)],
        ),
        compiler_params=pltpu.CompilerParams(**PARAMS),
        cost_estimate=cost(chunks * heads * 60 * 3 * 2 * 128**3, 30 * rows * width * 4),
        name="intra",
    )(scalars, *pieces, *pieces, *rims, narrow, taps, params)


def outward_kernel(heads, s_in, w_ref, u_ref, qt_ref, ou_ref, t_ref, o_ref, gate_ref, gain_ref,
                   out_ref, v2_ref, s_ref, mixed_ref, run):
    step = pl.program_id(0)

    @pl.when(step == 0)
    def _():
        run[...] = s_in[...]

    hs = range(heads)
    state = [run[h] for h in hs]
    full = [
        mm(
            jnp.concatenate([qt_ref[:, lanes(h)], w_ref[:, lanes(h)], t_ref[0, h]], axis=0),
            state[h],
        )
        for h in hs
    ]
    for h in hs:
        out = full[h][:128] + ou_ref[:, lanes(h)]
        v2_ref[:, lanes(h)] = u_ref[:, lanes(h)] - full[h][128:256]
        s_ref[0, h] = state[h]
        run[h] = full[h][256:] + o_ref[0, h]
        out_ref[:, lanes(h)] = out
        gate = gate_ref[:, lanes(h)]
        scale = lax.rsqrt(jnp.mean(out * out, axis=-1, keepdims=True) + epsilon)
        mixed_ref[:, lanes(h)] = (
            out * scale * gain_ref[0:1, lanes(h)] * (gate * jax.nn.sigmoid(gate))
        ).astype(LOW)


def outward(s_in, w, u, qt, ou, t, o, gate, gain, heads):
    rows, width = w.shape
    chunks = rows // CHUNK
    flat, tiles = rows_spec(width, chunks), tile_spec(heads, chunks)
    return pl.pallas_call(
        functools.partial(outward_kernel, heads),
        out_shape=(sds(rows, width), sds(rows, width), sds(chunks, heads, 128, 128), sds(rows, width, dtype=LOW)),
        grid=(chunks,),
        in_specs=[whole_spec(heads, 128, 128), flat, flat, flat, flat, tiles, tiles, flat, whole_spec(8, width)],
        out_specs=[flat, flat, tiles, flat],
        scratch_shapes=[pltpu.VMEM((heads, 128, 128), F32)],
        compiler_params=pltpu.CompilerParams(**PARAMS),
        cost_estimate=cost(chunks * heads * 9 * 2 * 128**3, 11 * rows * width * 4),
        name="outward",
    )(s_in, w, u, qt, ou, t, o, gate, gain)


def inward_kernel(heads, scalars, gm_ref, out_ref, gate_ref, gain_ref, qt_ref, t_ref, maps_ref,
                  do_ref, dgate_ref, dgain_ref, tot_ref, run):
    step = pl.program_id(0)

    @pl.when(step == 0)
    def _():
        run[...] = jnp.zeros_like(run)
        dgain_ref[...] = jnp.zeros_like(dgain_ref)

    hs = range(heads)
    grads = []
    core = scalars[scalars.shape[0] - 1]
    for h in hs:
        out, gate = out_ref[:, lanes(h)], gate_ref[:, lanes(h)]
        other = (h + heads // 2) % heads
        gm = jnp.where(
            core == 0, gm_ref[:, lanes(h)].astype(F32), gm_ref[:, lanes(other)].astype(F32)
        )
        gain = gain_ref[0:1, lanes(h)]
        scale = lax.rsqrt(jnp.mean(out * out, axis=-1, keepdims=True) + epsilon)
        normed = out * scale
        sg = jax.nn.sigmoid(gate)
        act = gate * sg
        gn = gm * normed
        dgate_ref[:, lanes(h)] = (gn * gain * (sg * (1.0 + gate * (1.0 - sg)))).astype(LOW)
        dgain_ref[:, lanes(h)] += jnp.sum((gn * act).reshape(CHUNK // 8, 8, 128), axis=0)
        dn = gm * gain * act
        do = scale * (dn - normed * jnp.mean(dn * normed, axis=-1, keepdims=True))
        do_ref[:, lanes(h)] = do
        grads.append(do)
    for h in hs:
        left = jnp.concatenate([qt_ref[:, lanes(h)], t_ref[0, h]], axis=0)
        new = mm(left, jnp.concatenate([grads[h], run[h]], axis=0), TN)
        run[h] = new
        tot_ref[h] = jnp.concatenate([new, maps_ref[h, :, 128:]], axis=1)


def inward(scalars, gm, out, gate, gain, qt, t, maps, heads):
    rows, width = gm.shape
    chunks = rows // CHUNK
    flat, tiles = rows_spec(width, chunks, True), tile_spec(heads, chunks, True)
    return pl.pallas_call(
        functools.partial(inward_kernel, heads),
        out_shape=(sds(rows, width), sds(rows, width, dtype=LOW), sds(8, width), sds(heads, 128, 256)),
        grid_spec=pltpu.PrefetchScalarGridSpec(
            num_scalar_prefetch=1,
            grid=(chunks,),
            in_specs=[flat, flat, flat, whole_spec(8, width), flat, tiles, whole_spec(heads, 128, 256)],
            out_specs=[flat, flat, whole_spec(8, width), whole_spec(heads, 128, 256)],
            scratch_shapes=[pltpu.VMEM((heads, 128, 128), F32)],
        ),
        compiler_params=pltpu.CompilerParams(**PARAMS),
        cost_estimate=cost(chunks * heads * 6 * 2 * 128**3, 7 * rows * width * 4),
        name="inward",
    )(scalars, gm, out, gate, gain, qt, t, maps)


def back_kernel(docs, heads, steps, scalars, *refs):
    mains, priors, rims = refs[0:3], refs[3:6], refs[6:9]
    narrow_ref, taps_ref, params_ref, ds_in = refs[9:13]
    (do_ref, v2_ref, s_ref, x_ref, p_ref, kg_ref, w_ref, u_ref, qt_ref, t_ref) = refs[13:23]
    dgate_ref, grads_ref, tail_ref, rim_ref, gtaps_ref, gparams_ref = refs[23:29]
    run, after = refs[29:31]
    rev = pl.program_id(0)
    step = steps - 1 - rev
    position = scalars[0] + step * (CHUNK * GROUP)

    @pl.when(rev == 0)
    def _():
        run[...] = ds_in[...]
        after[...] = jnp.zeros_like(after)
        gtaps_ref[...] = jnp.zeros_like(gtaps_ref)
        gparams_ref[...] = jnp.zeros_like(gparams_ref)

    taps = taps_ref[...]
    inputs = chunk_inputs(
        step, position, mains, priors, rims, narrow_ref, taps, params_ref[...], scalars, docs, heads
    )
    lane, row = inputs[0][1]["col"], inputs[0][1]["row"]
    items = [(j, h) for j in reversed(range(GROUP)) for h in range(heads)]
    every = range(len(items))
    q, k, v, uq, uk, cq, ck, terms, b, rows, masks = [], [], [], [], [], [], [], [], [], [], []
    root = 1.0 / math.sqrt(128.0)
    for i, (j, h) in enumerate(items):
        rows_j, masks_j, feats, (_, _, _, beta, total, total_row) = inputs[j]
        conv = [pre[:, lanes(h)] * sg[:, lanes(h)] for _, pre, sg in feats]
        cq.append(conv[0])
        ck.append(conv[1])
        uq.append(unit(conv[0]))
        uk.append(unit(conv[1]))
        q.append(conv[0] * (uq[i] * root))
        k.append(conv[1] * uk[i])
        v.append(conv[2])
        terms.append(decay_terms(h, total, total_row, masks_j))
        b.append(beta[:, heads + h : heads + h + 1])
        rows.append(rows_j)
        masks.append(masks_j)
    do = [do_ref[rows[i], lanes(h)] for i, (j, h) in enumerate(items)]
    dsn = []
    for i, (j, h) in enumerate(items):
        dsn.append(run[h])
        left = jnp.concatenate([qt_ref[rows[i], lanes(h)], t_ref[j, h]], axis=0)
        run[h] = mm(left, jnp.concatenate([do[i], dsn[i]], axis=0), TN)
    v2 = [v2_ref[rows[i], lanes(h)] for i, (j, h) in enumerate(items)]
    kt = [terms[i][2] * k[i] for i in every]
    dv2 = [mm(p_ref[j, h], do[i], TN) + mm(kt[i], dsn[i]) for i, (j, h) in enumerate(items)]
    states = [s_ref[j, h] for j, h in items]
    both = [mm(jnp.concatenate([do[i], dv2[i]], axis=0), states[i], NT) for i in every]
    dp = [jnp.where(masks[i]["inside"], mm(do[i], v2[i], NT), 0.0) for i in every]
    dkt = [mm(v2[i], dsn[i], NT) for i in every]
    dx = [
        mm(x_ref[j, h], jnp.concatenate([-both[i][128:], dv2[i]], axis=1), TN)
        for i, (j, h) in enumerate(items)
    ]
    da = [
        jnp.where(
            masks[i]["strict"],
            -mm(
                dx[i],
                jnp.concatenate([w_ref[rows[i], lanes(h)], u_ref[rows[i], lanes(h)]], axis=1),
                NT,
            ),
            0.0,
        )
        for i, (j, h) in enumerate(items)
    ]
    zero = jnp.zeros((CHUNK, CHUNK), F32)
    gdecay, gbeta, minus = [zero] * GROUP, [zero] * GROUP, [zero] * GROUP
    dq, dk, dv = [], [], []
    for i, (j, h) in enumerate(items):
        spread, start, to_last, keep = terms[i]
        doq = both[i][:128]
        dqk = dp[i] * spread
        z = da[i] * kg_ref[j, h]
        dkk = b[i] * da[i] * spread
        dxk, dxv = dx[i][:, :128], dx[i][:, 128:]
        stacked = jnp.concatenate([dqk, dkk], axis=0)
        forward = mm(stacked, k[i])
        backward = mm(stacked, jnp.concatenate([q[i], k[i]], axis=0), TN)
        kx = jnp.sum(k[i] * dxk, axis=-1, keepdims=True)
        dq.append(start * doq + forward[:128])
        dk.append(backward + forward[128:] + to_last * dkt[i] + (b[i] * start) * dxk)
        dv.append(b[i] * dxv)
        gb = (
            jnp.sum(z, axis=-1, keepdims=True)
            + jnp.sum(v[i] * dxv, axis=-1, keepdims=True)
            + start * kx
        )
        gamgrad = b[i] * z + dp[i] * p_ref[j, h]
        dstart = jnp.sum(q[i] * doq, axis=-1, keepdims=True) + b[i] * kx
        dlast = jnp.sum(k[i] * dkt[i], axis=-1, keepdims=True) * to_last
        dkeep = jnp.sum(states[i] * dsn[i], keepdims=True) * keep
        gcol = jnp.sum(gamgrad, axis=-1, keepdims=True) + dstart * start - dlast
        end = jnp.sum(dlast, keepdims=True) + dkeep
        gcol = gcol + jnp.where(row[:, :1] == CHUNK - 1, end, 0.0)
        grow = jnp.sum(gamgrad, axis=0, keepdims=True)
        gdecay[j] = jnp.where(lane == h, gcol, gdecay[j])
        gbeta[j] = jnp.where(lane == heads + h, gb, gbeta[j])
        minus[j] = jnp.where(row == h, grow, minus[j])
    upper = jnp.where(row <= lane, 1.0, 0.0)
    width = mains[0].shape[1]
    grads_ref[:, 3 * width + 128 :] = dgate_ref[...]
    for j in reversed(range(GROUP)):
        rows_j, masks_j, feats, (shifted, rate, decays, beta, _, _) = inputs[j]
        dg = mm_full(upper, gdecay[j] - minus[j].T)
        galpha = dg * rate * jax.nn.sigmoid(shifted)
        grads_ref[rows_j, 3 * width : 3 * width + 128] = jnp.where(
            lane < heads, galpha, gbeta[j] * beta * (1.0 - beta)
        ).astype(LOW)
        gparams_ref[0:8, :] += jnp.sum((galpha).reshape(CHUNK // 8, 8, 128), axis=0)
        gparams_ref[8:16, :] += jnp.sum((dg * decays).reshape(CHUNK // 8, 8, 128), axis=0)
        for i in range(3):
            shift_rows, pre, sg = feats[i]
            pieces_d = []
            for h in range(heads):
                at = items.index((j, h))
                if i == 2:
                    pieces_d.append(dv[at])
                else:
                    inv = uq[at] if i == 0 else uk[at]
                    grad = dq[at] * root if i == 0 else dk[at]
                    normal = (cq[at] if i == 0 else ck[at]) * inv
                    pieces_d.append(
                        inv * (grad - normal * jnp.sum(grad * normal, axis=-1, keepdims=True))
                    )
            dc = jnp.concatenate(pieces_d, axis=1)
            ds = dc * (sg * (1.0 + pre * (1.0 - sg)))
            grad = ds * taps[4 * i + 3 : 4 * i + 4, :]
            rim = jnp.zeros((8, ds.shape[1]), F32)
            gtaps_ref[4 * i + 3] += jnp.sum((ds * shift_rows[0]).reshape(CHUNK // 8, 8, -1), axis=0)
            for s in range(1, 4):
                tap = taps[4 * i + 3 - s : 4 * i + 4 - s, :]
                masked = jnp.where(masks_j["back"][s], ds, 0.0)
                gtaps_ref[4 * i + 3 - s] += jnp.sum(
                    (ds * shift_rows[s]).reshape(CHUNK // 8, 8, -1), axis=0
                )
                ext = jnp.concatenate([masked, after[3 * i + s - 1]], axis=0)
                grad = grad + pltpu.roll(ext, CHUNK + 8 - s, 0)[:CHUNK] * tap
                after[3 * i + s - 1] = masked[:8]
                front = jnp.concatenate([jnp.zeros_like(masked[:8]), masked[:8]], axis=0)
                rim = rim + pltpu.roll(front, 16 - s, 0)[:8] * tap
            grads_ref[rows_j, i * width : (i + 1) * width] = grad.astype(LOW)
            if j == 0:
                rim_ref[:, i * width : (i + 1) * width] = rim
            if j == GROUP - 1:

                @pl.when(rev == 0)
                def _():
                    tail_ref[:, i * width : (i + 1) * width] = grad[CHUNK - HALO :]


def back(scalars, pieces, rims, narrow, taps, params, ds_in, do, v2, s, x, p, kg, w, u, qt, t, dgate, docs, heads):
    rows, width = pieces[0].shape
    chunks = rows // CHUNK
    flat, tiles = rows_spec(width, chunks, True, GROUP), tile_spec(heads, chunks, True, GROUP)
    return pl.pallas_call(
        functools.partial(back_kernel, docs, heads, chunks // GROUP),
        out_shape=(
            sds(rows, 4 * width + 128, dtype=LOW), sds(HALO, 3 * width), sds(8, 3 * width),
            sds(12, 8, width), sds(16, 128),
        ),
        grid_spec=pltpu.PrefetchScalarGridSpec(
            num_scalar_prefetch=1,
            grid=(chunks // GROUP,),
            in_specs=[flat] * 3
            + [halo_spec(width, chunks, True, GROUP)] * 3
            + [whole_spec(HALO, width)] * 3
            + [rows_spec(128, chunks, True, GROUP), whole_spec(16, width), whole_spec(8, 128)]
            + [whole_spec(heads, 128, 128), flat, flat, tiles, tiles, tiles, tiles, flat, flat, flat, tiles, flat],
            out_specs=[rows_spec(4 * width + 128, chunks, True, GROUP)]
            + [whole_spec(HALO, 3 * width), whole_spec(8, 3 * width)]
            + [whole_spec(12, 8, width), whole_spec(16, 128)],
            scratch_shapes=[pltpu.VMEM((heads, 128, 128), F32), pltpu.VMEM((9, 8, width), F32)],
        ),
        compiler_params=pltpu.CompilerParams(**PARAMS),
        cost_estimate=cost(chunks * heads * 60 * 2 * 128**3, 16 * rows * width * 4),
        name="back",
    )(scalars, *pieces, *pieces, *rims, narrow, taps, params, ds_in, do, v2, s, x, p, kg, w, u, qt, t, dgate)


def contract_rows(left, right):
    return lax.dot_general(left, right, TN, preferred_element_type=F32)


def contract_cols(left, right):
    return lax.dot_general(left, right, NT, preferred_element_type=F32)


def dot(left, right):
    return jnp.dot(left, right, preferred_element_type=F32)


def row_norm(values, gain):
    return values * lax.rsqrt(jnp.mean(values * values, axis=-1, keepdims=True) + epsilon) * gain


def norm_back(values, gain, grad):
    inv = lax.rsqrt(jnp.mean(values * values, axis=-1, keepdims=True) + epsilon)
    scaled = grad * gain
    inner = jnp.mean(scaled * values, axis=-1, keepdims=True)
    return inv * scaled - values * (inner * inv * inv * inv), jnp.sum(grad * values * inv, axis=0)


MESH = pl.DeviceIdType.MESH


def greet(axis, parts):
    me = lax.axis_index(axis)
    barrier = pltpu.get_barrier_semaphore()

    @pl.when(me > 0)
    def _():
        pl.semaphore_signal(barrier, inc=1, device_id={axis: me - 1}, device_id_type=MESH)

    @pl.when(me < parts - 1)
    def _():
        pl.semaphore_signal(barrier, inc=1, device_id={axis: me + 1}, device_id_type=MESH)

    inner = (me > 0) & (me < parts - 1)

    @pl.when(inner)
    def _():
        pl.semaphore_wait(barrier, 2)

    @pl.when(jnp.logical_not(inner))
    def _():
        pl.semaphore_wait(barrier, 1)


def line_gather(parts, buf, sems, first, use):
    me = lax.axis_index("tensor")
    send_right, send_left, from_left, from_right = sems

    def rightward(piece, step):
        return pltpu.make_async_remote_copy(
            src_ref=buf.at[piece],
            dst_ref=buf.at[piece],
            send_sem=send_right.at[step],
            recv_sem=from_left.at[step],
            device_id={"tensor": me + 1},
            device_id_type=MESH,
        )

    def leftward(piece, step):
        return pltpu.make_async_remote_copy(
            src_ref=buf.at[piece],
            dst_ref=buf.at[piece],
            send_sem=send_left.at[step],
            recv_sem=from_right.at[step],
            device_id={"tensor": me - 1},
            device_id_type=MESH,
        )

    def body(step, _):
        low, high = me - step, me + step

        @pl.when((step > 0) & (low >= 0))
        def _():
            rightward(low, step - 1).wait_recv()

        @pl.when((low >= 0) & (me < parts - 1))
        def _():
            rightward(low, step).start()

        @pl.when((step > 0) & (high < parts))
        def _():
            leftward(high, step - 1).wait_recv()

        @pl.when((high < parts) & (me > 0))
        def _():
            leftward(high, step).start()

        @pl.when(step == 0)
        def _():
            first()

        def visit(side, _):
            piece = me + step * (2 * side - 1)

            @pl.when((piece >= 0) & (piece < parts) & ((step > 0) | (side == 0)))
            def _():
                use(piece)

            return 0

        lax.fori_loop(0, 2, visit, 0)
        return 0

    lax.fori_loop(0, parts, body, 0)

    def finish(step, _):
        low, high = me - step, me + step

        @pl.when((low >= 0) & (me < parts - 1))
        def _():
            rightward(low, step).wait_send()

        @pl.when((high < parts) & (me > 0))
        def _():
            leftward(high, step).wait_send()

        return 0

    lax.fori_loop(0, parts, finish, 0)


def norm_into(buf, me, source, gain):
    rows = source.shape[0]

    def body(i, _):
        at = pl.ds(pl.multiple_of(i * 64, 64), 64)
        values = source[at, :].astype(F32)
        scale = lax.rsqrt(jnp.mean(values * values, axis=-1, keepdims=True) + epsilon)
        buf[me, at, :] = (values * scale * gain[0:1, :]).astype(LOW)
        return 0

    lax.fori_loop(0, rows // 64, body, 0)


def project_kernel(parts, tok_ref, gain_ref, narrow_w, *refs):
    weights_in, all_ref = refs[0:4], refs[4]
    q_ref, k_ref, v_ref, gate_ref, narrow_ref, tails_ref = refs[5:11]
    buf, weights = refs[11], refs[12:16]
    sems, load_sem, store_sem = refs[16:20], refs[20], refs[21]
    me = lax.axis_index("tensor")
    rows = tok_ref.shape[0]
    loads = [
        pltpu.make_async_copy(weights_in[i], weights[i], load_sem.at[i]) for i in range(4)
    ]
    for load in loads:
        load.start()
    norm_into(buf, me, tok_ref, gain_ref)
    greet("tensor", parts)

    def first():
        for load in loads:
            load.wait()

    def stored(piece):
        at = pl.ds(pl.multiple_of(piece * rows, rows), rows)
        return pltpu.make_async_copy(buf.at[piece], all_ref.at[at, :], store_sem.at[piece])

    def use(piece):
        at = pl.ds(pl.multiple_of(piece * rows, rows), rows)
        stored(piece).start()
        values = buf[piece]
        for w, out in zip(weights, (q_ref, k_ref, v_ref, gate_ref)):
            out[at, :] = dot(values, w[...]).astype(out.dtype)
        narrow_ref[at, :] = dot(values, narrow_w[...])

    line_gather(parts, buf, sems, first, use)
    for i, out in enumerate((q_ref, k_ref, v_ref)):
        tails_ref[i] = out[rows * parts - HALO :, :]
    for piece in range(parts):
        stored(piece).wait()


def vmem():
    return pl.BlockSpec(memory_space=pltpu.VMEM)


def hbm():
    return pl.BlockSpec(memory_space=pl.ANY)


def line_sems(parts):
    return [pltpu.SemaphoreType.DMA((parts,))] * 4


def comm_params(number):
    return pltpu.CompilerParams(
        collective_id=number, has_side_effects=True, vmem_limit_bytes=60 * 1024 * 1024
    )


def project(parts, tokens, gain, narrow_w, weights):
    rows, model = tokens.shape
    width = weights[0].shape[1]
    total = rows * parts
    low = sds(total, width, dtype=LOW)
    return pl.pallas_call(
        functools.partial(project_kernel, parts),
        out_shape=(
            sds(total, model, dtype=LOW), low, low, low, sds(total, width), sds(total, 128),
            sds(3, HALO, width, dtype=LOW),
        ),
        in_specs=[vmem()] * 3 + [hbm()] * 4,
        out_specs=[hbm()] + [vmem()] * 6,
        scratch_shapes=[pltpu.VMEM((parts, rows, model), LOW)]
        + [pltpu.VMEM((model, width), LOW)] * 4
        + line_sems(parts)
        + [pltpu.SemaphoreType.DMA((4,)), pltpu.SemaphoreType.DMA((parts,))],
        compiler_params=comm_params(1),
        cost_estimate=cost(2 * total * model * (4 * width + 128), 60 * 2**20),
        name="project",
    )(tokens, gain, narrow_w, *weights)


SUBS = 2
FEED_SUBS = 4


def feed_kernel(parts, res_ref, gain_ref, *refs):
    weights_in, og_in = refs[0:3], refs[3]
    mlp_ref, out_ref, grads_ref = refs[4:7]
    buf, weights, og, sent, got = refs[7], refs[8:11], refs[11], refs[12], refs[13]
    sems, load_sem = refs[14:18], refs[18]
    sem_sr, sem_sl, sem_gl, sem_gr = refs[19:23]
    act_ref, gu_ref, stage, stage_sem = refs[23:27]
    me = lax.axis_index("tensor")
    rows, model = res_ref.shape
    size = rows // FEED_SUBS
    units = weights_in[0].shape[1]
    loads = [
        pltpu.make_async_copy(src, dst, load_sem.at[i])
        for i, (src, dst) in enumerate(zip(weights_in + (og_in,), weights + (og,)))
    ]
    for load in loads:
        load.start()
    norm_into(buf, me, res_ref, gain_ref)
    greet("tensor", parts)
    wg, wu, wd = weights

    def first():
        for load in loads:
            load.wait()

    def rightward(piece, sub):
        slot = piece * FEED_SUBS + sub
        return pltpu.make_async_remote_copy(
            src_ref=sent.at[slot],
            dst_ref=got.at[slot],
            send_sem=sem_sr.at[slot],
            recv_sem=sem_gl.at[slot],
            device_id={"tensor": me + 1},
            device_id_type=MESH,
        )

    def leftward(piece, sub, to):
        slot = piece * FEED_SUBS + sub
        landing = jnp.where(piece == to, parts * FEED_SUBS + sub, slot)
        return pltpu.make_async_remote_copy(
            src_ref=sent.at[slot],
            dst_ref=got.at[landing],
            send_sem=sem_sl.at[slot],
            recv_sem=sem_gr.at[slot],
            device_id={"tensor": me - 1},
            device_id_type=MESH,
        )

    def tile(at, piece, column, wide):
        cols = pl.ds(pl.multiple_of(column, 128), wide)
        values = buf[piece]
        gate = dot(values, wg[:, cols])
        up = dot(values, wu[:, cols])
        grad = contract_cols(og[at, :], wd[cols, :])
        sg = jax.nn.sigmoid(gate)
        act = gate * sg
        act_ref[at, cols] = (act * up).astype(LOW)
        gu_ref[at, cols] = (grad * up * sg * (1.0 + gate * (1.0 - sg))).astype(LOW)
        gu_ref[at, pl.ds(pl.multiple_of(units + column, 128), wide)] = (grad * act).astype(LOW)

    def use(piece):
        at = pl.ds(pl.multiple_of(piece * rows, rows), rows)

        def body(i, _):
            tile(at, piece, i * 256, 256)
            return 0

        lax.fori_loop(0, units // 256, body, 0)
        if units % 256:
            tile(at, piece, units - units % 256, units % 256)

        def product(j, _):
            cols = pl.ds(pl.multiple_of(j * 256, 256), 256)
            total = contract_cols(gu_ref[at, :units], wg[cols, :])
            total = total + contract_cols(gu_ref[at, units:], wu[cols, :])

            @pl.when(piece == me)
            def _():
                out_ref[:, cols] = total

            @pl.when(piece != me)
            def _():
                for sub in range(FEED_SUBS):
                    sent[piece * FEED_SUBS + sub, :, cols] = total[sub * size : sub * size + size].astype(LOW)

            return 0

        lax.fori_loop(0, model // 256, product, 0)

        @pl.when((piece > me) & (me == 0))
        def _():
            for sub in range(FEED_SUBS):
                rightward(piece, sub).start()

        @pl.when((piece < me) & (me == parts - 1))
        def _():
            for sub in range(FEED_SUBS):
                leftward(piece, sub, me - 1).start()

    line_gather(parts, buf, sems, first, use)

    def down(item, _):
        piece, i = item // (model // 256), item % (model // 256)
        at = pl.ds(pl.multiple_of(piece * rows, rows), rows)
        cols = pl.ds(pl.multiple_of(i * 256, 256), 256)
        mlp_ref[at, cols] = dot(act_ref[at, :], wd[:, cols]).astype(LOW)
        return 0

    talls = model // 256
    tiles = 3 * talls

    def staged(tile):
        at = pl.ds(pl.multiple_of((tile % talls) * 256, 256), 256)
        cols = pl.ds(pl.multiple_of((tile // talls) * units, 128), units)
        return pltpu.make_async_copy(
            stage.at[tile % 2], grads_ref.at[at, cols], stage_sem.at[tile % 2]
        )

    def grad_tile(tile):
        column = tile // talls
        over = pl.ds(pl.multiple_of((tile % talls) * 256, 256), 256)

        @pl.when(tile >= 2)
        def _():
            staged(tile - 2).wait()

        def summed(left, right):
            total = None
            for p in range(parts):
                term = contract_rows(left(p), right(slice(p * rows, p * rows + rows)))
                total = term if total is None else total + term
            stage[tile % 2] = total.astype(LOW)

        @pl.when(column < 2)
        def _():
            cols = pl.ds(pl.multiple_of(column * units, 128), units)
            summed(lambda p: buf[p, :, over], lambda at: gu_ref[at, cols])

        @pl.when(column == 2)
        def _():
            summed(lambda p: og[p * rows : p * rows + rows, over], lambda at: act_ref[at, :])

        staged(tile).start()

    turns = 2 * (parts - 1) * FEED_SUBS
    per_turn = -(-tiles // turns)
    right_first = 2 * me < parts

    def pass_on(item, _):
        turn = item // ((parts - 1) * FEED_SUBS)
        rest = item % ((parts - 1) * FEED_SUBS)
        step, sub = 1 + rest // FEED_SUBS, rest % FEED_SUBS
        right = (turn == 0) == right_first
        going_right = right & (me + step < parts) & (me > 0)
        going_left = jnp.logical_not(right) & (me - step >= 0) & (me < parts - 1)

        @pl.when(going_right)
        def _():
            piece = me + step
            slot = piece * FEED_SUBS + sub
            rightward(piece, sub).wait_recv()
            sent[slot] = (sent[slot].astype(F32) + got[slot].astype(F32)).astype(LOW)
            rightward(piece, sub).start()

        @pl.when(going_left)
        def _():
            piece = me - step
            slot = piece * FEED_SUBS + sub
            leftward(piece, sub, me).wait_recv()
            sent[slot] = (sent[slot].astype(F32) + got[slot].astype(F32)).astype(LOW)
            leftward(piece, sub, me - 1).start()

        for i in range(per_turn):
            tile = item * per_turn + i
            if per_turn * turns == tiles:
                grad_tile(tile)
            else:
                pl.when(tile < tiles)(functools.partial(grad_tile, tile))
        return 0

    lax.fori_loop(0, turns, pass_on, 0)
    lax.fori_loop(0, parts * (model // 256), down, 0)
    for sub in range(FEED_SUBS):
        at = slice(sub * size, sub * size + size)

        @pl.when(me > 0)
        def _():
            rightward(me, sub).wait_recv()
            out_ref[at, :] = out_ref[at, :] + got[me * FEED_SUBS + sub].astype(F32)

        @pl.when(me < parts - 1)
        def _():
            leftward(me, sub, me).wait_recv()
            out_ref[at, :] = out_ref[at, :] + got[parts * FEED_SUBS + sub].astype(F32)

    def finish(slot, _):
        piece, sub = slot // FEED_SUBS, slot % FEED_SUBS

        @pl.when(piece > me)
        def _():
            rightward(piece, sub).wait_send()

        @pl.when(piece < me)
        def _():
            leftward(piece, sub, me - 1).wait_send()

        return 0

    lax.fori_loop(0, parts * FEED_SUBS, finish, 0)
    for slot in range(2):
        staged(tiles - 2 + slot).wait()


def feed(parts, residual, gain, weights, out_grad):
    rows, model = residual.shape
    units = weights[0].shape[1]
    total = rows * parts
    low = sds(total, model, dtype=LOW)
    return pl.pallas_call(
        functools.partial(feed_kernel, parts),
        out_shape=(low, sds(rows, model), sds(model, 3 * units, dtype=LOW)),
        in_specs=[vmem()] * 2 + [hbm()] * 4,
        out_specs=[vmem()] * 2 + [hbm()],
        scratch_shapes=[pltpu.VMEM((parts, rows, model), LOW)]
        + [pltpu.VMEM(w.shape, LOW) for w in weights]
        + [pltpu.VMEM((total, model), LOW)]
        + [pltpu.VMEM((parts * FEED_SUBS, rows // FEED_SUBS, model), LOW)]
        + [pltpu.VMEM((parts * FEED_SUBS + FEED_SUBS, rows // FEED_SUBS, model), LOW)]
        + line_sems(parts)
        + [pltpu.SemaphoreType.DMA((4,))]
        + line_sems(parts * FEED_SUBS)
        + [
            pltpu.VMEM((total, units), LOW),
            pltpu.VMEM((total, 2 * units), LOW),
            pltpu.VMEM((2, 256, units), LOW),
            pltpu.SemaphoreType.DMA((2,)),
        ],
        compiler_params=comm_params(2),
        cost_estimate=cost(18 * total * model * units, 120 * 2**20),
        name="feed",
    )(residual, gain, *weights, out_grad)


class Plain:
    inputs, outputs = 0, 1

    def __init__(self, parts):
        self.parts = parts

    def begin(self, given, scratch):
        greet("tensor", self.parts)

    def tile(self, at, cols, total, given, scratch):
        pass

    def middle(self, given, scratch):
        pass

    def end(self, given, out, scratch):
        pass

    def shapes(self, rows, model):
        return (sds(rows, model),)

    def scratch(self, rows, model):
        return []


def each(total, me, action):
    def body(k, _):
        action(lax.rem(me + k, total))
        return 0

    lax.fori_loop(1, total, body, 0)


class Exchange:
    def __init__(self, axis, total, buf, send_sem, got_sem):
        self.axis, self.total = axis, total
        self.buf, self.send_sem, self.got_sem = buf, send_sem, got_sem

    def copy(self, source, target):
        return pltpu.make_async_remote_copy(
            src_ref=self.buf.at[source],
            dst_ref=self.buf.at[source],
            send_sem=self.send_sem.at[target],
            recv_sem=self.got_sem.at[source],
            device_id={self.axis: target},
            device_id_type=MESH,
        )

    def send(self):
        me = lax.axis_index(self.axis)
        each(self.total, me, lambda other: self.copy(me, other).start())

    def receive(self):
        me = lax.axis_index(self.axis)
        each(self.total, me, lambda other: self.copy(other, me).wait_recv())

    def drain(self):
        me = lax.axis_index(self.axis)
        each(self.total, me, lambda other: self.copy(me, other).wait_send())

    def sum(self, at=slice(None)):
        total = self.buf[0, at]
        for i in range(1, self.total):
            total = total + self.buf[i, at]
        return total


class Closing:
    inputs, outputs = 4, 4

    def __init__(self, count, parts, kept, flat):
        self.count, self.parts, self.kept, self.flat = count, parts, kept, flat

    def stages(self, scratch):
        return (
            Exchange("dp", self.count, *scratch[0:3]),
            Exchange("tensor", self.parts, *scratch[3:6]),
            Exchange("dp", self.count, *scratch[6:9]),
            Exchange("tensor", self.parts, *scratch[9:12]),
        )

    def begin(self, given, scratch):
        dp, z = lax.axis_index("dp"), lax.axis_index("tensor")
        barrier = pltpu.get_barrier_semaphore()

        def hello(axis):
            def one(other):
                pl.semaphore_signal(
                    barrier, inc=1, device_id={axis: other}, device_id_type=MESH
                )

            return one

        each(self.count, dp, hello("dp"))
        each(self.parts, z, hello("tensor"))
        first = self.stages(scratch)[0]
        first.buf[dp] = given[2][...]
        scratch[12][...] = jnp.zeros_like(scratch[12])
        pl.semaphore_wait(barrier, self.count + self.parts - 2)
        first.send()

    def tile(self, at, cols, total, given, scratch):
        terms = total * given[3][at, cols].astype(F32)
        scratch[12][:, cols] += jnp.sum(terms.reshape(terms.shape[0] // 8, 8, -1), axis=0)

    def middle(self, given, scratch):
        dp, z = lax.axis_index("dp"), lax.axis_index("tensor")
        flat_dp, flat_z, gain_dp, gain_z = self.stages(scratch)
        total = jnp.sum(scratch[12][...], axis=0, keepdims=True) / given[1][0:1, :]
        wide = total.shape[1] // 8
        gain_dp.buf[dp] = jnp.concatenate(
            [total[:, i * wide : (i + 1) * wide] for i in range(8)], axis=0
        )
        gain_dp.send()
        flat_dp.receive()
        flat_z.buf[z] = flat_dp.sum()
        flat_z.send()
        gain_dp.receive()
        gain_z.buf[z] = gain_dp.sum()
        gain_z.send()

    def end(self, given, out, scratch):
        tok_ref, gain_ref, flat_ref, _ = given
        out_ref, wide_ref, rest_ref, gain_out = out
        flat_dp, flat_z, gain_dp, gain_z = self.stages(scratch)
        rows, model = out_ref.shape

        def body(i, _):
            at = pl.ds(pl.multiple_of(i * 32, 32), 32)
            values, grad = tok_ref[at, :].astype(F32), out_ref[at, :]
            inv = lax.rsqrt(jnp.mean(values * values, axis=-1, keepdims=True) + epsilon)
            scaled = grad * gain_ref[0:1, :]
            inner = jnp.mean(scaled * values, axis=-1, keepdims=True)
            out_ref[at, :] = inv * scaled - values * (inner * inv * inv * inv)
            return 0

        lax.fori_loop(0, rows // 32, body, 0)
        flat_z.receive()
        width = flat_ref.shape[1]
        for i in range(self.parts):
            wide_ref[:, i * width : (i + 1) * width] = flat_z.buf[i, : self.kept, :]
        rest_ref[...] = flat_z.sum(slice(self.kept, None))
        gain_z.receive()
        gain_out[...] = gain_z.sum()
        for stage in (flat_dp, flat_z, gain_dp, gain_z):
            stage.drain()

    def shapes(self, rows, model):
        height, width = self.flat
        return (
            sds(rows, model), sds(self.kept, width * self.parts), sds(height - self.kept, width),
            sds(8, model // 8),
        )

    def scratch(self, rows, model):
        out = []
        for shape in (self.flat, (8, model // 8)):
            for total in (self.count, self.parts):
                out.append(pltpu.VMEM((total,) + shape, F32))
                out.extend([pltpu.SemaphoreType.DMA((total,))] * 2)
        return out + [pltpu.VMEM((8, model), F32)]


def scatter_kernel(parts, given, count, splits, ending, *refs):
    lefts, rights_in = refs[0:given], refs[given : given + count]
    refs = refs[given + count :]
    extra_in, refs = refs[: ending.inputs], refs[ending.inputs :]
    extra_out, refs = refs[: ending.outputs], refs[ending.outputs :]
    rights, (part, send_r, send_l, got_l, got_r) = refs[0:count], refs[count : count + 5]
    sem_sr, sem_sl, sem_gl, sem_gr, load_sem = refs[count + 5 : count + 10]
    extra = refs[count + 10 :]
    out_ref = extra_out[0]
    me = lax.axis_index("tensor")
    rows, model = out_ref.shape
    size = rows // SUBS
    loads = [
        pltpu.make_async_copy(rights_in[i], rights[i], load_sem.at[i]) for i in range(count)
    ]
    for load in loads:
        load.start()
    ending.begin(extra_in, extra)
    for load in loads:
        load.wait()

    def rightward(slot):
        return pltpu.make_async_remote_copy(
            src_ref=send_r.at[slot],
            dst_ref=got_l.at[slot],
            send_sem=sem_sr.at[slot],
            recv_sem=sem_gl.at[slot],
            device_id={"tensor": me + 1},
            device_id_type=MESH,
        )

    def leftward(slot):
        return pltpu.make_async_remote_copy(
            src_ref=send_l.at[slot],
            dst_ref=got_r.at[slot],
            send_sem=sem_sl.at[slot],
            recv_sem=sem_gr.at[slot],
            device_id={"tensor": me - 1},
            device_id_type=MESH,
        )

    def product(start, many, target):
        at = pl.ds(pl.multiple_of(start, 128), many)

        def body(j, _):
            cols = pl.ds(pl.multiple_of(j * 256, 256), 256)
            total = None
            for i, (index, first, wide) in enumerate(splits):
                term = contract_cols(lefts[index][at, first : first + wide], rights[i][cols, :])
                total = term if total is None else total + term
            target[:, cols] = total
            ending.tile(at, cols, total, extra_in, extra)
            return 0

        lax.fori_loop(0, model // 256, body, 0)

    half = part.at[pl.ds(0, size), :]

    right_first = 2 * me < parts

    def body(item, _):
        step, sub = item // (2 * SUBS), (item // 2) % SUBS
        right = (item % 2 == 0) == right_first
        piece = jnp.where(right, parts - 1 - step, step)
        slot = piece * SUBS + sub
        go_right = right & (piece > me)
        go_left = jnp.logical_not(right) & (piece < me)

        @pl.when(go_right | go_left)
        def _():
            product(piece * rows + sub * size, size, half)

        @pl.when(go_right)
        def _():
            @pl.when(me > 0)
            def _():
                rightward(slot).wait_recv()
                send_r[slot] = (half[...] + got_l[slot].astype(F32)).astype(LOW)

            @pl.when(me == 0)
            def _():
                send_r[slot] = half[...].astype(LOW)

            rightward(slot).start()

        @pl.when(go_left)
        def _():
            @pl.when(me < parts - 1)
            def _():
                leftward(slot).wait_recv()
                send_l[slot] = (half[...] + got_r[slot].astype(F32)).astype(LOW)

            @pl.when(me == parts - 1)
            def _():
                send_l[slot] = half[...].astype(LOW)

            leftward(slot).start()

        return 0

    lax.fori_loop(0, (parts - 1) * SUBS * 2, body, 0)
    product(me * rows, rows, part)
    ending.middle(extra_in, extra)
    for sub in range(SUBS):
        at = slice(sub * size, sub * size + size)
        slot = me * SUBS + sub
        out_ref[at, :] = part[at, :]

        @pl.when(me > 0)
        def _():
            rightward(slot).wait_recv()
            out_ref[at, :] = out_ref[at, :] + got_l[slot].astype(F32)

        @pl.when(me < parts - 1)
        def _():
            leftward(slot).wait_recv()
            out_ref[at, :] = out_ref[at, :] + got_r[slot].astype(F32)

    ending.end(extra_in, extra_out, extra)

    def finish(slot, _):
        piece = slot // SUBS

        @pl.when(piece > me)
        def _():
            rightward(slot).wait_send()

        @pl.when(piece < me)
        def _():
            leftward(slot).wait_send()

        return 0

    lax.fori_loop(0, parts * SUBS, finish, 0)


def scatter(parts, lefts, rights, splits, number, ending=None, extra=()):
    total = lefts[0].shape[0]
    model = rights[0].shape[0]
    rows = total // parts
    count = len(rights)
    ending = ending or Plain(parts)
    slots = pltpu.VMEM((parts * SUBS, rows // SUBS, model), LOW)
    shapes = ending.shapes(rows, model)
    return pl.pallas_call(
        functools.partial(scatter_kernel, parts, len(lefts), count, splits, ending),
        out_shape=shapes,
        in_specs=[vmem()] * len(lefts) + [hbm()] * count + [vmem()] * len(extra),
        out_specs=[vmem()] * len(shapes),
        scratch_shapes=[pltpu.VMEM(w.shape, LOW) for w in rights]
        + [pltpu.VMEM((rows, model), F32)]
        + [slots] * 4
        + line_sems(parts * SUBS)
        + [pltpu.SemaphoreType.DMA((count,))]
        + ending.scratch(rows, model),
        compiler_params=comm_params(number),
        cost_estimate=cost(2 * total * model * sum(w.shape[1] for w in rights), 60 * 2**20),
        name="scatter%d" % number,
    )(*lefts, *rights, *extra)


def state_kernel(count, heads, backward, own_ref, out_ref, buf, send_sem, pass_sem, got_sem):
    me = lax.axis_index("dp")
    core = lax.rem(me, 2)
    sibling = me + 1 - 2 * core
    half = count // 2
    barrier = pltpu.get_barrier_semaphore()

    def peer(k):
        return lax.rem(me + 2 * k, count)

    def hello(k, _):
        pl.semaphore_signal(barrier, inc=1, device_id={"dp": peer(k)}, device_id_type=MESH)
        return 0

    lax.fori_loop(1, half, hello, 0)
    pl.semaphore_signal(barrier, inc=1, device_id={"dp": sibling}, device_id_type=MESH)
    buf[me] = own_ref[...].astype(LOW)
    pl.semaphore_wait(barrier, half)

    def needed(source, target):
        return source > target if backward else source < target

    def copy(piece, target, sem):
        return pltpu.make_async_remote_copy(
            src_ref=buf.at[piece],
            dst_ref=buf.at[piece],
            send_sem=sem,
            recv_sem=got_sem.at[piece],
            device_id={"dp": target},
            device_id_type=MESH,
        )

    def send(k, _):
        target = peer(k)

        @pl.when(needed(me, target))
        def _():
            copy(me, target, send_sem.at[target]).start()

        return 0

    @pl.when(needed(me, sibling))
    def _():
        copy(me, sibling, pass_sem.at[me]).start()

    lax.fori_loop(1, half, send, 0)

    def relay(k, _):
        source = lax.rem(me + count - 2 * k, count)

        @pl.when(needed(source, me))
        def _():
            copy(source, me, send_sem.at[source]).wait_recv()

        @pl.when(needed(source, me) & needed(source, sibling))
        def _():
            copy(source, sibling, pass_sem.at[source]).start()

        return 0

    lax.fori_loop(1, half, relay, 0)
    for h in range(heads):
        out_ref[h] = jnp.zeros_like(out_ref[h])

    def chain(step, _):
        piece = count - 1 - step if backward else step

        @pl.when(needed(piece, me) & (lax.rem(piece, 2) != core))
        def _():
            copy(piece, me, pass_sem.at[piece]).wait_recv()

        @pl.when(needed(piece, me))
        def _():
            for h in range(heads):
                both = buf[piece, h].astype(F32)
                if backward:
                    out_ref[h] = mm(both[:, 128:], out_ref[h], TN) + both[:, :128]
                else:
                    out_ref[h] = mm(both[:, 128:], out_ref[h]) + both[:, :128]

        return 0

    lax.fori_loop(0, count, chain, 0)

    def finish(k, _):
        target = peer(k)
        source = lax.rem(me + count - 2 * k, count)

        @pl.when(needed(me, target))
        def _():
            copy(me, target, send_sem.at[target]).wait_send()

        @pl.when(needed(source, me) & needed(source, sibling))
        def _():
            copy(source, sibling, pass_sem.at[source]).wait_send()

        return 0

    lax.fori_loop(1, half, finish, 0)

    @pl.when(needed(me, sibling))
    def _():
        copy(me, sibling, pass_sem.at[me]).wait_send()


def exchange(count, own, heads, backward, number):
    return pl.pallas_call(
        functools.partial(state_kernel, count, heads, backward),
        out_shape=sds(heads, 128, 128),
        in_specs=[vmem()],
        out_specs=vmem(),
        scratch_shapes=[pltpu.VMEM((count, heads, 128, 256), LOW)]
        + [pltpu.SemaphoreType.DMA((count,))] * 3,
        compiler_params=comm_params(number),
        cost_estimate=cost(count * heads * 6 * 128**3, count * heads * 256 * 128 * 4),
        name="exchange%d" % number,
    )(own)


def after(values, *first):
    out = lax.optimization_barrier((values,) + first)
    return out[0]


def local(
    tokens,
    gain_in,
    w_query,
    w_key,
    w_value,
    w_alpha,
    w_beta,
    w_gate_out,
    conv_query,
    conv_key,
    conv_value,
    decay_log,
    decay_bias,
    head_gain,
    w_out,
    gain_mid,
    w_gate,
    w_up,
    w_down,
    out_grad,
    doc_lengths,
):
    rows_own, model = tokens.shape
    tensor_parts, dp_parts = lax.axis_size("tensor"), lax.axis_size("dp")
    tensor_index, dp_index = lax.axis_index("tensor"), lax.axis_index("dp")
    group_rows = rows_own * tensor_parts
    seq_total = group_rows * dp_parts
    heads = w_alpha.shape[1]
    width = w_query.shape[1]
    core = lax.rem(dp_index, 2)
    docs = doc_lengths.shape[0] * doc_lengths.shape[1]
    starts = (
        jnp.cumsum(doc_lengths, axis=1)
        - doc_lengths
        + seq_total * lax.broadcasted_iota(jnp.int32, doc_lengths.shape, 0)
    ).reshape(-1)
    scalars = jnp.concatenate([(dp_index * group_rows).reshape(1), starts, core.reshape(1)]).astype(jnp.int32)
    taps = jnp.concatenate([conv_query, conv_key, conv_value, jnp.zeros((4, width), F32)])
    params = jnp.zeros((8, 128), F32).at[0, :heads].set(decay_bias).at[1, :heads].set(decay_log)
    gain_heads = jnp.broadcast_to(head_gain[None], (8, width))
    w_narrow = jnp.pad(jnp.concatenate([w_alpha, w_beta], axis=1), ((0, 0), (0, 128 - 2 * heads)))

    own_rows = tokens.astype(F32)
    gain_in_rows = gain_in[None]
    gain_mid_rows = gain_mid[None]
    normed_all, *pieces, gate_raw, narrow, rims = project(
        tensor_parts, tokens, gain_in_rows, w_narrow, (w_query, w_key, w_value, w_gate_out)
    )
    half = width // 2
    out_half = lax.dynamic_slice_in_dim(after(w_out, narrow), core * half, half, 0)
    out_mine = lax.all_gather(out_half, "tensor", axis=0)
    forth = [(i, i + 1) for i in range(dp_parts - 1)]
    rims = lax.ppermute(rims, "dp", forth)
    rims = [rims[i] for i in range(3)]
    x, p, kg, w, u, qt, ou, t, o, totals = intra(
        scalars, pieces, rims, narrow, taps, params, docs, heads
    )
    state_in = exchange(dp_parts, totals, heads, False, 3)
    rows_out, v2, s, mixed = outward(state_in, w, u, qt, ou, t, o, gate_raw, gain_heads, heads)

    mixed_all = lax.all_to_all(
        mixed.reshape(tensor_parts, rows_own, width), "tensor", split_axis=0, concat_axis=0, tiled=True
    )
    out_mine, _ = lax.optimization_barrier((out_mine, mixed))
    out_other = lax.ppermute(out_mine, "dp", [(i, i ^ 1) for i in range(dp_parts)])

    def of_core(index, weight):
        return lax.dot_general(
            lax.dynamic_slice_in_dim(mixed_all, index * half, half, 2), weight,
            (((0, 2), (0, 1)), ((), ())), preferred_element_type=F32,
        )

    residual = own_rows + (of_core(core, out_mine) + of_core(1 - core, out_other))
    mlp_part, grad_mid, units_grad = feed(
        tensor_parts, residual, gain_mid_rows, (w_gate, w_up, w_down), out_grad
    )
    units = w_gate.shape[1]
    right = [(i, (i + 1) % tensor_parts) for i in range(tensor_parts)]
    left = [(i, (i - 1) % tensor_parts) for i in range(tensor_parts)]

    def part_for(values, ahead):
        index = lax.rem(tensor_index + ahead + tensor_parts, tensor_parts)
        return lax.dynamic_slice_in_dim(values, index * rows_own, rows_own, 0)

    units_grad_sum = lax.psum_scatter(units_grad, "dp", scatter_dimension=0, tiled=True)
    grad_res_norm, gain_mid_grad = norm_back(residual, gain_mid, grad_mid)
    grad_own = lax.dynamic_slice_in_dim(out_grad, tensor_index * rows_own, rows_own, 0)
    grad_residual = grad_own.astype(F32) + grad_res_norm
    grad_mixer = grad_residual.astype(LOW)
    grad_mixed = jnp.concatenate(
        [
            lax.dot_general(
                grad_mixer, weight, (((1,), (2,)), ((), ())),
                preferred_element_type=F32,
            ).astype(LOW).swapaxes(0, 1)
            for weight in (out_mine, out_other)
        ],
        axis=2,
    )
    grad_mixed = lax.all_to_all(
        grad_mixed, "tensor", split_axis=0, concat_axis=0, tiled=True
    ).reshape(group_rows, width)
    mlp_late = after(mlp_part, grad_mixed)
    mlp_run = part_for(mlp_late, tensor_parts - 2)
    for ahead in range(tensor_parts - 2, 1, -1):
        mlp_run = lax.ppermute(mlp_run, "tensor", right)
        if ahead > 2:
            mlp_run = (mlp_run.astype(F32) + part_for(mlp_part, ahead - 1).astype(F32)).astype(LOW)
    mlp_left = lax.ppermute(part_for(mlp_late, -1), "tensor", left)
    mixed_own = mixed_all.swapaxes(0, 1).reshape(rows_own, -1)
    out_w = contract_rows(grad_mixer, mixed_own).astype(LOW)
    out_w_sum = lax.psum_scatter(out_w, "dp", scatter_dimension=0, tiled=True)
    do, gate_low, head_gain_part, ds_total = inward(
        scalars, grad_mixed, rows_out, gate_raw, gain_heads, qt, t, totals, heads
    )
    grad_end = exchange(dp_parts, ds_total, heads, True, 5)
    grad_end, mlp_run = lax.optimization_barrier((grad_end, mlp_run))
    mlp_right = lax.ppermute(
        (mlp_run.astype(F32) + part_for(mlp_part, 1).astype(F32)).astype(LOW), "tensor", right
    )
    grads, tails, rim_grad, taps_grad, params_grad = back(
        scalars, pieces, rims, narrow, taps, params, grad_end, do, v2, s, x, p, kg, w, u, qt, t,
        gate_low, docs, heads,
    )
    grads, tails, rim_grad, taps_grad, params_grad, mlp_right, mlp_left, units_grad_sum = (
        lax.optimization_barrier(
            (grads, tails, rim_grad, taps_grad, params_grad, mlp_right, mlp_left, units_grad_sum)
        )
    )
    rim_back = lax.ppermute(rim_grad, "dp", [(i + 1, i) for i in range(dp_parts - 1)])
    tails = tails.at[HALO - 8 :].add(rim_back).astype(LOW)
    grads = lax.dynamic_update_slice(grads, tails, (group_rows - HALO, 0))
    mixer_grad = contract_rows(normed_all, grads).astype(LOW)
    mixer_sum = lax.psum_scatter(mixer_grad, "dp", scatter_dimension=0, tiled=True).astype(F32)
    params_grad = params_grad.reshape(2, 8, 128).sum(1)
    flat = jnp.concatenate(
        [
            taps_grad.sum(1),
            head_gain_part.sum(0)[None],
            jnp.pad(params_grad, ((0, 1), (0, width - 128))),
            jnp.pad(gain_mid_grad.reshape(-1, width), ((0, 4), (0, 0))),
        ],
        axis=0,
    )
    grad_tokens, wide, rest, gain_in_grad = scatter(
        tensor_parts, [after(grads, mixer_grad)],
        [w_query, w_key, w_value, w_narrow, w_gate_out],
        ((0, 0, width), (0, width, width), (0, 2 * width, width), (0, 3 * width, 128), (0, 3 * width + 128, width)),
        6, Closing(dp_parts, tensor_parts, 16, flat.shape),
        (tokens, gain_in_rows, flat, normed_all),
    )
    out_w_dp, units_grad_sum, mlp_right, mlp_left, _ = lax.optimization_barrier(
        (out_w_sum, units_grad_sum, mlp_right, mlp_left, gain_in_grad)
    )
    out_pieces = [
        lax.dynamic_slice_in_dim(
            out_w_dp, lax.rem(tensor_index + ahead, tensor_parts) * width, width, 1
        )
        for ahead in range(tensor_parts)
    ]
    wide, rest, units_grad_sum, mlp_right, *out_pieces = lax.optimization_barrier(
        (wide, rest, units_grad_sum, mlp_right, *out_pieces)
    )
    for ahead in range(1, tensor_parts):
        shift = [(i, (i + ahead) % tensor_parts) for i in range(tensor_parts)]
        out_pieces[ahead] = lax.ppermute(out_pieces[ahead], "tensor", shift)
    output = residual + part_for(mlp_part, 0).astype(F32)
    output = (output + (mlp_right.astype(F32) + mlp_left.astype(F32))).astype(LOW)
    start = 3 * width
    ready = [
        output,
        grad_residual + grad_tokens,
        mixer_sum[:, :width],
        mixer_sum[:, width : 2 * width],
        mixer_sum[:, 2 * width : start],
        mixer_sum[:, start : start + heads],
        mixer_sum[:, start + heads : start + 2 * heads],
        mixer_sum[:, start + 128 :],
        units_grad_sum[:, :units].astype(F32),
        units_grad_sum[:, units : 2 * units].astype(F32),
        units_grad_sum[:, 2 * units :].T.astype(F32),
    ]
    out_w_sum = sum(piece.astype(F32) for piece in out_pieces)
    by_head = wide[13:15].reshape(2, tensor_parts, width)[:, :, :heads].reshape(2, -1)
    return (
        ready[0],
        ready[1],
        gain_in_grad.reshape(model),
        *ready[2:8],
        wide[0:4],
        wide[4:8],
        wide[8:12],
        by_head[1],
        by_head[0],
        wide[12],
        out_w_sum.T,
        rest[: model // width].reshape(model),
        *ready[8:11],
    )


def solution(mesh):
    placed = (
        P(("dp", "tensor"), None),
        P(),
        P(None, "tensor"),
        P(None, "tensor"),
        P(None, "tensor"),
        P(None, "tensor"),
        P(None, "tensor"),
        P(None, "tensor"),
        P(None, "tensor"),
        P(None, "tensor"),
        P(None, "tensor"),
        P("tensor"),
        P("tensor"),
        P("tensor"),
        P("tensor", None),
        P(),
        P(None, "tensor"),
        P(None, "tensor"),
        P("tensor", None),
        P("dp", None),
        P(),
    )
    return jax.shard_map(
        local,
        mesh=mesh,
        in_specs=placed,
        out_specs=(
            P(("dp", "tensor"), None),
            P(("dp", "tensor"), None),
            P(),
            P("dp", "tensor"),
            P("dp", "tensor"),
            P("dp", "tensor"),
            P("dp", "tensor"),
            P("dp", "tensor"),
            P("dp", "tensor"),
            P(),
            P(),
            P(),
            P(),
            P(),
            P(),
            P("tensor", "dp"),
            P(),
            P("dp", "tensor"),
            P("dp", "tensor"),
            P("tensor", "dp"),
        ),
        check_vma=False,
    )
```
